32 devices in a mesh: shard: 2 (over core), rep: 16 (over z, y, x).
Axes of the slice: x: 2, y: 2, z: 4, core: 2. Of those that a mesh axis runs over, the one named last changes fastest.
Arguments:
- tokens: bfloat16 [128, 512, 768], P(('shard', 'rep')), may hold values from -6 to 6
- teacher: bfloat16 [128, 512, 768], P(('shard', 'rep')), may hold values from -6 to 6
- block_ids: int32 [128, 512], P(('shard', 'rep')), may hold values from 0 to 3, never falling along the last dimension, each value on 1 to 256 neighbouring positions
- qkv_weight: bfloat16 [768, 2304], P('shard'), may hold values from -0.21875 to 0.21875
- out_weight: bfloat16 [768, 768], P('shard'), may hold values from -0.875 to 0.875
- up_weight: bfloat16 [768, 3072], P('shard'), may hold values from -0.21875 to 0.21875
- down_weight: bfloat16 [3072, 768], P('shard'), may hold values from -0.109375 to 0.109375
- biases: bfloat16 [768, 4], P('shard'), may hold values from -1.5 to 1.5
- hidden_bias: bfloat16 [3072], P('shard'), may hold values from -1.5 to 1.5
- norm_gain: bfloat16 [768, 2], P('shard'), may hold values from 0.25 to 1.75
- norm_shift: bfloat16 [768, 2], P('shard'), may hold values from -1.5 to 1.5
Outputs:
- layer_out: bfloat16 [128, 512, 768], P(('shard', 'rep'))
- token_grad: float32 [128, 512, 768], P(('shard', 'rep'))
- qkv_grad: float32 [768, 2304], P('shard')
- out_grad: float32 [768, 768], P('shard')
- up_grad: float32 [768, 3072], P('shard')
- down_grad: float32 [3072, 768], P('shard')
- bias_grad: float32 [768, 4], P('shard')
- hidden_grad: float32 [3072], P('shard')
- gain_grad: float32 [768, 2], P('shard')
- shift_grad: float32 [768, 2], P('shard')
The draws below stay inside these ranges and needn't reach their ends.
Inputs may be any that keep to these rules, and one draw needn't show every extreme that they name: `block_ids`: along each sequence the block ids never fall; each block has 1 to 256 tokens and some block has exactly 256.
All inputs are finite; a program needn't handle non-finite values.
Results may differ from the reference program's by a relative error of at most 0.01.
Values may be sent and summed in bfloat16 or wider, within the bound.
A program may use at most 384 MiB of HBM per device.

```python
import math
import jax
import jax.numpy as jnp
import numpy as np
from jax import lax

D = 768
FF = 3072
HEAD_DIM = 64
LEN = 512
BLK = 256
SEGS = 4
SEQS = 128


def level_of(own_key, extent, cuts, least, largest):
    loudness = 1.0
    for position, parts in cuts:
        heights = jax.random.uniform(jax.random.fold_in(jax.random.fold_in(own_key, 6), position), (parts,), jnp.float32, least / len(cuts), largest / len(cuts))
        loudness = loudness * jnp.repeat(jnp.exp(heights), extent[position] // parts).reshape((-1,) + (1,) * (len(extent) - 1 - position))
    return loudness


def length_profile(count, total, limit, lean):
    weights = [(1 << 20) // math.isqrt(grade ** lean) + 1 for grade in range(2, count + 1)]
    rest, holding = total - limit - (count - 1), [1] * (count - 1)
    while rest > 0:
        candidates = [i for i in range(count - 1) if holding[i] < limit]
        whole, budget = sum([weights[i] for i in candidates]), rest
        for i in candidates:
            extra = min(limit - holding[i], max(1, budget * weights[i] // whole), rest)
            holding[i] = holding[i] + extra
            rest = rest - extra
    return np.array([limit] + holding)


def uneven_parts(stream_key, count, total, limit, skew):
    if count == 2:
        one = jax.random.randint(stream_key, (), max(1, total - limit), min(limit, total - 1) + 1)
        return jnp.stack([one, total - one])
    lengths = jnp.asarray(length_profile(count, total, limit, skew), jnp.int32)
    twos = (count - 1) // 2
    giver, taker = lengths[1:1 + 2 * twos:2], lengths[2:2 + 2 * twos:2]
    room = jnp.minimum(giver - 1, limit - taker)
    moved = jax.random.randint(jax.random.fold_in(stream_key, 1), (twos,), 0, 1 << 20) % (room + 1)
    lengths = lengths.at[1:1 + 2 * twos:2].set(giver - moved).at[2:2 + 2 * twos:2].set(taker + moved)
    return lengths[jax.random.permutation(jax.random.fold_in(stream_key, 2), count)]


def normal_values(key, dims, deviation, reach, split=(), held_as=jnp.bfloat16):
    result = deviation * jax.random.normal(key, dims, jnp.float32)
    if split:
        result = result * level_of(key, dims, split, -0.22, 0.18)
    return jnp.clip(result, -reach, reach).astype(held_as)


def setup_inputs(seed: int = 0) -> dict:
    key_list = jax.random.split(jax.random.key(seed), 12)
    return {
        "tokens": normal_values(key_list[0], (SEQS, LEN, D), 1.0, 6.0, ((0, 32),)),
        "teacher": normal_values(key_list[1], (SEQS, LEN, D), 1.0, 6.0, ((0, 32),)),
        "block_ids": jax.vmap(lambda own: jnp.searchsorted(jnp.cumsum(uneven_parts(own, SEGS, LEN, BLK, 1)), jnp.arange(LEN), side="right"))(jax.random.split(key_list[2], SEQS)).reshape((SEQS, LEN)).astype(jnp.int32),
        "qkv_weight": normal_values(key_list[3], (D, 3 * D), D ** -0.5, 0.21875, ((0, 2),)),
        "out_weight": normal_values(key_list[4], (D, D), (D // 16) ** -0.5, 0.875, ((0, 2),)),
        "up_weight": normal_values(key_list[5], (D, FF), D ** -0.5, 0.21875, ((0, 2),)),
        "down_weight": normal_values(key_list[6], (FF, D), FF ** -0.5, 0.109375, ((0, 2),)),
        "biases": normal_values(key_list[7], (D, 4), 0.3, 1.5, ((0, 2),)),
        "hidden_bias": normal_values(key_list[8], (FF,), 0.3, 1.5, ((0, 2),)),
        "norm_gain": jnp.clip(1.0 + 0.15 * jax.random.normal(key_list[9], (D, 2), jnp.float32), 0.25, 1.75).astype(jnp.bfloat16),
        "norm_shift": normal_values(key_list[10], (D, 2), 0.3, 1.5, ((0, 2),)),
    }


@jax.custom_vjp
def low(v):
    return lax.optimization_barrier(v.astype(jnp.bfloat16)).astype(jnp.float32)

@jax.custom_vjp
def low_back(v):
    return v

def low_keep(v):
    return (low(v), None)

def low_pass(kept, grad):
    return (grad,)

def back_keep(v):
    return (v, None)

def back_low(kept, grad):
    return (low(grad),)
low.defvjp(low_keep, low_pass)
low_back.defvjp(back_keep, back_low)
EPS = 1e-05

def binarize(latent):
    matrix = latent.astype(jnp.float32)
    scales = lax.optimization_barrier(jnp.mean(jnp.abs(matrix), axis=0))
    signed = jnp.where(matrix >= 0, 1.0, -1.0).astype(jnp.float32)
    return (scales * signed).astype(jnp.bfloat16).astype(jnp.float32)

def layer_norm(resid, gain, shift):
    center = resid - lax.optimization_barrier(jnp.mean(resid, axis=-1, keepdims=True))
    spread = lax.optimization_barrier(jnp.mean(center * center, axis=-1, keepdims=True))
    return center * lax.rsqrt(spread + EPS) * gain + shift

def product(left, right, form):
    return jnp.einsum(form, left, right, precision=lax.Precision.HIGHEST)

def forward(inputs, blocks, qkv_bin, out_bin, up_bin, down_bin, biases, hidden_bias, gains, shifts):
    group, length, width = inputs.shape
    heads = width // HEAD_DIM
    joined = low_back(product(inputs, qkv_bin, 'gld,de->gle'))
    query_low = low(joined[..., :width] + biases[:, 0]).reshape(group, length, heads, HEAD_DIM)
    key_low = low(joined[..., width:2 * width]).reshape(group, length, heads, HEAD_DIM)
    value_low = low(joined[..., 2 * width:] + biases[:, 1]).reshape(group, length, heads, HEAD_DIM)
    scores = low_back(product(query_low, key_low, 'gqhd,gkhd->ghqk') * HEAD_DIM ** (-0.5))
    allowed = (blocks[:, :, None] >= blocks[:, None, :])[:, None]
    scores = jnp.where(allowed, scores, -1e+30)
    shifted = jnp.exp(scores - lax.optimization_barrier(jnp.max(scores, axis=-1, keepdims=True)))
    probs = low(shifted / lax.optimization_barrier(jnp.sum(shifted, axis=-1, keepdims=True)))
    context = low_back(low(product(probs, value_low, 'ghqk,gkhd->gqhd'))).reshape(group, length, width)
    attended = low_back(product(context, out_bin, 'gld,de->gle')) + biases[:, 2]
    first = layer_norm(inputs + attended, gains[:, 0], shifts[:, 0])
    pre_act = low_back(product(low(first), up_bin, 'gld,df->glf')) + hidden_bias
    hidden = low(jax.nn.gelu(pre_act, approximate=False))
    mixed = low_back(product(hidden, down_bin, 'glf,fd->gld')) + biases[:, 3]
    return layer_norm(first + mixed, gains[:, 1], shifts[:, 1])

def reference(tokens, teacher, block_ids, qkv_weight, out_weight, up_weight, down_weight, biases, hidden_bias, norm_gain, norm_shift):
    weights = (binarize(qkv_weight), binarize(out_weight), binarize(up_weight), binarize(down_weight), biases.astype(jnp.float32), hidden_bias.astype(jnp.float32), norm_gain.astype(jnp.float32), norm_shift.astype(jnp.float32))
    group = 2
    inputs = tokens.astype(jnp.float32).reshape(SEQS // group, group, LEN, D)
    targets = teacher.astype(jnp.float32).reshape(SEQS // group, group, LEN, D)
    blocks = block_ids.reshape(SEQS // group, group, LEN)

    def step(totals, item):
        inputs_now, target_now, blocks_now = item

        def run(inputs_arg, *weight_args):
            return forward(inputs_arg, blocks_now, *weight_args)
        final, pull = jax.vjp(run, inputs_now, *weights)
        grads = pull(final - target_now)
        totals = tuple((earlier + later for earlier, later in zip(totals, grads[1:])))
        return (totals, (final.astype(jnp.bfloat16), grads[0]))
    zeros = tuple((jnp.zeros_like(weight) for weight in weights))
    totals, (finals, token_grads) = lax.scan(step, zeros, (inputs, targets, blocks))
    return (finals.reshape(SEQS, LEN, D), token_grads.reshape(SEQS, LEN, D), totals[0], totals[1], totals[2], totals[3], totals[4], totals[5], totals[6], totals[7])
```

```python
import functools

import jax
import jax.numpy as jnp
from jax import lax
from jax.experimental import pallas as pl
from jax.experimental.pallas import tpu as pltpu
from jax.sharding import PartitionSpec as P

HEAD_DIM = 64
EPS = 1e-05
NEG = -1e30
BF = jnp.bfloat16
F32 = jnp.float32
MB = 1 << 20


def params(mb=56, **kw):
    return pltpu.CompilerParams(vmem_limit_bytes=mb * MB, **kw)


def dot(a, b):
    return jnp.dot(a, b, preferred_element_type=F32)


def dot_nt(a, b):
    return lax.dot_general(a, b, (((1,), (1,)), ((), ())), preferred_element_type=F32)


def dot_tn(a, b):
    return lax.dot_general(a, b, (((0,), (0,)), ((), ())), preferred_element_type=F32)


def full(shape):
    return pl.BlockSpec(shape, lambda *_: (0,) * len(shape))


def cost(flops, nbytes, trans=0):
    return pl.CostEstimate(flops=int(flops), bytes_accessed=int(nbytes), transcendentals=int(trans))


def binary_halves(first, second):
    rows = 2 * first.shape[0]
    total = jnp.sum(jnp.abs(first.astype(F32)), axis=0, keepdims=True) + jnp.sum(
        jnp.abs(second.astype(F32)), axis=0, keepdims=True
    )
    scale = (total / rows).astype(BF)
    return (
        jnp.where(first >= 0, scale, -scale).astype(BF),
        jnp.where(second >= 0, scale, -scale).astype(BF),
    )


def prep_qkv_kernel(core_ref, own_ref, other_ref, small_own_ref, small_other_ref, out_ref, small_ref):
    core = core_ref[0]
    half = own_ref.shape[0]
    own_at = pl.multiple_of(core * half, half)
    other_at = pl.multiple_of((1 - core) * half, half)
    own, other = binary_halves(own_ref[...], other_ref[...])
    out_ref[pl.ds(own_at, half), :] = own
    out_ref[pl.ds(other_at, half), :] = other

    @pl.when(pl.program_id(0) == 0)
    def _():
        small_ref[:, pl.ds(own_at, half)] = small_own_ref[...].astype(F32)
        small_ref[:, pl.ds(other_at, half)] = small_other_ref[...].astype(F32)


def prep_qkv(core, own, other, small_own, small_other):
    half, cols = own.shape
    rows = 2 * half
    step = rows
    return pl.pallas_call(
        prep_qkv_kernel,
        grid_spec=pltpu.PrefetchScalarGridSpec(
            num_scalar_prefetch=1,
            grid=(cols // step,),
            in_specs=[
                pl.BlockSpec((half, step), lambda j, c: (0, j)),
                pl.BlockSpec((half, step), lambda j, c: (0, j)),
                full(small_own.shape),
                full(small_own.shape),
            ],
            out_specs=[
                pl.BlockSpec((rows, step), lambda j, c: (0, j)),
                full((small_own.shape[0], rows)),
            ],
        ),
        out_shape=[
            jax.ShapeDtypeStruct((rows, cols), BF),
            jax.ShapeDtypeStruct((small_own.shape[0], rows), F32),
        ],
        compiler_params=params(),
        cost_estimate=cost(4 * rows * cols, 4 * rows * cols),
        name="prep_qkv",
    )(core, own, other, small_own, small_other)


def prep_rest_kernel(core_ref, out_a, out_b, up_a, up_b, dn_a, dn_b, out_ref, up_ref, dn_ref):
    core = core_ref[0]
    half = out_a.shape[0]
    width = 2 * half
    own_at = pl.multiple_of(core * half, half)
    other_at = pl.multiple_of((1 - core) * half, half)
    own, other = binary_halves(out_a[...], out_b[...])
    out_ref[pl.ds(own_at, half), :] = own
    out_ref[pl.ds(other_at, half), :] = other
    hidden = up_a.shape[1]
    chunks = hidden // width
    for j in range(hidden // half):
        own, other = binary_halves(up_a[:, j * half : (j + 1) * half], up_b[:, j * half : (j + 1) * half])
        at = (j % chunks) * width + (j // chunks) * half
        up_ref[pl.ds(own_at, half), at : at + half] = own
        up_ref[pl.ds(other_at, half), at : at + half] = other
    own, other = binary_halves(dn_a[...], dn_b[...])
    for c in range(chunks):
        dn_ref[pl.ds(pl.multiple_of(c * width + own_at, half), half), :] = own[c * half : (c + 1) * half]
        dn_ref[pl.ds(pl.multiple_of(c * width + other_at, half), half), :] = other[c * half : (c + 1) * half]


def prep_rest(core, out_a, out_b, up_a, up_b, dn_a, dn_b):
    half, width = out_a.shape
    hidden = up_a.shape[1]
    vm = pl.BlockSpec(memory_space=pltpu.VMEM)
    return pl.pallas_call(
        prep_rest_kernel,
        in_specs=[pl.BlockSpec(memory_space=pltpu.SMEM)] + [vm] * 6,
        out_specs=[vm] * 3,
        out_shape=[
            jax.ShapeDtypeStruct((width, width), BF),
            jax.ShapeDtypeStruct((width, hidden), BF),
            jax.ShapeDtypeStruct((hidden, width), BF),
        ],
        compiler_params=params(),
        cost_estimate=cost(8 * width * hidden, 8 * width * hidden),
        name="prep_rest",
    )(core, out_a, out_b, up_a, up_b, dn_a, dn_b)


def attend_kernel(
    tokens_ref, rows_ref, cols_ref, qkv_ref, out_ref, small_ref, joined_ref, ctx_ref, lse_ref, norm_ref, inv_ref,
    bias_ref,
):
    length, width = tokens_ref.shape[1:]
    x = tokens_ref[0]
    for part, bias_row in ((0, 0), (1, None), (2, 1)):
        joined = dot(x, qkv_ref[:, part * width : (part + 1) * width])
        if bias_row is not None:
            joined = joined + small_ref[bias_row : bias_row + 1, :]
        joined_ref[0, :, part * width : (part + 1) * width] = joined.astype(BF)
    bias_ref[...] = jnp.where(cols_ref[0] >= rows_ref[0], 0.0, NEG).astype(F32)
    lane = lax.broadcasted_iota(jnp.int32, (length, 128), 1)
    low = lane < HEAD_DIM
    lse_all = jnp.zeros((length, 128), F32)
    tile = min(TILE_F, length)
    for pair in range(width // 128):
        q2 = joined_ref[0, :, pair * 128 : pair * 128 + 128] * BF(0.125)
        k2 = joined_ref[0, :, width + pair * 128 : width + pair * 128 + 128]
        v2 = joined_ref[0, :, 2 * width + pair * 128 : 2 * width + pair * 128 + 128]
        for t in range(length // tile):
            rows = slice(t * tile, (t + 1) * tile)
            parts = []
            for h in range(2):
                mine = low[rows] if h == 0 else ~low[rows]
                qm = jnp.where(mine, q2[rows], BF(0))
                scores = dot_nt(qm, k2) + bias_ref[rows, :]
                peak = jnp.max(scores, axis=-1, keepdims=True)
                raised = jnp.exp(scores - peak)
                total = jnp.sum(raised, axis=-1, keepdims=True)
                parts.append(dot(raised.astype(BF), v2) / total)
                lse_ref_col = peak + jnp.log(total)
                bias_lane = lane[rows] == 2 * pair + h
                lse_cols = jnp.where(bias_lane, lse_ref_col, 0.0)
                if h == 0:
                    pair_lse = lse_cols
                else:
                    pair_lse = pair_lse + lse_cols
            ctx_ref[0, rows, pair * 128 : pair * 128 + 128] = jnp.where(low[rows], parts[0], parts[1]).astype(BF)
            if t == 0:
                tiles_lse = [pair_lse]
            else:
                tiles_lse.append(pair_lse)
        lse_all = lse_all + jnp.concatenate(tiles_lse, axis=0)
    lse_ref[0] = lse_all.T[0:16, :]
    resid = x.astype(F32) + dot(ctx_ref[0], out_ref[...]) + small_ref[2:3, :]
    center = resid - jnp.mean(resid, axis=-1, keepdims=True)
    inverse = lax.rsqrt(jnp.mean(center * center, axis=-1, keepdims=True) + EPS)
    norm_ref[0] = center * inverse
    inv_ref[0] = inverse


TILE_F = 256


def attend(tokens, block_ids, qkv_bin, out_bin, small):
    seqs, length, width = tokens.shape
    rows = block_ids.reshape(seqs, 1, length)
    cols = block_ids.reshape(seqs, length, 1)
    per_seq = lambda *shape: pl.BlockSpec((1,) + shape, lambda s: (s,) + (0,) * len(shape))
    return pl.pallas_call(
        attend_kernel,
        grid=(seqs,),
        in_specs=[
            per_seq(length, width),
            per_seq(1, length),
            per_seq(length, 1),
            full(qkv_bin.shape),
            full(out_bin.shape),
            full(small.shape),
        ],
        out_specs=[
            per_seq(length, 3 * width),
            per_seq(length, width),
            per_seq(16, length),
            per_seq(length, width),
            per_seq(length, 1),
        ],
        out_shape=[
            jax.ShapeDtypeStruct((seqs, length, 3 * width), BF),
            jax.ShapeDtypeStruct((seqs, length, width), BF),
            jax.ShapeDtypeStruct((seqs, 16, length), F32),
            jax.ShapeDtypeStruct((seqs, length, width), F32),
            jax.ShapeDtypeStruct((seqs, length, 1), F32),
        ],
        scratch_shapes=[pltpu.VMEM((length, length), F32)],
        compiler_params=params(),
        cost_estimate=cost(seqs * length * width * (8 * width + 16 * length), 30 * seqs * length * width),
        name="attend",
    )(tokens, rows, cols, qkv_bin, out_bin, small)


def gelu_pair(u):
    cdf = 0.5 + 0.5 * lax.erf(u * 0.7071067811865476)
    density = jnp.exp(-0.5 * u * u) * 0.3989422804014327
    return u * cdf, cdf + u * density


def norm_back(upstream, normed, inverse, gain):
    scaled = upstream * gain
    weighted = upstream * normed
    centered = (
        scaled
        - jnp.mean(scaled, axis=-1, keepdims=True)
        - normed * jnp.mean(weighted * gain, axis=-1, keepdims=True)
    )
    return centered * inverse, jnp.sum(weighted, axis=0, keepdims=True), jnp.sum(upstream, axis=0, keepdims=True)


def feed_kernel(
    norm_ref, teacher_ref, small_ref, up_ref, dn_ref,
    final_ref, first_low_ref, hidden_ref, slope_ref, second_ref, mixed_ref, sums_ref,
):
    width = norm_ref.shape[2]
    first = norm_ref[0] * small_ref[4:5, :] + small_ref[6:7, :]
    first_low = first.astype(BF)
    first_low_ref[0] = first_low
    acc = first + small_ref[3:4, :]
    for c in range(up_ref.shape[1] // width):
        cols = slice(c * width, (c + 1) * width)
        pre = dot(first_low, up_ref[:, cols]) + small_ref[8 + c : 9 + c, :]
        value, slope = gelu_pair(pre)
        value = value.astype(BF)
        hidden_ref[0, :, cols] = value
        slope_ref[0, :, cols] = slope.astype(BF)
        acc = acc + dot(value, dn_ref[cols, :])
    center = acc - jnp.mean(acc, axis=-1, keepdims=True)
    inverse = lax.rsqrt(jnp.mean(center * center, axis=-1, keepdims=True) + EPS)
    normed = center * inverse
    gain = small_ref[5:6, :]
    final = normed * gain + small_ref[7:8, :]
    final_ref[0] = final.astype(BF)
    upstream = final - teacher_ref[0].astype(F32)
    second, gain_sum, shift_sum = norm_back(upstream, normed, inverse, gain)
    second_ref[0] = second
    mixed_ref[0] = second.astype(BF)

    @pl.when(pl.program_id(0) == 0)
    def _():
        sums_ref[...] = jnp.zeros_like(sums_ref)

    sums_ref[0:1, :] += gain_sum
    sums_ref[1:2, :] += shift_sum
    sums_ref[2:3, :] += jnp.sum(second, axis=0, keepdims=True)


def feed(norm, teacher, small, up_bin, dn_bin):
    seqs, length, width = norm.shape
    hidden = up_bin.shape[1]
    per_seq = lambda *shape: pl.BlockSpec((1,) + shape, lambda s: (s,) + (0,) * len(shape))
    like = lambda n, dt: jax.ShapeDtypeStruct((seqs, length, n), dt)
    return pl.pallas_call(
        feed_kernel,
        grid=(seqs,),
        in_specs=[
            per_seq(length, width),
            per_seq(length, width),
            full(small.shape),
            full(up_bin.shape),
            full(dn_bin.shape),
        ],
        out_specs=[
            per_seq(length, width),
            per_seq(length, width),
            per_seq(length, hidden),
            per_seq(length, hidden),
            per_seq(length, width),
            per_seq(length, width),
            full((8, width)),
        ],
        out_shape=[
            like(width, BF), like(width, BF), like(hidden, BF), like(hidden, BF), like(width, F32), like(width, BF),
            jax.ShapeDtypeStruct((8, width), F32),
        ],
        compiler_params=params(),
        cost_estimate=cost(4 * seqs * length * width * hidden, 36 * seqs * length * width),
        name="feed",
    )(norm, teacher, small, up_bin, dn_bin)


def feed_back_kernel(
    mixed_ref, first_ref, hidden_ref, slope_ref, up_ref, dn_ref,
    pre_ref, dgrad_ref, ugrad_ref, hsum_ref, dacc, uacc,
):
    tile = pl.program_id(1)
    mixed = mixed_ref[0]
    pre_back = dot_nt(mixed, dn_ref[...]) * slope_ref[0].astype(F32)
    pre_low = pre_back.astype(BF)
    pre_ref[0] = pre_low
    dpart = dot_tn(hidden_ref[0], mixed)
    upart = dot_tn(first_ref[0], pre_low)
    hpart = jnp.sum(pre_back, axis=0, keepdims=True)

    @pl.when(tile == 0)
    def _():
        dacc[...] = dpart
        uacc[...] = upart
        hsum_ref[0, 0:1, :] = hpart

    @pl.when(tile > 0)
    def _():
        dacc[...] += dpart
        uacc[...] += upart
        hsum_ref[0, 0:1, :] += hpart

    @pl.when(tile == pl.num_programs(1) - 1)
    def _():
        dgrad_ref[...] = dacc[...].astype(BF)
        ugrad_ref[...] = uacc[...].astype(BF)


def feed_back(mixed, first_low, hidden, slope, up_bin, dn_bin):
    seqs, length, width = mixed.shape
    units = hidden.shape[2]
    chunks = units // width
    return pl.pallas_call(
        feed_back_kernel,
        grid=(chunks, seqs),
        in_specs=[
            pl.BlockSpec((1, length, width), lambda c, s: (s, 0, 0)),
            pl.BlockSpec((1, length, width), lambda c, s: (s, 0, 0)),
            pl.BlockSpec((1, length, width), lambda c, s: (s, 0, c)),
            pl.BlockSpec((1, length, width), lambda c, s: (s, 0, c)),
            pl.BlockSpec((width, width), lambda c, s: (0, c)),
            pl.BlockSpec((width, width), lambda c, s: (c, 0)),
        ],
        out_specs=[
            pl.BlockSpec((1, length, width), lambda c, s: (s, 0, c)),
            pl.BlockSpec((width, width), lambda c, s: (c, 0)),
            pl.BlockSpec((width, width), lambda c, s: (c, 0)),
            pl.BlockSpec((1, 8, width), lambda c, s: (c, 0, 0)),
        ],
        out_shape=[
            jax.ShapeDtypeStruct((seqs, length, units), BF),
            jax.ShapeDtypeStruct((units, width), BF),
            jax.ShapeDtypeStruct((units, width), BF),
            jax.ShapeDtypeStruct((chunks, 8, width), F32),
        ],
        scratch_shapes=[pltpu.VMEM((width, width), F32), pltpu.VMEM((width, width), F32)],
        compiler_params=params(),
        cost_estimate=cost(6 * seqs * length * width * units, 20 * seqs * length * units),
        name="feed_back",
    )(mixed, first_low, hidden, slope, up_bin, dn_bin)


def norm_kernel(
    second_ref, pre_ref, norm_ref, inv_ref, ctx_ref, up_ref, out_ref, small_ref,
    resid_ref, cback_ref, rowdot_ref, ograd_ref, sums_ref, oacc,
):
    s = pl.program_id(0)
    width = second_ref.shape[2]
    back = second_ref[0] + dot_nt(pre_ref[0], up_ref[...])
    resid, gain_sum, shift_sum = norm_back(back, norm_ref[0], inv_ref[0], small_ref[4:5, :])
    resid_ref[0] = resid
    low = resid.astype(BF)
    cback = dot_nt(low, out_ref[...]).astype(BF)
    cback_ref[0] = cback
    ctx = ctx_ref[0]
    opart = dot_tn(ctx, low)
    prod = cback.astype(F32) * ctx.astype(F32)
    high = prod.astype(BF)
    rest = (prod - high.astype(F32)).astype(BF)
    heads = lax.broadcasted_iota(jnp.int32, (16, width), 0)
    lanes = lax.broadcasted_iota(jnp.int32, (16, width), 1)
    pick = jnp.where((lanes >= heads * HEAD_DIM) & (lanes < heads * HEAD_DIM + HEAD_DIM), 1.0, 0.0).astype(BF)
    rowdot_ref[0] = dot_nt(pick, high) + dot_nt(pick, rest)

    @pl.when(s == 0)
    def _():
        oacc[...] = opart
        sums_ref[...] = jnp.zeros_like(sums_ref)

    @pl.when(s > 0)
    def _():
        oacc[...] += opart

    sums_ref[0:1, :] += gain_sum
    sums_ref[1:2, :] += shift_sum
    sums_ref[2:3, :] += jnp.sum(resid, axis=0, keepdims=True)

    @pl.when(s == pl.num_programs(0) - 1)
    def _():
        ograd_ref[...] = oacc[...].astype(BF)


def norm_one_back(second, pre_low, norm, inv, ctx, up_bin, out_bin, small):
    seqs, length, width = second.shape
    per_seq = lambda *shape: pl.BlockSpec((1,) + shape, lambda s: (s,) + (0,) * len(shape))
    return pl.pallas_call(
        norm_kernel,
        grid=(seqs,),
        in_specs=[
            per_seq(length, width),
            per_seq(length, pre_low.shape[2]),
            per_seq(length, width),
            per_seq(length, 1),
            per_seq(length, width),
            full(up_bin.shape),
            full(out_bin.shape),
            full(small.shape),
        ],
        out_specs=[
            per_seq(length, width),
            per_seq(length, width),
            per_seq(16, length),
            full((width, width)),
            full((8, width)),
        ],
        out_shape=[
            jax.ShapeDtypeStruct((seqs, length, width), F32),
            jax.ShapeDtypeStruct((seqs, length, width), BF),
            jax.ShapeDtypeStruct((seqs, 16, length), F32),
            jax.ShapeDtypeStruct((width, width), BF),
            jax.ShapeDtypeStruct((8, width), F32),
        ],
        scratch_shapes=[pltpu.VMEM((width, width), F32)],
        compiler_params=params(),
        cost_estimate=cost(2 * seqs * length * width * 6 * width, 40 * seqs * length * width),
        name="norm_one_back",
    )(second, pre_low, norm, inv, ctx, up_bin, out_bin, small)


GROUP = 256
TILE_B = 256


def attend_back_kernel(
    tokens_ref, rows_ref, cols_ref, q_ref, k_ref, v_ref, cback_ref, lse_ref, rowdot_ref,
    jlow_ref, grad_ref, sums_ref, acc, bias_ref,
):
    g, s = pl.program_id(0), pl.program_id(1)
    length = tokens_ref.shape[1]
    tile = min(TILE_B, length)
    bias_ref[...] = jnp.where(rows_ref[0] >= cols_ref[0], 0.0, NEG).astype(F32)
    lane = lax.broadcasted_iota(jnp.int32, (length, 128), 1)
    low = lane < HEAD_DIM

    for pair in range(GROUP // 128):
        at = slice(pair * 128, pair * 128 + 128)
        q2 = q_ref[0, :, at] * BF(0.125)
        k2 = k_ref[0, :, at]
        v2 = v_ref[0, :, at]
        do2 = cback_ref[0, :, at]
        dq = None
        for t in range(length // tile):
            rows = slice(t * tile, (t + 1) * tile)
            dks, dvs = [], []
            for h in range(2):
                mine = low[rows] if h == 0 else ~low[rows]
                km = jnp.where(mine, k2[rows], BF(0))
                vm = jnp.where(mine, v2[rows], BF(0))
                head = g * (GROUP // HEAD_DIM) + pair * 2 + h
                lse = lse_ref[0, pl.ds(head, 1), :]
                rowdot = rowdot_ref[0, pl.ds(head, 1), :]
                probs = jnp.exp(dot_nt(km, q2) + bias_ref[rows, :] - lse)
                dprobs = dot_nt(vm, do2)
                dscore = (probs * (dprobs - rowdot)).astype(BF)
                dvs.append(dot(probs.astype(BF), do2))
                dks.append(dot(dscore, q2))
                part = dot_tn(dscore, km * BF(0.125))
                dq = part if dq is None else dq + part
            dk = jnp.where(low[rows], dks[0], dks[1])
            dv = jnp.where(low[rows], dvs[0], dvs[1])
            jlow_ref[0, rows, GROUP + pair * 128 : GROUP + pair * 128 + 128] = dk.astype(BF)
            jlow_ref[0, rows, 2 * GROUP + pair * 128 : 2 * GROUP + pair * 128 + 128] = dv.astype(BF)
            vsum = jnp.sum(dv, axis=0, keepdims=True)
            vtotal = vsum if t == 0 else vtotal + vsum
        jlow_ref[0, :, at] = dq.astype(BF)
        qsum = jnp.sum(dq, axis=0, keepdims=True)

        @pl.when(s == 0)
        def _():
            sums_ref[0, 0:1, at] = qsum
            sums_ref[0, 1:2, at] = vtotal

        @pl.when(s > 0)
        def _():
            sums_ref[0, 0:1, at] += qsum
            sums_ref[0, 1:2, at] += vtotal

    part = dot_tn(tokens_ref[0], jlow_ref[0])

    @pl.when(s == 0)
    def _():
        acc[...] = part

    @pl.when(s > 0)
    def _():
        acc[...] += part

    @pl.when(s == pl.num_programs(1) - 1)
    def _():
        grad_ref[...] = acc[...].astype(BF)


def attend_back(tokens, block_ids, joined, cback, lse, rowdot):
    seqs, length, width = tokens.shape
    rows = block_ids.reshape(seqs, 1, length)
    cols = block_ids.reshape(seqs, length, 1)
    groups = width // GROUP
    whole = lambda *shape: pl.BlockSpec((1,) + shape, lambda g, s: (s,) + (0,) * len(shape))
    part = lambda k: pl.BlockSpec((1, length, GROUP), lambda g, s: (s, 0, k * groups + g))
    return pl.pallas_call(
        attend_back_kernel,
        grid=(groups, seqs),
        in_specs=[
            whole(length, width),
            whole(1, length),
            whole(length, 1),
            part(0),
            part(1),
            part(2),
            part(0),
            whole(16, length),
            whole(16, length),
        ],
        out_specs=[
            pl.BlockSpec((1, length, 3 * GROUP), lambda g, s: (s, 0, g)),
            pl.BlockSpec((width, 3 * GROUP), lambda g, s: (g, 0)),
            pl.BlockSpec((1, 8, GROUP), lambda g, s: (g, 0, 0)),
        ],
        out_shape=[
            jax.ShapeDtypeStruct((seqs, length, 3 * width), BF),
            jax.ShapeDtypeStruct((groups * width, 3 * GROUP), BF),
            jax.ShapeDtypeStruct((groups, 8, GROUP), F32),
        ],
        scratch_shapes=[pltpu.VMEM((width, 3 * GROUP), F32), pltpu.VMEM((length, length), F32)],
        compiler_params=params(),
        cost_estimate=cost(seqs * length * width * (6 * width + 40 * length), 30 * seqs * length * width),
        name="attend_back",
    )(tokens, rows, cols, joined, joined, joined, cback, lse, rowdot)


def token_kernel(resid_ref, jlow_ref, qkv_ref, grad_ref):
    width = resid_ref.shape[2]
    groups = width // GROUP
    total = resid_ref[0]
    for g in range(groups):
        for k in range(3):
            at = (3 * g + k) * GROUP
            col = k * width + g * GROUP
            total = total + dot_nt(jlow_ref[0, :, at : at + GROUP], qkv_ref[:, col : col + GROUP])
    grad_ref[0] = total


def token_back(resid, jlow, qkv_bin):
    seqs, length, width = resid.shape
    per_seq = lambda *shape: pl.BlockSpec((1,) + shape, lambda s: (s,) + (0,) * len(shape))
    return pl.pallas_call(
        token_kernel,
        grid=(seqs,),
        in_specs=[per_seq(length, width), per_seq(length, 3 * width), full(qkv_bin.shape)],
        out_specs=per_seq(length, width),
        out_shape=jax.ShapeDtypeStruct((seqs, length, width), F32),
        compiler_params=params(),
        cost_estimate=cost(6 * seqs * length * width * width, 16 * seqs * length * width),
        name="token_back",
    )(resid, jlow, qkv_bin)


def layer(core, tokens, teacher, block_ids, own, other, small_own, small_other):
    qkv_bin, small = prep_qkv(core, own[0], other[0], small_own, small_other)
    out_bin, up_bin, dn_bin = prep_rest(core, own[1], other[1], own[2], other[2], own[3], other[3])
    joined, ctx, lse, norm, inv = attend(tokens, block_ids, qkv_bin, out_bin, small)
    final, first_low, hidden, slope, second, mixed, sums_two = feed(norm, teacher, small, up_bin, dn_bin)
    pre_low, dgrad, ugrad, hsum = feed_back(mixed, first_low, hidden, slope, up_bin, dn_bin)
    resid, cback, rowdot, ograd, sums_one = norm_one_back(second, pre_low, norm, inv, ctx, up_bin, out_bin, small)
    jlow, qgrad, sums_qv = attend_back(tokens, block_ids, joined, cback, lse, rowdot)
    token_grad = token_back(resid, jlow, qkv_bin)
    return final, token_grad, dgrad, ugrad, ograd, qgrad, sums_two, hsum, sums_one, sums_qv


def as_sent(value):
    return jax.tree.map(lambda a: a.astype(BF), value)


def swap(value):
    return lax.ppermute(value, "shard", [(0, 1), (1, 0)])


def small_rows(biases, gain, shift, hidden_bias):
    rows = biases.shape[0]
    return jnp.concatenate([biases.T, gain.T, shift.T, hidden_bias.reshape(-1, rows)], axis=0)


def body(tokens, teacher, block_ids, *weights):
    qkv, out, up, down, biases, hidden_bias, gain, shift = weights
    shards = lax.axis_size("shard")
    if shards == 2:
        core = lax.axis_index("shard").reshape(1)
        own = (qkv, out, up, down)
        small_own = small_rows(biases, gain, shift, hidden_bias)
        small_other = swap(small_own)
        other = tuple(swap(w) for w in own)
    else:
        core = jnp.zeros((1,), jnp.int32)
        gathered = [lax.all_gather(w, "shard", axis=0, tiled=True) for w in weights]
        cut = [jnp.split(w, 2, axis=0) for w in gathered]
        own, other = (tuple(c[i] for c in cut[:4]) for i in range(2))
        small_own, small_other = (
            small_rows(cut[4][i], cut[6][i], cut[7][i], cut[5][i]) for i in range(2)
        )
    final, token_grad, dgrad, ugrad, ograd, qgrad, sums_two, hsum, sums_one, sums_qv = layer(
        core, tokens, teacher, block_ids, own, other, small_own, small_other
    )
    width, units = ograd.shape[0], dgrad.shape[0]
    chunks, half = units // width, width // 2
    groups = width // GROUP
    grads = (
        qgrad.reshape(groups, width, 3, GROUP).transpose(1, 2, 0, 3).reshape(width, 3 * width),
        ograd,
        ugrad.reshape(chunks, width, 2, half).transpose(1, 2, 0, 3).reshape(width, units),
        dgrad.reshape(chunks, 2, half, width).transpose(1, 0, 2, 3).reshape(units, width),
        jnp.stack([sums_qv[:, 0].reshape(-1), sums_qv[:, 1].reshape(-1), sums_one[2], sums_two[2]], axis=1),
        hsum[:, 0].reshape(chunks, 2, half).transpose(1, 0, 2).reshape(-1),
        jnp.stack([sums_one[0], sums_two[0]], axis=1),
        jnp.stack([sums_one[1], sums_two[1]], axis=1),
    )
    owned = lax.psum_scatter(as_sent(grads), "shard", scatter_dimension=0, tiled=True)
    summed = jax.tree.map(lambda part: part.astype(F32), lax.psum(owned, "rep"))
    return (final, token_grad) + tuple(summed)


def solution(mesh):
    placed = (
        P(("shard", "rep"), None, None),
        P(("shard", "rep"), None, None),
        P(("shard", "rep"), None),
        P("shard", None),
        P("shard", None),
        P("shard", None),
        P("shard", None),
        P("shard", None),
        P("shard"),
        P("shard", None),
        P("shard", None),
    )
    return jax.shard_map(
        body,
        mesh=mesh,
        in_specs=placed,
        out_specs=placed[:2] + placed[3:],
        check_vma=False,
    )
```

```python
import functools

import jax
import jax.numpy as jnp
from jax import lax
from jax.experimental import pallas as pl
from jax.experimental.pallas import tpu as pltpu
from jax.sharding import PartitionSpec as P

HEAD_DIM = 64
EPS = 1e-05
NEG = -1e30
BF = jnp.bfloat16
F32 = jnp.float32
MB = 1 << 20


def params(mb=56, **kw):
    return pltpu.CompilerParams(vmem_limit_bytes=mb * MB, **kw)


def dot(a, b):
    return jnp.dot(a, b, preferred_element_type=F32)


def dot_nt(a, b):
    return lax.dot_general(a, b, (((1,), (1,)), ((), ())), preferred_element_type=F32)


def dot_tn(a, b):
    return lax.dot_general(a, b, (((0,), (0,)), ((), ())), preferred_element_type=F32)


def full(shape):
    return pl.BlockSpec(shape, lambda *_: (0,) * len(shape))


def cost(flops, nbytes, trans=0):
    return pl.CostEstimate(flops=int(flops), bytes_accessed=int(nbytes), transcendentals=int(trans))


def deal(core, acc, mine_ref, theirs_ref, at=0):
    half = acc.shape[0] // 2
    wide = acc.shape[1] // 2
    for ref, who in ((mine_ref, core), (theirs_ref, 1 - core)):
        rows = pl.ds(pl.multiple_of(who * half, half), half)
        ref[at, 0:half, :] = acc[rows, 0:wide].astype(BF)
        ref[at, half : 2 * half, :] = acc[rows, wide : 2 * wide].astype(BF)


def binary_halves(first, second):
    rows = 2 * first.shape[0]
    total = jnp.sum(jnp.abs(first.astype(F32)), axis=0, keepdims=True) + jnp.sum(
        jnp.abs(second.astype(F32)), axis=0, keepdims=True
    )
    scale = (total / rows).astype(BF)
    return (
        jnp.where(first >= 0, scale, -scale).astype(BF),
        jnp.where(second >= 0, scale, -scale).astype(BF),
    )


def prep_qkv_kernel(core_ref, own_ref, other_ref, small_own_ref, small_other_ref, out_ref, small_ref):
    core = core_ref[0]
    half = own_ref.shape[0]
    own_at = pl.multiple_of(core * half, half)
    other_at = pl.multiple_of((1 - core) * half, half)
    own, other = binary_halves(own_ref[...], other_ref[...])
    out_ref[pl.ds(own_at, half), :] = own
    out_ref[pl.ds(other_at, half), :] = other

    @pl.when(pl.program_id(0) == 0)
    def _():
        small_ref[:, pl.ds(own_at, half)] = small_own_ref[...].astype(F32)
        small_ref[:, pl.ds(other_at, half)] = small_other_ref[...].astype(F32)


def prep_qkv(core, own, other, small_own, small_other):
    half, cols = own.shape
    rows = 2 * half
    step = rows
    return pl.pallas_call(
        prep_qkv_kernel,
        grid_spec=pltpu.PrefetchScalarGridSpec(
            num_scalar_prefetch=1,
            grid=(cols // step,),
            in_specs=[
                pl.BlockSpec((half, step), lambda j, c: (0, j)),
                pl.BlockSpec((half, step), lambda j, c: (0, j)),
                full(small_own.shape),
                full(small_own.shape),
            ],
            out_specs=[
                pl.BlockSpec((rows, step), lambda j, c: (0, j)),
                full((small_own.shape[0], rows)),
            ],
        ),
        out_shape=[
            jax.ShapeDtypeStruct((rows, cols), BF),
            jax.ShapeDtypeStruct((small_own.shape[0], rows), F32),
        ],
        compiler_params=params(),
        cost_estimate=cost(4 * rows * cols, 4 * rows * cols),
        name="prep_qkv",
    )(core, own, other, small_own, small_other)


def prep_rest_kernel(core_ref, out_a, out_b, up_a, up_b, dn_a, dn_b, out_ref, up_ref, dn_ref):
    core = core_ref[0]
    half = out_a.shape[0]
    width = 2 * half
    own_at = pl.multiple_of(core * half, half)
    other_at = pl.multiple_of((1 - core) * half, half)
    own, other = binary_halves(out_a[...], out_b[...])
    out_ref[pl.ds(own_at, half), :] = own
    out_ref[pl.ds(other_at, half), :] = other
    hidden = up_a.shape[1]
    chunks = hidden // width
    for j in range(hidden // half):
        own, other = binary_halves(up_a[:, j * half : (j + 1) * half], up_b[:, j * half : (j + 1) * half])
        at = (j % chunks) * width + (j // chunks) * half
        up_ref[pl.ds(own_at, half), at : at + half] = own
        up_ref[pl.ds(other_at, half), at : at + half] = other
    own, other = binary_halves(dn_a[...], dn_b[...])
    for c in range(chunks):
        dn_ref[pl.ds(pl.multiple_of(c * width + own_at, half), half), :] = own[c * half : (c + 1) * half]
        dn_ref[pl.ds(pl.multiple_of(c * width + other_at, half), half), :] = other[c * half : (c + 1) * half]


def prep_rest(core, out_a, out_b, up_a, up_b, dn_a, dn_b):
    half, width = out_a.shape
    hidden = up_a.shape[1]
    vm = pl.BlockSpec(memory_space=pltpu.VMEM)
    return pl.pallas_call(
        prep_rest_kernel,
        in_specs=[pl.BlockSpec(memory_space=pltpu.SMEM)] + [vm] * 6,
        out_specs=[vm] * 3,
        out_shape=[
            jax.ShapeDtypeStruct((width, width), BF),
            jax.ShapeDtypeStruct((width, hidden), BF),
            jax.ShapeDtypeStruct((hidden, width), BF),
        ],
        compiler_params=params(),
        cost_estimate=cost(8 * width * hidden, 8 * width * hidden),
        name="prep_rest",
    )(core, out_a, out_b, up_a, up_b, dn_a, dn_b)


def attend_kernel(
    tokens_ref, rows_ref, cols_ref, qkv_ref, out_ref, small_ref, joined_ref, ctx_ref, lse_ref, norm_ref, inv_ref,
    bias_ref,
):
    length, width = tokens_ref.shape[1:]
    x = tokens_ref[0]
    for part, bias_row in ((0, 0), (1, None), (2, 1)):
        joined = dot(x, qkv_ref[:, part * width : (part + 1) * width])
        if bias_row is not None:
            joined = joined + small_ref[bias_row : bias_row + 1, :]
        joined_ref[0, :, part * width : (part + 1) * width] = joined.astype(BF)
    bias_ref[...] = jnp.where(cols_ref[0] >= rows_ref[0], 0.0, NEG).astype(F32)
    lane = lax.broadcasted_iota(jnp.int32, (length, 128), 1)
    low = lane < HEAD_DIM
    lse_all = jnp.zeros((length, 128), F32)
    tile = min(TILE_F, length)
    for pair in range(width // 128):
        q2 = joined_ref[0, :, pair * 128 : pair * 128 + 128] * BF(0.125)
        k2 = joined_ref[0, :, width + pair * 128 : width + pair * 128 + 128]
        v2 = joined_ref[0, :, 2 * width + pair * 128 : 2 * width + pair * 128 + 128]
        for t in range(length // tile):
            rows = slice(t * tile, (t + 1) * tile)
            parts = []
            for h in range(2):
                mine = low[rows] if h == 0 else ~low[rows]
                qm = jnp.where(mine, q2[rows], BF(0))
                scores = dot_nt(qm, k2) + bias_ref[rows, :]
                peak = jnp.max(scores, axis=-1, keepdims=True)
                raised = jnp.exp(scores - peak)
                total = jnp.sum(raised, axis=-1, keepdims=True)
                parts.append(dot(raised.astype(BF), v2) / total)
                lse_ref_col = peak + jnp.log(total)
                bias_lane = lane[rows] == 2 * pair + h
                lse_cols = jnp.where(bias_lane, lse_ref_col, 0.0)
                if h == 0:
                    pair_lse = lse_cols
                else:
                    pair_lse = pair_lse + lse_cols
            ctx_ref[0, rows, pair * 128 : pair * 128 + 128] = jnp.where(low[rows], parts[0], parts[1]).astype(BF)
            if t == 0:
                tiles_lse = [pair_lse]
            else:
                tiles_lse.append(pair_lse)
        lse_all = lse_all + jnp.concatenate(tiles_lse, axis=0)
    lse_ref[0] = lse_all.T[0:16, :]
    resid = x.astype(F32) + dot(ctx_ref[0], out_ref[...]) + small_ref[2:3, :]
    center = resid - jnp.mean(resid, axis=-1, keepdims=True)
    inverse = lax.rsqrt(jnp.mean(center * center, axis=-1, keepdims=True) + EPS)
    norm_ref[0] = center * inverse
    inv_ref[0] = inverse


TILE_F = 256


def attend(tokens, block_ids, qkv_bin, out_bin, small):
    seqs, length, width = tokens.shape
    rows = block_ids.reshape(seqs, 1, length)
    cols = block_ids.reshape(seqs, length, 1)
    per_seq = lambda *shape: pl.BlockSpec((1,) + shape, lambda s: (s,) + (0,) * len(shape))
    return pl.pallas_call(
        attend_kernel,
        grid=(seqs,),
        in_specs=[
            per_seq(length, width),
            per_seq(1, length),
            per_seq(length, 1),
            full(qkv_bin.shape),
            full(out_bin.shape),
            full(small.shape),
        ],
        out_specs=[
            per_seq(length, 3 * width),
            per_seq(length, width),
            per_seq(16, length),
            per_seq(length, width),
            per_seq(length, 1),
        ],
        out_shape=[
            jax.ShapeDtypeStruct((seqs, length, 3 * width), BF),
            jax.ShapeDtypeStruct((seqs, length, width), BF),
            jax.ShapeDtypeStruct((seqs, 16, length), F32),
            jax.ShapeDtypeStruct((seqs, length, width), F32),
            jax.ShapeDtypeStruct((seqs, length, 1), F32),
        ],
        scratch_shapes=[pltpu.VMEM((length, length), F32)],
        compiler_params=params(),
        cost_estimate=cost(seqs * length * width * (8 * width + 16 * length), 30 * seqs * length * width),
        name="attend",
    )(tokens, rows, cols, qkv_bin, out_bin, small)


def gelu_pair(u):
    cdf = 0.5 + 0.5 * lax.erf(u * 0.7071067811865476)
    density = jnp.exp(-0.5 * u * u) * 0.3989422804014327
    return u * cdf, cdf + u * density


def norm_back(upstream, normed, inverse, gain):
    scaled = upstream * gain
    weighted = upstream * normed
    centered = (
        scaled
        - jnp.mean(scaled, axis=-1, keepdims=True)
        - normed * jnp.mean(weighted * gain, axis=-1, keepdims=True)
    )
    return centered * inverse, jnp.sum(weighted, axis=0, keepdims=True), jnp.sum(upstream, axis=0, keepdims=True)


def feed_kernel(
    norm_ref, teacher_ref, small_ref, up_ref, dn_ref,
    final_ref, first_low_ref, hidden_ref, slope_ref, second_ref, mixed_ref, sums_ref,
):
    width = norm_ref.shape[2]
    first = norm_ref[0] * small_ref[4:5, :] + small_ref[6:7, :]
    first_low = first.astype(BF)
    first_low_ref[0] = first_low
    acc = first + small_ref[3:4, :]
    for c in range(up_ref.shape[1] // width):
        cols = slice(c * width, (c + 1) * width)
        pre = dot(first_low, up_ref[:, cols]) + small_ref[8 + c : 9 + c, :]
        value, slope = gelu_pair(pre)
        value = value.astype(BF)
        hidden_ref[0, :, cols] = value
        slope_ref[0, :, cols] = slope.astype(BF)
        acc = acc + dot(value, dn_ref[cols, :])
    center = acc - jnp.mean(acc, axis=-1, keepdims=True)
    inverse = lax.rsqrt(jnp.mean(center * center, axis=-1, keepdims=True) + EPS)
    normed = center * inverse
    gain = small_ref[5:6, :]
    final = normed * gain + small_ref[7:8, :]
    final_ref[0] = final.astype(BF)
    upstream = final - teacher_ref[0].astype(F32)
    second, gain_sum, shift_sum = norm_back(upstream, normed, inverse, gain)
    second_ref[0] = second
    mixed_ref[0] = second.astype(BF)

    @pl.when(pl.program_id(0) == 0)
    def _():
        sums_ref[...] = jnp.zeros_like(sums_ref)

    sums_ref[0:1, :] += gain_sum
    sums_ref[1:2, :] += shift_sum
    sums_ref[2:3, :] += jnp.sum(second, axis=0, keepdims=True)


def feed(norm, teacher, small, up_bin, dn_bin):
    seqs, length, width = norm.shape
    hidden = up_bin.shape[1]
    per_seq = lambda *shape: pl.BlockSpec((1,) + shape, lambda s: (s,) + (0,) * len(shape))
    like = lambda n, dt: jax.ShapeDtypeStruct((seqs, length, n), dt)
    return pl.pallas_call(
        feed_kernel,
        grid=(seqs,),
        in_specs=[
            per_seq(length, width),
            per_seq(length, width),
            full(small.shape),
            full(up_bin.shape),
            full(dn_bin.shape),
        ],
        out_specs=[
            per_seq(length, width),
            per_seq(length, width),
            per_seq(length, hidden),
            per_seq(length, hidden),
            per_seq(length, width),
            per_seq(length, width),
            full((8, width)),
        ],
        out_shape=[
            like(width, BF), like(width, BF), like(hidden, BF), like(hidden, BF), like(width, F32), like(width, BF),
            jax.ShapeDtypeStruct((8, width), F32),
        ],
        compiler_params=params(),
        cost_estimate=cost(4 * seqs * length * width * hidden, 36 * seqs * length * width),
        name="feed",
    )(norm, teacher, small, up_bin, dn_bin)


def feed_back_kernel(
    core_ref, mixed_ref, first_ref, hidden_ref, slope_ref, dn_ref,
    pre_ref, mine_ref, theirs_ref, hsum_ref, dacc, uacc,
):
    tile = pl.program_id(1)
    mixed = mixed_ref[0]
    pre_back = dot_nt(mixed, dn_ref[...]) * slope_ref[0].astype(F32)
    pre_low = pre_back.astype(BF)
    pre_ref[0] = pre_low
    dpart = dot_tn(hidden_ref[0], mixed)
    upart = dot_tn(first_ref[0], pre_low)
    hpart = jnp.sum(pre_back, axis=0, keepdims=True)

    @pl.when(tile == 0)
    def _():
        dacc[...] = dpart
        uacc[...] = upart
        hsum_ref[0, 0:1, :] = hpart

    @pl.when(tile > 0)
    def _():
        dacc[...] += dpart
        uacc[...] += upart
        hsum_ref[0, 0:1, :] += hpart

    @pl.when(tile == pl.num_programs(1) - 1)
    def _():
        deal(core_ref[0], dacc, mine_ref, theirs_ref, 0)
        deal(core_ref[0], uacc, mine_ref, theirs_ref, 1)


def feed_back(core, mixed, first_low, hidden, slope, dn_bin):
    seqs, length, width = mixed.shape
    units = hidden.shape[2]
    chunks = units // width
    return pl.pallas_call(
        feed_back_kernel,
        grid_spec=pltpu.PrefetchScalarGridSpec(
            num_scalar_prefetch=1,
            grid=(chunks, seqs),
            in_specs=[
                pl.BlockSpec((1, length, width), lambda c, s, _: (s, 0, 0)),
                pl.BlockSpec((1, length, width), lambda c, s, _: (s, 0, 0)),
                pl.BlockSpec((1, length, width), lambda c, s, _: (s, 0, c)),
                pl.BlockSpec((1, length, width), lambda c, s, _: (s, 0, c)),
                pl.BlockSpec((width, width), lambda c, s, _: (c, 0)),
            ],
            out_specs=[
                pl.BlockSpec((1, length, width), lambda c, s, _: (s, 0, c)),
                pl.BlockSpec((2, width, width // 2), lambda c, s, _: (c, 0, 0)),
                pl.BlockSpec((2, width, width // 2), lambda c, s, _: (c, 0, 0)),
                pl.BlockSpec((1, 8, width), lambda c, s, _: (c, 0, 0)),
            ],
            scratch_shapes=[pltpu.VMEM((width, width), F32), pltpu.VMEM((width, width), F32)],
        ),
        out_shape=[
            jax.ShapeDtypeStruct((seqs, length, units), BF),
            jax.ShapeDtypeStruct((2 * chunks, width, width // 2), BF),
            jax.ShapeDtypeStruct((2 * chunks, width, width // 2), BF),
            jax.ShapeDtypeStruct((chunks, 8, width), F32),
        ],
        compiler_params=params(),
        cost_estimate=cost(6 * seqs * length * width * units, 20 * seqs * length * units),
        name="feed_back",
    )(core, mixed, first_low, hidden, slope, dn_bin)


def norm_kernel(
    core_ref, second_ref, pre_ref, norm_ref, inv_ref, ctx_ref, up_ref, out_ref, small_ref,
    resid_ref, cback_ref, rowdot_ref, mine_ref, theirs_ref, sums_ref, oacc,
):
    s = pl.program_id(0)
    width = second_ref.shape[2]
    back = second_ref[0] + dot_nt(pre_ref[0], up_ref[...])
    resid, gain_sum, shift_sum = norm_back(back, norm_ref[0], inv_ref[0], small_ref[4:5, :])
    resid_ref[0] = resid
    low = resid.astype(BF)
    cback = dot_nt(low, out_ref[...]).astype(BF)
    cback_ref[0] = cback
    ctx = ctx_ref[0]
    opart = dot_tn(ctx, low)
    prod = cback.astype(F32) * ctx.astype(F32)
    high = prod.astype(BF)
    rest = (prod - high.astype(F32)).astype(BF)
    heads = lax.broadcasted_iota(jnp.int32, (16, width), 0)
    lanes = lax.broadcasted_iota(jnp.int32, (16, width), 1)
    pick = jnp.where((lanes >= heads * HEAD_DIM) & (lanes < heads * HEAD_DIM + HEAD_DIM), 1.0, 0.0).astype(BF)
    rowdot_ref[0] = dot_nt(pick, high) + dot_nt(pick, rest)

    @pl.when(s == 0)
    def _():
        oacc[...] = opart
        sums_ref[...] = jnp.zeros_like(sums_ref)

    @pl.when(s > 0)
    def _():
        oacc[...] += opart

    sums_ref[0:1, :] += gain_sum
    sums_ref[1:2, :] += shift_sum
    sums_ref[2:3, :] += jnp.sum(resid, axis=0, keepdims=True)

    @pl.when(s == pl.num_programs(0) - 1)
    def _():
        deal(core_ref[0], oacc, mine_ref, theirs_ref)


def norm_one_back(core, second, pre_low, norm, inv, ctx, up_bin, out_bin, small):
    seqs, length, width = second.shape
    per_seq = lambda *shape: pl.BlockSpec((1,) + shape, lambda s, _: (s,) + (0,) * len(shape))
    return pl.pallas_call(
        norm_kernel,
        grid_spec=pltpu.PrefetchScalarGridSpec(
        num_scalar_prefetch=1,
        grid=(seqs,),
        in_specs=[
            per_seq(length, width),
            per_seq(length, pre_low.shape[2]),
            per_seq(length, width),
            per_seq(length, 1),
            per_seq(length, width),
            full(up_bin.shape),
            full(out_bin.shape),
            full(small.shape),
        ],
        out_specs=[
            per_seq(length, width),
            per_seq(length, width),
            per_seq(16, length),
            full((1, width, width // 2)),
            full((1, width, width // 2)),
            full((8, width)),
        ],
        scratch_shapes=[pltpu.VMEM((width, width), F32)],
        ),
        out_shape=[
            jax.ShapeDtypeStruct((seqs, length, width), F32),
            jax.ShapeDtypeStruct((seqs, length, width), BF),
            jax.ShapeDtypeStruct((seqs, 16, length), F32),
            jax.ShapeDtypeStruct((1, width, width // 2), BF),
            jax.ShapeDtypeStruct((1, width, width // 2), BF),
            jax.ShapeDtypeStruct((8, width), F32),
        ],
        compiler_params=params(),
        cost_estimate=cost(2 * seqs * length * width * 6 * width, 40 * seqs * length * width),
        name="norm_one_back",
    )(core, second, pre_low, norm, inv, ctx, up_bin, out_bin, small)


GROUP = 256
TILE_B = 256


def attend_back_kernel(
    core_ref, tokens_ref, rows_ref, cols_ref, q_ref, k_ref, v_ref, cback_ref, lse_ref, rowdot_ref,
    jlow_ref, mine_ref, theirs_ref, sums_ref, acc, bias_ref,
):
    g, s = pl.program_id(0), pl.program_id(1)
    length = tokens_ref.shape[1]
    tile = min(TILE_B, length)
    bias_ref[...] = jnp.where(rows_ref[0] >= cols_ref[0], 0.0, NEG).astype(F32)
    lane = lax.broadcasted_iota(jnp.int32, (length, 128), 1)
    low = lane < HEAD_DIM

    for pair in range(GROUP // 128):
        at = slice(pair * 128, pair * 128 + 128)
        q2 = q_ref[0, :, at] * BF(0.125)
        k2 = k_ref[0, :, at]
        v2 = v_ref[0, :, at]
        do2 = cback_ref[0, :, at]
        dq = None
        for t in range(length // tile):
            rows = slice(t * tile, (t + 1) * tile)
            dks, dvs = [], []
            for h in range(2):
                mine = low[rows] if h == 0 else ~low[rows]
                km = jnp.where(mine, k2[rows], BF(0))
                vm = jnp.where(mine, v2[rows], BF(0))
                head = g * (GROUP // HEAD_DIM) + pair * 2 + h
                lse = lse_ref[0, pl.ds(head, 1), :]
                rowdot = rowdot_ref[0, pl.ds(head, 1), :]
                probs = jnp.exp(dot_nt(km, q2) + bias_ref[rows, :] - lse)
                dprobs = dot_nt(vm, do2)
                dscore = (probs * (dprobs - rowdot)).astype(BF)
                dvs.append(dot(probs.astype(BF), do2))
                dks.append(dot(dscore, q2))
                part = dot_tn(dscore, km * BF(0.125))
                dq = part if dq is None else dq + part
            dk = jnp.where(low[rows], dks[0], dks[1])
            dv = jnp.where(low[rows], dvs[0], dvs[1])
            jlow_ref[0, rows, GROUP + pair * 128 : GROUP + pair * 128 + 128] = dk.astype(BF)
            jlow_ref[0, rows, 2 * GROUP + pair * 128 : 2 * GROUP + pair * 128 + 128] = dv.astype(BF)
            vsum = jnp.sum(dv, axis=0, keepdims=True)
            vtotal = vsum if t == 0 else vtotal + vsum
        jlow_ref[0, :, at] = dq.astype(BF)
        qsum = jnp.sum(dq, axis=0, keepdims=True)

        @pl.when(s == 0)
        def _():
            sums_ref[0, 0:1, at] = qsum
            sums_ref[0, 1:2, at] = vtotal

        @pl.when(s > 0)
        def _():
            sums_ref[0, 0:1, at] += qsum
            sums_ref[0, 1:2, at] += vtotal

    part = dot_tn(tokens_ref[0], jlow_ref[0])

    @pl.when(s == 0)
    def _():
        acc[...] = part

    @pl.when(s > 0)
    def _():
        acc[...] += part

    @pl.when(s == pl.num_programs(1) - 1)
    def _():
        deal(core_ref[0], acc, mine_ref, theirs_ref)


def attend_back(core, tokens, block_ids, joined, cback, lse, rowdot):
    seqs, length, width = tokens.shape
    rows = block_ids.reshape(seqs, 1, length)
    cols = block_ids.reshape(seqs, length, 1)
    groups = width // GROUP
    whole = lambda *shape: pl.BlockSpec((1,) + shape, lambda g, s, _: (s,) + (0,) * len(shape))
    part = lambda k: pl.BlockSpec((1, length, GROUP), lambda g, s, _: (s, 0, k * groups + g))
    return pl.pallas_call(
        attend_back_kernel,
        grid_spec=pltpu.PrefetchScalarGridSpec(
        num_scalar_prefetch=1,
        grid=(groups, seqs),
        in_specs=[
            whole(length, width),
            whole(1, length),
            whole(length, 1),
            part(0),
            part(1),
            part(2),
            part(0),
            whole(16, length),
            whole(16, length),
        ],
        out_specs=[
            pl.BlockSpec((1, length, 3 * GROUP), lambda g, s, _: (s, 0, g)),
            pl.BlockSpec((1, width, width // 2), lambda g, s, _: (g, 0, 0)),
            pl.BlockSpec((1, width, width // 2), lambda g, s, _: (g, 0, 0)),
            pl.BlockSpec((1, 8, GROUP), lambda g, s, _: (g, 0, 0)),
        ],
        scratch_shapes=[pltpu.VMEM((width, 3 * GROUP), F32), pltpu.VMEM((length, length), F32)],
        ),
        out_shape=[
            jax.ShapeDtypeStruct((seqs, length, 3 * width), BF),
            jax.ShapeDtypeStruct((groups, width, width // 2), BF),
            jax.ShapeDtypeStruct((groups, width, width // 2), BF),
            jax.ShapeDtypeStruct((groups, 8, GROUP), F32),
        ],
        compiler_params=params(),
        cost_estimate=cost(seqs * length * width * (6 * width + 40 * length), 30 * seqs * length * width),
        name="attend_back",
    )(core, tokens, rows, cols, joined, joined, joined, cback, lse, rowdot)


def token_kernel(resid_ref, jlow_ref, qkv_ref, grad_ref):
    width = resid_ref.shape[2]
    groups = width // GROUP
    total = resid_ref[0]
    for g in range(groups):
        for k in range(3):
            at = (3 * g + k) * GROUP
            col = k * width + g * GROUP
            total = total + dot_nt(jlow_ref[0, :, at : at + GROUP], qkv_ref[:, col : col + GROUP])
    grad_ref[0] = total


def token_back(resid, jlow, qkv_bin):
    seqs, length, width = resid.shape
    per_seq = lambda *shape: pl.BlockSpec((1,) + shape, lambda s: (s,) + (0,) * len(shape))
    return pl.pallas_call(
        token_kernel,
        grid=(seqs,),
        in_specs=[per_seq(length, width), per_seq(length, 3 * width), full(qkv_bin.shape)],
        out_specs=per_seq(length, width),
        out_shape=jax.ShapeDtypeStruct((seqs, length, width), F32),
        compiler_params=params(),
        cost_estimate=cost(6 * seqs * length * width * width, 16 * seqs * length * width),
        name="token_back",
    )(resid, jlow, qkv_bin)


def layer(core, tokens, teacher, block_ids, own, other, small_own, small_other):
    qkv_bin, small = prep_qkv(core, own[0], other[0], small_own, small_other)
    out_bin, up_bin, dn_bin = prep_rest(core, own[1], other[1], own[2], other[2], own[3], other[3])
    joined, ctx, lse, norm, inv = attend(tokens, block_ids, qkv_bin, out_bin, small)
    final, first_low, hidden, slope, second, mixed, sums_two = feed(norm, teacher, small, up_bin, dn_bin)
    pre_low, *feed_grads, hsum = feed_back(core, mixed, first_low, hidden, slope, dn_bin)
    resid, cback, rowdot, *out_grads, sums_one = norm_one_back(
        core, second, pre_low, norm, inv, ctx, up_bin, out_bin, small
    )
    jlow, *qkv_grads, sums_qv = attend_back(core, tokens, block_ids, joined, cback, lse, rowdot)
    token_grad = token_back(resid, jlow, qkv_bin)
    sums = jnp.concatenate(
        [
            sums_qv[:, 0].reshape(1, -1), sums_qv[:, 1].reshape(1, -1), sums_one[2:3], sums_two[2:3],
            sums_one[0:1], sums_two[0:1], sums_one[1:2], sums_two[1:2], hsum[:, 0],
        ],
        axis=0,
    )
    return final, token_grad, feed_grads, out_grads, qkv_grads, sums


MESH = pl.DeviceIdType.MESH


def reduce_kernel(
    feed_mine, feed_theirs, out_mine, out_theirs, qkv_mine, qkv_theirs, sums_ref,
    result_ref, total_ref,
    held, from_core, from_one, from_two, from_line, kept, came,
    local_sem, core_send, core_recv, one_send, one_recv, two_send, two_recv, line_send, line_recv,
    line_back_send, line_back_recv, two_back_send, two_back_recv, one_back_send, one_back_recv,
    small_send, small_recv, done_sem,
):
    core, rep = lax.axis_index("shard"), lax.axis_index("rep")
    x, y, z = rep % 2, (rep // 2) % 2, rep // 4
    units, rows = held.shape[0], held.shape[1]
    half, quarter, piece = rows // 2, rows // 4, rows // 16
    partner_x, partner_y = rep + 1 - 2 * x, rep + 2 - 4 * y
    sibling = {"shard": 1 - core}

    def along(step):
        return {"rep": rep % 4 + 4 * ((z + step) % 4)}

    barrier = pltpu.get_barrier_semaphore()
    peers = [sibling, {"rep": partner_x}, {"rep": partner_y}, along(1), along(2), along(3)]
    for peer in peers:
        pl.semaphore_signal(barrier, inc=1, device_id=peer, device_id_type=MESH)
    pl.semaphore_wait(barrier, len(peers))

    def send(src, dst, send_sem, recv_sem, peer):
        return pltpu.make_async_remote_copy(
            src_ref=src, dst_ref=dst, send_sem=send_sem, recv_sem=recv_sem, device_id=peer, device_id_type=MESH
        )

    sources = [(feed_mine, feed_theirs)] * feed_mine.shape[0]
    places = list(range(feed_mine.shape[0]))
    sources += [(out_mine, out_theirs)] + [(qkv_mine, qkv_theirs)] * qkv_mine.shape[0]
    places += [0] + list(range(qkv_mine.shape[0]))

    for u in range(units):
        mine, theirs = sources[u]
        send(theirs.at[places[u]], from_core.at[u], core_send.at[u], core_recv.at[u], sibling).start()
        pltpu.make_async_copy(mine.at[places[u]], held.at[u], local_sem.at[u]).start()

    def where(u):
        odd = u % 2
        bit_one = x + odd * (y - x)
        bit_two = y + odd * (x - y)
        peer_one = {"rep": partner_x + odd * (partner_y - partner_x)}
        peer_two = {"rep": partner_y + odd * (partner_x - partner_y)}
        base_one = bit_one * half
        base_two = base_one + bit_two * quarter
        return bit_one, bit_two, peer_one, peer_two, base_one, base_two

    def block(at, size):
        return pl.ds(pl.multiple_of(at, piece), size)

    def add(u, at, size, other):
        here = block(at, size)
        held[u, here, :] = (held[u, here, :].astype(F32) + other.astype(F32)).astype(BF)

    def copy_core(u):
        return send(from_core.at[u], from_core.at[u], core_send.at[u], core_recv.at[u], sibling)

    def copy_one(u):
        bit_one, _, peer_one, _, _, _ = where(u)
        away = block((1 - bit_one) * half, half)
        return send(held.at[u, away], from_one.at[u], one_send.at[u], one_recv.at[u], peer_one)

    def copy_two(u):
        _, bit_two, _, peer_two, base_one, _ = where(u)
        away = block(base_one + (1 - bit_two) * quarter, quarter)
        return send(held.at[u, away], from_two.at[u], two_send.at[u], two_recv.at[u], peer_two)

    def copy_line(u, d):
        base_two = where(u)[5]
        away = block(base_two + ((z + d) % 4) * piece, piece)
        return send(held.at[u, away], from_line.at[u, d - 1], line_send.at[u, d - 1], line_recv.at[u, d - 1], along(d))

    def copy_line_back(u, d):
        base_two = where(u)[5]
        mine = from_core.at[u, block(base_two + z * piece, piece)]
        return send(mine, mine, line_back_send.at[u, d - 1], line_back_recv.at[u, d - 1], along(d))

    def copy_two_back(u):
        _, _, _, peer_two, _, base_two = where(u)
        mine = from_core.at[u, block(base_two, quarter)]
        return send(mine, mine, two_back_send.at[u], two_back_recv.at[u], peer_two)

    def copy_one_back(u):
        _, _, peer_one, _, base_one, _ = where(u)
        mine = from_core.at[u, block(base_one, half)]
        return send(mine, mine, one_back_send.at[u], one_back_recv.at[u], peer_one)

    def copy_done(u):
        return pltpu.make_async_copy(from_core.at[u], result_ref.at[u], done_sem.at[u])

    def stage_one(u):
        pltpu.make_async_copy(feed_mine.at[0], held.at[u], local_sem.at[u]).wait()
        copy_core(u).wait_recv()
        base_one = where(u)[4]
        away = half - base_one
        add(u, away, half, from_core[u, block(away, half), :])
        copy_one(u).start()
        add(u, base_one, half, from_core[u, block(base_one, half), :])

    def stage_two(u):
        copy_one(u).wait_recv()
        _, bit_two, _, _, base_one, base_two = where(u)
        off = (1 - bit_two) * quarter
        add(u, base_one + off, quarter, from_one[u, block(off, quarter), :])
        copy_two(u).start()
        add(u, base_two, quarter, from_one[u, block(bit_two * quarter, quarter), :])

    def stage_three(u):
        copy_two(u).wait_recv()
        base_two = where(u)[5]
        add(u, base_two, quarter, from_two[u])
        for d in (2, 1, 3):
            copy_line(u, d).start()

    def stage_four(u):
        for d in (1, 2, 3):
            copy_line(u, d).wait_recv()
        base_two = where(u)[5]
        here = block(base_two + z * piece, piece)
        total = held[u, here, :].astype(F32) + from_line[u, 0].astype(F32)
        total = total + from_line[u, 1].astype(F32) + from_line[u, 2].astype(F32)
        from_core[u, here, :] = total.astype(BF)
        for d in (2, 1, 3):
            copy_line_back(u, d).start()

    def stage_five(u):
        for d in (1, 2, 3):
            copy_line_back(u, d).wait_recv()
        copy_two_back(u).start()

    def stage_six(u):
        copy_two_back(u).wait_recv()
        copy_one_back(u).start()

    def stage_seven(u):
        copy_one_back(u).wait_recv()
        copy_done(u).start()

    stages = (stage_one, stage_two, stage_three, stage_four, stage_five, stage_six, stage_seven)

    kept[0] = sums_ref[...]
    small_peers = [
        sibling, {"rep": partner_x}, {"rep": partner_y},
        {"rep": rep + 4 - 8 * (z % 2)}, {"rep": rep + 8 - 16 * (z // 2)},
    ]

    def copy_small(k):
        return send(kept.at[k], came.at[k], small_send.at[k], small_recv.at[k], small_peers[k])

    def tick(t, _):
        for k in reversed(range(len(stages))):
            u = t - k

            @pl.when((u >= 0) & (u < units))
            def _():
                stages[k](u)

        return 0

    copy_small(0).start()
    for k in range(len(small_peers)):
        tick(k, 0)
        copy_small(k).wait_recv()
        kept[k + 1] = kept[k] + came[k]
        if k + 1 < len(small_peers):
            copy_small(k + 1).start()
    lax.fori_loop(len(small_peers), units + len(stages) - 1, tick, 0)
    total_ref[...] = kept[len(small_peers)]

    for k in range(len(small_peers)):
        copy_small(k).wait_send()

    def finish(u, _):
        copy_core(u).wait_send()
        copy_one(u).wait_send()
        copy_two(u).wait_send()
        for d in (1, 2, 3):
            copy_line(u, d).wait_send()
            copy_line_back(u, d).wait_send()
        copy_two_back(u).wait_send()
        copy_one_back(u).wait_send()
        copy_done(u).wait()
        return 0

    lax.fori_loop(0, units, finish, 0)


def reduce_all(feed_grads, out_grads, qkv_grads, sums):
    rows, cols = out_grads[0].shape[1:]
    units = feed_grads[0].shape[0] + out_grads[0].shape[0] + qkv_grads[0].shape[0]
    anywhere = pl.BlockSpec(memory_space=pl.ANY)
    vm = pl.BlockSpec(memory_space=pltpu.VMEM)
    dma = pltpu.SemaphoreType.DMA
    return pl.pallas_call(
        reduce_kernel,
        in_specs=[anywhere] * 6 + [vm],
        out_specs=[anywhere, vm],
        out_shape=[
            jax.ShapeDtypeStruct((units, rows, cols), BF),
            jax.ShapeDtypeStruct(sums.shape, F32),
        ],
        scratch_shapes=[
            pltpu.VMEM((units, rows, cols), BF),
            pltpu.VMEM((units, rows, cols), BF),
            pltpu.VMEM((units, rows // 2, cols), BF),
            pltpu.VMEM((units, rows // 4, cols), BF),
            pltpu.VMEM((units, 3, rows // 16, cols), BF),
            pltpu.VMEM((6,) + sums.shape, F32),
            pltpu.VMEM((5,) + sums.shape, F32),
            dma((units,)), dma((units,)), dma((units,)), dma((units,)), dma((units,)), dma((units,)), dma((units,)),
            dma((units, 3)), dma((units, 3)), dma((units, 3)), dma((units, 3)),
            dma((units,)), dma((units,)), dma((units,)), dma((units,)),
            dma((5,)), dma((5,)), dma((units,)),
        ],
        compiler_params=params(collective_id=0, has_side_effects=True),
        cost_estimate=cost(0, 4 * units * rows * cols),
        name="reduce_all",
    )(*feed_grads, *out_grads, *qkv_grads, sums)


def finish_kernel(core_ref, units_ref, sums_ref, qkv_ref, out_ref, up_ref, dn_ref, small_ref):
    units, rows, half = units_ref.shape
    groups = rows // GROUP
    chunks = (units - 1 - groups) // 2
    wide = [slice(0, rows // 2), slice(rows // 2, rows)]
    for c in range(chunks):
        for p in range(2):
            dn_ref[c * half : (c + 1) * half, p * half : (p + 1) * half] = units_ref[2 * c, wide[p], :].astype(F32)
            at = p * chunks * half + c * half
            up_ref[:, at : at + half] = units_ref[2 * c + 1, wide[p], :].astype(F32)
    for p in range(2):
        out_ref[:, p * half : (p + 1) * half] = units_ref[2 * chunks, wide[p], :].astype(F32)
    for g in range(groups):
        for j in range(3 * GROUP // 128):
            col = j * 128
            at = (col // GROUP) * rows + g * GROUP + col % GROUP
            qkv_ref[:, at : at + 128] = units_ref[
                2 * chunks + 1 + g, wide[col // half], col % half : col % half + 128
            ].astype(F32)
    mine = pl.ds(pl.multiple_of(core_ref[0] * half, half), half)
    small_ref[...] = sums_ref[:, mine]


def finish(core, units, sums):
    count, rows, half = units.shape
    groups = rows // GROUP
    hidden = (count - 1 - groups) // 2 * rows
    vm = pl.BlockSpec(memory_space=pltpu.VMEM)
    return pl.pallas_call(
        finish_kernel,
        in_specs=[pl.BlockSpec(memory_space=pltpu.SMEM), vm, vm],
        out_specs=[vm] * 5,
        out_shape=[
            jax.ShapeDtypeStruct((half, 3 * rows), F32),
            jax.ShapeDtypeStruct((half, rows), F32),
            jax.ShapeDtypeStruct((half, hidden), F32),
            jax.ShapeDtypeStruct((hidden // 2, rows), F32),
            jax.ShapeDtypeStruct((sums.shape[0], half), F32),
        ],
        compiler_params=params(),
        name="finish",
    )(core, units, sums)


def swap(value):
    return lax.ppermute(value, "shard", [(0, 1), (1, 0)])


def small_rows(biases, gain, shift, hidden_bias):
    rows = biases.shape[0]
    return jnp.concatenate([biases.T, gain.T, shift.T, hidden_bias.reshape(-1, rows)], axis=0)


def reduce_plain(feed_grads, out_grads, qkv_grads, sums):
    def whole(mine, theirs):
        count, rows, half = mine.shape
        cut = lambda a: a.reshape(count, 2, half, half).transpose(0, 2, 1, 3).reshape(count, half, rows)
        return jnp.concatenate([cut(mine), cut(theirs)], axis=1)

    feed_all, out_all, qkv_all = whole(*feed_grads), whole(*out_grads), whole(*qkv_grads)
    chunks, groups, width = feed_all.shape[0] // 2, qkv_all.shape[0], feed_all.shape[2]
    half, units = width // 2, chunks * width
    grads = (
        qkv_all.reshape(groups, width, 3, GROUP).transpose(1, 2, 0, 3).reshape(width, 3 * width),
        out_all[0],
        feed_all[1::2].reshape(chunks, width, 2, half).transpose(1, 2, 0, 3).reshape(width, units),
        feed_all[0::2].reshape(chunks, 2, half, width).transpose(1, 0, 2, 3).reshape(units, width),
        sums[0:4].T.astype(BF),
        sums[8:].reshape(chunks, 2, half).transpose(1, 0, 2).reshape(-1).astype(BF),
        sums[4:6].T.astype(BF),
        sums[6:8].T.astype(BF),
    )
    owned = lax.psum_scatter(grads, "shard", scatter_dimension=0, tiled=True)
    return jax.tree.map(lambda part: part.astype(F32), lax.psum(owned, "rep"))


def body(tokens, teacher, block_ids, *weights):
    qkv, out, up, down, biases, hidden_bias, gain, shift = weights
    paired = lax.axis_size("shard") == 2 and lax.axis_size("rep") == 16
    if paired:
        core = lax.axis_index("shard").reshape(1)
        own = (qkv, out, up, down)
        small_own = small_rows(biases, gain, shift, hidden_bias)
        small_other = swap(small_own)
        other = tuple(swap(w) for w in own)
    else:
        core = jnp.zeros((1,), jnp.int32)
        gathered = [lax.all_gather(w, "shard", axis=0, tiled=True) for w in weights]
        cut = [jnp.split(w, 2, axis=0) for w in gathered]
        own, other = (tuple(c[i] for c in cut[:4]) for i in range(2))
        small_own, small_other = (small_rows(cut[4][i], cut[6][i], cut[7][i], cut[5][i]) for i in range(2))
    final, token_grad, *grads, sums = layer(core, tokens, teacher, block_ids, own, other, small_own, small_other)
    if not paired:
        return (final, token_grad) + tuple(reduce_plain(*grads, sums))
    sums = jnp.concatenate([sums, jnp.zeros((16 - sums.shape[0], sums.shape[1]), F32)], axis=0)
    qkv_grad, out_grad, up_grad, dn_grad, small = finish(core, *reduce_all(*grads, sums))
    hidden_rows = hidden_bias.shape[0] // small.shape[1]
    return (
        final, token_grad, qkv_grad, out_grad, up_grad, dn_grad,
        small[0:4].T, small[8 : 8 + hidden_rows].reshape(-1), small[4:6].T, small[6:8].T,
    )


def solution(mesh):
    placed = (
        P(("shard", "rep"), None, None),
        P(("shard", "rep"), None, None),
        P(("shard", "rep"), None),
        P("shard", None),
        P("shard", None),
        P("shard", None),
        P("shard", None),
        P("shard", None),
        P("shard"),
        P("shard", None),
        P("shard", None),
    )
    return jax.shard_map(
        body,
        mesh=mesh,
        in_specs=placed,
        out_specs=placed[:2] + placed[3:],
        check_vma=False,
    )
```

```python
import functools

import jax
import jax.numpy as jnp
from jax import lax
from jax.experimental import pallas as pl
from jax.experimental.pallas import tpu as pltpu
from jax.sharding import PartitionSpec as P

HEAD_DIM = 64
EPS = 1e-05
NEG = -1e30
BF = jnp.bfloat16
F32 = jnp.float32
MB = 1 << 20


def params(mb=56, **kw):
    return pltpu.CompilerParams(vmem_limit_bytes=mb * MB, **kw)


def dot(a, b):
    return jnp.dot(a, b, preferred_element_type=F32)


def dot_nt(a, b):
    return lax.dot_general(a, b, (((1,), (1,)), ((), ())), preferred_element_type=F32)


def dot_tn(a, b):
    return lax.dot_general(a, b, (((0,), (0,)), ((), ())), preferred_element_type=F32)


def full(shape):
    return pl.BlockSpec(shape, lambda *_: (0,) * len(shape))


def cost(flops, nbytes, trans=0):
    return pl.CostEstimate(flops=int(flops), bytes_accessed=int(nbytes), transcendentals=int(trans))


def deal(core, acc, mine_ref, theirs_ref, at=0):
    half = acc.shape[0] // 2
    wide = acc.shape[1] // 2
    for ref, who in ((mine_ref, core), (theirs_ref, 1 - core)):
        rows = pl.ds(pl.multiple_of(who * half, half), half)
        ref[at, 0:half, :] = acc[rows, 0:wide].astype(BF)
        ref[at, half : 2 * half, :] = acc[rows, wide : 2 * wide].astype(BF)


def binary_halves(first, second):
    rows = 2 * first.shape[0]
    total = jnp.sum(jnp.abs(first.astype(F32)), axis=0, keepdims=True) + jnp.sum(
        jnp.abs(second.astype(F32)), axis=0, keepdims=True
    )
    scale = (total / rows).astype(BF)
    return (
        jnp.where(first >= 0, scale, -scale).astype(BF),
        jnp.where(second >= 0, scale, -scale).astype(BF),
    )


def prep_qkv_kernel(core_ref, own_ref, other_ref, small_own_ref, small_other_ref, out_ref, small_ref):
    core = core_ref[0]
    half = own_ref.shape[0]
    own_at = pl.multiple_of(core * half, half)
    other_at = pl.multiple_of((1 - core) * half, half)
    own, other = binary_halves(own_ref[...], other_ref[...])
    out_ref[pl.ds(own_at, half), :] = own
    out_ref[pl.ds(other_at, half), :] = other

    @pl.when(pl.program_id(0) == 0)
    def _():
        small_ref[:, pl.ds(own_at, half)] = small_own_ref[...].astype(F32)
        small_ref[:, pl.ds(other_at, half)] = small_other_ref[...].astype(F32)


def prep_qkv(core, own, other, small_own, small_other):
    half, cols = own.shape
    rows = 2 * half
    step = rows
    return pl.pallas_call(
        prep_qkv_kernel,
        grid_spec=pltpu.PrefetchScalarGridSpec(
            num_scalar_prefetch=1,
            grid=(cols // step,),
            in_specs=[
                pl.BlockSpec((half, step), lambda j, c: (0, j)),
                pl.BlockSpec((half, step), lambda j, c: (0, j)),
                full(small_own.shape),
                full(small_own.shape),
            ],
            out_specs=[
                pl.BlockSpec((rows, step), lambda j, c: (0, j)),
                full((small_own.shape[0], rows)),
            ],
        ),
        out_shape=[
            jax.ShapeDtypeStruct((rows, cols), BF),
            jax.ShapeDtypeStruct((small_own.shape[0], rows), F32),
        ],
        compiler_params=params(),
        cost_estimate=cost(4 * rows * cols, 4 * rows * cols),
        name="prep_qkv",
    )(core, own, other, small_own, small_other)


def prep_rest_kernel(core_ref, out_a, out_b, up_a, up_b, dn_a, dn_b, out_ref, up_ref, dn_ref):
    core = core_ref[0]
    half = out_a.shape[0]
    width = 2 * half
    own_at = pl.multiple_of(core * half, half)
    other_at = pl.multiple_of((1 - core) * half, half)
    own, other = binary_halves(out_a[...], out_b[...])
    out_ref[pl.ds(own_at, half), :] = own
    out_ref[pl.ds(other_at, half), :] = other
    hidden = up_a.shape[1]
    chunks = hidden // width
    for j in range(hidden // half):
        own, other = binary_halves(up_a[:, j * half : (j + 1) * half], up_b[:, j * half : (j + 1) * half])
        at = (j % chunks) * width + (j // chunks) * half
        up_ref[pl.ds(own_at, half), at : at + half] = own
        up_ref[pl.ds(other_at, half), at : at + half] = other
    own, other = binary_halves(dn_a[...], dn_b[...])
    for c in range(chunks):
        dn_ref[pl.ds(pl.multiple_of(c * width + own_at, half), half), :] = own[c * half : (c + 1) * half]
        dn_ref[pl.ds(pl.multiple_of(c * width + other_at, half), half), :] = other[c * half : (c + 1) * half]


def prep_rest(core, out_a, out_b, up_a, up_b, dn_a, dn_b):
    half, width = out_a.shape
    hidden = up_a.shape[1]
    vm = pl.BlockSpec(memory_space=pltpu.VMEM)
    return pl.pallas_call(
        prep_rest_kernel,
        in_specs=[pl.BlockSpec(memory_space=pltpu.SMEM)] + [vm] * 6,
        out_specs=[vm] * 3,
        out_shape=[
            jax.ShapeDtypeStruct((width, width), BF),
            jax.ShapeDtypeStruct((width, hidden), BF),
            jax.ShapeDtypeStruct((hidden, width), BF),
        ],
        compiler_params=params(),
        cost_estimate=cost(8 * width * hidden, 8 * width * hidden),
        name="prep_rest",
    )(core, out_a, out_b, up_a, up_b, dn_a, dn_b)


def attend_kernel(
    tokens_ref, rows_ref, cols_ref, qkv_ref, out_ref, small_ref, joined_ref, ctx_ref, lse_ref, norm_ref, inv_ref,
    bias_ref,
):
    length, width = tokens_ref.shape[1:]
    x = tokens_ref[0]
    for part, bias_row in ((0, 0), (1, None), (2, 1)):
        joined = dot(x, qkv_ref[:, part * width : (part + 1) * width])
        if bias_row is not None:
            joined = joined + small_ref[bias_row : bias_row + 1, :]
        joined_ref[0, :, part * width : (part + 1) * width] = joined.astype(BF)
    bias_ref[...] = jnp.where(cols_ref[0] >= rows_ref[0], 0.0, NEG).astype(F32)
    lane = lax.broadcasted_iota(jnp.int32, (length, 128), 1)
    low = lane < HEAD_DIM
    lse_all = jnp.zeros((length, 128), F32)
    tile = min(TILE_F, length)
    for pair in range(width // 128):
        q2 = joined_ref[0, :, pair * 128 : pair * 128 + 128] * BF(0.125)
        k2 = joined_ref[0, :, width + pair * 128 : width + pair * 128 + 128]
        v2 = joined_ref[0, :, 2 * width + pair * 128 : 2 * width + pair * 128 + 128]
        for t in range(length // tile):
            rows = slice(t * tile, (t + 1) * tile)
            parts = []
            for h in range(2):
                mine = low[rows] if h == 0 else ~low[rows]
                qm = jnp.where(mine, q2[rows], BF(0))
                scores = dot_nt(qm, k2) + bias_ref[rows, :]
                peak = jnp.max(scores, axis=-1, keepdims=True)
                raised = jnp.exp(scores - peak)
                total = jnp.sum(raised, axis=-1, keepdims=True)
                parts.append(dot(raised.astype(BF), v2) / total)
                lse_ref_col = peak + jnp.log(total)
                bias_lane = lane[rows] == 2 * pair + h
                lse_cols = jnp.where(bias_lane, lse_ref_col, 0.0)
                if h == 0:
                    pair_lse = lse_cols
                else:
                    pair_lse = pair_lse + lse_cols
            ctx_ref[0, rows, pair * 128 : pair * 128 + 128] = jnp.where(low[rows], parts[0], parts[1]).astype(BF)
            if t == 0:
                tiles_lse = [pair_lse]
            else:
                tiles_lse.append(pair_lse)
        lse_all = lse_all + jnp.concatenate(tiles_lse, axis=0)
    lse_ref[0] = lse_all.T[0:16, :]
    resid = x.astype(F32) + dot(ctx_ref[0], out_ref[...]) + small_ref[2:3, :]
    center = resid - jnp.mean(resid, axis=-1, keepdims=True)
    inverse = lax.rsqrt(jnp.mean(center * center, axis=-1, keepdims=True) + EPS)
    norm_ref[0] = center * inverse
    inv_ref[0] = inverse


TILE_F = 256


def attend(tokens, block_ids, qkv_bin, out_bin, small):
    seqs, length, width = tokens.shape
    rows = block_ids.reshape(seqs, 1, length)
    cols = block_ids.reshape(seqs, length, 1)
    per_seq = lambda *shape: pl.BlockSpec((1,) + shape, lambda s: (s,) + (0,) * len(shape))
    return pl.pallas_call(
        attend_kernel,
        grid=(seqs,),
        in_specs=[
            per_seq(length, width),
            per_seq(1, length),
            per_seq(length, 1),
            full(qkv_bin.shape),
            full(out_bin.shape),
            full(small.shape),
        ],
        out_specs=[
            per_seq(length, 3 * width),
            per_seq(length, width),
            per_seq(16, length),
            per_seq(length, width),
            per_seq(length, 1),
        ],
        out_shape=[
            jax.ShapeDtypeStruct((seqs, length, 3 * width), BF),
            jax.ShapeDtypeStruct((seqs, length, width), BF),
            jax.ShapeDtypeStruct((seqs, 16, length), F32),
            jax.ShapeDtypeStruct((seqs, length, width), F32),
            jax.ShapeDtypeStruct((seqs, length, 1), F32),
        ],
        scratch_shapes=[pltpu.VMEM((length, length), F32)],
        compiler_params=params(),
        cost_estimate=cost(seqs * length * width * (8 * width + 16 * length), 30 * seqs * length * width),
        name="attend",
    )(tokens, rows, cols, qkv_bin, out_bin, small)


def gelu_pair(u):
    cdf = 0.5 + 0.5 * lax.erf(u * 0.7071067811865476)
    density = jnp.exp(-0.5 * u * u) * 0.3989422804014327
    return u * cdf, cdf + u * density


def norm_back(upstream, normed, inverse, gain):
    scaled = upstream * gain
    weighted = upstream * normed
    centered = (
        scaled
        - jnp.mean(scaled, axis=-1, keepdims=True)
        - normed * jnp.mean(weighted * gain, axis=-1, keepdims=True)
    )
    return centered * inverse, jnp.sum(weighted, axis=0, keepdims=True), jnp.sum(upstream, axis=0, keepdims=True)


def feed_kernel(
    norm_ref, teacher_ref, small_ref, up_ref, dn_ref,
    final_ref, first_low_ref, hidden_ref, slope_ref, second_ref, mixed_ref, sums_ref,
):
    width = norm_ref.shape[2]
    first = norm_ref[0] * small_ref[4:5, :] + small_ref[6:7, :]
    first_low = first.astype(BF)
    first_low_ref[0] = first_low
    acc = first + small_ref[3:4, :]
    for c in range(up_ref.shape[1] // width):
        cols = slice(c * width, (c + 1) * width)
        pre = dot(first_low, up_ref[:, cols]) + small_ref[8 + c : 9 + c, :]
        value, slope = gelu_pair(pre)
        value = value.astype(BF)
        hidden_ref[0, :, cols] = value
        slope_ref[0, :, cols] = slope.astype(BF)
        acc = acc + dot(value, dn_ref[cols, :])
    center = acc - jnp.mean(acc, axis=-1, keepdims=True)
    inverse = lax.rsqrt(jnp.mean(center * center, axis=-1, keepdims=True) + EPS)
    normed = center * inverse
    gain = small_ref[5:6, :]
    final = normed * gain + small_ref[7:8, :]
    final_ref[0] = final.astype(BF)
    upstream = final - teacher_ref[0].astype(F32)
    second, gain_sum, shift_sum = norm_back(upstream, normed, inverse, gain)
    second_ref[0] = second
    mixed_ref[0] = second.astype(BF)

    @pl.when(pl.program_id(0) == 0)
    def _():
        sums_ref[...] = jnp.zeros_like(sums_ref)

    sums_ref[3:4, :] += jnp.sum(second, axis=0, keepdims=True)
    sums_ref[5:6, :] += gain_sum
    sums_ref[7:8, :] += shift_sum


def feed(norm, teacher, small, up_bin, dn_bin):
    seqs, length, width = norm.shape
    hidden = up_bin.shape[1]
    per_seq = lambda *shape: pl.BlockSpec((1,) + shape, lambda s: (s,) + (0,) * len(shape))
    like = lambda n, dt: jax.ShapeDtypeStruct((seqs, length, n), dt)
    return pl.pallas_call(
        feed_kernel,
        grid=(seqs,),
        in_specs=[
            per_seq(length, width),
            per_seq(length, width),
            full(small.shape),
            full(up_bin.shape),
            full(dn_bin.shape),
        ],
        out_specs=[
            per_seq(length, width),
            per_seq(length, width),
            per_seq(length, hidden),
            per_seq(length, hidden),
            per_seq(length, width),
            per_seq(length, width),
            full((16, width)),
        ],
        out_shape=[
            like(width, BF), like(width, BF), like(hidden, BF), like(hidden, BF), like(width, F32), like(width, BF),
            jax.ShapeDtypeStruct((16, width), F32),
        ],
        compiler_params=params(),
        cost_estimate=cost(4 * seqs * length * width * hidden, 36 * seqs * length * width),
        name="feed",
    )(norm, teacher, small, up_bin, dn_bin)


def feed_back_kernel(
    core_ref, mixed_ref, first_ref, hidden_ref, slope_ref, dn_ref, sums_in_ref,
    pre_ref, mine_ref, theirs_ref, sums_ref, dacc, uacc,
):
    chunk, tile = pl.program_id(0), pl.program_id(1)

    @pl.when((chunk == 0) & (tile == 0))
    def _():
        sums_ref[...] = sums_in_ref[...]

    mixed = mixed_ref[0]
    pre_back = dot_nt(mixed, dn_ref[...]) * slope_ref[0].astype(F32)
    pre_low = pre_back.astype(BF)
    pre_ref[0] = pre_low
    dpart = dot_tn(hidden_ref[0], mixed)
    upart = dot_tn(first_ref[0], pre_low)
    hpart = jnp.sum(pre_back, axis=0, keepdims=True)

    @pl.when(tile == 0)
    def _():
        dacc[...] = dpart
        uacc[...] = upart

    @pl.when(tile > 0)
    def _():
        dacc[...] += dpart
        uacc[...] += upart

    sums_ref[pl.ds(8 + chunk, 1), :] += hpart

    @pl.when(tile == pl.num_programs(1) - 1)
    def _():
        deal(core_ref[0], dacc, mine_ref, theirs_ref, 0)
        deal(core_ref[0], uacc, mine_ref, theirs_ref, 1)


def feed_back(core, mixed, first_low, hidden, slope, dn_bin, sums):
    seqs, length, width = mixed.shape
    units = hidden.shape[2]
    chunks = units // width
    return pl.pallas_call(
        feed_back_kernel,
        grid_spec=pltpu.PrefetchScalarGridSpec(
            num_scalar_prefetch=1,
            grid=(chunks, seqs),
            in_specs=[
                pl.BlockSpec((1, length, width), lambda c, s, _: (s, 0, 0)),
                pl.BlockSpec((1, length, width), lambda c, s, _: (s, 0, 0)),
                pl.BlockSpec((1, length, width), lambda c, s, _: (s, 0, c)),
                pl.BlockSpec((1, length, width), lambda c, s, _: (s, 0, c)),
                pl.BlockSpec((width, width), lambda c, s, _: (c, 0)),
                full(sums.shape),
            ],
            out_specs=[
                pl.BlockSpec((1, length, width), lambda c, s, _: (s, 0, c)),
                pl.BlockSpec((2, width, width // 2), lambda c, s, _: (c, 0, 0)),
                pl.BlockSpec((2, width, width // 2), lambda c, s, _: (c, 0, 0)),
                full(sums.shape),
            ],
            scratch_shapes=[pltpu.VMEM((width, width), F32), pltpu.VMEM((width, width), F32)],
        ),
        out_shape=[
            jax.ShapeDtypeStruct((seqs, length, units), BF),
            jax.ShapeDtypeStruct((2 * chunks, width, width // 2), BF),
            jax.ShapeDtypeStruct((2 * chunks, width, width // 2), BF),
            jax.ShapeDtypeStruct(sums.shape, F32),
        ],
        compiler_params=params(),
        cost_estimate=cost(6 * seqs * length * width * units, 20 * seqs * length * units),
        name="feed_back",
    )(core, mixed, first_low, hidden, slope, dn_bin, sums)


def norm_kernel(
    core_ref, second_ref, pre_ref, norm_ref, inv_ref, ctx_ref, up_ref, out_ref, small_ref, sums_in_ref,
    resid_ref, cback_ref, rowdot_ref, mine_ref, theirs_ref, sums_ref, oacc,
):
    s = pl.program_id(0)
    width = second_ref.shape[2]
    back = second_ref[0] + dot_nt(pre_ref[0], up_ref[...])
    resid, gain_sum, shift_sum = norm_back(back, norm_ref[0], inv_ref[0], small_ref[4:5, :])
    resid_ref[0] = resid
    low = resid.astype(BF)
    cback = dot_nt(low, out_ref[...]).astype(BF)
    cback_ref[0] = cback
    ctx = ctx_ref[0]
    opart = dot_tn(ctx, low)
    prod = cback.astype(F32) * ctx.astype(F32)
    high = prod.astype(BF)
    rest = (prod - high.astype(F32)).astype(BF)
    heads = lax.broadcasted_iota(jnp.int32, (16, width), 0)
    lanes = lax.broadcasted_iota(jnp.int32, (16, width), 1)
    pick = jnp.where((lanes >= heads * HEAD_DIM) & (lanes < heads * HEAD_DIM + HEAD_DIM), 1.0, 0.0).astype(BF)
    rowdot_ref[0] = dot_nt(pick, high) + dot_nt(pick, rest)

    @pl.when(s == 0)
    def _():
        oacc[...] = opart
        sums_ref[...] = sums_in_ref[...]

    @pl.when(s > 0)
    def _():
        oacc[...] += opart

    sums_ref[2:3, :] += jnp.sum(resid, axis=0, keepdims=True)
    sums_ref[4:5, :] += gain_sum
    sums_ref[6:7, :] += shift_sum

    @pl.when(s == pl.num_programs(0) - 1)
    def _():
        deal(core_ref[0], oacc, mine_ref, theirs_ref)


def norm_one_back(core, second, pre_low, norm, inv, ctx, up_bin, out_bin, small, sums):
    seqs, length, width = second.shape
    per_seq = lambda *shape: pl.BlockSpec((1,) + shape, lambda s, _: (s,) + (0,) * len(shape))
    return pl.pallas_call(
        norm_kernel,
        grid_spec=pltpu.PrefetchScalarGridSpec(
        num_scalar_prefetch=1,
        grid=(seqs,),
        in_specs=[
            per_seq(length, width),
            per_seq(length, pre_low.shape[2]),
            per_seq(length, width),
            per_seq(length, 1),
            per_seq(length, width),
            full(up_bin.shape),
            full(out_bin.shape),
            full(small.shape),
            full(sums.shape),
        ],
        out_specs=[
            per_seq(length, width),
            per_seq(length, width),
            per_seq(16, length),
            full((1, width, width // 2)),
            full((1, width, width // 2)),
            full(sums.shape),
        ],
        scratch_shapes=[pltpu.VMEM((width, width), F32)],
        ),
        out_shape=[
            jax.ShapeDtypeStruct((seqs, length, width), F32),
            jax.ShapeDtypeStruct((seqs, length, width), BF),
            jax.ShapeDtypeStruct((seqs, 16, length), F32),
            jax.ShapeDtypeStruct((1, width, width // 2), BF),
            jax.ShapeDtypeStruct((1, width, width // 2), BF),
            jax.ShapeDtypeStruct(sums.shape, F32),
        ],
        compiler_params=params(),
        cost_estimate=cost(2 * seqs * length * width * 6 * width, 40 * seqs * length * width),
        name="norm_one_back",
    )(core, second, pre_low, norm, inv, ctx, up_bin, out_bin, small, sums)


MESH = pl.DeviceIdType.MESH

LATE = (0, 2, 4, 6, 8, 10, 12)
SMALL = 5


class Exchange:
    def __init__(self, result_ref, held, from_core, from_one, from_two, from_line, kept, came, sems):
        (
            local_sem, core_send, core_recv, one_send, one_recv, two_send, two_recv, line_send, line_recv,
            line_back_send, line_back_recv, two_back_send, two_back_recv, one_back_send, one_back_recv,
            small_send, small_recv, done_sem,
        ) = sems
        core, rep = lax.axis_index("shard"), lax.axis_index("rep")
        x, y, z = rep % 2, (rep // 2) % 2, rep // 4
        units, rows = held.shape[0], held.shape[1]
        half, quarter, piece = rows // 2, rows // 4, rows // 16
        partner_x, partner_y = rep + 1 - 2 * x, rep + 2 - 4 * y
        sibling = {"shard": 1 - core}

        def along(step):
            return {"rep": rep % 4 + 4 * ((z + step) % 4)}

        def meet():
            barrier = pltpu.get_barrier_semaphore()
            peers = [sibling, {"rep": partner_x}, {"rep": partner_y}, along(1), along(2), along(3)]
            for peer in peers:
                pl.semaphore_signal(barrier, inc=1, device_id=peer, device_id_type=MESH)
            pl.semaphore_wait(barrier, len(peers))

        def send(src, dst, send_sem, recv_sem, peer):
            return pltpu.make_async_remote_copy(
                src_ref=src, dst_ref=dst, send_sem=send_sem, recv_sem=recv_sem, device_id=peer, device_id_type=MESH
            )

        def begin(u, theirs, mine=None):
            send(theirs, from_core.at[u], core_send.at[u], core_recv.at[u], sibling).start()
            if mine is not None:
                pltpu.make_async_copy(mine, held.at[u], local_sem.at[u]).start()

        def fetched(u):
            pltpu.make_async_copy(from_core.at[u], held.at[u], local_sem.at[u]).wait()

        def where(u):
            odd = u % 2
            bit_one = x + odd * (y - x)
            bit_two = y + odd * (x - y)
            peer_one = {"rep": partner_x + odd * (partner_y - partner_x)}
            peer_two = {"rep": partner_y + odd * (partner_x - partner_y)}
            base_one = bit_one * half
            base_two = base_one + bit_two * quarter
            return bit_one, bit_two, peer_one, peer_two, base_one, base_two

        def block(at, size):
            return pl.ds(pl.multiple_of(at, piece), size)

        def add(u, at, size, other):
            here = block(at, size)
            held[u, here, :] = (held[u, here, :].astype(F32) + other.astype(F32)).astype(BF)

        def copy_core(u):
            return send(from_core.at[u], from_core.at[u], core_send.at[u], core_recv.at[u], sibling)

        def copy_one(u):
            bit_one, _, peer_one, _, _, _ = where(u)
            away = block((1 - bit_one) * half, half)
            return send(held.at[u, away], from_one.at[u], one_send.at[u], one_recv.at[u], peer_one)

        def copy_two(u):
            _, bit_two, _, peer_two, base_one, _ = where(u)
            away = block(base_one + (1 - bit_two) * quarter, quarter)
            return send(held.at[u, away], from_two.at[u], two_send.at[u], two_recv.at[u], peer_two)

        def copy_line(u, d):
            base_two = where(u)[5]
            away = block(base_two + ((z + d) % 4) * piece, piece)
            return send(held.at[u, away], from_line.at[u, d - 1], line_send.at[u, d - 1], line_recv.at[u, d - 1], along(d))

        def copy_line_back(u, d):
            base_two = where(u)[5]
            mine = from_core.at[u, block(base_two + z * piece, piece)]
            return send(mine, mine, line_back_send.at[u, d - 1], line_back_recv.at[u, d - 1], along(d))

        def copy_two_back(u):
            _, _, _, peer_two, _, base_two = where(u)
            mine = from_core.at[u, block(base_two, quarter)]
            return send(mine, mine, two_back_send.at[u], two_back_recv.at[u], peer_two)

        def copy_one_back(u):
            _, _, peer_one, _, base_one, _ = where(u)
            mine = from_core.at[u, block(base_one, half)]
            return send(mine, mine, one_back_send.at[u], one_back_recv.at[u], peer_one)

        def copy_done(u):
            return pltpu.make_async_copy(from_core.at[u], result_ref.at[u], done_sem.at[u])

        def stage_one(u):
            copy_core(u).wait_recv()
            base_one = where(u)[4]
            away = half - base_one
            add(u, away, half, from_core[u, block(away, half), :])
            copy_one(u).start()
            add(u, base_one, half, from_core[u, block(base_one, half), :])

        def stage_two(u):
            copy_one(u).wait_recv()
            _, bit_two, _, _, base_one, base_two = where(u)
            off = (1 - bit_two) * quarter
            add(u, base_one + off, quarter, from_one[u, block(off, quarter), :])
            copy_two(u).start()
            add(u, base_two, quarter, from_one[u, block(bit_two * quarter, quarter), :])

        def stage_three(u):
            copy_two(u).wait_recv()
            base_two = where(u)[5]
            add(u, base_two, quarter, from_two[u])
            for d in (2, 1, 3):
                copy_line(u, d).start()

        def stage_four(u):
            for d in (1, 2, 3):
                copy_line(u, d).wait_recv()
            base_two = where(u)[5]
            here = block(base_two + z * piece, piece)
            total = held[u, here, :].astype(F32) + from_line[u, 0].astype(F32)
            total = total + from_line[u, 1].astype(F32) + from_line[u, 2].astype(F32)
            from_core[u, here, :] = total.astype(BF)
            for d in (2, 1, 3):
                copy_line_back(u, d).start()

        def stage_five(u):
            for d in (1, 2, 3):
                copy_line_back(u, d).wait_recv()
            copy_two_back(u).start()

        def stage_six(u):
            copy_two_back(u).wait_recv()
            copy_one_back(u).start()

        def stage_seven(u):
            copy_one_back(u).wait_recv()
            copy_done(u).start()

        stages = (stage_one, stage_two, stage_three, stage_four, stage_five, stage_six, stage_seven)

        small_peers = [
            sibling, {"rep": partner_x}, {"rep": partner_y},
            {"rep": rep + 4 - 8 * (z % 2)}, {"rep": rep + 8 - 16 * (z // 2)},
        ]

        def copy_small(k):
            return send(kept.at[k], came.at[k], small_send.at[k], small_recv.at[k], small_peers[k])

        def small_next(k):
            copy_small(k).wait_recv()
            kept[k + 1] = kept[k] + came[k]
            if k + 1 < SMALL:
                copy_small(k + 1).start()

        def tick(t, _=0):
            for k, late in enumerate(LATE):
                u = t - late

                @pl.when((u >= 0) & (u < units))
                def _():
                    stages[k](u)

            return 0

        def settle():
            for k in range(SMALL):
                copy_small(k).wait_send()

            def finish(u, _):
                copy_core(u).wait_send()
                copy_one(u).wait_send()
                copy_two(u).wait_send()
                for d in (1, 2, 3):
                    copy_line(u, d).wait_send()
                    copy_line_back(u, d).wait_send()
                copy_two_back(u).wait_send()
                copy_one_back(u).wait_send()
                copy_done(u).wait()
                return 0

            lax.fori_loop(0, units, finish, 0)

        self.meet, self.begin, self.fetched, self.tick, self.settle = meet, begin, fetched, tick, settle
        self.small_start, self.small_next = (lambda: copy_small(0).start()), small_next
        self.ticks = units + LATE[-1]

    @staticmethod
    def buffers(units, rows, cols, small):
        dma = pltpu.SemaphoreType.DMA
        return [
            pltpu.VMEM((units, rows, cols), BF),
            pltpu.VMEM((units, rows, cols), BF),
            pltpu.VMEM((units, rows // 2, cols), BF),
            pltpu.VMEM((units, rows // 4, cols), BF),
            pltpu.VMEM((units, 3, rows // 16, cols), BF),
            pltpu.VMEM((SMALL + 1,) + small, F32),
            pltpu.VMEM((SMALL,) + small, F32),
        ] + [dma((units,))] * 7 + [dma((units, 3))] * 4 + [dma((units,))] * 4 + [dma((SMALL,))] * 2 + [dma((units,))]


GROUP = 256
TILE_B = 256


def attend_back_kernel(linked, *refs):
    (tokens_ref, rows_ref, cols_ref, q_ref, k_ref, v_ref, cback_ref, lse_ref, rowdot_ref, sums_in_ref), refs = (
        refs[:10], refs[10:]
    )
    g, s = pl.program_id(0), pl.program_id(1)
    last_g, last_s = pl.num_programs(0) - 1, pl.num_programs(1) - 1
    if linked:
        feed_mine, feed_theirs, out_mine, out_theirs, jlow_ref, result_ref, total_ref, acc, bias_ref, theirs = refs[:10]
        buffers, sems = refs[10:17], refs[17:]
        exchange = Exchange(result_ref, *buffers, sems)
        held, kept = buffers[0], buffers[5]
        core = lax.axis_index("shard")
        early = feed_mine.shape[0] + 1
        sums_ref = kept.at[0]
        step = g * pl.num_programs(1) + s
    else:
        jlow_ref, mine_ref, theirs_ref, sums_ref, acc, bias_ref = refs
        core = 0

    @pl.when((g == 0) & (s == 0))
    def _():
        if linked:
            exchange.meet()
            for u in range(early - 1):
                exchange.begin(u, feed_theirs.at[u], feed_mine.at[u])
            exchange.begin(early - 1, out_theirs.at[0], out_mine.at[0])
            for u in range(early):
                exchange.fetched(u)
        sums_ref[...] = sums_in_ref[...]

    if linked:

        @pl.when(step < pl.num_programs(0) * pl.num_programs(1) - 1)
        def _():
            exchange.tick(step)

    length = tokens_ref.shape[1]
    tile = min(TILE_B, length)
    bias_ref[...] = jnp.where(rows_ref[0] >= cols_ref[0], 0.0, NEG).astype(F32)
    lane = lax.broadcasted_iota(jnp.int32, (length, 128), 1)
    low = lane < HEAD_DIM

    for pair in range(GROUP // 128):
        at = slice(pair * 128, pair * 128 + 128)
        q2 = q_ref[0, :, at] * BF(0.125)
        k2 = k_ref[0, :, at]
        v2 = v_ref[0, :, at]
        do2 = cback_ref[0, :, at]
        dq = None
        for t in range(length // tile):
            rows = slice(t * tile, (t + 1) * tile)
            dks, dvs = [], []
            for h in range(2):
                mine = low[rows] if h == 0 else ~low[rows]
                km = jnp.where(mine, k2[rows], BF(0))
                vm = jnp.where(mine, v2[rows], BF(0))
                head = g * (GROUP // HEAD_DIM) + pair * 2 + h
                lse = lse_ref[0, pl.ds(head, 1), :]
                rowdot = rowdot_ref[0, pl.ds(head, 1), :]
                probs = jnp.exp(dot_nt(km, q2) + bias_ref[rows, :] - lse)
                dprobs = dot_nt(vm, do2)
                dscore = (probs * (dprobs - rowdot)).astype(BF)
                dvs.append(dot(probs.astype(BF), do2))
                dks.append(dot(dscore, q2))
                part = dot_tn(dscore, km * BF(0.125))
                dq = part if dq is None else dq + part
            dk = jnp.where(low[rows], dks[0], dks[1])
            dv = jnp.where(low[rows], dvs[0], dvs[1])
            jlow_ref[0, rows, GROUP + pair * 128 : GROUP + pair * 128 + 128] = dk.astype(BF)
            jlow_ref[0, rows, 2 * GROUP + pair * 128 : 2 * GROUP + pair * 128 + 128] = dv.astype(BF)
            vsum = jnp.sum(dv, axis=0, keepdims=True)
            vtotal = vsum if t == 0 else vtotal + vsum
        jlow_ref[0, :, at] = dq.astype(BF)
        lanes = pl.ds(pl.multiple_of(g * GROUP + pair * 128, 128), 128)
        sums_ref[0:1, lanes] += jnp.sum(dq, axis=0, keepdims=True)
        sums_ref[1:2, lanes] += vtotal

    part = dot_tn(tokens_ref[0], jlow_ref[0])

    @pl.when(s == 0)
    def _():
        acc[...] = part

    @pl.when(s > 0)
    def _():
        acc[...] += part

    @pl.when(s == last_s)
    def _():
        if linked:
            deal(core, acc, held.at[pl.ds(early + g, 1)], theirs.at[pl.ds(g, 1)])
            exchange.begin(early + g, theirs.at[g])
        else:
            deal(core, acc, mine_ref, theirs_ref)

    if linked:

        @pl.when((g == last_g) & (s == last_s))
        def _():
            start = pl.num_programs(0) * pl.num_programs(1) - 1
            exchange.small_start()
            for k in range(SMALL):
                exchange.tick(start + k)
                exchange.small_next(k)
            lax.fori_loop(start + SMALL, exchange.ticks, exchange.tick, 0)
            total_ref[...] = kept[SMALL]
            exchange.settle()


def attend_back(tokens, block_ids, joined, cback, lse, rowdot, sums, feed_grads=None, out_grads=None):
    seqs, length, width = tokens.shape
    rows = block_ids.reshape(seqs, 1, length)
    cols = block_ids.reshape(seqs, length, 1)
    groups = width // GROUP
    linked = feed_grads is not None
    whole = lambda *shape: pl.BlockSpec((1,) + shape, lambda g, s: (s,) + (0,) * len(shape))
    part = lambda k: pl.BlockSpec((1, length, GROUP), lambda g, s: (s, 0, k * groups + g))
    anywhere = pl.BlockSpec(memory_space=pl.ANY)
    unit = (width, width // 2)
    like = jax.ShapeDtypeStruct
    in_specs = [
        whole(length, width), whole(1, length), whole(length, 1), part(0), part(1), part(2), part(0),
        whole(16, length), whole(16, length), full(sums.shape),
    ]
    operands = [tokens, rows, cols, joined, joined, joined, cback, lse, rowdot, sums]
    out_specs = [pl.BlockSpec((1, length, 3 * GROUP), lambda g, s: (s, 0, g))]
    out_shape = [like((seqs, length, 3 * width), BF)]
    scratch = [pltpu.VMEM((width, 3 * GROUP), F32), pltpu.VMEM((length, length), F32)]
    if linked:
        units = feed_grads[0].shape[0] + 1 + groups
        in_specs += [anywhere] * 4
        operands += [*feed_grads, *out_grads]
        out_specs += [anywhere, full(sums.shape)]
        out_shape += [like((units,) + unit, BF), like(sums.shape, F32)]
        scratch += [pltpu.VMEM((groups,) + unit, BF)] + Exchange.buffers(units, *unit, sums.shape)
        extra = dict(collective_id=0, has_side_effects=True)
    else:
        out_specs += [pl.BlockSpec((1,) + unit, lambda g, s: (g, 0, 0))] * 2 + [full(sums.shape)]
        out_shape += [like((groups,) + unit, BF)] * 2 + [like(sums.shape, F32)]
        extra = {}
    return pl.pallas_call(
        functools.partial(attend_back_kernel, linked),
        grid=(groups, seqs),
        in_specs=in_specs,
        out_specs=out_specs,
        out_shape=out_shape,
        scratch_shapes=scratch,
        compiler_params=params(**extra),
        cost_estimate=cost(seqs * length * width * (6 * width + 40 * length), 30 * seqs * length * width),
        name="attend_back",
    )(*operands)


def token_kernel(resid_ref, jlow_ref, qkv_ref, grad_ref):
    width = resid_ref.shape[2]
    groups = width // GROUP
    total = resid_ref[0]
    for g in range(groups):
        for k in range(3):
            at = (3 * g + k) * GROUP
            col = k * width + g * GROUP
            total = total + dot_nt(jlow_ref[0, :, at : at + GROUP], qkv_ref[:, col : col + GROUP])
    grad_ref[0] = total


def token_back(resid, jlow, qkv_bin):
    seqs, length, width = resid.shape
    per_seq = lambda *shape: pl.BlockSpec((1,) + shape, lambda s: (s,) + (0,) * len(shape))
    return pl.pallas_call(
        token_kernel,
        grid=(seqs,),
        in_specs=[per_seq(length, width), per_seq(length, 3 * width), full(qkv_bin.shape)],
        out_specs=per_seq(length, width),
        out_shape=jax.ShapeDtypeStruct((seqs, length, width), F32),
        compiler_params=params(),
        cost_estimate=cost(6 * seqs * length * width * width, 16 * seqs * length * width),
        name="token_back",
    )(resid, jlow, qkv_bin)


def finish_kernel(core_ref, units_ref, sums_ref, qkv_ref, out_ref, up_ref, dn_ref, small_ref):
    units, rows, half = units_ref.shape
    groups = rows // GROUP
    chunks = (units - 1 - groups) // 2
    wide = [slice(0, rows // 2), slice(rows // 2, rows)]
    for c in range(chunks):
        for p in range(2):
            dn_ref[c * half : (c + 1) * half, p * half : (p + 1) * half] = units_ref[2 * c, wide[p], :].astype(F32)
            at = p * chunks * half + c * half
            up_ref[:, at : at + half] = units_ref[2 * c + 1, wide[p], :].astype(F32)
    for p in range(2):
        out_ref[:, p * half : (p + 1) * half] = units_ref[2 * chunks, wide[p], :].astype(F32)
    for g in range(groups):
        for j in range(3 * GROUP // 128):
            col = j * 128
            at = (col // GROUP) * rows + g * GROUP + col % GROUP
            qkv_ref[:, at : at + 128] = units_ref[
                2 * chunks + 1 + g, wide[col // half], col % half : col % half + 128
            ].astype(F32)
    mine = pl.ds(pl.multiple_of(core_ref[0] * half, half), half)
    small_ref[...] = sums_ref[:, mine]


def finish(core, units, sums):
    count, rows, half = units.shape
    groups = rows // GROUP
    hidden = (count - 1 - groups) // 2 * rows
    vm = pl.BlockSpec(memory_space=pltpu.VMEM)
    return pl.pallas_call(
        finish_kernel,
        in_specs=[pl.BlockSpec(memory_space=pltpu.SMEM), vm, vm],
        out_specs=[vm] * 5,
        out_shape=[
            jax.ShapeDtypeStruct((half, 3 * rows), F32),
            jax.ShapeDtypeStruct((half, rows), F32),
            jax.ShapeDtypeStruct((half, hidden), F32),
            jax.ShapeDtypeStruct((hidden // 2, rows), F32),
            jax.ShapeDtypeStruct((sums.shape[0], half), F32),
        ],
        compiler_params=params(),
        name="finish",
    )(core, units, sums)


def swap(value):
    return lax.ppermute(value, "shard", [(0, 1), (1, 0)])


def small_rows(biases, gain, shift, hidden_bias):
    rows = biases.shape[0]
    return jnp.concatenate([biases.T, gain.T, shift.T, hidden_bias.reshape(-1, rows)], axis=0)


def reduce_plain(feed_grads, out_grads, qkv_grads, sums):
    def whole(mine, theirs):
        count, rows, half = mine.shape
        cut = lambda a: a.reshape(count, 2, half, half).transpose(0, 2, 1, 3).reshape(count, half, rows)
        return jnp.concatenate([cut(mine), cut(theirs)], axis=1)

    feed_all, out_all, qkv_all = whole(*feed_grads), whole(*out_grads), whole(*qkv_grads)
    chunks, groups, width = feed_all.shape[0] // 2, qkv_all.shape[0], feed_all.shape[2]
    half, units = width // 2, chunks * width
    grads = (
        qkv_all.reshape(groups, width, 3, GROUP).transpose(1, 2, 0, 3).reshape(width, 3 * width),
        out_all[0],
        feed_all[1::2].reshape(chunks, width, 2, half).transpose(1, 2, 0, 3).reshape(width, units),
        feed_all[0::2].reshape(chunks, 2, half, width).transpose(1, 0, 2, 3).reshape(units, width),
        sums[0:4].T.astype(BF),
        sums[8:].reshape(chunks, 2, half).transpose(1, 0, 2).reshape(-1).astype(BF),
        sums[4:6].T.astype(BF),
        sums[6:8].T.astype(BF),
    )
    owned = lax.psum_scatter(grads, "shard", scatter_dimension=0, tiled=True)
    return jax.tree.map(lambda part: part.astype(F32), lax.psum(owned, "rep"))


def body(tokens, teacher, block_ids, *weights):
    qkv, out, up, down, biases, hidden_bias, gain, shift = weights
    paired = lax.axis_size("shard") == 2 and lax.axis_size("rep") == 16
    if paired:
        core = lax.axis_index("shard").reshape(1)
        own = (qkv, out, up, down)
        small_own = small_rows(biases, gain, shift, hidden_bias)
        small_other = swap(small_own)
        other = tuple(swap(w) for w in own)
    else:
        core = jnp.zeros((1,), jnp.int32)
        gathered = [lax.all_gather(w, "shard", axis=0, tiled=True) for w in weights]
        cut = [jnp.split(w, 2, axis=0) for w in gathered]
        own, other = (tuple(c[i] for c in cut[:4]) for i in range(2))
        small_own, small_other = (small_rows(cut[4][i], cut[6][i], cut[7][i], cut[5][i]) for i in range(2))
    qkv_bin, small = prep_qkv(core, own[0], other[0], small_own, small_other)
    out_bin, up_bin, dn_bin = prep_rest(core, own[1], other[1], own[2], other[2], own[3], other[3])
    joined, ctx, lse, norm, inv = attend(tokens, block_ids, qkv_bin, out_bin, small)
    final, first_low, hidden, slope, second, mixed, sums = feed(norm, teacher, small, up_bin, dn_bin)
    pre_low, *feed_grads, sums = feed_back(core, mixed, first_low, hidden, slope, dn_bin, sums)
    resid, cback, rowdot, *out_grads, sums = norm_one_back(
        core, second, pre_low, norm, inv, ctx, up_bin, out_bin, small, sums
    )
    if not paired:
        jlow, *qkv_grads, sums = attend_back(tokens, block_ids, joined, cback, lse, rowdot, sums)
        token_grad = token_back(resid, jlow, qkv_bin)
        return (final, token_grad) + tuple(reduce_plain(feed_grads, out_grads, qkv_grads, sums[:12]))
    jlow, units, sums = attend_back(
        tokens, block_ids, joined, cback, lse, rowdot, sums, feed_grads, out_grads
    )
    token_grad = token_back(resid, jlow, qkv_bin)
    qkv_grad, out_grad, up_grad, dn_grad, small = finish(core, units, sums)
    hidden_rows = hidden_bias.shape[0] // small.shape[1]
    return (
        final, token_grad, qkv_grad, out_grad, up_grad, dn_grad,
        small[0:4].T, small[8 : 8 + hidden_rows].reshape(-1), small[4:6].T, small[6:8].T,
    )


def solution(mesh):
    placed = (
        P(("shard", "rep"), None, None),
        P(("shard", "rep"), None, None),
        P(("shard", "rep"), None),
        P("shard", None),
        P("shard", None),
        P("shard", None),
        P("shard", None),
        P("shard", None),
        P("shard"),
        P("shard", None),
        P("shard", None),
    )
    return jax.shard_map(
        body,
        mesh=mesh,
        in_specs=placed,
        out_specs=placed[:2] + placed[3:],
        check_vma=False,
    )
```

```python
import functools

import jax
import jax.numpy as jnp
from jax import lax
from jax.experimental import pallas as pl
from jax.experimental.pallas import tpu as pltpu
from jax.sharding import PartitionSpec as P

HEAD_DIM = 64
EPS = 1e-05
NEG = -1e30
BF = jnp.bfloat16
F32 = jnp.float32
MB = 1 << 20


def params(mb=56, **kw):
    return pltpu.CompilerParams(vmem_limit_bytes=mb * MB, **kw)


def dot(a, b):
    return jnp.dot(a, b, preferred_element_type=F32)


def dot_nt(a, b):
    return lax.dot_general(a, b, (((1,), (1,)), ((), ())), preferred_element_type=F32)


def dot_tn(a, b):
    return lax.dot_general(a, b, (((0,), (0,)), ((), ())), preferred_element_type=F32)


def full(shape):
    return pl.BlockSpec(shape, lambda *_: (0,) * len(shape))


def cost(flops, nbytes, trans=0):
    return pl.CostEstimate(flops=int(flops), bytes_accessed=int(nbytes), transcendentals=int(trans))


def deal(core, acc, mine_ref, theirs_ref, at=0):
    half = acc.shape[0] // 2
    wide = acc.shape[1] // 2
    for ref, who in ((mine_ref, core), (theirs_ref, 1 - core)):
        rows = pl.ds(pl.multiple_of(who * half, half), half)
        ref[at, 0:half, :] = acc[rows, 0:wide].astype(BF)
        ref[at, half : 2 * half, :] = acc[rows, wide : 2 * wide].astype(BF)


def binary_halves(first, second):
    rows = 2 * first.shape[0]
    total = jnp.sum(jnp.abs(first.astype(F32)), axis=0, keepdims=True) + jnp.sum(
        jnp.abs(second.astype(F32)), axis=0, keepdims=True
    )
    scale = (total / rows).astype(BF)
    return (
        jnp.where(first >= 0, scale, -scale).astype(BF),
        jnp.where(second >= 0, scale, -scale).astype(BF),
    )


def prep_qkv_kernel(core_ref, own_ref, other_ref, small_own_ref, small_other_ref, out_ref, small_ref):
    core = core_ref[0]
    half = own_ref.shape[0]
    own_at = pl.multiple_of(core * half, half)
    other_at = pl.multiple_of((1 - core) * half, half)
    own, other = binary_halves(own_ref[...], other_ref[...])
    out_ref[pl.ds(own_at, half), :] = own
    out_ref[pl.ds(other_at, half), :] = other

    @pl.when(pl.program_id(0) == 0)
    def _():
        small_ref[:, pl.ds(own_at, half)] = small_own_ref[...].astype(F32)
        small_ref[:, pl.ds(other_at, half)] = small_other_ref[...].astype(F32)


def prep_qkv(core, own, other, small_own, small_other):
    half, cols = own.shape
    rows = 2 * half
    step = rows
    return pl.pallas_call(
        prep_qkv_kernel,
        grid_spec=pltpu.PrefetchScalarGridSpec(
            num_scalar_prefetch=1,
            grid=(cols // step,),
            in_specs=[
                pl.BlockSpec((half, step), lambda j, c: (0, j)),
                pl.BlockSpec((half, step), lambda j, c: (0, j)),
                full(small_own.shape),
                full(small_own.shape),
            ],
            out_specs=[
                pl.BlockSpec((rows, step), lambda j, c: (0, j)),
                full((small_own.shape[0], rows)),
            ],
        ),
        out_shape=[
            jax.ShapeDtypeStruct((rows, cols), BF),
            jax.ShapeDtypeStruct((small_own.shape[0], rows), F32),
        ],
        compiler_params=params(),
        cost_estimate=cost(4 * rows * cols, 4 * rows * cols),
        name="prep_qkv",
    )(core, own, other, small_own, small_other)


def prep_rest_kernel(core_ref, out_a, out_b, up_a, up_b, dn_a, dn_b, out_ref, up_ref, dn_ref):
    core = core_ref[0]
    half = out_a.shape[0]
    width = 2 * half
    own_at = pl.multiple_of(core * half, half)
    other_at = pl.multiple_of((1 - core) * half, half)
    own, other = binary_halves(out_a[...], out_b[...])
    out_ref[pl.ds(own_at, half), :] = own
    out_ref[pl.ds(other_at, half), :] = other
    hidden = up_a.shape[1]
    chunks = hidden // width
    for j in range(hidden // half):
        own, other = binary_halves(up_a[:, j * half : (j + 1) * half], up_b[:, j * half : (j + 1) * half])
        at = (j % chunks) * width + (j // chunks) * half
        up_ref[pl.ds(own_at, half), at : at + half] = own
        up_ref[pl.ds(other_at, half), at : at + half] = other
    own, other = binary_halves(dn_a[...], dn_b[...])
    for c in range(chunks):
        dn_ref[pl.ds(pl.multiple_of(c * width + own_at, half), half), :] = own[c * half : (c + 1) * half]
        dn_ref[pl.ds(pl.multiple_of(c * width + other_at, half), half), :] = other[c * half : (c + 1) * half]


def prep_rest(core, out_a, out_b, up_a, up_b, dn_a, dn_b):
    half, width = out_a.shape
    hidden = up_a.shape[1]
    vm = pl.BlockSpec(memory_space=pltpu.VMEM)
    return pl.pallas_call(
        prep_rest_kernel,
        in_specs=[pl.BlockSpec(memory_space=pltpu.SMEM)] + [vm] * 6,
        out_specs=[vm] * 3,
        out_shape=[
            jax.ShapeDtypeStruct((width, width), BF),
            jax.ShapeDtypeStruct((width, hidden), BF),
            jax.ShapeDtypeStruct((hidden, width), BF),
        ],
        compiler_params=params(),
        cost_estimate=cost(8 * width * hidden, 8 * width * hidden),
        name="prep_rest",
    )(core, out_a, out_b, up_a, up_b, dn_a, dn_b)


def attend_kernel(
    tokens_ref, rows_ref, cols_ref, qkv_ref, out_ref, small_ref, joined_ref, ctx_ref, lse_ref, norm_ref, inv_ref,
    bias_ref,
):
    length, width = tokens_ref.shape[1:]
    x = tokens_ref[0]
    for part, bias_row in ((0, 0), (1, None), (2, 1)):
        joined = dot(x, qkv_ref[:, part * width : (part + 1) * width])
        if bias_row is not None:
            joined = joined + small_ref[bias_row : bias_row + 1, :]
        joined_ref[0, :, part * width : (part + 1) * width] = joined.astype(BF)
    bias_ref[...] = jnp.where(cols_ref[0] >= rows_ref[0], 0.0, NEG).astype(F32)
    lane = lax.broadcasted_iota(jnp.int32, (length, 128), 1)
    low = lane < HEAD_DIM
    lse_all = jnp.zeros((length, 128), F32)
    tile = min(TILE_F, length)
    for pair in range(width // 128):
        q2 = joined_ref[0, :, pair * 128 : pair * 128 + 128] * BF(0.125)
        k2 = joined_ref[0, :, width + pair * 128 : width + pair * 128 + 128]
        v2 = joined_ref[0, :, 2 * width + pair * 128 : 2 * width + pair * 128 + 128]
        for t in range(length // tile):
            rows = slice(t * tile, (t + 1) * tile)
            parts = []
            for h in range(2):
                mine = low[rows] if h == 0 else ~low[rows]
                qm = jnp.where(mine, q2[rows], BF(0))
                scores = dot_nt(qm, k2) + bias_ref[rows, :]
                peak = jnp.max(scores, axis=-1, keepdims=True)
                raised = jnp.exp(scores - peak)
                total = jnp.sum(raised, axis=-1, keepdims=True)
                parts.append(dot(raised.astype(BF), v2) / total)
                lse_ref_col = peak + jnp.log(total)
                bias_lane = lane[rows] == 2 * pair + h
                lse_cols = jnp.where(bias_lane, lse_ref_col, 0.0)
                if h == 0:
                    pair_lse = lse_cols
                else:
                    pair_lse = pair_lse + lse_cols
            ctx_ref[0, rows, pair * 128 : pair * 128 + 128] = jnp.where(low[rows], parts[0], parts[1]).astype(BF)
            if t == 0:
                tiles_lse = [pair_lse]
            else:
                tiles_lse.append(pair_lse)
        lse_all = lse_all + jnp.concatenate(tiles_lse, axis=0)
    lse_ref[0] = lse_all.T[0:16, :]
    resid = x.astype(F32) + dot(ctx_ref[0], out_ref[...]) + small_ref[2:3, :]
    center = resid - jnp.mean(resid, axis=-1, keepdims=True)
    inverse = lax.rsqrt(jnp.mean(center * center, axis=-1, keepdims=True) + EPS)
    norm_ref[0] = center * inverse
    inv_ref[0] = inverse


TILE_F = 256


def attend(tokens, block_ids, qkv_bin, out_bin, small):
    seqs, length, width = tokens.shape
    rows = block_ids.reshape(seqs, 1, length)
    cols = block_ids.reshape(seqs, length, 1)
    per_seq = lambda *shape: pl.BlockSpec((1,) + shape, lambda s: (s,) + (0,) * len(shape))
    return pl.pallas_call(
        attend_kernel,
        grid=(seqs,),
        in_specs=[
            per_seq(length, width),
            per_seq(1, length),
            per_seq(length, 1),
            full(qkv_bin.shape),
            full(out_bin.shape),
            full(small.shape),
        ],
        out_specs=[
            per_seq(length, 3 * width),
            per_seq(length, width),
            per_seq(16, length),
            per_seq(length, width),
            per_seq(length, 1),
        ],
        out_shape=[
            jax.ShapeDtypeStruct((seqs, length, 3 * width), BF),
            jax.ShapeDtypeStruct((seqs, length, width), BF),
            jax.ShapeDtypeStruct((seqs, 16, length), F32),
            jax.ShapeDtypeStruct((seqs, length, width), F32),
            jax.ShapeDtypeStruct((seqs, length, 1), F32),
        ],
        scratch_shapes=[pltpu.VMEM((length, length), F32)],
        compiler_params=params(),
        cost_estimate=cost(seqs * length * width * (8 * width + 16 * length), 30 * seqs * length * width),
        name="attend",
    )(tokens, rows, cols, qkv_bin, out_bin, small)


def gelu_pair(u):
    cdf = 0.5 + 0.5 * lax.erf(u * 0.7071067811865476)
    density = jnp.exp(-0.5 * u * u) * 0.3989422804014327
    return u * cdf, cdf + u * density


def norm_back(upstream, normed, inverse, gain):
    scaled = upstream * gain
    weighted = upstream * normed
    centered = (
        scaled
        - jnp.mean(scaled, axis=-1, keepdims=True)
        - normed * jnp.mean(weighted * gain, axis=-1, keepdims=True)
    )
    return centered * inverse, jnp.sum(weighted, axis=0, keepdims=True), jnp.sum(upstream, axis=0, keepdims=True)


def feed_kernel(
    norm_ref, teacher_ref, small_ref, up_ref, dn_ref,
    final_ref, first_low_ref, hidden_ref, slope_ref, second_ref, mixed_ref, sums_ref,
):
    width = norm_ref.shape[2]
    first = norm_ref[0] * small_ref[4:5, :] + small_ref[6:7, :]
    first_low = first.astype(BF)
    first_low_ref[0] = first_low
    acc = first + small_ref[3:4, :]
    for c in range(up_ref.shape[1] // width):
        cols = slice(c * width, (c + 1) * width)
        pre = dot(first_low, up_ref[:, cols]) + small_ref[8 + c : 9 + c, :]
        value, slope = gelu_pair(pre)
        value = value.astype(BF)
        hidden_ref[0, :, cols] = value
        slope_ref[0, :, cols] = slope.astype(BF)
        acc = acc + dot(value, dn_ref[cols, :])
    center = acc - jnp.mean(acc, axis=-1, keepdims=True)
    inverse = lax.rsqrt(jnp.mean(center * center, axis=-1, keepdims=True) + EPS)
    normed = center * inverse
    gain = small_ref[5:6, :]
    final = normed * gain + small_ref[7:8, :]
    final_ref[0] = final.astype(BF)
    upstream = final - teacher_ref[0].astype(F32)
    second, gain_sum, shift_sum = norm_back(upstream, normed, inverse, gain)
    second_ref[0] = second
    mixed_ref[0] = second.astype(BF)

    @pl.when(pl.program_id(0) == 0)
    def _():
        sums_ref[...] = jnp.zeros_like(sums_ref)

    sums_ref[3:4, :] += jnp.sum(second, axis=0, keepdims=True)
    sums_ref[5:6, :] += gain_sum
    sums_ref[7:8, :] += shift_sum


def feed(norm, teacher, small, up_bin, dn_bin):
    seqs, length, width = norm.shape
    hidden = up_bin.shape[1]
    per_seq = lambda *shape: pl.BlockSpec((1,) + shape, lambda s: (s,) + (0,) * len(shape))
    like = lambda n, dt: jax.ShapeDtypeStruct((seqs, length, n), dt)
    return pl.pallas_call(
        feed_kernel,
        grid=(seqs,),
        in_specs=[
            per_seq(length, width),
            per_seq(length, width),
            full(small.shape),
            full(up_bin.shape),
            full(dn_bin.shape),
        ],
        out_specs=[
            per_seq(length, width),
            per_seq(length, width),
            per_seq(length, hidden),
            per_seq(length, hidden),
            per_seq(length, width),
            per_seq(length, width),
            full((16, width)),
        ],
        out_shape=[
            like(width, BF), like(width, BF), like(hidden, BF), like(hidden, BF), like(width, F32), like(width, BF),
            jax.ShapeDtypeStruct((16, width), F32),
        ],
        compiler_params=params(),
        cost_estimate=cost(4 * seqs * length * width * hidden, 36 * seqs * length * width),
        name="feed",
    )(norm, teacher, small, up_bin, dn_bin)


def feed_back_kernel(
    core_ref, mixed_ref, first_ref, hidden_ref, slope_ref, dn_ref, sums_in_ref,
    pre_ref, mine_ref, theirs_ref, sums_ref, dacc, uacc,
):
    chunk, tile = pl.program_id(0), pl.program_id(1)

    @pl.when((chunk == 0) & (tile == 0))
    def _():
        sums_ref[...] = sums_in_ref[...]

    mixed = mixed_ref[0]
    pre_back = dot_nt(mixed, dn_ref[...]) * slope_ref[0].astype(F32)
    pre_low = pre_back.astype(BF)
    pre_ref[0] = pre_low
    dpart = dot_tn(hidden_ref[0], mixed)
    upart = dot_tn(first_ref[0], pre_low)
    hpart = jnp.sum(pre_back, axis=0, keepdims=True)

    @pl.when(tile == 0)
    def _():
        dacc[...] = dpart
        uacc[...] = upart

    @pl.when(tile > 0)
    def _():
        dacc[...] += dpart
        uacc[...] += upart

    sums_ref[pl.ds(8 + chunk, 1), :] += hpart

    @pl.when(tile == pl.num_programs(1) - 1)
    def _():
        deal(core_ref[0], dacc, mine_ref, theirs_ref, 0)
        deal(core_ref[0], uacc, mine_ref, theirs_ref, 1)


def feed_back(core, mixed, first_low, hidden, slope, dn_bin, sums):
    seqs, length, width = mixed.shape
    units = hidden.shape[2]
    chunks = units // width
    return pl.pallas_call(
        feed_back_kernel,
        grid_spec=pltpu.PrefetchScalarGridSpec(
            num_scalar_prefetch=1,
            grid=(chunks, seqs),
            in_specs=[
                pl.BlockSpec((1, length, width), lambda c, s, _: (s, 0, 0)),
                pl.BlockSpec((1, length, width), lambda c, s, _: (s, 0, 0)),
                pl.BlockSpec((1, length, width), lambda c, s, _: (s, 0, c)),
                pl.BlockSpec((1, length, width), lambda c, s, _: (s, 0, c)),
                pl.BlockSpec((width, width), lambda c, s, _: (c, 0)),
                full(sums.shape),
            ],
            out_specs=[
                pl.BlockSpec((1, length, width), lambda c, s, _: (s, 0, c)),
                pl.BlockSpec((2, width, width // 2), lambda c, s, _: (c, 0, 0)),
                pl.BlockSpec((2, width, width // 2), lambda c, s, _: (c, 0, 0)),
                full(sums.shape),
            ],
            scratch_shapes=[pltpu.VMEM((width, width), F32), pltpu.VMEM((width, width), F32)],
        ),
        out_shape=[
            jax.ShapeDtypeStruct((seqs, length, units), BF),
            jax.ShapeDtypeStruct((2 * chunks, width, width // 2), BF),
            jax.ShapeDtypeStruct((2 * chunks, width, width // 2), BF),
            jax.ShapeDtypeStruct(sums.shape, F32),
        ],
        compiler_params=params(),
        cost_estimate=cost(6 * seqs * length * width * units, 20 * seqs * length * units),
        name="feed_back",
    )(core, mixed, first_low, hidden, slope, dn_bin, sums)


def norm_step(second, pre_low, norm, inv, ctx, up_ref, out_ref, small_ref, sums_ref):
    width = second.shape[1]
    back = second + dot_nt(pre_low, up_ref[...])
    resid, gain_sum, shift_sum = norm_back(back, norm, inv, small_ref[4:5, :])
    sums_ref[2:3, :] += jnp.sum(resid, axis=0, keepdims=True)
    sums_ref[4:5, :] += gain_sum
    sums_ref[6:7, :] += shift_sum
    low = resid.astype(BF)
    cback = dot_nt(low, out_ref[...]).astype(BF)
    prod = cback.astype(F32) * ctx.astype(F32)
    high = prod.astype(BF)
    rest = (prod - high.astype(F32)).astype(BF)
    heads = lax.broadcasted_iota(jnp.int32, (16, width), 0)
    lanes = lax.broadcasted_iota(jnp.int32, (16, width), 1)
    pick = jnp.where((lanes >= heads * HEAD_DIM) & (lanes < heads * HEAD_DIM + HEAD_DIM), 1.0, 0.0).astype(BF)
    return resid, cback, dot_nt(pick, high) + dot_nt(pick, rest), dot_tn(ctx, low)


MESH = pl.DeviceIdType.MESH

LATE = (0, 2, 4, 6, 8, 10, 12)
EARLY = 9
SMALL = 5


class Exchange:
    def __init__(self, result_ref, held, from_core, from_one, from_two, from_line, kept, came, sems):
        (
            local_sem, core_send, core_recv, one_send, one_recv, two_send, two_recv, line_send, line_recv,
            line_back_send, line_back_recv, two_back_send, two_back_recv, one_back_send, one_back_recv,
            small_send, small_recv, done_sem,
        ) = sems
        core, rep = lax.axis_index("shard"), lax.axis_index("rep")
        x, y, z = rep % 2, (rep // 2) % 2, rep // 4
        units, rows = held.shape[0], held.shape[1]
        half, quarter, piece = rows // 2, rows // 4, rows // 16
        partner_x, partner_y = rep + 1 - 2 * x, rep + 2 - 4 * y
        sibling = {"shard": 1 - core}

        def along(step):
            return {"rep": rep % 4 + 4 * ((z + step) % 4)}

        def meet():
            barrier = pltpu.get_barrier_semaphore()
            peers = [sibling, {"rep": partner_x}, {"rep": partner_y}, along(1), along(2), along(3)]
            for peer in peers:
                pl.semaphore_signal(barrier, inc=1, device_id=peer, device_id_type=MESH)
            pl.semaphore_wait(barrier, len(peers))

        def send(src, dst, send_sem, recv_sem, peer):
            return pltpu.make_async_remote_copy(
                src_ref=src, dst_ref=dst, send_sem=send_sem, recv_sem=recv_sem, device_id=peer, device_id_type=MESH
            )

        def begin(u, theirs, mine=None):
            send(theirs, from_core.at[u], core_send.at[u], core_recv.at[u], sibling).start()
            if mine is not None:
                pltpu.make_async_copy(mine, held.at[u], local_sem.at[u]).start()

        def fetched(u):
            pltpu.make_async_copy(from_core.at[u], held.at[u], local_sem.at[u]).wait()

        def where(u):
            odd = u % 2
            bit_one = x + odd * (y - x)
            bit_two = y + odd * (x - y)
            peer_one = {"rep": partner_x + odd * (partner_y - partner_x)}
            peer_two = {"rep": partner_y + odd * (partner_x - partner_y)}
            base_one = bit_one * half
            base_two = base_one + bit_two * quarter
            return bit_one, bit_two, peer_one, peer_two, base_one, base_two

        def block(at, size):
            return pl.ds(pl.multiple_of(at, piece), size)

        def add(u, at, size, other):
            here = block(at, size)
            held[u, here, :] = (held[u, here, :].astype(F32) + other.astype(F32)).astype(BF)

        def copy_core(u):
            return send(from_core.at[u], from_core.at[u], core_send.at[u], core_recv.at[u], sibling)

        def copy_one(u):
            bit_one, _, peer_one, _, _, _ = where(u)
            away = block((1 - bit_one) * half, half)
            return send(held.at[u, away], from_one.at[u], one_send.at[u], one_recv.at[u], peer_one)

        def copy_two(u):
            _, bit_two, _, peer_two, base_one, _ = where(u)
            away = block(base_one + (1 - bit_two) * quarter, quarter)
            return send(held.at[u, away], from_two.at[u], two_send.at[u], two_recv.at[u], peer_two)

        def copy_line(u, d):
            base_two = where(u)[5]
            away = block(base_two + ((z + d) % 4) * piece, piece)
            return send(held.at[u, away], from_line.at[u, d - 1], line_send.at[u, d - 1], line_recv.at[u, d - 1], along(d))

        def copy_line_back(u, d):
            base_two = where(u)[5]
            mine = from_core.at[u, block(base_two + z * piece, piece)]
            return send(mine, mine, line_back_send.at[u, d - 1], line_back_recv.at[u, d - 1], along(d))

        def copy_two_back(u):
            _, _, _, peer_two, _, base_two = where(u)
            mine = from_core.at[u, block(base_two, quarter)]
            return send(mine, mine, two_back_send.at[u], two_back_recv.at[u], peer_two)

        def copy_one_back(u):
            _, _, peer_one, _, base_one, _ = where(u)
            mine = from_core.at[u, block(base_one, half)]
            return send(mine, mine, one_back_send.at[u], one_back_recv.at[u], peer_one)

        def copy_done(u):
            return pltpu.make_async_copy(from_core.at[u], result_ref.at[u], done_sem.at[u])

        def stage_one(u):
            copy_core(u).wait_recv()
            base_one = where(u)[4]
            away = half - base_one
            add(u, away, half, from_core[u, block(away, half), :])
            copy_one(u).start()
            add(u, base_one, half, from_core[u, block(base_one, half), :])

        def stage_two(u):
            copy_one(u).wait_recv()
            _, bit_two, _, _, base_one, base_two = where(u)
            off = (1 - bit_two) * quarter
            add(u, base_one + off, quarter, from_one[u, block(off, quarter), :])
            copy_two(u).start()
            add(u, base_two, quarter, from_one[u, block(bit_two * quarter, quarter), :])

        def stage_three(u):
            copy_two(u).wait_recv()
            base_two = where(u)[5]
            add(u, base_two, quarter, from_two[u])
            for d in (2, 1, 3):
                copy_line(u, d).start()

        def stage_four(u):
            for d in (1, 2, 3):
                copy_line(u, d).wait_recv()
            base_two = where(u)[5]
            here = block(base_two + z * piece, piece)
            total = held[u, here, :].astype(F32) + from_line[u, 0].astype(F32)
            total = total + from_line[u, 1].astype(F32) + from_line[u, 2].astype(F32)
            from_core[u, here, :] = total.astype(BF)
            for d in (2, 1, 3):
                copy_line_back(u, d).start()

        def stage_five(u):
            for d in (1, 2, 3):
                copy_line_back(u, d).wait_recv()
            copy_two_back(u).start()

        def stage_six(u):
            copy_two_back(u).wait_recv()
            copy_one_back(u).start()

        def stage_seven(u):
            copy_one_back(u).wait_recv()
            copy_done(u).start()

        stages = (stage_one, stage_two, stage_three, stage_four, stage_five, stage_six, stage_seven)

        small_peers = [
            sibling, {"rep": partner_x}, {"rep": partner_y},
            {"rep": rep + 4 - 8 * (z % 2)}, {"rep": rep + 8 - 16 * (z // 2)},
        ]

        def copy_small(k):
            return send(kept.at[k], came.at[k], small_send.at[k], small_recv.at[k], small_peers[k])

        def small_next(k):
            copy_small(k).wait_recv()
            kept[k + 1] = kept[k] + came[k]
            if k + 1 < SMALL:
                copy_small(k + 1).start()

        def tick(t, _=0):
            for k, late in enumerate(LATE):
                slot = t - late
                spread = (slot + 64 - EARLY) // 64
                u = slot + spread * (slot // 4 + 6 - slot)

                @pl.when((slot >= 0) & (u < units) & (spread * (slot % 4) == 0))
                def _():
                    stages[k](u)

            return 0

        def settle():
            for k in range(SMALL):
                copy_small(k).wait_send()

            def finish(u, _):
                copy_core(u).wait_send()
                copy_one(u).wait_send()
                copy_two(u).wait_send()
                for d in (1, 2, 3):
                    copy_line(u, d).wait_send()
                    copy_line_back(u, d).wait_send()
                copy_two_back(u).wait_send()
                copy_one_back(u).wait_send()
                copy_done(u).wait()
                return 0

            lax.fori_loop(0, units, finish, 0)

        self.meet, self.begin, self.fetched, self.tick, self.settle = meet, begin, fetched, tick, settle
        self.small_start, self.small_next = (lambda: copy_small(0).start()), small_next
        self.ticks = (units - 1 - 6) * 4 + 1 + LATE[-1]

    @staticmethod
    def buffers(units, rows, cols, small):
        dma = pltpu.SemaphoreType.DMA
        return [
            pltpu.VMEM((units, rows, cols), BF),
            pltpu.VMEM((units, rows, cols), BF),
            pltpu.VMEM((units, rows // 2, cols), BF),
            pltpu.VMEM((units, rows // 4, cols), BF),
            pltpu.VMEM((units, 3, rows // 16, cols), BF),
            pltpu.VMEM((SMALL + 1,) + small, F32),
            pltpu.VMEM((SMALL,) + small, F32),
        ] + [dma((units,))] * 7 + [dma((units, 3))] * 4 + [dma((units,))] * 4 + [dma((SMALL,))] * 2 + [dma((units,))]


GROUP = 256
TILE_B = 256


def late_back_kernel(linked, seqs, groups, *refs):
    (
        second_ref, pre_ref, norm_ref, inv_ref, ctx_ref, up_ref, out_ref, small_ref,
        tokens_ref, rows_ref, cols_ref, q_ref, k_ref, v_ref, lse_ref, sums_in_ref,
    ), refs = refs[:16], refs[16:]
    step = pl.program_id(0)
    last = pl.num_programs(0) - 1
    if linked:
        feed_mine, feed_theirs, resid_ref, jlow_ref, result_ref, total_ref = refs[:6]
        cback_ref, rowdot_ref, acc, bias_ref, theirs = refs[6:11]
        buffers, sems = refs[11:18], refs[18:]
        exchange = Exchange(result_ref, *buffers, sems)
        held, kept = buffers[0], buffers[5]
        core = lax.axis_index("shard")
        early = feed_mine.shape[0]
        sums_ref = kept.at[0]
    else:
        resid_ref, jlow_ref, mine_ref, theirs_ref, sums_ref, cback_ref, rowdot_ref, acc, bias_ref = refs

    def hand_over(n):
        if linked:
            deal(core, acc, held.at[pl.ds(early + n, 1)], theirs.at[pl.ds(n, 1)])
            exchange.begin(early + n, theirs.at[n])
        else:
            deal(0, acc, mine_ref.at[pl.ds(n, 1)], theirs_ref.at[pl.ds(n, 1)])

    @pl.when(step == 0)
    def _():
        if linked:
            exchange.meet()
            for u in range(early):
                exchange.begin(u, feed_theirs.at[u], feed_mine.at[u])
            for u in range(early):
                exchange.fetched(u)
        sums_ref[...] = sums_in_ref[...]

    @pl.when(step < seqs)
    def _():
        if linked:
            exchange.tick(2 * step)
        resid, cback, rowdot, part = norm_step(
            second_ref[0], pre_ref[0], norm_ref[0], inv_ref[0], ctx_ref[0], up_ref, out_ref, small_ref, sums_ref
        )
        resid_ref[0] = resid
        for n in range(groups):
            cback_ref[step, n] = cback[:, n * GROUP : (n + 1) * GROUP]
        rowdot_ref[step] = rowdot

        @pl.when(step == 0)
        def _():
            acc[...] = part

        @pl.when(step > 0)
        def _():
            acc[...] += part

        @pl.when(step == seqs - 1)
        def _():
            hand_over(0)

        if linked:
            exchange.tick(2 * step + 1)

    @pl.when(step >= seqs)
    def _():
        g, s = (step - seqs) // seqs, step % seqs
        if linked:
            exchange.tick(2 * seqs + step - seqs)
        attend_step(
            g, s, tokens_ref, rows_ref, cols_ref, q_ref, k_ref, v_ref, cback_ref, lse_ref, rowdot_ref,
            jlow_ref, sums_ref, bias_ref, acc,
        )

        @pl.when(s == seqs - 1)
        def _():
            hand_over(1 + g)

    if linked:

        @pl.when(step == last)
        def _():
            start = 2 * seqs + seqs * groups
            exchange.small_start()
            for k in range(SMALL):
                exchange.tick(start + k)
                exchange.small_next(k)
            lax.fori_loop(start + SMALL, exchange.ticks, exchange.tick, 0)
            total_ref[...] = kept[SMALL]
            exchange.settle()


def attend_step(
    g, s, tokens_ref, rows_ref, cols_ref, q_ref, k_ref, v_ref, cback_ref, lse_ref, rowdot_ref,
    jlow_ref, sums_ref, bias_ref, acc,
):
    length = tokens_ref.shape[1]
    tile = min(TILE_B, length)
    bias_ref[...] = jnp.where(rows_ref[0] >= cols_ref[0], 0.0, NEG).astype(F32)
    lane = lax.broadcasted_iota(jnp.int32, (length, 128), 1)
    low = lane < HEAD_DIM

    for pair in range(GROUP // 128):
        at = slice(pair * 128, pair * 128 + 128)
        q2 = q_ref[0, :, at] * BF(0.125)
        k2 = k_ref[0, :, at]
        v2 = v_ref[0, :, at]
        do2 = cback_ref[s, g, :, at]
        dq = None
        for t in range(length // tile):
            rows = slice(t * tile, (t + 1) * tile)
            dks, dvs = [], []
            for h in range(2):
                mine = low[rows] if h == 0 else ~low[rows]
                km = jnp.where(mine, k2[rows], BF(0))
                vm = jnp.where(mine, v2[rows], BF(0))
                head = g * (GROUP // HEAD_DIM) + pair * 2 + h
                lse = lse_ref[0, pl.ds(head, 1), :]
                rowdot = rowdot_ref[s, pl.ds(head, 1), :]
                probs = jnp.exp(dot_nt(km, q2) + bias_ref[rows, :] - lse)
                dprobs = dot_nt(vm, do2)
                dscore = (probs * (dprobs - rowdot)).astype(BF)
                dvs.append(dot(probs.astype(BF), do2))
                dks.append(dot(dscore, q2))
                part = dot_tn(dscore, km * BF(0.125))
                dq = part if dq is None else dq + part
            dk = jnp.where(low[rows], dks[0], dks[1])
            dv = jnp.where(low[rows], dvs[0], dvs[1])
            jlow_ref[0, rows, GROUP + pair * 128 : GROUP + pair * 128 + 128] = dk.astype(BF)
            jlow_ref[0, rows, 2 * GROUP + pair * 128 : 2 * GROUP + pair * 128 + 128] = dv.astype(BF)
            vsum = jnp.sum(dv, axis=0, keepdims=True)
            vtotal = vsum if t == 0 else vtotal + vsum
        jlow_ref[0, :, at] = dq.astype(BF)
        lanes = pl.ds(pl.multiple_of(g * GROUP + pair * 128, 128), 128)
        sums_ref[0:1, lanes] += jnp.sum(dq, axis=0, keepdims=True)
        sums_ref[1:2, lanes] += vtotal

    part = dot_tn(tokens_ref[0], jlow_ref[0])

    @pl.when(s == 0)
    def _():
        acc[...] = part

    @pl.when(s > 0)
    def _():
        acc[...] += part


def late_back(second, pre_low, norm, inv, ctx, up_bin, out_bin, small, tokens, block_ids, joined, lse, sums, feed_grads=None):
    seqs, length, width = tokens.shape
    rows = block_ids.reshape(seqs, 1, length)
    cols = block_ids.reshape(seqs, length, 1)
    groups = width // GROUP
    linked = feed_grads is not None
    phase = lambda i: (i + 64 - seqs) // 64
    seq_one = lambda i: i + phase(i) * (seqs - 1 - i)
    seq_two = lambda i: phase(i) * (i % seqs)
    group_two = lambda i: phase(i) * ((i - seqs) // seqs)
    one = lambda *shape: pl.BlockSpec((1,) + shape, lambda i: (seq_one(i),) + (0,) * len(shape))
    two = lambda *shape: pl.BlockSpec((1,) + shape, lambda i: (seq_two(i),) + (0,) * len(shape))
    part = lambda k: pl.BlockSpec((1, length, GROUP), lambda i: (seq_two(i), 0, k * groups + group_two(i)))
    held = lambda a: pl.BlockSpec(a.shape, lambda i: (0,) * a.ndim, pipeline_mode=pl.Buffered(1))
    anywhere = pl.BlockSpec(memory_space=pl.ANY)
    unit = (width, width // 2)
    like = jax.ShapeDtypeStruct
    in_specs = [
        one(length, width), one(length, pre_low.shape[2]), one(length, width), one(length, 1), one(length, width),
        held(up_bin), held(out_bin), held(small),
        two(length, width), two(1, length), two(length, 1), part(0), part(1), part(2), two(16, length), held(sums),
    ]
    operands = [
        second, pre_low, norm, inv, ctx, up_bin, out_bin, small,
        tokens, rows, cols, joined, joined, joined, lse, sums,
    ]
    out_specs = [one(length, width), pl.BlockSpec((1, length, 3 * GROUP), lambda i: (seq_two(i), 0, group_two(i)))]
    out_shape = [like((seqs, length, width), F32), like((seqs, length, 3 * width), BF)]
    scratch = [
        pltpu.VMEM((seqs, groups, length, GROUP), BF), pltpu.VMEM((seqs, 16, length), F32),
        pltpu.VMEM((width, width), F32), pltpu.VMEM((length, length), F32),
    ]
    if linked:
        units = feed_grads[0].shape[0] + 1 + groups
        in_specs += [anywhere] * 2
        operands += feed_grads
        out_specs += [anywhere, full(sums.shape)]
        out_shape += [like((units,) + unit, BF), like(sums.shape, F32)]
        scratch += [pltpu.VMEM((1 + groups,) + unit, BF)] + Exchange.buffers(units, *unit, sums.shape)
        extra = dict(collective_id=0, has_side_effects=True)
    else:
        out_specs += [full((1 + groups,) + unit)] * 2 + [full(sums.shape)]
        out_shape += [like((1 + groups,) + unit, BF)] * 2 + [like(sums.shape, F32)]
        extra = {}
    return pl.pallas_call(
        functools.partial(late_back_kernel, linked, seqs, groups),
        grid=(seqs * (1 + groups),),
        in_specs=in_specs,
        out_specs=out_specs,
        out_shape=out_shape,
        scratch_shapes=scratch,
        compiler_params=params(62, **extra),
        cost_estimate=cost(seqs * length * width * (20 * width + 40 * length), 70 * seqs * length * width),
        name="late_back",
    )(*operands)


def token_total(resid_ref, jlow_ref, qkv_ref):
    width = resid_ref.shape[2]
    groups = width // GROUP
    total = resid_ref[0]
    for g in range(groups):
        for k in range(3):
            at = (3 * g + k) * GROUP
            col = k * width + g * GROUP
            total = total + dot_nt(jlow_ref[0, :, at : at + GROUP], qkv_ref[:, col : col + GROUP])
    return total


def token_kernel(resid_ref, jlow_ref, qkv_ref, grad_ref):
    grad_ref[0] = token_total(resid_ref, jlow_ref, qkv_ref)


def finish_kernel(
    core_ref, resid_ref, jlow_ref, qkv_bin_ref, feed_ref, out_unit_ref, qkv_unit_ref, sums_ref,
    grad_ref, qkv_ref, out_ref, up_ref, dn_ref, small_ref, up_stage, qkv_stage, up_sem, qkv_sem,
):
    step, last = pl.program_id(0), pl.num_programs(0) - 1
    _, rows, half = feed_ref.shape
    groups = qkv_sem.shape[0]
    parts = (slice(0, half), slice(half, rows))

    def up_copy(c, p):
        at = pl.ds(pl.multiple_of((p * (last + 1) + c) * half, half), half)
        return pltpu.make_async_copy(up_stage.at[c, p], up_ref.at[:, at], up_sem.at[c, p])

    def qkv_copy(g, k):
        at = pl.ds(pl.multiple_of(k * rows + g * GROUP, GROUP), GROUP)
        return pltpu.make_async_copy(qkv_stage.at[g, k], qkv_ref.at[:, at], qkv_sem.at[g, k])

    for p in range(2):
        up_stage[step, p] = feed_ref[1, parts[p], :].astype(F32)
        up_copy(step, p).start()
        dn_ref[:, parts[p]] = feed_ref[0, parts[p], :].astype(F32)

    @pl.when(step == 0)
    def _():
        for p in range(2):
            out_ref[:, parts[p]] = out_unit_ref[0, parts[p], :].astype(F32)
        mine = pl.ds(pl.multiple_of(core_ref[0] * half, half), half)
        small_ref[...] = sums_ref[:, mine]

    @pl.when(step > 0)
    def _():
        for j in range(3 * GROUP // 128):
            col = j * 128
            qkv_stage[step - 1, col // GROUP, :, col % GROUP : col % GROUP + 128] = qkv_unit_ref[
                0, parts[col // half], col % half : col % half + 128
            ].astype(F32)
        for k in range(3):
            qkv_copy(step - 1, k).start()

    grad_ref[0] = token_total(resid_ref, jlow_ref, qkv_bin_ref)

    @pl.when(step == last)
    def _():
        for c in range(up_sem.shape[0]):
            for p in range(2):
                up_copy(c, p).wait()
        for g in range(groups):
            for k in range(3):
                qkv_copy(g, k).wait()


def finish(core, resid, jlow, qkv_bin, units, sums):
    seqs, length, width = resid.shape
    count, rows, half = units.shape
    groups = rows // GROUP
    chunks = (count - 1 - groups) // 2
    assert chunks == seqs and groups == seqs - 1
    per_seq = lambda *shape: pl.BlockSpec((1,) + shape, lambda s, _: (s,) + (0,) * len(shape))
    late = lambda s: s - (s + 63) // 64
    like = lambda *shape: jax.ShapeDtypeStruct(shape, F32)
    anywhere = pl.BlockSpec(memory_space=pl.ANY)
    return pl.pallas_call(
        finish_kernel,
        grid_spec=pltpu.PrefetchScalarGridSpec(
            num_scalar_prefetch=1,
            grid=(chunks,),
            in_specs=[
                per_seq(length, width),
                per_seq(length, 3 * width),
                full(qkv_bin.shape),
                pl.BlockSpec((2, rows, half), lambda s, _: (s, 0, 0)),
                pl.BlockSpec((1, rows, half), lambda s, _: (2 * chunks, 0, 0)),
                pl.BlockSpec((1, rows, half), lambda s, _: (2 * chunks + 1 + late(s), 0, 0)),
                full(sums.shape),
            ],
            out_specs=[
                per_seq(length, width),
                anywhere,
                full((half, rows)),
                anywhere,
                pl.BlockSpec((half, rows), lambda s, _: (s, 0)),
                full((sums.shape[0], half)),
            ],
            scratch_shapes=[
                pltpu.VMEM((chunks, 2, half, half), F32),
                pltpu.VMEM((groups, 3, half, GROUP), F32),
                pltpu.SemaphoreType.DMA((chunks, 2)),
                pltpu.SemaphoreType.DMA((groups, 3)),
            ],
        ),
        out_shape=[
            like(seqs, length, width), like(half, 3 * rows), like(half, rows), like(half, 2 * chunks * half),
            like(chunks * half, rows), like(sums.shape[0], half),
        ],
        compiler_params=params(),
        cost_estimate=cost(6 * seqs * length * width * width, 16 * seqs * length * width),
        name="finish",
    )(core, resid, jlow, qkv_bin, units, units, units, sums)


def token_back(resid, jlow, qkv_bin):
    seqs, length, width = resid.shape
    per_seq = lambda *shape: pl.BlockSpec((1,) + shape, lambda s: (s,) + (0,) * len(shape))
    return pl.pallas_call(
        token_kernel,
        grid=(seqs,),
        in_specs=[per_seq(length, width), per_seq(length, 3 * width), full(qkv_bin.shape)],
        out_specs=per_seq(length, width),
        out_shape=jax.ShapeDtypeStruct((seqs, length, width), F32),
        compiler_params=params(),
        cost_estimate=cost(6 * seqs * length * width * width, 16 * seqs * length * width),
        name="token_back",
    )(resid, jlow, qkv_bin)


def swap(value):
    return lax.ppermute(value, "shard", [(0, 1), (1, 0)])


def small_rows(biases, gain, shift, hidden_bias):
    rows = biases.shape[0]
    return jnp.concatenate([biases.T, gain.T, shift.T, hidden_bias.reshape(-1, rows)], axis=0)


def reduce_plain(feed_grads, out_grads, qkv_grads, sums):
    def whole(mine, theirs):
        count, rows, half = mine.shape
        cut = lambda a: a.reshape(count, 2, half, half).transpose(0, 2, 1, 3).reshape(count, half, rows)
        return jnp.concatenate([cut(mine), cut(theirs)], axis=1)

    feed_all, out_all, qkv_all = whole(*feed_grads), whole(*out_grads), whole(*qkv_grads)
    chunks, groups, width = feed_all.shape[0] // 2, qkv_all.shape[0], feed_all.shape[2]
    half, units = width // 2, chunks * width
    grads = (
        qkv_all.reshape(groups, width, 3, GROUP).transpose(1, 2, 0, 3).reshape(width, 3 * width),
        out_all[0],
        feed_all[1::2].reshape(chunks, width, 2, half).transpose(1, 2, 0, 3).reshape(width, units),
        feed_all[0::2].reshape(chunks, 2, half, width).transpose(1, 0, 2, 3).reshape(units, width),
        sums[0:4].T.astype(BF),
        sums[8:].reshape(chunks, 2, half).transpose(1, 0, 2).reshape(-1).astype(BF),
        sums[4:6].T.astype(BF),
        sums[6:8].T.astype(BF),
    )
    owned = lax.psum_scatter(grads, "shard", scatter_dimension=0, tiled=True)
    return jax.tree.map(lambda part: part.astype(F32), lax.psum(owned, "rep"))


def body(tokens, teacher, block_ids, *weights):
    qkv, out, up, down, biases, hidden_bias, gain, shift = weights
    paired = lax.axis_size("shard") == 2 and lax.axis_size("rep") == 16
    if paired:
        core = lax.axis_index("shard").reshape(1)
        own = (qkv, out, up, down)
        small_own = small_rows(biases, gain, shift, hidden_bias)
        small_other = swap(small_own)
        other = tuple(swap(w) for w in own)
    else:
        core = jnp.zeros((1,), jnp.int32)
        gathered = [lax.all_gather(w, "shard", axis=0, tiled=True) for w in weights]
        cut = [jnp.split(w, 2, axis=0) for w in gathered]
        own, other = (tuple(c[i] for c in cut[:4]) for i in range(2))
        small_own, small_other = (small_rows(cut[4][i], cut[6][i], cut[7][i], cut[5][i]) for i in range(2))
    qkv_bin, small = prep_qkv(core, own[0], other[0], small_own, small_other)
    out_bin, up_bin, dn_bin = prep_rest(core, own[1], other[1], own[2], other[2], own[3], other[3])
    joined, ctx, lse, norm, inv = attend(tokens, block_ids, qkv_bin, out_bin, small)
    final, first_low, hidden, slope, second, mixed, sums = feed(norm, teacher, small, up_bin, dn_bin)
    pre_low, *feed_grads, sums = feed_back(core, mixed, first_low, hidden, slope, dn_bin, sums)
    operands = (second, pre_low, norm, inv, ctx, up_bin, out_bin, small, tokens, block_ids, joined, lse, sums)
    if not paired:
        resid, jlow, *grads, sums = late_back(*operands)
        token_grad = token_back(resid, jlow, qkv_bin)
        out_grads, qkv_grads = ([a[cut] for a in grads] for cut in (slice(0, 1), slice(1, None)))
        return (final, token_grad) + tuple(reduce_plain(feed_grads, out_grads, qkv_grads, sums[:12]))
    resid, jlow, units, sums = late_back(*operands, feed_grads)
    token_grad, qkv_grad, out_grad, up_grad, dn_grad, small = finish(core, resid, jlow, qkv_bin, units, sums)
    hidden_rows = hidden_bias.shape[0] // small.shape[1]
    return (
        final, token_grad, qkv_grad, out_grad, up_grad, dn_grad,
        small[0:4].T, small[8 : 8 + hidden_rows].reshape(-1), small[4:6].T, small[6:8].T,
    )


def solution(mesh):
    placed = (
        P(("shard", "rep"), None, None),
        P(("shard", "rep"), None, None),
        P(("shard", "rep"), None),
        P("shard", None),
        P("shard", None),
        P("shard", None),
        P("shard", None),
        P("shard", None),
        P("shard"),
        P("shard", None),
        P("shard", None),
    )
    return jax.shard_map(
        body,
        mesh=mesh,
        in_specs=placed,
        out_specs=placed[:2] + placed[3:],
        check_vma=False,
    )
```

```python
import functools

import jax
import jax.numpy as jnp
from jax import lax
from jax.experimental import pallas as pl
from jax.experimental.pallas import tpu as pltpu
from jax.sharding import PartitionSpec as P

HEAD_DIM = 64
EPS = 1e-05
NEG = -1e30
BF = jnp.bfloat16
F32 = jnp.float32
MB = 1 << 20


def params(mb=56, **kw):
    return pltpu.CompilerParams(vmem_limit_bytes=mb * MB, **kw)


def dot(a, b):
    return jnp.dot(a, b, preferred_element_type=F32)


def dot_nt(a, b):
    return lax.dot_general(a, b, (((1,), (1,)), ((), ())), preferred_element_type=F32)


def dot_tn(a, b):
    return lax.dot_general(a, b, (((0,), (0,)), ((), ())), preferred_element_type=F32)


def full(shape):
    return pl.BlockSpec(shape, lambda *_: (0,) * len(shape))


def cost(flops, nbytes, trans=0):
    return pl.CostEstimate(flops=int(flops), bytes_accessed=int(nbytes), transcendentals=int(trans))


def column(row):
    return jnp.broadcast_to(row.astype(F32), (8, row.shape[1])).T[:, 0:1]


def deal(core, acc, mine_ref, theirs_ref, at=0):
    half = acc.shape[0] // 2
    wide = acc.shape[1] // 2
    for ref, who in ((mine_ref, core), (theirs_ref, 1 - core)):
        rows = pl.ds(pl.multiple_of(who * half, half), half)
        ref[at, 0:half, :] = acc[rows, 0:wide].astype(BF)
        ref[at, half : 2 * half, :] = acc[rows, wide : 2 * wide].astype(BF)


def binary_halves(first, second):
    rows = 2 * first.shape[0]
    total = jnp.sum(jnp.abs(first.astype(F32)), axis=0, keepdims=True) + jnp.sum(
        jnp.abs(second.astype(F32)), axis=0, keepdims=True
    )
    scale = (total / rows).astype(BF)
    return (
        jnp.where(first >= 0, scale, -scale).astype(BF),
        jnp.where(second >= 0, scale, -scale).astype(BF),
    )


def prep_qkv_kernel(core_ref, own_ref, other_ref, small_own_ref, small_other_ref, out_ref, small_ref):
    core = core_ref[0]
    half = own_ref.shape[0]
    own_at = pl.multiple_of(core * half, half)
    other_at = pl.multiple_of((1 - core) * half, half)
    own, other = binary_halves(own_ref[...], other_ref[...])
    out_ref[pl.ds(own_at, half), :] = own
    out_ref[pl.ds(other_at, half), :] = other

    @pl.when(pl.program_id(0) == 0)
    def _():
        small_ref[:, pl.ds(own_at, half)] = small_own_ref[...].astype(F32)
        small_ref[:, pl.ds(other_at, half)] = small_other_ref[...].astype(F32)


def prep_qkv(core, own, other, small_own, small_other):
    half, cols = own.shape
    rows = 2 * half
    step = rows
    return pl.pallas_call(
        prep_qkv_kernel,
        grid_spec=pltpu.PrefetchScalarGridSpec(
            num_scalar_prefetch=1,
            grid=(cols // step,),
            in_specs=[
                pl.BlockSpec((half, step), lambda j, c: (0, j)),
                pl.BlockSpec((half, step), lambda j, c: (0, j)),
                full(small_own.shape),
                full(small_own.shape),
            ],
            out_specs=[
                pl.BlockSpec((rows, step), lambda j, c: (0, j)),
                full((small_own.shape[0], rows)),
            ],
        ),
        out_shape=[
            jax.ShapeDtypeStruct((rows, cols), BF),
            jax.ShapeDtypeStruct((small_own.shape[0], rows), F32),
        ],
        compiler_params=params(),
        cost_estimate=cost(4 * rows * cols, 4 * rows * cols),
        name="prep_qkv",
    )(core, own, other, small_own, small_other)


def prep_rest_kernel(core_ref, out_a, out_b, up_a, up_b, dn_a, dn_b, out_ref, up_ref, dn_ref):
    core = core_ref[0]
    half = out_a.shape[0]
    width = 2 * half
    own_at = pl.multiple_of(core * half, half)
    other_at = pl.multiple_of((1 - core) * half, half)
    own, other = binary_halves(out_a[...], out_b[...])
    out_ref[pl.ds(own_at, half), :] = own
    out_ref[pl.ds(other_at, half), :] = other
    hidden = up_a.shape[1]
    chunks = hidden // width
    for j in range(hidden // half):
        own, other = binary_halves(up_a[:, j * half : (j + 1) * half], up_b[:, j * half : (j + 1) * half])
        at = (j % chunks) * width + (j // chunks) * half
        up_ref[pl.ds(own_at, half), at : at + half] = own
        up_ref[pl.ds(other_at, half), at : at + half] = other
    own, other = binary_halves(dn_a[...], dn_b[...])
    for c in range(chunks):
        dn_ref[pl.ds(pl.multiple_of(c * width + own_at, half), half), :] = own[c * half : (c + 1) * half]
        dn_ref[pl.ds(pl.multiple_of(c * width + other_at, half), half), :] = other[c * half : (c + 1) * half]


def prep_rest(core, out_a, out_b, up_a, up_b, dn_a, dn_b):
    half, width = out_a.shape
    hidden = up_a.shape[1]
    vm = pl.BlockSpec(memory_space=pltpu.VMEM)
    return pl.pallas_call(
        prep_rest_kernel,
        in_specs=[pl.BlockSpec(memory_space=pltpu.SMEM)] + [vm] * 6,
        out_specs=[vm] * 3,
        out_shape=[
            jax.ShapeDtypeStruct((width, width), BF),
            jax.ShapeDtypeStruct((width, hidden), BF),
            jax.ShapeDtypeStruct((hidden, width), BF),
        ],
        compiler_params=params(),
        cost_estimate=cost(8 * width * hidden, 8 * width * hidden),
        name="prep_rest",
    )(core, out_a, out_b, up_a, up_b, dn_a, dn_b)


def attend_kernel(
    tokens_ref, rows_ref, qkv_ref, out_ref, small_ref, joined_ref, ctx_ref, lse_ref, norm_ref, inv_ref,
    bias_ref,
):
    length, width = tokens_ref.shape[1:]
    x = tokens_ref[0]
    for part, bias_row in ((0, 0), (1, None), (2, 1)):
        joined = dot(x, qkv_ref[:, part * width : (part + 1) * width])
        if bias_row is not None:
            joined = joined + small_ref[bias_row : bias_row + 1, :]
        joined_ref[0, :, part * width : (part + 1) * width] = joined.astype(BF)
    ids = rows_ref[0]
    bias_ref[...] = jnp.where(column(ids) >= ids.astype(F32), 0.0, NEG)
    lane = lax.broadcasted_iota(jnp.int32, (length, 128), 1)
    low = lane < HEAD_DIM
    lse_all = jnp.zeros((length, 128), F32)
    tile = min(TILE_F, length)
    for pair in range(width // 128):
        q2 = joined_ref[0, :, pair * 128 : pair * 128 + 128] * BF(0.125)
        k2 = joined_ref[0, :, width + pair * 128 : width + pair * 128 + 128]
        v2 = joined_ref[0, :, 2 * width + pair * 128 : 2 * width + pair * 128 + 128]
        for t in range(length // tile):
            rows = slice(t * tile, (t + 1) * tile)
            parts = []
            for h in range(2):
                mine = low[rows] if h == 0 else ~low[rows]
                qm = jnp.where(mine, q2[rows], BF(0))
                scores = dot_nt(qm, k2) + bias_ref[rows, :]
                peak = jnp.max(scores, axis=-1, keepdims=True)
                raised = jnp.exp(scores - peak)
                total = jnp.sum(raised, axis=-1, keepdims=True)
                parts.append(dot(raised.astype(BF), v2) / total)
                lse_ref_col = peak + jnp.log(total)
                bias_lane = lane[rows] == 2 * pair + h
                lse_cols = jnp.where(bias_lane, lse_ref_col, 0.0)
                if h == 0:
                    pair_lse = lse_cols
                else:
                    pair_lse = pair_lse + lse_cols
            ctx_ref[0, rows, pair * 128 : pair * 128 + 128] = jnp.where(low[rows], parts[0], parts[1]).astype(BF)
            if t == 0:
                tiles_lse = [pair_lse]
            else:
                tiles_lse.append(pair_lse)
        lse_all = lse_all + jnp.concatenate(tiles_lse, axis=0)
    lse_ref[0] = lse_all.T[0:16, :]
    resid = x.astype(F32) + dot(ctx_ref[0], out_ref[...]) + small_ref[2:3, :]
    center = resid - jnp.mean(resid, axis=-1, keepdims=True)
    inverse = lax.rsqrt(jnp.mean(center * center, axis=-1, keepdims=True) + EPS)
    norm_ref[0] = center * inverse
    inv_ref[0] = inverse


TILE_F = 512


def attend(tokens, block_ids, qkv_bin, out_bin, small):
    seqs, length, width = tokens.shape
    rows = block_ids.reshape(seqs, 1, length)
    per_seq = lambda *shape: pl.BlockSpec((1,) + shape, lambda s: (s,) + (0,) * len(shape))
    return pl.pallas_call(
        attend_kernel,
        grid=(seqs,),
        in_specs=[
            per_seq(length, width),
            per_seq(1, length),
            full(qkv_bin.shape),
            full(out_bin.shape),
            full(small.shape),
        ],
        out_specs=[
            per_seq(length, 3 * width),
            per_seq(length, width),
            per_seq(16, length),
            per_seq(length, width),
            per_seq(length, 1),
        ],
        out_shape=[
            jax.ShapeDtypeStruct((seqs, length, 3 * width), BF),
            jax.ShapeDtypeStruct((seqs, length, width), BF),
            jax.ShapeDtypeStruct((seqs, 16, length), F32),
            jax.ShapeDtypeStruct((seqs, length, width), F32),
            jax.ShapeDtypeStruct((seqs, length, 1), F32),
        ],
        scratch_shapes=[pltpu.VMEM((length, length), F32)],
        compiler_params=params(),
        cost_estimate=cost(seqs * length * width * (8 * width + 16 * length), 30 * seqs * length * width),
        name="attend",
    )(tokens, rows, qkv_bin, out_bin, small)


def gelu_pair(u):
    cdf = 0.5 + 0.5 * lax.erf(u * 0.7071067811865476)
    density = jnp.exp(-0.5 * u * u) * 0.3989422804014327
    return u * cdf, cdf + u * density


def norm_back(upstream, normed, inverse, gain):
    scaled = upstream * gain
    weighted = upstream * normed
    centered = (
        scaled
        - jnp.mean(scaled, axis=-1, keepdims=True)
        - normed * jnp.mean(weighted * gain, axis=-1, keepdims=True)
    )
    return centered * inverse, jnp.sum(weighted, axis=0, keepdims=True), jnp.sum(upstream, axis=0, keepdims=True)


def feed_kernel(
    norm_ref, teacher_ref, small_ref, up_ref, dn_ref,
    final_ref, first_low_ref, hidden_ref, slope_ref, second_ref, mixed_ref, sums_ref,
):
    width = norm_ref.shape[2]
    first = norm_ref[0] * small_ref[4:5, :] + small_ref[6:7, :]
    first_low = first.astype(BF)
    first_low_ref[0] = first_low
    acc = first + small_ref[3:4, :]
    for c in range(up_ref.shape[1] // width):
        cols = slice(c * width, (c + 1) * width)
        pre = dot(first_low, up_ref[:, cols]) + small_ref[8 + c : 9 + c, :]
        value, slope = gelu_pair(pre)
        value = value.astype(BF)
        hidden_ref[0, :, cols] = value
        slope_ref[0, :, cols] = slope.astype(BF)
        acc = acc + dot(value, dn_ref[cols, :])
    center = acc - jnp.mean(acc, axis=-1, keepdims=True)
    inverse = lax.rsqrt(jnp.mean(center * center, axis=-1, keepdims=True) + EPS)
    normed = center * inverse
    gain = small_ref[5:6, :]
    final = normed * gain + small_ref[7:8, :]
    final_ref[0] = final.astype(BF)
    upstream = final - teacher_ref[0].astype(F32)
    second, gain_sum, shift_sum = norm_back(upstream, normed, inverse, gain)
    second_ref[0] = second
    mixed_ref[0] = second.astype(BF)

    @pl.when(pl.program_id(0) == 0)
    def _():
        sums_ref[...] = jnp.zeros_like(sums_ref)

    sums_ref[3:4, :] += jnp.sum(second, axis=0, keepdims=True)
    sums_ref[5:6, :] += gain_sum
    sums_ref[7:8, :] += shift_sum


def feed(norm, teacher, small, up_bin, dn_bin):
    seqs, length, width = norm.shape
    hidden = up_bin.shape[1]
    per_seq = lambda *shape: pl.BlockSpec((1,) + shape, lambda s: (s,) + (0,) * len(shape))
    like = lambda n, dt: jax.ShapeDtypeStruct((seqs, length, n), dt)
    return pl.pallas_call(
        feed_kernel,
        grid=(seqs,),
        in_specs=[
            per_seq(length, width),
            per_seq(length, width),
            full(small.shape),
            full(up_bin.shape),
            full(dn_bin.shape),
        ],
        out_specs=[
            per_seq(length, width),
            per_seq(length, width),
            per_seq(length, hidden),
            per_seq(length, hidden),
            per_seq(length, width),
            per_seq(length, width),
            full((16, width)),
        ],
        out_shape=[
            like(width, BF), like(width, BF), like(hidden, BF), like(hidden, BF), like(width, F32), like(width, BF),
            jax.ShapeDtypeStruct((16, width), F32),
        ],
        compiler_params=params(),
        cost_estimate=cost(4 * seqs * length * width * hidden, 36 * seqs * length * width),
        name="feed",
    )(norm, teacher, small, up_bin, dn_bin)


def feed_back_kernel(
    core_ref, mixed_ref, first_ref, hidden_ref, slope_ref, dn_ref, sums_in_ref,
    pre_ref, mine_ref, theirs_ref, sums_ref, acc,
):
    chunk = pl.program_id(0)

    @pl.when(chunk == 0)
    def _():
        sums_ref[...] = sums_in_ref[...]

    mixed = mixed_ref[0]
    pre_back = dot_nt(mixed, dn_ref[...]) * slope_ref[0].astype(F32)
    pre_low = pre_back.astype(BF)
    pre_ref[0] = pre_low
    acc[...] = dot_tn(hidden_ref[0], mixed)
    deal(core_ref[0], acc, mine_ref, theirs_ref, 0)
    acc[...] = dot_tn(first_ref[0], pre_low)
    deal(core_ref[0], acc, mine_ref, theirs_ref, 1)
    sums_ref[pl.ds(8 + chunk, 1), :] += jnp.sum(pre_back, axis=0, keepdims=True)


def feed_back(core, mixed, first_low, hidden, slope, dn_bin, sums):
    mixed, first_low, hidden, slope = (a.reshape(1, -1, a.shape[2]) for a in (mixed, first_low, hidden, slope))
    seqs, length, width = mixed.shape
    units = hidden.shape[2]
    chunks = units // width
    return pl.pallas_call(
        feed_back_kernel,
        grid_spec=pltpu.PrefetchScalarGridSpec(
            num_scalar_prefetch=1,
            grid=(chunks,),
            in_specs=[
                pl.BlockSpec((1, length, width), lambda c, _: (0, 0, 0)),
                pl.BlockSpec((1, length, width), lambda c, _: (0, 0, 0)),
                pl.BlockSpec((1, length, width), lambda c, _: (0, 0, c)),
                pl.BlockSpec((1, length, width), lambda c, _: (0, 0, c)),
                pl.BlockSpec((width, width), lambda c, _: (c, 0)),
                full(sums.shape),
            ],
            out_specs=[
                pl.BlockSpec((1, length, width), lambda c, _: (0, 0, c)),
                pl.BlockSpec((2, width, width // 2), lambda c, _: (c, 0, 0)),
                pl.BlockSpec((2, width, width // 2), lambda c, _: (c, 0, 0)),
                full(sums.shape),
            ],
            scratch_shapes=[pltpu.VMEM((width, width), F32)],
        ),
        out_shape=[
            jax.ShapeDtypeStruct((seqs, length, units), BF),
            jax.ShapeDtypeStruct((2 * chunks, width, width // 2), BF),
            jax.ShapeDtypeStruct((2 * chunks, width, width // 2), BF),
            jax.ShapeDtypeStruct(sums.shape, F32),
        ],
        compiler_params=params(),
        cost_estimate=cost(6 * seqs * length * width * units, 20 * seqs * length * units),
        name="feed_back",
    )(core, mixed, first_low, hidden, slope, dn_bin, sums)


def norm_step(second, pre_low, norm, inv, ctx, up_ref, out_ref, small_ref, sums_ref):
    width = second.shape[1]
    back = second + dot_nt(pre_low, up_ref[...])
    resid, gain_sum, shift_sum = norm_back(back, norm, inv, small_ref[4:5, :])
    sums_ref[2:3, :] += jnp.sum(resid, axis=0, keepdims=True)
    sums_ref[4:5, :] += gain_sum
    sums_ref[6:7, :] += shift_sum
    low = resid.astype(BF)
    cback = dot_nt(low, out_ref[...]).astype(BF)
    prod = cback.astype(F32) * ctx.astype(F32)
    high = prod.astype(BF)
    rest = (prod - high.astype(F32)).astype(BF)
    heads = lax.broadcasted_iota(jnp.int32, (16, width), 0)
    lanes = lax.broadcasted_iota(jnp.int32, (16, width), 1)
    pick = jnp.where((lanes >= heads * HEAD_DIM) & (lanes < heads * HEAD_DIM + HEAD_DIM), 1.0, 0.0).astype(BF)
    return resid, cback, dot_nt(pick, high) + dot_nt(pick, rest), dot_tn(ctx, low)


MESH = pl.DeviceIdType.MESH

LATE = (0, 2, 4, 6, 8, 10, 12)
EARLY = 9
SMALL = 5


class Exchange:
    def __init__(self, result_ref, held, from_core, from_one, from_two, from_line, kept, came, sems):
        (
            local_sem, core_send, core_recv, one_send, one_recv, two_send, two_recv, line_send, line_recv,
            line_back_send, line_back_recv, two_back_send, two_back_recv, one_back_send, one_back_recv,
            small_send, small_recv, done_sem,
        ) = sems
        core, rep = lax.axis_index("shard"), lax.axis_index("rep")
        x, y, z = rep % 2, (rep // 2) % 2, rep // 4
        units, rows = held.shape[0], held.shape[1]
        half, quarter, piece = rows // 2, rows // 4, rows // 16
        partner_x, partner_y = rep + 1 - 2 * x, rep + 2 - 4 * y
        sibling = {"shard": 1 - core}

        def along(step):
            return {"rep": rep % 4 + 4 * ((z + step) % 4)}

        def meet():
            barrier = pltpu.get_barrier_semaphore()
            peers = [sibling, {"rep": partner_x}, {"rep": partner_y}, along(1), along(2), along(3)]
            for peer in peers:
                pl.semaphore_signal(barrier, inc=1, device_id=peer, device_id_type=MESH)
            pl.semaphore_wait(barrier, len(peers))

        def send(src, dst, send_sem, recv_sem, peer):
            return pltpu.make_async_remote_copy(
                src_ref=src, dst_ref=dst, send_sem=send_sem, recv_sem=recv_sem, device_id=peer, device_id_type=MESH
            )

        def begin(u, theirs, mine=None):
            send(theirs, from_core.at[u], core_send.at[u], core_recv.at[u], sibling).start()
            if mine is not None:
                pltpu.make_async_copy(mine, held.at[u], local_sem.at[u]).start()

        def fetched(u):
            pltpu.make_async_copy(from_core.at[u], held.at[u], local_sem.at[u]).wait()

        def where(u):
            odd = u % 2
            bit_one = x + odd * (y - x)
            bit_two = y + odd * (x - y)
            peer_one = {"rep": partner_x + odd * (partner_y - partner_x)}
            peer_two = {"rep": partner_y + odd * (partner_x - partner_y)}
            base_one = bit_one * half
            base_two = base_one + bit_two * quarter
            return bit_one, bit_two, peer_one, peer_two, base_one, base_two

        def block(at, size):
            return pl.ds(pl.multiple_of(at, piece), size)

        def add(u, at, size, other):
            here = block(at, size)
            held[u, here, :] = (held[u, here, :].astype(F32) + other.astype(F32)).astype(BF)

        def copy_core(u):
            return send(from_core.at[u], from_core.at[u], core_send.at[u], core_recv.at[u], sibling)

        def copy_one(u):
            bit_one, _, peer_one, _, _, _ = where(u)
            away = block((1 - bit_one) * half, half)
            return send(held.at[u, away], from_one.at[u], one_send.at[u], one_recv.at[u], peer_one)

        def copy_two(u):
            _, bit_two, _, peer_two, base_one, _ = where(u)
            away = block(base_one + (1 - bit_two) * quarter, quarter)
            return send(held.at[u, away], from_two.at[u], two_send.at[u], two_recv.at[u], peer_two)

        def copy_line(u, d):
            base_two = where(u)[5]
            away = block(base_two + ((z + d) % 4) * piece, piece)
            return send(held.at[u, away], from_line.at[u, d - 1], line_send.at[u, d - 1], line_recv.at[u, d - 1], along(d))

        def copy_line_back(u, d):
            base_two = where(u)[5]
            mine = from_core.at[u, block(base_two + z * piece, piece)]
            return send(mine, mine, line_back_send.at[u, d - 1], line_back_recv.at[u, d - 1], along(d))

        def copy_two_back(u):
            _, _, _, peer_two, _, base_two = where(u)
            mine = from_core.at[u, block(base_two, quarter)]
            return send(mine, mine, two_back_send.at[u], two_back_recv.at[u], peer_two)

        def copy_one_back(u):
            _, _, peer_one, _, base_one, _ = where(u)
            mine = from_core.at[u, block(base_one, half)]
            return send(mine, mine, one_back_send.at[u], one_back_recv.at[u], peer_one)

        def copy_done(u):
            return pltpu.make_async_copy(from_core.at[u], result_ref.at[u], done_sem.at[u])

        def stage_one(u):
            copy_core(u).wait_recv()
            base_one = where(u)[4]
            away = half - base_one
            add(u, away, half, from_core[u, block(away, half), :])
            copy_one(u).start()
            add(u, base_one, half, from_core[u, block(base_one, half), :])

        def stage_two(u):
            copy_one(u).wait_recv()
            _, bit_two, _, _, base_one, base_two = where(u)
            off = (1 - bit_two) * quarter
            add(u, base_one + off, quarter, from_one[u, block(off, quarter), :])
            copy_two(u).start()
            add(u, base_two, quarter, from_one[u, block(bit_two * quarter, quarter), :])

        def stage_three(u):
            copy_two(u).wait_recv()
            base_two = where(u)[5]
            add(u, base_two, quarter, from_two[u])
            for d in (2, 1, 3):
                copy_line(u, d).start()

        def stage_four(u):
            for d in (1, 2, 3):
                copy_line(u, d).wait_recv()
            base_two = where(u)[5]
            here = block(base_two + z * piece, piece)
            total = held[u, here, :].astype(F32) + from_line[u, 0].astype(F32)
            total = total + from_line[u, 1].astype(F32) + from_line[u, 2].astype(F32)
            from_core[u, here, :] = total.astype(BF)
            for d in (2, 1, 3):
                copy_line_back(u, d).start()

        def stage_five(u):
            for d in (1, 2, 3):
                copy_line_back(u, d).wait_recv()
            copy_two_back(u).start()

        def stage_six(u):
            copy_two_back(u).wait_recv()
            copy_one_back(u).start()

        def stage_seven(u):
            copy_one_back(u).wait_recv()
            copy_done(u).start()

        stages = (stage_one, stage_two, stage_three, stage_four, stage_five, stage_six, stage_seven)

        small_peers = [
            sibling, {"rep": partner_x}, {"rep": partner_y},
            {"rep": rep + 4 - 8 * (z % 2)}, {"rep": rep + 8 - 16 * (z // 2)},
        ]

        def copy_small(k):
            return send(kept.at[k], came.at[k], small_send.at[k], small_recv.at[k], small_peers[k])

        def small_next(k):
            copy_small(k).wait_recv()
            kept[k + 1] = kept[k] + came[k]
            if k + 1 < SMALL:
                copy_small(k + 1).start()

        def tick(t, _=0):
            for k, late in enumerate(LATE):
                slot = t - late
                spread = (slot + 64 - EARLY) // 64
                u = slot + spread * (slot // 4 + 6 - slot)

                @pl.when((slot >= 0) & (u < units) & (spread * (slot % 4) == 0))
                def _():
                    stages[k](u)

            return 0

        def settle():
            for k in range(SMALL):
                copy_small(k).wait_send()

            def finish(u, _):
                copy_core(u).wait_send()
                copy_one(u).wait_send()
                copy_two(u).wait_send()
                for d in (1, 2, 3):
                    copy_line(u, d).wait_send()
                    copy_line_back(u, d).wait_send()
                copy_two_back(u).wait_send()
                copy_one_back(u).wait_send()
                copy_done(u).wait()
                return 0

            lax.fori_loop(0, units, finish, 0)

        self.meet, self.begin, self.fetched, self.tick, self.settle = meet, begin, fetched, tick, settle
        self.small_start, self.small_next = (lambda: copy_small(0).start()), small_next
        self.ticks = (units - 1 - 6) * 4 + 1 + LATE[-1]

    @staticmethod
    def buffers(units, rows, cols, small):
        dma = pltpu.SemaphoreType.DMA
        return [
            pltpu.VMEM((units, rows, cols), BF),
            pltpu.VMEM((units, rows, cols), BF),
            pltpu.VMEM((units, rows // 2, cols), BF),
            pltpu.VMEM((units, rows // 4, cols), BF),
            pltpu.VMEM((units, 3, rows // 16, cols), BF),
            pltpu.VMEM((SMALL + 1,) + small, F32),
            pltpu.VMEM((SMALL,) + small, F32),
        ] + [dma((units,))] * 7 + [dma((units, 3))] * 4 + [dma((units,))] * 4 + [dma((SMALL,))] * 2 + [dma((units,))]


GROUP = 256
TILE_B = 256


def late_back_kernel(linked, seqs, groups, *refs):
    (
        second_ref, pre_ref, norm_ref, inv_ref, ctx_ref, up_ref, out_ref, small_ref,
        tokens_ref, rows_ref, q_ref, k_ref, v_ref, lse_ref, sums_in_ref,
    ), refs = refs[:15], refs[15:]
    step = pl.program_id(0)
    last = pl.num_programs(0) - 1
    if linked:
        feed_mine, feed_theirs, resid_ref, jlow_ref, result_ref, total_ref = refs[:6]
        cback_ref, rowdot_ref, acc, bias_ref, theirs = refs[6:11]
        buffers, sems = refs[11:18], refs[18:]
        exchange = Exchange(result_ref, *buffers, sems)
        held, kept = buffers[0], buffers[5]
        core = lax.axis_index("shard")
        early = feed_mine.shape[0]
        sums_ref = kept.at[0]
    else:
        resid_ref, jlow_ref, mine_ref, theirs_ref, sums_ref, cback_ref, rowdot_ref, acc, bias_ref = refs

    def hand_over(n):
        if linked:
            deal(core, acc, held.at[pl.ds(early + n, 1)], theirs.at[pl.ds(n, 1)])
            exchange.begin(early + n, theirs.at[n])
        else:
            deal(0, acc, mine_ref.at[pl.ds(n, 1)], theirs_ref.at[pl.ds(n, 1)])

    @pl.when(step == 0)
    def _():
        if linked:
            exchange.meet()
            for u in range(early):
                exchange.begin(u, feed_theirs.at[u], feed_mine.at[u])
            for u in range(early):
                exchange.fetched(u)
        sums_ref[...] = sums_in_ref[...]

    @pl.when(step < seqs)
    def _():
        if linked:
            exchange.tick(2 * step)
        resid, cback, rowdot, part = norm_step(
            second_ref[0], pre_ref[0], norm_ref[0], inv_ref[0], ctx_ref[0], up_ref, out_ref, small_ref, sums_ref
        )
        resid_ref[0] = resid
        for n in range(groups):
            cback_ref[step, n] = cback[:, n * GROUP : (n + 1) * GROUP]
        rowdot_ref[step] = rowdot

        @pl.when(step == 0)
        def _():
            acc[...] = part

        @pl.when(step > 0)
        def _():
            acc[...] += part

        @pl.when(step == seqs - 1)
        def _():
            hand_over(0)

        if linked:
            exchange.tick(2 * step + 1)

    @pl.when(step >= seqs)
    def _():
        g, s = (step - seqs) // seqs, step % seqs
        if linked:
            exchange.tick(2 * seqs + step - seqs)
        attend_step(
            g, s, tokens_ref, rows_ref, q_ref, k_ref, v_ref, cback_ref, lse_ref, rowdot_ref,
            jlow_ref, sums_ref, bias_ref, acc,
        )

        @pl.when(s == seqs - 1)
        def _():
            hand_over(1 + g)

    if linked:

        @pl.when(step == last)
        def _():
            start = 2 * seqs + seqs * groups
            exchange.small_start()
            for k in range(SMALL):
                exchange.tick(start + k)
                exchange.small_next(k)
            lax.fori_loop(start + SMALL, exchange.ticks, exchange.tick, 0)
            total_ref[...] = kept[SMALL]
            exchange.settle()


def attend_step(
    g, s, tokens_ref, rows_ref, q_ref, k_ref, v_ref, cback_ref, lse_ref, rowdot_ref,
    jlow_ref, sums_ref, bias_ref, acc,
):
    length = tokens_ref.shape[1]
    tile = min(TILE_B, length)
    ids = rows_ref[0]
    bias_ref[...] = jnp.where(ids.astype(F32) >= column(ids), 0.0, NEG)
    lane = lax.broadcasted_iota(jnp.int32, (length, 128), 1)
    low = lane < HEAD_DIM

    for pair in range(GROUP // 128):
        at = slice(pair * 128, pair * 128 + 128)
        q2 = q_ref[0, :, at] * BF(0.125)
        k2 = k_ref[0, :, at]
        v2 = v_ref[0, :, at]
        do2 = cback_ref[s, g, :, at]
        dq = None
        for t in range(length // tile):
            rows = slice(t * tile, (t + 1) * tile)
            dks, dvs = [], []
            for h in range(2):
                mine = low[rows] if h == 0 else ~low[rows]
                km = jnp.where(mine, k2[rows], BF(0))
                vm = jnp.where(mine, v2[rows], BF(0))
                head = g * (GROUP // HEAD_DIM) + pair * 2 + h
                lse = lse_ref[0, pl.ds(head, 1), :]
                rowdot = rowdot_ref[s, pl.ds(head, 1), :]
                probs = jnp.exp(dot_nt(km, q2) + bias_ref[rows, :] - lse)
                dprobs = dot_nt(vm, do2)
                dscore = (probs * (dprobs - rowdot)).astype(BF)
                dvs.append(dot(probs.astype(BF), do2))
                dks.append(dot(dscore, q2))
                part = dot_tn(dscore, km * BF(0.125))
                dq = part if dq is None else dq + part
            dk = jnp.where(low[rows], dks[0], dks[1])
            dv = jnp.where(low[rows], dvs[0], dvs[1])
            jlow_ref[0, rows, GROUP + pair * 128 : GROUP + pair * 128 + 128] = dk.astype(BF)
            jlow_ref[0, rows, 2 * GROUP + pair * 128 : 2 * GROUP + pair * 128 + 128] = dv.astype(BF)
            vsum = jnp.sum(dv, axis=0, keepdims=True)
            vtotal = vsum if t == 0 else vtotal + vsum
        jlow_ref[0, :, at] = dq.astype(BF)
        lanes = pl.ds(pl.multiple_of(g * GROUP + pair * 128, 128), 128)
        sums_ref[0:1, lanes] += jnp.sum(dq, axis=0, keepdims=True)
        sums_ref[1:2, lanes] += vtotal

    part = dot_tn(tokens_ref[0], jlow_ref[0])

    @pl.when(s == 0)
    def _():
        acc[...] = part

    @pl.when(s > 0)
    def _():
        acc[...] += part


def late_back(second, pre_low, norm, inv, ctx, up_bin, out_bin, small, tokens, block_ids, joined, lse, sums, feed_grads=None):
    seqs, length, width = tokens.shape
    rows = block_ids.reshape(seqs, 1, length)
    groups = width // GROUP
    linked = feed_grads is not None
    phase = lambda i: (i + 64 - seqs) // 64
    seq_one = lambda i: i + phase(i) * (seqs - 1 - i)
    seq_two = lambda i: phase(i) * (i % seqs)
    group_two = lambda i: phase(i) * ((i - seqs) // seqs)
    one = lambda *shape: pl.BlockSpec((1,) + shape, lambda i: (seq_one(i),) + (0,) * len(shape))
    two = lambda *shape: pl.BlockSpec((1,) + shape, lambda i: (seq_two(i),) + (0,) * len(shape))
    part = lambda k: pl.BlockSpec((1, length, GROUP), lambda i: (seq_two(i), 0, k * groups + group_two(i)))
    held = lambda a: pl.BlockSpec(a.shape, lambda i: (0,) * a.ndim, pipeline_mode=pl.Buffered(1))
    anywhere = pl.BlockSpec(memory_space=pl.ANY)
    unit = (width, width // 2)
    like = jax.ShapeDtypeStruct
    in_specs = [
        one(length, width), one(length, pre_low.shape[2]), one(length, width), one(length, 1), one(length, width),
        held(up_bin), held(out_bin), held(small),
        two(length, width), two(1, length), part(0), part(1), part(2), two(16, length), held(sums),
    ]
    operands = [
        second, pre_low, norm, inv, ctx, up_bin, out_bin, small,
        tokens, rows, joined, joined, joined, lse, sums,
    ]
    out_specs = [one(length, width), pl.BlockSpec((1, length, 3 * GROUP), lambda i: (seq_two(i), 0, group_two(i)))]
    out_shape = [like((seqs, length, width), F32), like((seqs, length, 3 * width), BF)]
    scratch = [
        pltpu.VMEM((seqs, groups, length, GROUP), BF), pltpu.VMEM((seqs, 16, length), F32),
        pltpu.VMEM((width, width), F32), pltpu.VMEM((length, length), F32),
    ]
    if linked:
        units = feed_grads[0].shape[0] + 1 + groups
        in_specs += [anywhere] * 2
        operands += feed_grads
        out_specs += [anywhere, full(sums.shape)]
        out_shape += [like((units,) + unit, BF), like(sums.shape, F32)]
        scratch += [pltpu.VMEM((1 + groups,) + unit, BF)] + Exchange.buffers(units, *unit, sums.shape)
        extra = dict(collective_id=0, has_side_effects=True)
    else:
        out_specs += [full((1 + groups,) + unit)] * 2 + [full(sums.shape)]
        out_shape += [like((1 + groups,) + unit, BF)] * 2 + [like(sums.shape, F32)]
        extra = {}
    return pl.pallas_call(
        functools.partial(late_back_kernel, linked, seqs, groups),
        grid=(seqs * (1 + groups),),
        in_specs=in_specs,
        out_specs=out_specs,
        out_shape=out_shape,
        scratch_shapes=scratch,
        compiler_params=params(62, **extra),
        cost_estimate=cost(seqs * length * width * (20 * width + 40 * length), 70 * seqs * length * width),
        name="late_back",
    )(*operands)


def token_total(resid_ref, jlow_ref, qkv_ref):
    width = resid_ref.shape[2]
    groups = width // GROUP
    total = resid_ref[0]
    for g in range(groups):
        for k in range(3):
            at = (3 * g + k) * GROUP
            col = k * width + g * GROUP
            total = total + dot_nt(jlow_ref[0, :, at : at + GROUP], qkv_ref[:, col : col + GROUP])
    return total


def token_kernel(resid_ref, jlow_ref, qkv_ref, grad_ref):
    grad_ref[0] = token_total(resid_ref, jlow_ref, qkv_ref)


def finish_kernel(
    core_ref, resid_ref, jlow_ref, qkv_bin_ref, feed_ref, out_unit_ref, qkv_unit_ref, sums_ref,
    grad_ref, qkv_ref, out_ref, up_ref, dn_ref, small_ref, up_stage, qkv_stage, up_sem, qkv_sem,
):
    step, last = pl.program_id(0), pl.num_programs(0) - 1
    _, rows, half = feed_ref.shape
    groups = qkv_sem.shape[0]
    parts = (slice(0, half), slice(half, rows))

    def up_copy(c, p):
        at = pl.ds(pl.multiple_of((p * (last + 1) + c) * half, half), half)
        return pltpu.make_async_copy(up_stage.at[c, p], up_ref.at[:, at], up_sem.at[c, p])

    def qkv_copy(g, k):
        at = pl.ds(pl.multiple_of(k * rows + g * GROUP, GROUP), GROUP)
        return pltpu.make_async_copy(qkv_stage.at[g, k], qkv_ref.at[:, at], qkv_sem.at[g, k])

    for p in range(2):
        up_stage[step, p] = feed_ref[1, parts[p], :].astype(F32)
        up_copy(step, p).start()
        dn_ref[:, parts[p]] = feed_ref[0, parts[p], :].astype(F32)

    @pl.when(step == 0)
    def _():
        for p in range(2):
            out_ref[:, parts[p]] = out_unit_ref[0, parts[p], :].astype(F32)
        mine = pl.ds(pl.multiple_of(core_ref[0] * half, half), half)
        small_ref[...] = sums_ref[:, mine]

    @pl.when(step > 0)
    def _():
        for j in range(3 * GROUP // 128):
            col = j * 128
            qkv_stage[step - 1, col // GROUP, :, col % GROUP : col % GROUP + 128] = qkv_unit_ref[
                0, parts[col // half], col % half : col % half + 128
            ].astype(F32)
        for k in range(3):
            qkv_copy(step - 1, k).start()

    grad_ref[0] = token_total(resid_ref, jlow_ref, qkv_bin_ref)

    @pl.when(step == last)
    def _():
        for c in range(up_sem.shape[0]):
            for p in range(2):
                up_copy(c, p).wait()
        for g in range(groups):
            for k in range(3):
                qkv_copy(g, k).wait()


def finish(core, resid, jlow, qkv_bin, units, sums):
    seqs, length, width = resid.shape
    count, rows, half = units.shape
    groups = rows // GROUP
    chunks = (count - 1 - groups) // 2
    assert chunks == seqs and groups == seqs - 1
    per_seq = lambda *shape: pl.BlockSpec((1,) + shape, lambda s, _: (s,) + (0,) * len(shape))
    late = lambda s: s - (s + 63) // 64
    like = lambda *shape: jax.ShapeDtypeStruct(shape, F32)
    anywhere = pl.BlockSpec(memory_space=pl.ANY)
    return pl.pallas_call(
        finish_kernel,
        grid_spec=pltpu.PrefetchScalarGridSpec(
            num_scalar_prefetch=1,
            grid=(chunks,),
            in_specs=[
                per_seq(length, width),
                per_seq(length, 3 * width),
                full(qkv_bin.shape),
                pl.BlockSpec((2, rows, half), lambda s, _: (s, 0, 0)),
                pl.BlockSpec((1, rows, half), lambda s, _: (2 * chunks, 0, 0)),
                pl.BlockSpec((1, rows, half), lambda s, _: (2 * chunks + 1 + late(s), 0, 0)),
                full(sums.shape),
            ],
            out_specs=[
                per_seq(length, width),
                anywhere,
                full((half, rows)),
                anywhere,
                pl.BlockSpec((half, rows), lambda s, _: (s, 0)),
                full((sums.shape[0], half)),
            ],
            scratch_shapes=[
                pltpu.VMEM((chunks, 2, half, half), F32),
                pltpu.VMEM((groups, 3, half, GROUP), F32),
                pltpu.SemaphoreType.DMA((chunks, 2)),
                pltpu.SemaphoreType.DMA((groups, 3)),
            ],
        ),
        out_shape=[
            like(seqs, length, width), like(half, 3 * rows), like(half, rows), like(half, 2 * chunks * half),
            like(chunks * half, rows), like(sums.shape[0], half),
        ],
        compiler_params=params(),
        cost_estimate=cost(6 * seqs * length * width * width, 16 * seqs * length * width),
        name="finish",
    )(core, resid, jlow, qkv_bin, units, units, units, sums)


def token_back(resid, jlow, qkv_bin):
    seqs, length, width = resid.shape
    per_seq = lambda *shape: pl.BlockSpec((1,) + shape, lambda s: (s,) + (0,) * len(shape))
    return pl.pallas_call(
        token_kernel,
        grid=(seqs,),
        in_specs=[per_seq(length, width), per_seq(length, 3 * width), full(qkv_bin.shape)],
        out_specs=per_seq(length, width),
        out_shape=jax.ShapeDtypeStruct((seqs, length, width), F32),
        compiler_params=params(),
        cost_estimate=cost(6 * seqs * length * width * width, 16 * seqs * length * width),
        name="token_back",
    )(resid, jlow, qkv_bin)


def swap(value):
    return lax.ppermute(value, "shard", [(0, 1), (1, 0)])


def small_rows(biases, gain, shift, hidden_bias):
    rows = biases.shape[0]
    return jnp.concatenate([biases.T, gain.T, shift.T, hidden_bias.reshape(-1, rows)], axis=0)


def reduce_plain(feed_grads, out_grads, qkv_grads, sums):
    def whole(mine, theirs):
        count, rows, half = mine.shape
        cut = lambda a: a.reshape(count, 2, half, half).transpose(0, 2, 1, 3).reshape(count, half, rows)
        return jnp.concatenate([cut(mine), cut(theirs)], axis=1)

    feed_all, out_all, qkv_all = whole(*feed_grads), whole(*out_grads), whole(*qkv_grads)
    chunks, groups, width = feed_all.shape[0] // 2, qkv_all.shape[0], feed_all.shape[2]
    half, units = width // 2, chunks * width
    grads = (
        qkv_all.reshape(groups, width, 3, GROUP).transpose(1, 2, 0, 3).reshape(width, 3 * width),
        out_all[0],
        feed_all[1::2].reshape(chunks, width, 2, half).transpose(1, 2, 0, 3).reshape(width, units),
        feed_all[0::2].reshape(chunks, 2, half, width).transpose(1, 0, 2, 3).reshape(units, width),
        sums[0:4].T.astype(BF),
        sums[8:].reshape(chunks, 2, half).transpose(1, 0, 2).reshape(-1).astype(BF),
        sums[4:6].T.astype(BF),
        sums[6:8].T.astype(BF),
    )
    owned = lax.psum_scatter(grads, "shard", scatter_dimension=0, tiled=True)
    return jax.tree.map(lambda part: part.astype(F32), lax.psum(owned, "rep"))


def body(tokens, teacher, block_ids, *weights):
    qkv, out, up, down, biases, hidden_bias, gain, shift = weights
    paired = lax.axis_size("shard") == 2 and lax.axis_size("rep") == 16
    if paired:
        core = lax.axis_index("shard").reshape(1)
        own = (qkv, out, up, down)
        small_own = small_rows(biases, gain, shift, hidden_bias)
        small_other = swap(small_own)
        other = tuple(swap(w) for w in own)
    else:
        core = jnp.zeros((1,), jnp.int32)
        gathered = [lax.all_gather(w, "shard", axis=0, tiled=True) for w in weights]
        cut = [jnp.split(w, 2, axis=0) for w in gathered]
        own, other = (tuple(c[i] for c in cut[:4]) for i in range(2))
        small_own, small_other = (small_rows(cut[4][i], cut[6][i], cut[7][i], cut[5][i]) for i in range(2))
    qkv_bin, small = prep_qkv(core, own[0], other[0], small_own, small_other)
    out_bin, up_bin, dn_bin = prep_rest(core, own[1], other[1], own[2], other[2], own[3], other[3])
    joined, ctx, lse, norm, inv = attend(tokens, block_ids, qkv_bin, out_bin, small)
    final, first_low, hidden, slope, second, mixed, sums = feed(norm, teacher, small, up_bin, dn_bin)
    pre_low, *feed_grads, sums = feed_back(core, mixed, first_low, hidden, slope, dn_bin, sums)
    pre_low = pre_low.reshape(hidden.shape)
    operands = (second, pre_low, norm, inv, ctx, up_bin, out_bin, small, tokens, block_ids, joined, lse, sums)
    if not paired:
        resid, jlow, *grads, sums = late_back(*operands)
        token_grad = token_back(resid, jlow, qkv_bin)
        out_grads, qkv_grads = ([a[cut] for a in grads] for cut in (slice(0, 1), slice(1, None)))
        return (final, token_grad) + tuple(reduce_plain(feed_grads, out_grads, qkv_grads, sums[:12]))
    resid, jlow, units, sums = late_back(*operands, feed_grads)
    token_grad, qkv_grad, out_grad, up_grad, dn_grad, small = finish(core, resid, jlow, qkv_bin, units, sums)
    hidden_rows = hidden_bias.shape[0] // small.shape[1]
    return (
        final, token_grad, qkv_grad, out_grad, up_grad, dn_grad,
        small[0:4].T, small[8 : 8 + hidden_rows].reshape(-1), small[4:6].T, small[6:8].T,
    )


def solution(mesh):
    placed = (
        P(("shard", "rep"), None, None),
        P(("shard", "rep"), None, None),
        P(("shard", "rep"), None),
        P("shard", None),
        P("shard", None),
        P("shard", None),
        P("shard", None),
        P("shard", None),
        P("shard"),
        P("shard", None),
        P("shard", None),
    )
    return jax.shard_map(
        body,
        mesh=mesh,
        in_specs=placed,
        out_specs=placed[:2] + placed[3:],
        check_vma=False,
    )
```

```python
import functools

import jax
import jax.numpy as jnp
from jax import lax
from jax.experimental import pallas as pl
from jax.experimental.pallas import tpu as pltpu
from jax.sharding import PartitionSpec as P

HEAD_DIM = 64
GROUP = 256
EPS = 1e-05
NEG = -1e30
BF = jnp.bfloat16
F32 = jnp.float32
MB = 1 << 20


def params(mb=56, **kw):
    return pltpu.CompilerParams(vmem_limit_bytes=mb * MB, **kw)


def dot(a, b):
    return jnp.dot(a, b, preferred_element_type=F32)


def dot_nt(a, b):
    return lax.dot_general(a, b, (((1,), (1,)), ((), ())), preferred_element_type=F32)


def dot_tn(a, b):
    return lax.dot_general(a, b, (((0,), (0,)), ((), ())), preferred_element_type=F32)


def full(shape):
    return pl.BlockSpec(shape, lambda *_: (0,) * len(shape))


def cost(flops, nbytes, trans=0):
    return pl.CostEstimate(flops=int(flops), bytes_accessed=int(nbytes), transcendentals=int(trans))


def column(row):
    return jnp.broadcast_to(row.astype(F32), (8, row.shape[1])).T[:, 0:1]


def deal(core, acc, mine_ref, theirs_ref, at=0):
    half = acc.shape[0] // 2
    wide = acc.shape[1] // 2
    for ref, who in ((mine_ref, core), (theirs_ref, 1 - core)):
        rows = pl.ds(pl.multiple_of(who * half, half), half)
        ref[at, 0:half, :] = acc[rows, 0:wide].astype(BF)
        ref[at, half : 2 * half, :] = acc[rows, wide : 2 * wide].astype(BF)


def binary_halves(first, second):
    rows = 2 * first.shape[0]
    total = jnp.sum(jnp.abs(first.astype(F32)), axis=0, keepdims=True) + jnp.sum(
        jnp.abs(second.astype(F32)), axis=0, keepdims=True
    )
    scale = (total / rows).astype(BF)
    return (
        jnp.where(first >= 0, scale, -scale).astype(BF),
        jnp.where(second >= 0, scale, -scale).astype(BF),
    )


def binary_rows(core, own_ref, other_ref, out_ref):
    half, cols = own_ref.shape
    own_at = pl.ds(pl.multiple_of(core * half, half), half)
    other_at = pl.ds(pl.multiple_of((1 - core) * half, half), half)
    for j in range(0, cols, GROUP):
        at = slice(j, j + GROUP)
        out_ref[own_at, at], out_ref[other_at, at] = binary_halves(own_ref[:, at], other_ref[:, at])


def binary_up(core, own_ref, other_ref, out_ref):
    half, cols = own_ref.shape
    chunks = cols // (2 * half)
    own_at = pl.ds(pl.multiple_of(core * half, half), half)
    other_at = pl.ds(pl.multiple_of((1 - core) * half, half), half)
    for j in range(2 * chunks):
        to = (j % chunks) * 2 * half + (j // chunks) * half
        own, other = binary_halves(own_ref[:, j * half : (j + 1) * half], other_ref[:, j * half : (j + 1) * half])
        out_ref[own_at, to : to + half] = own
        out_ref[other_at, to : to + half] = other


def binary_down(core, own_ref, other_ref, out_ref):
    rows, cols = own_ref.shape
    half = cols // 2
    for j in range(0, cols, GROUP):
        at = slice(j, j + GROUP)
        own, other = binary_halves(own_ref[:, at], other_ref[:, at])
        for c in range(rows // half):
            part = slice(c * half, (c + 1) * half)
            out_ref[pl.ds(pl.multiple_of((2 * c + core) * half, half), half), at] = own[part]
            out_ref[pl.ds(pl.multiple_of((2 * c + 1 - core) * half, half), half), at] = other[part]


def attend_kernel(
    core_ref, tokens_ref, rows_ref, qkv_own, qkv_other, out_own, out_other, small_own, small_other,
    joined_ref, ctx_ref, lse_ref, norm_ref, inv_ref, small_ref, qkv_any, out_any,
    bias_ref, qkv_ref, out_ref, sems,
):
    length, width = tokens_ref.shape[1:]
    keep = (
        pltpu.make_async_copy(qkv_ref, qkv_any, sems.at[0]),
        pltpu.make_async_copy(out_ref, out_any, sems.at[1]),
    )

    @pl.when(pl.program_id(0) == 0)
    def _():
        core, half = core_ref[0], width // 2
        binary_rows(core, qkv_own, qkv_other, qkv_ref)
        binary_rows(core, out_own, out_other, out_ref)
        small_ref[:, pl.ds(pl.multiple_of(core * half, half), half)] = small_own[...].astype(F32)
        small_ref[:, pl.ds(pl.multiple_of((1 - core) * half, half), half)] = small_other[...].astype(F32)
        for copy in keep:
            copy.start()

    x = tokens_ref[0]
    for part, bias_row in ((0, 0), (1, None), (2, 1)):
        joined = dot(x, qkv_ref[:, part * width : (part + 1) * width])
        if bias_row is not None:
            joined = joined + small_ref[bias_row : bias_row + 1, :]
        joined_ref[0, :, part * width : (part + 1) * width] = joined.astype(BF)
    ids = rows_ref[0]
    bias_ref[...] = jnp.where(column(ids) >= ids.astype(F32), 0.0, NEG)
    lane = lax.broadcasted_iota(jnp.int32, (length, 128), 1)
    low = lane < HEAD_DIM
    lse_all = jnp.zeros((length, 128), F32)
    tile = min(TILE_F, length)
    for pair in range(width // 128):
        q2 = joined_ref[0, :, pair * 128 : pair * 128 + 128] * BF(0.125)
        k2 = joined_ref[0, :, width + pair * 128 : width + pair * 128 + 128]
        v2 = joined_ref[0, :, 2 * width + pair * 128 : 2 * width + pair * 128 + 128]
        for t in range(length // tile):
            rows = slice(t * tile, (t + 1) * tile)
            parts = []
            for h in range(2):
                mine = low[rows] if h == 0 else ~low[rows]
                qm = jnp.where(mine, q2[rows], BF(0))
                scores = dot_nt(qm, k2) + bias_ref[rows, :]
                peak = jnp.max(scores, axis=-1, keepdims=True)
                raised = jnp.exp(scores - peak)
                total = jnp.sum(raised, axis=-1, keepdims=True)
                parts.append(dot(raised.astype(BF), v2) / total)
                lse_ref_col = peak + jnp.log(total)
                bias_lane = lane[rows] == 2 * pair + h
                lse_cols = jnp.where(bias_lane, lse_ref_col, 0.0)
                if h == 0:
                    pair_lse = lse_cols
                else:
                    pair_lse = pair_lse + lse_cols
            ctx_ref[0, rows, pair * 128 : pair * 128 + 128] = jnp.where(low[rows], parts[0], parts[1]).astype(BF)
            if t == 0:
                tiles_lse = [pair_lse]
            else:
                tiles_lse.append(pair_lse)
        lse_all = lse_all + jnp.concatenate(tiles_lse, axis=0)
    lse_ref[0] = lse_all.T[0:16, :]
    resid = x.astype(F32) + dot(ctx_ref[0], out_ref[...]) + small_ref[2:3, :]
    center = resid - jnp.mean(resid, axis=-1, keepdims=True)
    inverse = lax.rsqrt(jnp.mean(center * center, axis=-1, keepdims=True) + EPS)
    norm_ref[0] = center * inverse
    inv_ref[0] = inverse

    @pl.when(pl.program_id(0) == pl.num_programs(0) - 1)
    def _():
        for copy in keep:
            copy.wait()


TILE_F = 512


def attend(core, tokens, block_ids, qkv, out, small):
    seqs, length, width = tokens.shape
    rows = block_ids.reshape(seqs, 1, length)
    per_seq = lambda *shape: pl.BlockSpec((1,) + shape, lambda s, _: (s,) + (0,) * len(shape))
    once = lambda a: pl.BlockSpec(a.shape, lambda s, _: (0,) * a.ndim, pipeline_mode=pl.Buffered(1))
    anywhere = pl.BlockSpec(memory_space=pl.ANY)
    like = jax.ShapeDtypeStruct
    joined_width = qkv[0].shape[1]
    whole = (small[0].shape[0], width)
    return pl.pallas_call(
        attend_kernel,
        grid_spec=pltpu.PrefetchScalarGridSpec(
            num_scalar_prefetch=1,
            grid=(seqs,),
            in_specs=[per_seq(length, width), per_seq(1, length)] + [once(a) for a in (*qkv, *out, *small)],
            out_specs=[
                per_seq(length, joined_width),
                per_seq(length, width),
                per_seq(16, length),
                per_seq(length, width),
                per_seq(length, 1),
                full(whole),
                anywhere,
                anywhere,
            ],
            scratch_shapes=[
                pltpu.VMEM((length, length), F32),
                pltpu.VMEM((width, joined_width), BF),
                pltpu.VMEM((width, width), BF),
                pltpu.SemaphoreType.DMA((2,)),
            ],
        ),
        out_shape=[
            like((seqs, length, joined_width), BF),
            like((seqs, length, width), BF),
            like((seqs, 16, length), F32),
            like((seqs, length, width), F32),
            like((seqs, length, 1), F32),
            like(whole, F32),
            like((width, joined_width), BF),
            like((width, width), BF),
        ],
        compiler_params=params(),
        cost_estimate=cost(seqs * length * width * (8 * width + 16 * length), 30 * seqs * length * width),
        name="attend",
    )(core, tokens, rows, *qkv, *out, *small)


def gelu_pair(u):
    cdf = 0.5 + 0.5 * lax.erf(u * 0.7071067811865476)
    density = jnp.exp(-0.5 * u * u) * 0.3989422804014327
    return u * cdf, cdf + u * density


def norm_back(upstream, normed, inverse, gain):
    scaled = upstream * gain
    weighted = upstream * normed
    centered = (
        scaled
        - jnp.mean(scaled, axis=-1, keepdims=True)
        - normed * jnp.mean(weighted * gain, axis=-1, keepdims=True)
    )
    return centered * inverse, jnp.sum(weighted, axis=0, keepdims=True), jnp.sum(upstream, axis=0, keepdims=True)


def feed_kernel(
    core_ref, norm_ref, teacher_ref, small_ref, up_own, up_other, dn_own, dn_other,
    final_ref, first_low_ref, hidden_ref, slope_ref, second_ref, mixed_ref, sums_ref, up_any, dn_any,
    up_ref, dn_ref, sems,
):
    width = norm_ref.shape[2]
    keep = (
        pltpu.make_async_copy(up_ref, up_any, sems.at[0]),
        pltpu.make_async_copy(dn_ref, dn_any, sems.at[1]),
    )

    @pl.when(pl.program_id(0) == 0)
    def _():
        binary_up(core_ref[0], up_own, up_other, up_ref)
        binary_down(core_ref[0], dn_own, dn_other, dn_ref)
        for copy in keep:
            copy.start()

    first = norm_ref[0] * small_ref[4:5, :] + small_ref[6:7, :]
    first_low = first.astype(BF)
    first_low_ref[0] = first_low
    acc = first + small_ref[3:4, :]
    for c in range(up_ref.shape[1] // width):
        cols = slice(c * width, (c + 1) * width)
        pre = dot(first_low, up_ref[:, cols]) + small_ref[8 + c : 9 + c, :]
        value, slope = gelu_pair(pre)
        value = value.astype(BF)
        hidden_ref[0, :, cols] = value
        slope_ref[0, :, cols] = slope.astype(BF)
        acc = acc + dot(value, dn_ref[cols, :])
    center = acc - jnp.mean(acc, axis=-1, keepdims=True)
    inverse = lax.rsqrt(jnp.mean(center * center, axis=-1, keepdims=True) + EPS)
    normed = center * inverse
    gain = small_ref[5:6, :]
    final = normed * gain + small_ref[7:8, :]
    final_ref[0] = final.astype(BF)
    upstream = final - teacher_ref[0].astype(F32)
    second, gain_sum, shift_sum = norm_back(upstream, normed, inverse, gain)
    second_ref[0] = second
    mixed_ref[0] = second.astype(BF)

    @pl.when(pl.program_id(0) == 0)
    def _():
        sums_ref[...] = jnp.zeros_like(sums_ref)

    sums_ref[3:4, :] += jnp.sum(second, axis=0, keepdims=True)
    sums_ref[5:6, :] += gain_sum
    sums_ref[7:8, :] += shift_sum

    @pl.when(pl.program_id(0) == pl.num_programs(0) - 1)
    def _():
        for copy in keep:
            copy.wait()


def feed(core, norm, teacher, small, up, dn):
    seqs, length, width = norm.shape
    hidden = up[0].shape[1]
    per_seq = lambda *shape: pl.BlockSpec((1,) + shape, lambda s, _: (s,) + (0,) * len(shape))
    once = lambda a: pl.BlockSpec(a.shape, lambda s, _: (0,) * a.ndim, pipeline_mode=pl.Buffered(1))
    anywhere = pl.BlockSpec(memory_space=pl.ANY)
    like = jax.ShapeDtypeStruct
    row = lambda n, dt: like((seqs, length, n), dt)
    return pl.pallas_call(
        feed_kernel,
        grid_spec=pltpu.PrefetchScalarGridSpec(
            num_scalar_prefetch=1,
            grid=(seqs,),
            in_specs=[per_seq(length, width), per_seq(length, width)] + [once(a) for a in (small, *up, *dn)],
            out_specs=[
                per_seq(length, width),
                per_seq(length, width),
                per_seq(length, hidden),
                per_seq(length, hidden),
                per_seq(length, width),
                per_seq(length, width),
                full((16, width)),
                anywhere,
                anywhere,
            ],
            scratch_shapes=[
                pltpu.VMEM((width, hidden), BF),
                pltpu.VMEM((hidden, width), BF),
                pltpu.SemaphoreType.DMA((2,)),
            ],
        ),
        out_shape=[
            row(width, BF), row(width, BF), row(hidden, BF), row(hidden, BF), row(width, F32), row(width, BF),
            like((16, width), F32), like((width, hidden), BF), like((hidden, width), BF),
        ],
        compiler_params=params(60),
        cost_estimate=cost(4 * seqs * length * width * hidden, 36 * seqs * length * width),
        name="feed",
    )(core, norm, teacher, small, *up, *dn)


def feed_back_kernel(
    core_ref, mixed_ref, first_ref, hidden_ref, slope_ref, dn_ref, sums_in_ref,
    pre_ref, mine_ref, theirs_ref, sums_ref, acc,
):
    chunk = pl.program_id(0)

    @pl.when(chunk == 0)
    def _():
        sums_ref[...] = sums_in_ref[...]

    mixed = mixed_ref[0]
    pre_back = dot_nt(mixed, dn_ref[...]) * slope_ref[0].astype(F32)
    pre_low = pre_back.astype(BF)
    pre_ref[0] = pre_low
    acc[...] = dot_tn(hidden_ref[0], mixed)
    deal(core_ref[0], acc, mine_ref, theirs_ref, 0)
    acc[...] = dot_tn(first_ref[0], pre_low)
    deal(core_ref[0], acc, mine_ref, theirs_ref, 1)
    sums_ref[pl.ds(8 + chunk, 1), :] += jnp.sum(pre_back, axis=0, keepdims=True)


def feed_back(core, mixed, first_low, hidden, slope, dn_bin, sums):
    mixed, first_low, hidden, slope = (a.reshape(1, -1, a.shape[2]) for a in (mixed, first_low, hidden, slope))
    seqs, length, width = mixed.shape
    units = hidden.shape[2]
    chunks = units // width
    return pl.pallas_call(
        feed_back_kernel,
        grid_spec=pltpu.PrefetchScalarGridSpec(
            num_scalar_prefetch=1,
            grid=(chunks,),
            in_specs=[
                pl.BlockSpec((1, length, width), lambda c, _: (0, 0, 0)),
                pl.BlockSpec((1, length, width), lambda c, _: (0, 0, 0)),
                pl.BlockSpec((1, length, width), lambda c, _: (0, 0, c)),
                pl.BlockSpec((1, length, width), lambda c, _: (0, 0, c)),
                pl.BlockSpec((width, width), lambda c, _: (c, 0)),
                full(sums.shape),
            ],
            out_specs=[
                pl.BlockSpec((1, length, width), lambda c, _: (0, 0, c)),
                pl.BlockSpec((2, width, width // 2), lambda c, _: (c, 0, 0)),
                pl.BlockSpec((2, width, width // 2), lambda c, _: (c, 0, 0)),
                full(sums.shape),
            ],
            scratch_shapes=[pltpu.VMEM((width, width), F32)],
        ),
        out_shape=[
            jax.ShapeDtypeStruct((seqs, length, units), BF),
            jax.ShapeDtypeStruct((2 * chunks, width, width // 2), BF),
            jax.ShapeDtypeStruct((2 * chunks, width, width // 2), BF),
            jax.ShapeDtypeStruct(sums.shape, F32),
        ],
        compiler_params=params(),
        cost_estimate=cost(6 * seqs * length * width * units, 20 * seqs * length * units),
        name="feed_back",
    )(core, mixed, first_low, hidden, slope, dn_bin, sums)


def norm_step(second, pre_low, norm, inv, ctx, up_ref, out_ref, small_ref, sums_ref, pause):
    width = second.shape[1]
    back = second + dot_nt(pre_low, up_ref[...])
    pause(1)
    resid, gain_sum, shift_sum = norm_back(back, norm, inv, small_ref[4:5, :])
    sums_ref[2:3, :] += jnp.sum(resid, axis=0, keepdims=True)
    sums_ref[4:5, :] += gain_sum
    sums_ref[6:7, :] += shift_sum
    low = resid.astype(BF)
    cback = dot_nt(low, out_ref[...]).astype(BF)
    prod = cback.astype(F32) * ctx.astype(F32)
    high = prod.astype(BF)
    rest = (prod - high.astype(F32)).astype(BF)
    heads = lax.broadcasted_iota(jnp.int32, (16, width), 0)
    lanes = lax.broadcasted_iota(jnp.int32, (16, width), 1)
    pick = jnp.where((lanes >= heads * HEAD_DIM) & (lanes < heads * HEAD_DIM + HEAD_DIM), 1.0, 0.0).astype(BF)
    return resid, cback, dot_nt(pick, high) + dot_nt(pick, rest), dot_tn(ctx, low)


MESH = pl.DeviceIdType.MESH

SMALL = 5

LOTS = (
    (0, 0, 384, "xyz"),
    (1, 0, 384, "yxz"),
    (2, 0, 384, "yxz"),
    (3, 0, 384, "yxz"),
    (4, 0, 384, "yxz"),
    (5, 0, 384, "xyz"),
    (6, 0, 384, "zxy"),
    (7, 0, 384, "yxz"),
    (8, 0, 384, "xyz"),
    (9, 0, 384, "xyz"),
    (10, 0, 384, "xyz"),
    (11, 0, 128, "zxy"),
    (11, 128, 128, "yxz"),
    (11, 256, 128, "yxz"),
)
EVENTS = (
    (),
    ((0, 0), (1, 0), (2, 0), (3, 0),),
    ((4, 0), (5, 0),),
    ((6, 0), (7, 0),),
    ((0, 1), (1, 1),),
    (),
    (),
    ((5, 1),),
    ((2, 1),),
    ((1, 2),),
    (),
    ((2, 2), (3, 1), (6, 1),),
    ((1, 3),),
    (),
    ((2, 3), (3, 2), (4, 1),),
    ((1, 4), (6, 2),),
    (),
    ((2, 4), (4, 2), (7, 1),),
    ((1, 5), (3, 3), (0, 2), (8, 0),),
    (),
    ((2, 5), (4, 3), (6, 3), (5, 2),),
    ((3, 4), (7, 2),),
    ((0, 3),),
    ((1, 6),),
    ((4, 4), (8, 1),),
    ((3, 5), (5, 3),),
    ((2, 6), (6, 4), (9, 0), (4, 5), (7, 3),),
    ((8, 2),),
    ((6, 5), (0, 4),),
    ((5, 4),),
    ((3, 6),),
    ((7, 4), (9, 1),),
    ((8, 3),),
    ((4, 6),),
    ((0, 5), (7, 5), (10, 0),),
    (),
    ((5, 5),),
    ((9, 2),),
    ((0, 6), (6, 6),),
    ((8, 4),),
    ((7, 6), (9, 3), (10, 1), (11, 0), (12, 0), (13, 0), (8, 5), (9, 4), (10, 2), (5, 6), (12, 1), (11, 1), (13, 1), (10, 3), (9, 5), (8, 6), (12, 2), (11, 2), (13, 2), (11, 3), (10, 4), (12, 3), (11, 4), (13, 3), (12, 4), (9, 6), (13, 4), (10, 5), (11, 5), (12, 5), (13, 5), (12, 6), (11, 6), (13, 6), (10, 6),),
)


class Exchange:
    def __init__(self, lots, result_ref, held, from_core, inbox, kept, came, sems):
        (
            local_sem, core_send, core_recv, out_send, out_recv, back_send, back_recv, small_send, small_recv, done_sem
        ) = sems
        core, rep = lax.axis_index("shard"), lax.axis_index("rep")
        place = {"x": rep % 2, "y": (rep // 2) % 2, "z": rep // 4}
        ways = {"x": 2, "y": 2, "z": 4}
        sibling = {"shard": 1 - core}
        rows = held.shape[1]
        step_rows = rows // 16

        def peers(axis):
            if axis == "z":
                return [{"rep": rep % 4 + 4 * ((place["z"] + d) % 4)} for d in (1, 2, 3)]
            stride = {"x": 1, "y": 2}[axis]
            return [{"rep": rep + stride - 2 * stride * place[axis]}]

        def meet():
            barrier = pltpu.get_barrier_semaphore()
            everyone = [sibling] + peers("x") + peers("y") + peers("z")
            for peer in everyone:
                pl.semaphore_signal(barrier, inc=1, device_id=peer, device_id_type=MESH)
            pl.semaphore_wait(barrier, len(everyone))

        def send(src, dst, send_sem, recv_sem, peer):
            return pltpu.make_async_remote_copy(
                src_ref=src, dst_ref=dst, send_sem=send_sem, recv_sem=recv_sem, device_id=peer, device_id_type=MESH
            )

        def block(at, size):
            return pl.ds(at if isinstance(at, int) else pl.multiple_of(at, step_rows), size)

        def columns(lot):
            return pl.ds(lots[lot][1], lots[lot][2])

        def chain(lot):
            base, size, inside, sem, out = 0, rows, 0, 0, []
            for axis in lots[lot][3]:
                part = size // ways[axis]
                mine = base + place[axis] * part
                out.append((axis, base, part, mine, inside, sem))
                base, size, inside, sem = mine, part, inside + size - part, sem + ways[axis] - 1
            return out

        def core_copy(lot, theirs=None):
            u, cols = lots[lot][0], columns(lot)
            here = from_core.at[u, :, cols]
            return send(here if theirs is None else theirs.at[:, cols], here, core_send.at[lot], core_recv.at[lot], sibling)

        def out_copies(lot, s):
            u, cols = lots[lot][0], columns(lot)
            axis, base, part, _, inside, sem = chain(lot)[s]
            copies = []
            for n, peer in enumerate(peers(axis)):
                away = base + ((place[axis] + n + 1) % ways[axis]) * part
                copy = send(
                    held.at[u, block(away, part), cols], inbox.at[u, block(inside + n * part, part), cols],
                    out_send.at[lot, sem + n], out_recv.at[lot, sem + n], peer,
                )
                copies.append((away, copy))
            return copies

        def back_copies(lot, s):
            u, cols = lots[lot][0], columns(lot)
            axis, _, part, mine, _, sem = chain(lot)[s]
            own = from_core.at[u, block(mine, part), cols]
            return [
                send(own, own, back_send.at[lot, sem + n], back_recv.at[lot, sem + n], peer)
                for n, peer in enumerate(peers(axis))
            ]

        def done_copy(lot):
            u, cols = lots[lot][0], columns(lot)
            return pltpu.make_async_copy(from_core.at[u, :, cols], result_ref.at[u, :, cols], done_sem.at[lot])

        def add(lot, at, size, terms, target):
            u, cols = lots[lot][0], columns(lot)
            some = min(size, rows // 4)

            def one(n, _):
                total = held[u, block(at + n * some, some), cols].astype(F32)
                for ref, shift in terms:
                    total = total + ref[u, block(at + shift + n * some, some), cols].astype(F32)
                target[u, block(at + n * some, some), cols] = total.astype(BF)
                return 0

            if size == some:
                one(0, 0)
            else:
                lax.fori_loop(0, size // some, one, 0)

        def fire(lot, k):
            links = chain(lot)
            last = len(links)
            if k == 0:
                core_copy(lot).wait_recv()
                terms = [(from_core, 0)]
            elif k <= last:
                for _, copy in out_copies(lot, k - 1):
                    copy.wait_recv()
                axis, _, part, mine, inside, _ = links[k - 1]
                terms = [(inbox, inside + n * part - mine) for n in range(ways[axis] - 1)]
            if k < last:
                _, _, part, mine, _, _ = links[k]
                for away, copy in out_copies(lot, k):
                    add(lot, away, part, terms, held)
                    copy.start()
                add(lot, mine, part, terms, held)
                return
            if k == last:
                _, _, part, mine, _, _ = links[k - 1]
                add(lot, mine, part, terms, from_core)
            else:
                for copy in back_copies(lot, 2 * last - k):
                    copy.wait_recv()
            if k < 2 * last:
                for copy in back_copies(lot, 2 * last - 1 - k):
                    copy.start()
            else:
                done_copy(lot).start()

        def begin(u, theirs, mine=None):
            for lot in range(len(lots)):
                if lots[lot][0] == u:
                    core_copy(lot, theirs).start()
            if mine is not None:
                pltpu.make_async_copy(mine, held.at[u], local_sem.at[u]).start()

        def fetched(u):
            pltpu.make_async_copy(from_core.at[u], held.at[u], local_sem.at[u]).wait()

        small_peers = [
            sibling, peers("x")[0], peers("y")[0],
            {"rep": rep + 4 - 8 * (place["z"] % 2)}, {"rep": rep + 8 - 16 * (place["z"] // 2)},
        ]

        def copy_small(k):
            return send(kept.at[k], came.at[k], small_send.at[k], small_recv.at[k], small_peers[k])

        def small_next(k):
            copy_small(k).wait_recv()
            kept[k + 1] = kept[k] + came[k]
            if k + 1 < SMALL:
                copy_small(k + 1).start()

        def settle():
            for k in range(SMALL):
                copy_small(k).wait_send()
            for lot in range(len(lots)):
                core_copy(lot).wait_send()
                for s in range(len(lots[lot][3])):
                    for _, copy in out_copies(lot, s):
                        copy.wait_send()
                    for copy in back_copies(lot, s):
                        copy.wait_send()
                done_copy(lot).wait()

        self.meet, self.begin, self.fetched, self.fire, self.settle = meet, begin, fetched, fire, settle
        self.small_start, self.small_next = (lambda: copy_small(0).start()), small_next

    @staticmethod
    def buffers(lots, units, rows, cols, small):
        dma = pltpu.SemaphoreType.DMA
        count = len(lots)
        return [
            pltpu.VMEM((units, rows, cols), BF),
            pltpu.VMEM((units, rows, cols), BF),
            pltpu.VMEM((units, rows - rows // 16, cols), BF),
            pltpu.VMEM((SMALL + 1,) + small, F32),
            pltpu.VMEM((SMALL,) + small, F32),
            dma((units,)), dma((count,)), dma((count,)),
        ] + [dma((count, 5))] * 4 + [dma((SMALL,))] * 2 + [dma((count,))]


HALVES = 2
TILE_B = 256


def late_back_kernel(linked, seqs, groups, *refs):
    (
        second_ref, pre_ref, norm_ref, inv_ref, ctx_ref, up_ref, out_ref, small_ref,
        tokens_ref, rows_ref, q_ref, k_ref, v_ref, lse_ref, sums_in_ref,
    ), refs = refs[:15], refs[15:]
    step = pl.program_id(0)
    last = pl.num_programs(0) - 1
    first = seqs * HALVES
    if linked:
        feed_mine, feed_theirs, resid_ref, jlow_ref, result_ref, total_ref = refs[:6]
        cback_ref, rowdot_ref, acc, bias_ref, theirs = refs[6:11]
        buffers, sems = refs[11:16], refs[16:]
        exchange = Exchange(LOTS, result_ref, *buffers, sems)
        held, kept = buffers[0], buffers[3]
        core = lax.axis_index("shard")
        early = feed_mine.shape[0]
        sums_ref = kept.at[0]
    else:
        resid_ref, jlow_ref, mine_ref, theirs_ref, sums_ref, cback_ref, rowdot_ref, acc, bias_ref = refs

    def pause(start, count, each, n):
        for i in range(count if linked else 0):
            events = EVENTS[start[1] + each * i + n]
            if events:

                @pl.when(step == start[0] + i)
                def _():
                    for lot, k in events:
                        exchange.fire(lot, k)

    pause_norm = functools.partial(pause, (0, 0), first, 2)
    pause_attend = functools.partial(pause, (first, 2 * first), seqs * groups, 2)

    def hand_over(n):
        if linked:
            deal(core, acc, held.at[pl.ds(early + n, 1)], theirs.at[pl.ds(n, 1)])
            for m in range(1 + groups):

                @pl.when(n == m)
                def _():
                    exchange.begin(early + m, theirs.at[m])

        else:
            deal(0, acc, mine_ref.at[pl.ds(n, 1)], theirs_ref.at[pl.ds(n, 1)])

    @pl.when(step == 0)
    def _():
        if linked:
            exchange.meet()
            for u in range(early):
                exchange.begin(u, feed_theirs.at[u], feed_mine.at[u])
            for u in range(early):
                exchange.fetched(u)
        sums_ref[...] = sums_in_ref[...]

    @pl.when(step < first)
    def _():
        pause_norm(0)
        resid, cback, rowdot, part = norm_step(
            second_ref[0], pre_ref[0], norm_ref[0], inv_ref[0], ctx_ref[0], up_ref, out_ref, small_ref, sums_ref,
            pause_norm,
        )
        resid_ref[0] = resid
        size = resid.shape[0]
        s, some = step // HALVES, pl.ds(pl.multiple_of(step % HALVES * size, size), size)
        for n in range(groups):
            cback_ref[s, n, some, :] = cback[:, n * GROUP : (n + 1) * GROUP]
        rowdot_ref[s, :, some] = rowdot

        @pl.when(step == 0)
        def _():
            acc[...] = part

        @pl.when(step > 0)
        def _():
            acc[...] += part

        @pl.when(step == first - 1)
        def _():
            hand_over(step - (first - 1))

    @pl.when(step >= first)
    def _():
        g, s = (step - first) // seqs, (step - first) % seqs
        attend_step(
            g, s, tokens_ref, rows_ref, q_ref, k_ref, v_ref, cback_ref, lse_ref, rowdot_ref,
            jlow_ref, sums_ref, bias_ref, acc, pause_attend,
        )

        @pl.when(s == seqs - 1)
        def _():
            hand_over(1 + g)

    if linked:

        @pl.when(step == last)
        def _():
            exchange.small_start()
            rest = EVENTS[-1]
            share = -(-len(rest) // (SMALL + 1))
            for k in range(SMALL + 1):
                for lot, stage in rest[k * share : (k + 1) * share]:
                    exchange.fire(lot, stage)
                if k < SMALL:
                    exchange.small_next(k)
            total_ref[...] = kept[SMALL]
            exchange.settle()


def attend_step(
    g, s, tokens_ref, rows_ref, q_ref, k_ref, v_ref, cback_ref, lse_ref, rowdot_ref,
    jlow_ref, sums_ref, bias_ref, acc, pause,
):
    length = tokens_ref.shape[1]
    tile = min(TILE_B, length)
    ids = rows_ref[0]
    bias_ref[...] = jnp.where(ids.astype(F32) >= column(ids), 0.0, NEG)
    lane = lax.broadcasted_iota(jnp.int32, (length, 128), 1)
    low = lane < HEAD_DIM

    for pair in range(GROUP // 128):
        pause(pair)
        at = slice(pair * 128, pair * 128 + 128)
        q2 = q_ref[0, :, at] * BF(0.125)
        k2 = k_ref[0, :, at]
        v2 = v_ref[0, :, at]
        do2 = cback_ref[s, g, :, at]
        dq = None
        for t in range(length // tile):
            rows = slice(t * tile, (t + 1) * tile)
            dks, dvs = [], []
            for h in range(2):
                mine = low[rows] if h == 0 else ~low[rows]
                km = jnp.where(mine, k2[rows], BF(0))
                vm = jnp.where(mine, v2[rows], BF(0))
                head = g * (GROUP // HEAD_DIM) + pair * 2 + h
                lse = lse_ref[0, pl.ds(head, 1), :]
                rowdot = rowdot_ref[s, pl.ds(head, 1), :]
                probs = jnp.exp(dot_nt(km, q2) + bias_ref[rows, :] - lse)
                dprobs = dot_nt(vm, do2)
                dscore = (probs * (dprobs - rowdot)).astype(BF)
                dvs.append(dot(probs.astype(BF), do2))
                dks.append(dot(dscore, q2))
                part = dot_tn(dscore, km * BF(0.125))
                dq = part if dq is None else dq + part
            dk = jnp.where(low[rows], dks[0], dks[1])
            dv = jnp.where(low[rows], dvs[0], dvs[1])
            jlow_ref[0, rows, GROUP + pair * 128 : GROUP + pair * 128 + 128] = dk.astype(BF)
            jlow_ref[0, rows, 2 * GROUP + pair * 128 : 2 * GROUP + pair * 128 + 128] = dv.astype(BF)
            vsum = jnp.sum(dv, axis=0, keepdims=True)
            vtotal = vsum if t == 0 else vtotal + vsum
        jlow_ref[0, :, at] = dq.astype(BF)
        lanes = pl.ds(pl.multiple_of(g * GROUP + pair * 128, 128), 128)
        sums_ref[0:1, lanes] += jnp.sum(dq, axis=0, keepdims=True)
        sums_ref[1:2, lanes] += vtotal

    part = dot_tn(tokens_ref[0], jlow_ref[0])

    @pl.when(s == 0)
    def _():
        acc[...] = part

    @pl.when(s > 0)
    def _():
        acc[...] += part


def late_back(second, pre_low, norm, inv, ctx, up_bin, out_bin, small, tokens, block_ids, joined, lse, sums, feed_grads=None):
    seqs, length, width = tokens.shape
    rows = block_ids.reshape(seqs, 1, length)
    groups = width // GROUP
    linked = feed_grads is not None
    first = seqs * HALVES
    phase = lambda i: (i + 64 - first) // 64
    seq_one = lambda i: i + phase(i) * (first - 1 - i)
    seq_two = lambda i: phase(i) * ((i - first + seqs * first) % seqs)
    group_two = lambda i: phase(i) * ((i - first) // seqs)
    some = length // HALVES
    second, pre_low, norm, inv, ctx = (a.reshape(first, some, a.shape[2]) for a in (second, pre_low, norm, inv, ctx))
    one = lambda *shape: pl.BlockSpec((1,) + shape, lambda i: (seq_one(i),) + (0,) * len(shape))
    two = lambda *shape: pl.BlockSpec((1,) + shape, lambda i: (seq_two(i),) + (0,) * len(shape))
    part = lambda k: pl.BlockSpec((1, length, GROUP), lambda i: (seq_two(i), 0, k * groups + group_two(i)))
    held = lambda a: pl.BlockSpec(a.shape, lambda i: (0,) * a.ndim, pipeline_mode=pl.Buffered(1))
    anywhere = pl.BlockSpec(memory_space=pl.ANY)
    unit = (width, width // 2)
    like = jax.ShapeDtypeStruct
    in_specs = [
        one(some, width), one(some, pre_low.shape[2]), one(some, width), one(some, 1), one(some, width),
        held(up_bin), held(out_bin), held(small),
        two(length, width), two(1, length), part(0), part(1), part(2), two(16, length), held(sums),
    ]
    operands = [
        second, pre_low, norm, inv, ctx, up_bin, out_bin, small,
        tokens, rows, joined, joined, joined, lse, sums,
    ]
    out_specs = [one(some, width), pl.BlockSpec((1, length, 3 * GROUP), lambda i: (seq_two(i), 0, group_two(i)))]
    out_shape = [like((first, some, width), F32), like((seqs, length, 3 * width), BF)]
    scratch = [
        pltpu.VMEM((seqs, groups, length, GROUP), BF), pltpu.VMEM((seqs, 16, length), F32),
        pltpu.VMEM((width, width), F32), pltpu.VMEM((length, length), F32),
    ]
    if linked:
        units = feed_grads[0].shape[0] + 1 + groups
        in_specs += [anywhere] * 2
        operands += feed_grads
        out_specs += [anywhere, full(sums.shape)]
        out_shape += [like((units,) + unit, BF), like(sums.shape, F32)]
        scratch += [pltpu.VMEM((1 + groups,) + unit, BF)] + Exchange.buffers(LOTS, units, *unit, sums.shape)
        extra = dict(collective_id=0, has_side_effects=True)
    else:
        out_specs += [full((1 + groups,) + unit)] * 2 + [full(sums.shape)]
        out_shape += [like((1 + groups,) + unit, BF)] * 2 + [like(sums.shape, F32)]
        extra = {}
    return pl.pallas_call(
        functools.partial(late_back_kernel, linked, seqs, groups),
        grid=(seqs * (HALVES + groups),),
        in_specs=in_specs,
        out_specs=out_specs,
        out_shape=out_shape,
        scratch_shapes=scratch,
        compiler_params=params(58, **extra),
        cost_estimate=cost(seqs * length * width * (20 * width + 40 * length), 70 * seqs * length * width),
        name="late_back",
    )(*operands)


def token_total(resid_ref, jlow_ref, qkv_ref):
    width = resid_ref.shape[2]
    groups = width // GROUP
    total = resid_ref[0]
    for g in range(groups):
        for k in range(3):
            at = (3 * g + k) * GROUP
            col = k * width + g * GROUP
            total = total + dot_nt(jlow_ref[0, :, at : at + GROUP], qkv_ref[:, col : col + GROUP])
    return total


def token_kernel(resid_ref, jlow_ref, qkv_ref, grad_ref):
    grad_ref[0] = token_total(resid_ref, jlow_ref, qkv_ref)


def finish_kernel(
    core_ref, resid_ref, jlow_ref, qkv_bin_ref, feed_ref, out_unit_ref, qkv_unit_ref, sums_ref,
    grad_ref, qkv_ref, out_ref, up_ref, dn_ref, small_ref, up_stage, qkv_stage, up_sem, qkv_sem,
):
    step, last = pl.program_id(0), pl.num_programs(0) - 1
    _, rows, half = feed_ref.shape
    groups = qkv_sem.shape[0]
    parts = (slice(0, half), slice(half, rows))

    def up_copy(c, p):
        at = pl.ds(pl.multiple_of((p * (last + 1) + c) * half, half), half)
        return pltpu.make_async_copy(up_stage.at[c, p], up_ref.at[:, at], up_sem.at[c, p])

    def qkv_copy(g, k):
        at = pl.ds(pl.multiple_of(k * rows + g * GROUP, GROUP), GROUP)
        return pltpu.make_async_copy(qkv_stage.at[g, k], qkv_ref.at[:, at], qkv_sem.at[g, k])

    for p in range(2):
        up_stage[step, p] = feed_ref[1, parts[p], :].astype(F32)
        up_copy(step, p).start()
        dn_ref[:, parts[p]] = feed_ref[0, parts[p], :].astype(F32)

    @pl.when(step == 0)
    def _():
        for p in range(2):
            out_ref[:, parts[p]] = out_unit_ref[0, parts[p], :].astype(F32)
        mine = pl.ds(pl.multiple_of(core_ref[0] * half, half), half)
        small_ref[...] = sums_ref[:, mine]

    @pl.when(step > 0)
    def _():
        for j in range(3 * GROUP // 128):
            col = j * 128
            qkv_stage[step - 1, col // GROUP, :, col % GROUP : col % GROUP + 128] = qkv_unit_ref[
                0, parts[col // half], col % half : col % half + 128
            ].astype(F32)
        for k in range(3):
            qkv_copy(step - 1, k).start()

    grad_ref[0] = token_total(resid_ref, jlow_ref, qkv_bin_ref)

    @pl.when(step == last)
    def _():
        for c in range(up_sem.shape[0]):
            for p in range(2):
                up_copy(c, p).wait()
        for g in range(groups):
            for k in range(3):
                qkv_copy(g, k).wait()


def finish(core, resid, jlow, qkv_bin, units, sums):
    seqs, length, width = resid.shape
    count, rows, half = units.shape
    groups = rows // GROUP
    chunks = (count - 1 - groups) // 2
    assert chunks == seqs and groups == seqs - 1
    per_seq = lambda *shape: pl.BlockSpec((1,) + shape, lambda s, _: (s,) + (0,) * len(shape))
    late = lambda s: s - (s + 63) // 64
    like = lambda *shape: jax.ShapeDtypeStruct(shape, F32)
    anywhere = pl.BlockSpec(memory_space=pl.ANY)
    return pl.pallas_call(
        finish_kernel,
        grid_spec=pltpu.PrefetchScalarGridSpec(
            num_scalar_prefetch=1,
            grid=(chunks,),
            in_specs=[
                per_seq(length, width),
                per_seq(length, 3 * width),
                full(qkv_bin.shape),
                pl.BlockSpec((2, rows, half), lambda s, _: (s, 0, 0)),
                pl.BlockSpec((1, rows, half), lambda s, _: (2 * chunks, 0, 0)),
                pl.BlockSpec((1, rows, half), lambda s, _: (2 * chunks + 1 + late(s), 0, 0)),
                full(sums.shape),
            ],
            out_specs=[
                per_seq(length, width),
                anywhere,
                full((half, rows)),
                anywhere,
                pl.BlockSpec((half, rows), lambda s, _: (s, 0)),
                full((sums.shape[0], half)),
            ],
            scratch_shapes=[
                pltpu.VMEM((chunks, 2, half, half), F32),
                pltpu.VMEM((groups, 3, half, GROUP), F32),
                pltpu.SemaphoreType.DMA((chunks, 2)),
                pltpu.SemaphoreType.DMA((groups, 3)),
            ],
        ),
        out_shape=[
            like(seqs, length, width), like(half, 3 * rows), like(half, rows), like(half, 2 * chunks * half),
            like(chunks * half, rows), like(sums.shape[0], half),
        ],
        compiler_params=params(),
        cost_estimate=cost(6 * seqs * length * width * width, 16 * seqs * length * width),
        name="finish",
    )(core, resid, jlow, qkv_bin, units, units, units, sums)


def token_back(resid, jlow, qkv_bin):
    seqs, length, width = resid.shape
    per_seq = lambda *shape: pl.BlockSpec((1,) + shape, lambda s: (s,) + (0,) * len(shape))
    return pl.pallas_call(
        token_kernel,
        grid=(seqs,),
        in_specs=[per_seq(length, width), per_seq(length, 3 * width), full(qkv_bin.shape)],
        out_specs=per_seq(length, width),
        out_shape=jax.ShapeDtypeStruct((seqs, length, width), F32),
        compiler_params=params(),
        cost_estimate=cost(6 * seqs * length * width * width, 16 * seqs * length * width),
        name="token_back",
    )(resid, jlow, qkv_bin)


def swap(value):
    return lax.ppermute(value, "shard", [(0, 1), (1, 0)])


def small_rows(biases, gain, shift, hidden_bias):
    rows = biases.shape[0]
    return jnp.concatenate([biases.T, gain.T, shift.T, hidden_bias.reshape(-1, rows)], axis=0)


def reduce_plain(feed_grads, out_grads, qkv_grads, sums):
    def whole(mine, theirs):
        count, rows, half = mine.shape
        cut = lambda a: a.reshape(count, 2, half, half).transpose(0, 2, 1, 3).reshape(count, half, rows)
        return jnp.concatenate([cut(mine), cut(theirs)], axis=1)

    feed_all, out_all, qkv_all = whole(*feed_grads), whole(*out_grads), whole(*qkv_grads)
    chunks, groups, width = feed_all.shape[0] // 2, qkv_all.shape[0], feed_all.shape[2]
    half, units = width // 2, chunks * width
    grads = (
        qkv_all.reshape(groups, width, 3, GROUP).transpose(1, 2, 0, 3).reshape(width, 3 * width),
        out_all[0],
        feed_all[1::2].reshape(chunks, width, 2, half).transpose(1, 2, 0, 3).reshape(width, units),
        feed_all[0::2].reshape(chunks, 2, half, width).transpose(1, 0, 2, 3).reshape(units, width),
        sums[0:4].T.astype(BF),
        sums[8:].reshape(chunks, 2, half).transpose(1, 0, 2).reshape(-1).astype(BF),
        sums[4:6].T.astype(BF),
        sums[6:8].T.astype(BF),
    )
    owned = lax.psum_scatter(grads, "shard", scatter_dimension=0, tiled=True)
    return jax.tree.map(lambda part: part.astype(F32), lax.psum(owned, "rep"))


def body(tokens, teacher, block_ids, *weights):
    qkv, out, up, down, biases, hidden_bias, gain, shift = weights
    paired = lax.axis_size("shard") == 2 and lax.axis_size("rep") == 16
    if paired:
        core = lax.axis_index("shard").reshape(1)
        small = small_rows(biases, gain, shift, hidden_bias)
        small, qkv, out = ((a, swap(a)) for a in (small, qkv, out))
        up, down, _ = lax.optimization_barrier((up, down, qkv[1]))
        up, down = ((a, swap(a)) for a in (up, down))
    else:
        core = jnp.zeros((1,), jnp.int32)
        gathered = [lax.all_gather(w, "shard", axis=0, tiled=True) for w in weights]
        qkv, out, up, down, *rest = (jnp.split(w, 2, axis=0) for w in gathered)
        small = [small_rows(rest[0][i], rest[2][i], rest[3][i], rest[1][i]) for i in range(2)]
    joined, ctx, lse, norm, inv, small, qkv_bin, out_bin = attend(core, tokens, block_ids, qkv, out, small)
    final, first_low, hidden, slope, second, mixed, sums, up_bin, dn_bin = feed(core, norm, teacher, small, up, down)
    pre_low, *feed_grads, sums = feed_back(core, mixed, first_low, hidden, slope, dn_bin, sums)
    pre_low = pre_low.reshape(hidden.shape)
    operands = (second, pre_low, norm, inv, ctx, up_bin, out_bin, small, tokens, block_ids, joined, lse, sums)
    if not paired:
        resid, jlow, *grads, sums = late_back(*operands)
        token_grad = token_back(resid.reshape(tokens.shape), jlow, qkv_bin)
        out_grads, qkv_grads = ([a[cut] for a in grads] for cut in (slice(0, 1), slice(1, None)))
        return (final, token_grad) + tuple(reduce_plain(feed_grads, out_grads, qkv_grads, sums[:12]))
    resid, jlow, units, sums = late_back(*operands, feed_grads)
    resid = resid.reshape(tokens.shape)
    token_grad, qkv_grad, out_grad, up_grad, dn_grad, small = finish(core, resid, jlow, qkv_bin, units, sums)
    hidden_rows = hidden_bias.shape[0] // small.shape[1]
    return (
        final, token_grad, qkv_grad, out_grad, up_grad, dn_grad,
        small[0:4].T, small[8 : 8 + hidden_rows].reshape(-1), small[4:6].T, small[6:8].T,
    )


def solution(mesh):
    placed = (
        P(("shard", "rep"), None, None),
        P(("shard", "rep"), None, None),
        P(("shard", "rep"), None),
        P("shard", None),
        P("shard", None),
        P("shard", None),
        P("shard", None),
        P("shard", None),
        P("shard"),
        P("shard", None),
        P("shard", None),
    )
    return jax.shard_map(
        body,
        mesh=mesh,
        in_specs=placed,
        out_specs=placed[:2] + placed[3:],
        check_vma=False,
    )
```

```python
import functools

import jax
import jax.numpy as jnp
from jax import lax
from jax.experimental import pallas as pl
from jax.experimental.pallas import tpu as pltpu
from jax.sharding import PartitionSpec as P

HEAD_DIM = 64
GROUP = 256
EPS = 1e-05
NEG = -1e30
BF = jnp.bfloat16
F32 = jnp.float32
MB = 1 << 20


def params(mb=56, **kw):
    return pltpu.CompilerParams(vmem_limit_bytes=mb * MB, **kw)


def dot(a, b):
    return jnp.dot(a, b, preferred_element_type=F32)


def dot_nt(a, b):
    return lax.dot_general(a, b, (((1,), (1,)), ((), ())), preferred_element_type=F32)


def dot_tn(a, b):
    return lax.dot_general(a, b, (((0,), (0,)), ((), ())), preferred_element_type=F32)


def full(shape):
    return pl.BlockSpec(shape, lambda *_: (0,) * len(shape))


def cost(flops, nbytes, trans=0):
    return pl.CostEstimate(flops=int(flops), bytes_accessed=int(nbytes), transcendentals=int(trans))


def column(row):
    return jnp.broadcast_to(row.astype(F32), (8, row.shape[1])).T[:, 0:1]


def deal(core, acc, mine_ref, theirs_ref, at=0):
    half = acc.shape[0] // 2
    wide = acc.shape[1] // 2
    for ref, who in ((mine_ref, core), (theirs_ref, 1 - core)):
        rows = pl.ds(pl.multiple_of(who * half, half), half)
        ref[at, 0:half, :] = acc[rows, 0:wide].astype(BF)
        ref[at, half : 2 * half, :] = acc[rows, wide : 2 * wide].astype(BF)


def binary_halves(first, second):
    rows = 2 * first.shape[0]
    total = jnp.sum(jnp.abs(first.astype(F32)), axis=0, keepdims=True) + jnp.sum(
        jnp.abs(second.astype(F32)), axis=0, keepdims=True
    )
    scale = (total / rows).astype(BF)
    return (
        jnp.where(first >= 0, scale, -scale).astype(BF),
        jnp.where(second >= 0, scale, -scale).astype(BF),
    )


def binary_rows(core, own_ref, other_ref, out_ref):
    half, cols = own_ref.shape
    own_at = pl.ds(pl.multiple_of(core * half, half), half)
    other_at = pl.ds(pl.multiple_of((1 - core) * half, half), half)
    for j in range(0, cols, GROUP):
        at = slice(j, j + GROUP)
        out_ref[own_at, at], out_ref[other_at, at] = binary_halves(own_ref[:, at], other_ref[:, at])


def binary_up(core, own_ref, other_ref, out_ref):
    half, cols = own_ref.shape
    chunks = cols // (2 * half)
    own_at = pl.ds(pl.multiple_of(core * half, half), half)
    other_at = pl.ds(pl.multiple_of((1 - core) * half, half), half)
    for j in range(2 * chunks):
        to = (j % chunks) * 2 * half + (j // chunks) * half
        own, other = binary_halves(own_ref[:, j * half : (j + 1) * half], other_ref[:, j * half : (j + 1) * half])
        out_ref[own_at, to : to + half] = own
        out_ref[other_at, to : to + half] = other


def binary_down(core, own_ref, other_ref, out_ref):
    rows, cols = own_ref.shape
    half = cols // 2
    for j in range(0, cols, GROUP):
        at = slice(j, j + GROUP)
        own, other = binary_halves(own_ref[:, at], other_ref[:, at])
        for c in range(rows // half):
            part = slice(c * half, (c + 1) * half)
            out_ref[pl.ds(pl.multiple_of((2 * c + core) * half, half), half), at] = own[part]
            out_ref[pl.ds(pl.multiple_of((2 * c + 1 - core) * half, half), half), at] = other[part]


def attend_kernel(
    core_ref, tokens_ref, rows_ref, qkv_own, qkv_other, out_own, out_other, small_own, small_other,
    joined_ref, ctx_ref, lse_ref, norm_ref, inv_ref, small_ref, qkv_any, out_any,
    bias_ref, qkv_ref, out_ref, sems,
):
    length, width = tokens_ref.shape[1:]
    keep = (
        pltpu.make_async_copy(qkv_ref, qkv_any, sems.at[0]),
        pltpu.make_async_copy(out_ref, out_any, sems.at[1]),
    )

    @pl.when(pl.program_id(0) == 0)
    def _():
        core, half = core_ref[0], width // 2
        binary_rows(core, qkv_own, qkv_other, qkv_ref)
        binary_rows(core, out_own, out_other, out_ref)
        small_ref[:, pl.ds(pl.multiple_of(core * half, half), half)] = small_own[...].astype(F32)
        small_ref[:, pl.ds(pl.multiple_of((1 - core) * half, half), half)] = small_other[...].astype(F32)
        for copy in keep:
            copy.start()

    x = tokens_ref[0]
    for part, bias_row in ((0, 0), (1, None), (2, 1)):
        joined = dot(x, qkv_ref[:, part * width : (part + 1) * width])
        if bias_row is not None:
            joined = joined + small_ref[bias_row : bias_row + 1, :]
        joined_ref[0, :, part * width : (part + 1) * width] = joined.astype(BF)
    ids = rows_ref[pl.ds(pl.program_id(0), 1), :]
    bias_ref[...] = jnp.where(column(ids) >= ids.astype(F32), 0.0, NEG)
    lane = lax.broadcasted_iota(jnp.int32, (length, 128), 1)
    low = lane < HEAD_DIM
    lse_all = jnp.zeros((length, 128), F32)
    tile = min(TILE_F, length)
    for pair in range(width // 128):
        q2 = joined_ref[0, :, pair * 128 : pair * 128 + 128] * BF(0.125)
        k2 = joined_ref[0, :, width + pair * 128 : width + pair * 128 + 128]
        v2 = joined_ref[0, :, 2 * width + pair * 128 : 2 * width + pair * 128 + 128]
        for t in range(length // tile):
            rows = slice(t * tile, (t + 1) * tile)
            parts = []
            for h in range(2):
                mine = low[rows] if h == 0 else ~low[rows]
                qm = jnp.where(mine, q2[rows], BF(0))
                scores = dot_nt(qm, k2) + bias_ref[rows, :]
                peak = jnp.max(scores, axis=-1, keepdims=True)
                raised = jnp.exp(scores - peak)
                total = jnp.sum(raised, axis=-1, keepdims=True)
                parts.append(dot(raised.astype(BF), v2) / total)
                lse_ref_col = peak + jnp.log(total)
                bias_lane = lane[rows] == 2 * pair + h
                lse_cols = jnp.where(bias_lane, lse_ref_col, 0.0)
                if h == 0:
                    pair_lse = lse_cols
                else:
                    pair_lse = pair_lse + lse_cols
            ctx_ref[0, rows, pair * 128 : pair * 128 + 128] = jnp.where(low[rows], parts[0], parts[1]).astype(BF)
            if t == 0:
                tiles_lse = [pair_lse]
            else:
                tiles_lse.append(pair_lse)
        lse_all = lse_all + jnp.concatenate(tiles_lse, axis=0)
    lse_ref[0] = lse_all.T[0:16, :]
    resid = x.astype(F32) + dot(ctx_ref[0], out_ref[...]) + small_ref[2:3, :]
    center = resid - jnp.mean(resid, axis=-1, keepdims=True)
    inverse = lax.rsqrt(jnp.mean(center * center, axis=-1, keepdims=True) + EPS)
    norm_ref[0] = center * inverse
    inv_ref[0] = inverse

    @pl.when(pl.program_id(0) == pl.num_programs(0) - 1)
    def _():
        for copy in keep:
            copy.wait()


TILE_F = 512


def attend(core, tokens, block_ids, qkv, out, small):
    seqs, length, width = tokens.shape
    per_seq = lambda *shape: pl.BlockSpec((1,) + shape, lambda s, _: (s,) + (0,) * len(shape))
    once = lambda a: pl.BlockSpec(a.shape, lambda s, _: (0,) * a.ndim, pipeline_mode=pl.Buffered(1))
    anywhere = pl.BlockSpec(memory_space=pl.ANY)
    like = jax.ShapeDtypeStruct
    joined_width = qkv[0].shape[1]
    whole = (small[0].shape[0], width)
    return pl.pallas_call(
        attend_kernel,
        grid_spec=pltpu.PrefetchScalarGridSpec(
            num_scalar_prefetch=1,
            grid=(seqs,),
            in_specs=[per_seq(length, width)] + [once(a) for a in (block_ids, *qkv, *out, *small)],
            out_specs=[
                per_seq(length, joined_width),
                per_seq(length, width),
                per_seq(16, length),
                per_seq(length, width),
                per_seq(length, 1),
                full(whole),
                anywhere,
                anywhere,
            ],
            scratch_shapes=[
                pltpu.VMEM((length, length), F32),
                pltpu.VMEM((width, joined_width), BF),
                pltpu.VMEM((width, width), BF),
                pltpu.SemaphoreType.DMA((2,)),
            ],
        ),
        out_shape=[
            like((seqs, length, joined_width), BF),
            like((seqs, length, width), BF),
            like((seqs, 16, length), F32),
            like((seqs, length, width), F32),
            like((seqs, length, 1), F32),
            like(whole, F32),
            like((width, joined_width), BF),
            like((width, width), BF),
        ],
        compiler_params=params(),
        cost_estimate=cost(seqs * length * width * (8 * width + 16 * length), 30 * seqs * length * width),
        name="attend",
    )(core, tokens, block_ids, *qkv, *out, *small)


def gelu_pair(u):
    cdf = 0.5 + 0.5 * lax.erf(u * 0.7071067811865476)
    density = jnp.exp(-0.5 * u * u) * 0.3989422804014327
    return u * cdf, cdf + u * density


def norm_back(upstream, normed, inverse, gain):
    scaled = upstream * gain
    weighted = upstream * normed
    centered = (
        scaled
        - jnp.mean(scaled, axis=-1, keepdims=True)
        - normed * jnp.mean(weighted * gain, axis=-1, keepdims=True)
    )
    return centered * inverse, jnp.sum(weighted, axis=0, keepdims=True), jnp.sum(upstream, axis=0, keepdims=True)


def feed_kernel(
    core_ref, norm_ref, teacher_ref, small_ref, up_own, up_other, dn_own, dn_other,
    final_ref, first_low_ref, hidden_ref, slope_ref, second_ref, mixed_ref, sums_ref, up_any, dn_any,
    up_ref, dn_ref, sems,
):
    width = norm_ref.shape[2]
    keep = (
        pltpu.make_async_copy(up_ref, up_any, sems.at[0]),
        pltpu.make_async_copy(dn_ref, dn_any, sems.at[1]),
    )

    @pl.when(pl.program_id(0) == 0)
    def _():
        binary_up(core_ref[0], up_own, up_other, up_ref)
        binary_down(core_ref[0], dn_own, dn_other, dn_ref)
        for copy in keep:
            copy.start()

    first = norm_ref[0] * small_ref[4:5, :] + small_ref[6:7, :]
    first_low = first.astype(BF)
    first_low_ref[0] = first_low
    acc = first + small_ref[3:4, :]
    for c in range(up_ref.shape[1] // width):
        cols = slice(c * width, (c + 1) * width)
        pre = dot(first_low, up_ref[:, cols]) + small_ref[8 + c : 9 + c, :]
        value, slope = gelu_pair(pre)
        value = value.astype(BF)
        hidden_ref[0, :, cols] = value
        slope_ref[0, :, cols] = slope.astype(BF)
        acc = acc + dot(value, dn_ref[cols, :])
    center = acc - jnp.mean(acc, axis=-1, keepdims=True)
    inverse = lax.rsqrt(jnp.mean(center * center, axis=-1, keepdims=True) + EPS)
    normed = center * inverse
    gain = small_ref[5:6, :]
    final = normed * gain + small_ref[7:8, :]
    final_ref[0] = final.astype(BF)
    upstream = final - teacher_ref[0].astype(F32)
    second, gain_sum, shift_sum = norm_back(upstream, normed, inverse, gain)
    second_ref[0] = second
    mixed_ref[0] = second.astype(BF)

    @pl.when(pl.program_id(0) == 0)
    def _():
        sums_ref[...] = jnp.zeros_like(sums_ref)

    sums_ref[3:4, :] += jnp.sum(second, axis=0, keepdims=True)
    sums_ref[5:6, :] += gain_sum
    sums_ref[7:8, :] += shift_sum

    @pl.when(pl.program_id(0) == pl.num_programs(0) - 1)
    def _():
        for copy in keep:
            copy.wait()


def feed(core, norm, teacher, small, up, dn):
    seqs, length, width = norm.shape
    hidden = up[0].shape[1]
    per_seq = lambda *shape: pl.BlockSpec((1,) + shape, lambda s, _: (s,) + (0,) * len(shape))
    once = lambda a: pl.BlockSpec(a.shape, lambda s, _: (0,) * a.ndim, pipeline_mode=pl.Buffered(1))
    anywhere = pl.BlockSpec(memory_space=pl.ANY)
    like = jax.ShapeDtypeStruct
    row = lambda n, dt: like((seqs, length, n), dt)
    return pl.pallas_call(
        feed_kernel,
        grid_spec=pltpu.PrefetchScalarGridSpec(
            num_scalar_prefetch=1,
            grid=(seqs,),
            in_specs=[per_seq(length, width), per_seq(length, width)] + [once(a) for a in (small, *up, *dn)],
            out_specs=[
                per_seq(length, width),
                per_seq(length, width),
                per_seq(length, hidden),
                per_seq(length, hidden),
                per_seq(length, width),
                per_seq(length, width),
                full((16, width)),
                anywhere,
                anywhere,
            ],
            scratch_shapes=[
                pltpu.VMEM((width, hidden), BF),
                pltpu.VMEM((hidden, width), BF),
                pltpu.SemaphoreType.DMA((2,)),
            ],
        ),
        out_shape=[
            row(width, BF), row(width, BF), row(hidden, BF), row(hidden, BF), row(width, F32), row(width, BF),
            like((16, width), F32), like((width, hidden), BF), like((hidden, width), BF),
        ],
        compiler_params=params(60),
        cost_estimate=cost(4 * seqs * length * width * hidden, 36 * seqs * length * width),
        name="feed",
    )(core, norm, teacher, small, *up, *dn)


def feed_back_kernel(
    core_ref, mixed_ref, first_ref, hidden_ref, slope_ref, dn_ref, sums_in_ref,
    pre_ref, mine_ref, theirs_ref, sums_ref, acc,
):
    chunk = pl.program_id(0)

    @pl.when(chunk == 0)
    def _():
        sums_ref[...] = sums_in_ref[...]

    mixed = mixed_ref[0]
    pre_back = dot_nt(mixed, dn_ref[...]) * slope_ref[0].astype(F32)
    pre_low = pre_back.astype(BF)
    pre_ref[0] = pre_low
    acc[...] = dot_tn(hidden_ref[0], mixed)
    deal(core_ref[0], acc, mine_ref, theirs_ref, 0)
    acc[...] = dot_tn(first_ref[0], pre_low)
    deal(core_ref[0], acc, mine_ref, theirs_ref, 1)
    sums_ref[pl.ds(8 + chunk, 1), :] += jnp.sum(pre_back, axis=0, keepdims=True)


def feed_back(core, mixed, first_low, hidden, slope, dn_bin, sums):
    mixed, first_low, hidden, slope = (a.reshape(1, -1, a.shape[2]) for a in (mixed, first_low, hidden, slope))
    seqs, length, width = mixed.shape
    units = hidden.shape[2]
    chunks = units // width
    return pl.pallas_call(
        feed_back_kernel,
        grid_spec=pltpu.PrefetchScalarGridSpec(
            num_scalar_prefetch=1,
            grid=(chunks,),
            in_specs=[
                pl.BlockSpec((1, length, width), lambda c, _: (0, 0, 0)),
                pl.BlockSpec((1, length, width), lambda c, _: (0, 0, 0)),
                pl.BlockSpec((1, length, width), lambda c, _: (0, 0, c)),
                pl.BlockSpec((1, length, width), lambda c, _: (0, 0, c)),
                pl.BlockSpec((width, width), lambda c, _: (c, 0)),
                full(sums.shape),
            ],
            out_specs=[
                pl.BlockSpec((1, length, width), lambda c, _: (0, 0, c)),
                pl.BlockSpec((2, width, width // 2), lambda c, _: (c, 0, 0)),
                pl.BlockSpec((2, width, width // 2), lambda c, _: (c, 0, 0)),
                full(sums.shape),
            ],
            scratch_shapes=[pltpu.VMEM((width, width), F32)],
        ),
        out_shape=[
            jax.ShapeDtypeStruct((seqs, length, units), BF),
            jax.ShapeDtypeStruct((2 * chunks, width, width // 2), BF),
            jax.ShapeDtypeStruct((2 * chunks, width, width // 2), BF),
            jax.ShapeDtypeStruct(sums.shape, F32),
        ],
        compiler_params=params(),
        cost_estimate=cost(6 * seqs * length * width * units, 20 * seqs * length * units),
        name="feed_back",
    )(core, mixed, first_low, hidden, slope, dn_bin, sums)


def norm_step(second, pre_low, norm, inv, ctx, up_ref, out_ref, small_ref, sums_ref, pause):
    width = second.shape[1]
    back = second + dot_nt(pre_low, up_ref[...])
    pause(1)
    resid, gain_sum, shift_sum = norm_back(back, norm, inv, small_ref[4:5, :])
    sums_ref[2:3, :] += jnp.sum(resid, axis=0, keepdims=True)
    sums_ref[4:5, :] += gain_sum
    sums_ref[6:7, :] += shift_sum
    low = resid.astype(BF)
    cback = dot_nt(low, out_ref[...]).astype(BF)
    prod = cback.astype(F32) * ctx.astype(F32)
    high = prod.astype(BF)
    rest = (prod - high.astype(F32)).astype(BF)
    heads = lax.broadcasted_iota(jnp.int32, (16, width), 0)
    lanes = lax.broadcasted_iota(jnp.int32, (16, width), 1)
    pick = jnp.where((lanes >= heads * HEAD_DIM) & (lanes < heads * HEAD_DIM + HEAD_DIM), 1.0, 0.0).astype(BF)
    return low, cback, dot_nt(pick, high) + dot_nt(pick, rest), dot_tn(ctx, low)


MESH = pl.DeviceIdType.MESH

SMALL = 5

LOTS = (
    (0, 0, 384, "xyz"),
    (1, 0, 384, "yxz"),
    (2, 0, 384, "yxz"),
    (3, 0, 384, "yxz"),
    (4, 0, 384, "yxz"),
    (5, 0, 384, "xyz"),
    (6, 0, 384, "zxy"),
    (7, 0, 384, "yxz"),
    (8, 0, 384, "xyz"),
    (9, 0, 384, "xyz"),
    (10, 0, 384, "xyz"),
    (11, 0, 128, "zxy"),
    (11, 128, 128, "yxz"),
    (11, 256, 128, "yxz"),
)
EVENTS = (
    (),
    ((0, 0), (1, 0), (2, 0), (3, 0),),
    ((4, 0), (5, 0),),
    ((6, 0), (7, 0),),
    ((0, 1), (1, 1),),
    (),
    (),
    ((5, 1),),
    ((2, 1),),
    ((1, 2),),
    (),
    ((2, 2), (3, 1), (6, 1),),
    ((1, 3),),
    (),
    ((2, 3), (3, 2), (4, 1),),
    ((1, 4), (6, 2),),
    (),
    ((2, 4), (4, 2), (7, 1),),
    ((1, 5), (3, 3), (0, 2), (8, 0),),
    (),
    ((2, 5), (4, 3), (6, 3), (5, 2),),
    ((3, 4), (7, 2),),
    ((0, 3),),
    ((1, 6),),
    ((4, 4), (8, 1),),
    ((3, 5), (5, 3),),
    ((2, 6), (6, 4), (9, 0), (4, 5), (7, 3),),
    ((8, 2),),
    ((6, 5), (0, 4),),
    ((5, 4),),
    ((3, 6),),
    ((7, 4), (9, 1),),
    ((8, 3),),
    ((4, 6),),
    ((0, 5), (7, 5), (10, 0),),
    (),
    ((5, 5),),
    ((9, 2),),
    ((0, 6), (6, 6),),
    ((8, 4),),
    ((7, 6), (9, 3), (10, 1), (11, 0), (12, 0), (13, 0), (8, 5), (9, 4), (10, 2), (5, 6), (12, 1), (11, 1), (13, 1), (10, 3), (9, 5), (8, 6), (12, 2), (11, 2), (13, 2), (11, 3), (10, 4), (12, 3), (11, 4), (13, 3), (12, 4), (9, 6), (13, 4), (10, 5), (11, 5), (12, 5), (13, 5), (12, 6), (11, 6), (13, 6), (10, 6),),
)


class Exchange:
    def __init__(self, lots, copied, result_ref, held, from_core, inbox, kept, came, sems):
        (
            local_sem, core_send, core_recv, out_send, out_recv, back_send, back_recv, small_send, small_recv, done_sem
        ) = sems
        self.copied = copied
        core, rep = lax.axis_index("shard"), lax.axis_index("rep")
        place = {"x": rep % 2, "y": (rep // 2) % 2, "z": rep // 4, "p": rep % 4}
        ways = {"x": 2, "y": 2, "z": 4, "p": 4}
        sibling = {"shard": 1 - core}
        rows = held.shape[1]
        step_rows = rows // 16

        def peers(axis):
            if axis == "p":
                return [{"rep": rep - place["p"] + (place["p"] + d) % 4} for d in (1, 2, 3)]
            if axis == "z":
                return [{"rep": rep % 4 + 4 * ((place["z"] + d) % 4)} for d in (1, 2, 3)]
            stride = {"x": 1, "y": 2}[axis]
            return [{"rep": rep + stride - 2 * stride * place[axis]}]

        def meet():
            barrier = pltpu.get_barrier_semaphore()
            everyone = [sibling] + peers("p") + peers("z")
            for peer in everyone:
                pl.semaphore_signal(barrier, inc=1, device_id=peer, device_id_type=MESH)
            pl.semaphore_wait(barrier, len(everyone))

        def send(src, dst, send_sem, recv_sem, peer):
            return pltpu.make_async_remote_copy(
                src_ref=src, dst_ref=dst, send_sem=send_sem, recv_sem=recv_sem, device_id=peer, device_id_type=MESH
            )

        def block(at, size):
            return pl.ds(at if isinstance(at, int) else pl.multiple_of(at, step_rows), size)

        def columns(lot):
            return pl.ds(lots[lot][1], lots[lot][2])

        def chain(lot):
            base, size, inside, sem, out = 0, rows, 0, 0, []
            for axis in lots[lot][3]:
                part = size // ways[axis]
                mine = base + place[axis] * part
                out.append((axis, base, part, mine, inside, sem))
                base, size, inside, sem = mine, part, inside + size - part, sem + ways[axis] - 1
            return out

        def core_copy(lot, theirs=None):
            u, cols = lots[lot][0], columns(lot)
            here = from_core.at[u, :, cols]
            return send(here if theirs is None else theirs.at[:, cols], here, core_send.at[lot], core_recv.at[lot], sibling)

        def out_copies(lot, s):
            u, cols = lots[lot][0], columns(lot)
            axis, base, part, _, inside, sem = chain(lot)[s]
            copies = []
            for n, peer in enumerate(peers(axis)):
                away = base + ((place[axis] + n + 1) % ways[axis]) * part
                copy = send(
                    held.at[u, block(away, part), cols], inbox.at[u, block(inside + n * part, part), cols],
                    out_send.at[lot, sem + n], out_recv.at[lot, sem + n], peer,
                )
                copies.append((away, copy))
            return copies

        def back_copies(lot, s):
            u, cols = lots[lot][0], columns(lot)
            axis, _, part, mine, _, sem = chain(lot)[s]
            own = from_core.at[u, block(mine, part), cols]
            return [
                send(own, own, back_send.at[lot, sem + n], back_recv.at[lot, sem + n], peer)
                for n, peer in enumerate(peers(axis))
            ]

        def done_copy(lot):
            u, cols = lots[lot][0], columns(lot)
            return pltpu.make_async_copy(from_core.at[u, :, cols], result_ref.at[u, :, cols], done_sem.at[lot])

        def add(lot, at, size, terms, target):
            u, cols = lots[lot][0], columns(lot)
            some = min(size, rows // 4)

            def one(n, _):
                total = held[u, block(at + n * some, some), cols].astype(F32)
                for ref, shift in terms:
                    total = total + ref[u, block(at + shift + n * some, some), cols].astype(F32)
                target[u, block(at + n * some, some), cols] = total.astype(BF)
                return 0

            if size == some:
                one(0, 0)
            else:
                lax.fori_loop(0, size // some, one, 0)

        def fire(lot, k):
            links = chain(lot)
            last = len(links)
            if k == 0:
                core_copy(lot).wait_recv()
                if lot < self.copied:
                    pltpu.make_async_copy(from_core.at[lot], held.at[lot], local_sem.at[lot]).wait()
                terms = [(from_core, 0)]
            elif k <= last:
                for _, copy in out_copies(lot, k - 1):
                    copy.wait_recv()
                axis, _, part, mine, inside, _ = links[k - 1]
                terms = [(inbox, inside + n * part - mine) for n in range(ways[axis] - 1)]
            if k < last:
                _, _, part, mine, _, _ = links[k]
                for away, copy in out_copies(lot, k):
                    add(lot, away, part, terms, held)
                    copy.start()
                add(lot, mine, part, terms, held)
                return
            if k == last:
                _, _, part, mine, _, _ = links[k - 1]
                add(lot, mine, part, terms, from_core)
            else:
                for copy in back_copies(lot, 2 * last - k):
                    copy.wait_recv()
            if k < 2 * last:
                for copy in back_copies(lot, 2 * last - 1 - k):
                    copy.start()
            else:
                done_copy(lot).start()

        def begin(u, theirs, mine=None):
            for lot in range(len(lots)):
                if lots[lot][0] == u:
                    core_copy(lot, theirs).start()
            if mine is not None:
                pltpu.make_async_copy(mine, held.at[u], local_sem.at[u]).start()

        small_peers = [
            sibling, peers("x")[0], peers("y")[0],
            {"rep": rep + 4 - 8 * (place["z"] % 2)}, {"rep": rep + 8 - 16 * (place["z"] // 2)},
        ]

        def copy_small(k):
            return send(kept.at[k], came.at[k], small_send.at[k], small_recv.at[k], small_peers[k])

        def small_next(k):
            copy_small(k).wait_recv()
            kept[k + 1] = kept[k] + came[k]
            if k + 1 < SMALL:
                copy_small(k + 1).start()

        def settle():
            for k in range(SMALL):
                copy_small(k).wait_send()
            for lot in range(len(lots)):
                core_copy(lot).wait_send()
                for s in range(len(lots[lot][3])):
                    for _, copy in out_copies(lot, s):
                        copy.wait_send()
                    for copy in back_copies(lot, s):
                        copy.wait_send()
                done_copy(lot).wait()

        self.meet, self.begin, self.fire, self.settle = meet, begin, fire, settle
        self.small_start, self.small_next = (lambda: copy_small(0).start()), small_next

    @staticmethod
    def buffers(lots, units, rows, cols, small):
        dma = pltpu.SemaphoreType.DMA
        count = len(lots)
        return [
            pltpu.VMEM((units, rows, cols), BF),
            pltpu.VMEM((units, rows, cols), BF),
            pltpu.VMEM((units, rows - rows // 16, cols), BF),
            pltpu.VMEM((SMALL + 1,) + small, F32),
            pltpu.VMEM((SMALL,) + small, F32),
            dma((units,)), dma((count,)), dma((count,)),
        ] + [dma((count, 6))] * 4 + [dma((SMALL,))] * 2 + [dma((count,))]


HALVES = 2
TILE_B = 256


def late_back_kernel(linked, seqs, groups, *refs):
    (
        second_ref, pre_ref, norm_ref, inv_ref, ctx_ref, up_ref, out_ref, small_ref,
        tokens_ref, rows_ref, q_ref, k_ref, v_ref, lse_ref, sums_in_ref,
    ), refs = refs[:15], refs[15:]
    step = pl.program_id(0)
    last = pl.num_programs(0) - 1
    first = seqs * HALVES
    if linked:
        feed_mine, feed_theirs, resid_ref, jlow_ref, result_ref, total_ref = refs[:6]
        cback_ref, rowdot_ref, acc, bias_ref, theirs = refs[6:11]
        buffers, sems = refs[11:16], refs[16:]
        early = feed_mine.shape[0]
        exchange = Exchange(LOTS, early, result_ref, *buffers, sems)
        held, kept = buffers[0], buffers[3]
        core = lax.axis_index("shard")
        sums_ref = kept.at[0]
    else:
        resid_ref, jlow_ref, mine_ref, theirs_ref, sums_ref, cback_ref, rowdot_ref, acc, bias_ref = refs

    def pause(start, count, each, n):
        for i in range(count if linked else 0):
            events = EVENTS[start[1] + each * i + n]
            if events:

                @pl.when(step == start[0] + i)
                def _():
                    for lot, k in events:
                        exchange.fire(lot, k)

    pause_norm = functools.partial(pause, (0, 0), first, 2)
    pause_attend = functools.partial(pause, (first, 2 * first), seqs * groups, 2)

    def hand_over(n):
        if linked:
            deal(core, acc, held.at[pl.ds(early + n, 1)], theirs.at[pl.ds(n, 1)])
            for m in range(1 + groups):

                @pl.when(n == m)
                def _():
                    exchange.begin(early + m, theirs.at[m])

        else:
            deal(0, acc, mine_ref.at[pl.ds(n, 1)], theirs_ref.at[pl.ds(n, 1)])

    @pl.when(step == 0)
    def _():
        if linked:
            exchange.meet()
            for u in range(early):
                exchange.begin(u, feed_theirs.at[u], feed_mine.at[u])
        sums_ref[...] = sums_in_ref[...]

    @pl.when(step < first)
    def _():
        pause_norm(0)
        resid, cback, rowdot, part = norm_step(
            second_ref[0], pre_ref[0], norm_ref[0], inv_ref[0], ctx_ref[0], up_ref, out_ref, small_ref, sums_ref,
            pause_norm,
        )
        resid_ref[0] = resid
        size = resid.shape[0]
        s, some = step // HALVES, pl.ds(pl.multiple_of(step % HALVES * size, size), size)
        for n in range(groups):
            cback_ref[s, n, some, :] = cback[:, n * GROUP : (n + 1) * GROUP]
        rowdot_ref[s, :, some] = rowdot

        @pl.when(step == 0)
        def _():
            acc[...] = part

        @pl.when(step > 0)
        def _():
            acc[...] += part

        @pl.when(step == first - 1)
        def _():
            hand_over(step - (first - 1))

    @pl.when(step >= first)
    def _():
        g, s = (step - first) // seqs, (step - first) % seqs
        attend_step(
            g, s, tokens_ref, rows_ref, q_ref, k_ref, v_ref, cback_ref, lse_ref, rowdot_ref,
            jlow_ref, sums_ref, bias_ref, acc, pause_attend,
        )

        @pl.when(s == seqs - 1)
        def _():
            hand_over(1 + g)

    if linked:

        @pl.when(step == last)
        def _():
            exchange.small_start()
            rest = EVENTS[-1]
            share = -(-len(rest) // (SMALL + 1))
            for k in range(SMALL + 1):
                for lot, stage in rest[k * share : (k + 1) * share]:
                    exchange.fire(lot, stage)
                if k < SMALL:
                    exchange.small_next(k)
            total_ref[...] = kept[SMALL]
            exchange.settle()


def attend_step(
    g, s, tokens_ref, rows_ref, q_ref, k_ref, v_ref, cback_ref, lse_ref, rowdot_ref,
    jlow_ref, sums_ref, bias_ref, acc, pause,
):
    length = tokens_ref.shape[1]
    tile = min(TILE_B, length)
    ids = rows_ref[pl.ds(s, 1), :]
    bias_ref[...] = jnp.where(ids.astype(F32) >= column(ids), 0.0, NEG)
    lane = lax.broadcasted_iota(jnp.int32, (length, 128), 1)
    low = lane < HEAD_DIM

    for pair in range(GROUP // 128):
        pause(pair)
        at = slice(pair * 128, pair * 128 + 128)
        q2 = q_ref[0, :, at] * BF(0.125)
        k2 = k_ref[0, :, at]
        v2 = v_ref[0, :, at]
        do2 = cback_ref[s, g, :, at]
        dq = None
        for t in range(length // tile):
            rows = slice(t * tile, (t + 1) * tile)
            dks, dvs = [], []
            for h in range(2):
                mine = low[rows] if h == 0 else ~low[rows]
                km = jnp.where(mine, k2[rows], BF(0))
                vm = jnp.where(mine, v2[rows], BF(0))
                head = g * (GROUP // HEAD_DIM) + pair * 2 + h
                lse = lse_ref[0, pl.ds(head, 1), :]
                rowdot = rowdot_ref[s, pl.ds(head, 1), :]
                probs = jnp.exp(dot_nt(km, q2) + bias_ref[rows, :] - lse)
                dprobs = dot_nt(vm, do2)
                dscore = (probs * (dprobs - rowdot)).astype(BF)
                dvs.append(dot(probs.astype(BF), do2))
                dks.append(dot(dscore, q2))
                part = dot_tn(dscore, km * BF(0.125))
                dq = part if dq is None else dq + part
            dk = jnp.where(low[rows], dks[0], dks[1])
            dv = jnp.where(low[rows], dvs[0], dvs[1])
            jlow_ref[0, rows, GROUP + pair * 128 : GROUP + pair * 128 + 128] = dk.astype(BF)
            jlow_ref[0, rows, 2 * GROUP + pair * 128 : 2 * GROUP + pair * 128 + 128] = dv.astype(BF)
            vsum = jnp.sum(dv, axis=0, keepdims=True)
            vtotal = vsum if t == 0 else vtotal + vsum
        jlow_ref[0, :, at] = dq.astype(BF)
        lanes = pl.ds(pl.multiple_of(g * GROUP + pair * 128, 128), 128)
        sums_ref[0:1, lanes] += jnp.sum(dq, axis=0, keepdims=True)
        sums_ref[1:2, lanes] += vtotal

    part = dot_tn(tokens_ref[0], jlow_ref[0])

    @pl.when(s == 0)
    def _():
        acc[...] = part

    @pl.when(s > 0)
    def _():
        acc[...] += part


def late_back(second, pre_low, norm, inv, ctx, up_bin, out_bin, small, tokens, block_ids, joined, lse, sums, feed_grads=None):
    seqs, length, width = tokens.shape
    groups = width // GROUP
    linked = feed_grads is not None
    first = seqs * HALVES
    phase = lambda i: (i + 64 - first) // 64
    seq_one = lambda i: i + phase(i) * (first - 1 - i)
    seq_two = lambda i: phase(i) * ((i - first + seqs * first) % seqs)
    group_two = lambda i: phase(i) * ((i - first) // seqs)
    some = length // HALVES
    second, pre_low, norm, inv, ctx = (a.reshape(first, some, a.shape[2]) for a in (second, pre_low, norm, inv, ctx))
    one = lambda *shape: pl.BlockSpec((1,) + shape, lambda i: (seq_one(i),) + (0,) * len(shape))
    two = lambda *shape: pl.BlockSpec((1,) + shape, lambda i: (seq_two(i),) + (0,) * len(shape))
    part = lambda k: pl.BlockSpec((1, length, GROUP), lambda i: (seq_two(i), 0, k * groups + group_two(i)))
    held = lambda a: pl.BlockSpec(a.shape, lambda i: (0,) * a.ndim, pipeline_mode=pl.Buffered(1))
    anywhere = pl.BlockSpec(memory_space=pl.ANY)
    unit = (width, width // 2)
    like = jax.ShapeDtypeStruct
    in_specs = [
        one(some, width), one(some, pre_low.shape[2]), one(some, width), one(some, 1), one(some, width),
        held(up_bin), held(out_bin), held(small),
        two(length, width), held(block_ids), part(0), part(1), part(2), two(16, length), held(sums),
    ]
    operands = [
        second, pre_low, norm, inv, ctx, up_bin, out_bin, small,
        tokens, block_ids, joined, joined, joined, lse, sums,
    ]
    out_specs = [one(some, width), pl.BlockSpec((1, length, 3 * GROUP), lambda i: (seq_two(i), 0, group_two(i)))]
    out_shape = [like((first, some, width), BF), like((seqs, length, 3 * width), BF)]
    scratch = [
        pltpu.VMEM((seqs, groups, length, GROUP), BF), pltpu.VMEM((seqs, 16, length), F32),
        pltpu.VMEM((width, width), F32), pltpu.VMEM((length, length), F32),
    ]
    if linked:
        units = feed_grads[0].shape[0] + 1 + groups
        in_specs += [anywhere] * 2
        operands += feed_grads
        out_specs += [anywhere, full(sums.shape)]
        out_shape += [like((units,) + unit, BF), like(sums.shape, F32)]
        scratch += [pltpu.VMEM((1 + groups,) + unit, BF)] + Exchange.buffers(LOTS, units, *unit, sums.shape)
        extra = dict(collective_id=0, has_side_effects=True)
    else:
        out_specs += [full((1 + groups,) + unit)] * 2 + [full(sums.shape)]
        out_shape += [like((1 + groups,) + unit, BF)] * 2 + [like(sums.shape, F32)]
        extra = {}
    return pl.pallas_call(
        functools.partial(late_back_kernel, linked, seqs, groups),
        grid=(seqs * (HALVES + groups),),
        in_specs=in_specs,
        out_specs=out_specs,
        out_shape=out_shape,
        scratch_shapes=scratch,
        compiler_params=params(58, **extra),
        cost_estimate=cost(seqs * length * width * (20 * width + 40 * length), 70 * seqs * length * width),
        name="late_back",
    )(*operands)


def token_total(resid_ref, jlow_ref, qkv_ref):
    width = resid_ref.shape[2]
    groups = width // GROUP
    total = resid_ref[0].astype(F32)
    for g in range(groups):
        for k in range(3):
            at = (3 * g + k) * GROUP
            col = k * width + g * GROUP
            total = total + dot_nt(jlow_ref[0, :, at : at + GROUP], qkv_ref[:, col : col + GROUP])
    return total


def token_kernel(resid_ref, jlow_ref, qkv_ref, grad_ref):
    grad_ref[0] = token_total(resid_ref, jlow_ref, qkv_ref)


def finish_kernel(
    core_ref, resid_ref, jlow_ref, qkv_bin_ref, feed_ref, out_unit_ref, qkv_unit_ref, sums_ref,
    grad_ref, qkv_ref, out_ref, up_ref, dn_ref, small_ref, up_stage, qkv_stage, up_sem, qkv_sem,
):
    step, last = pl.program_id(0), pl.num_programs(0) - 1
    _, rows, half = feed_ref.shape
    groups = qkv_sem.shape[0]
    parts = (slice(0, half), slice(half, rows))

    def up_copy(c, p):
        at = pl.ds(pl.multiple_of((p * (last + 1) + c) * half, half), half)
        return pltpu.make_async_copy(up_stage.at[c, p], up_ref.at[:, at], up_sem.at[c, p])

    def qkv_copy(g, k):
        at = pl.ds(pl.multiple_of(k * rows + g * GROUP, GROUP), GROUP)
        return pltpu.make_async_copy(qkv_stage.at[g, k], qkv_ref.at[:, at], qkv_sem.at[g, k])

    for p in range(2):
        up_stage[step, p] = feed_ref[1, parts[p], :].astype(F32)
        up_copy(step, p).start()
        dn_ref[:, parts[p]] = feed_ref[0, parts[p], :].astype(F32)

    @pl.when(step == 0)
    def _():
        for p in range(2):
            out_ref[:, parts[p]] = out_unit_ref[0, parts[p], :].astype(F32)
        mine = pl.ds(pl.multiple_of(core_ref[0] * half, half), half)
        small_ref[...] = sums_ref[:, mine]

    @pl.when(step > 0)
    def _():
        for j in range(3 * GROUP // 128):
            col = j * 128
            qkv_stage[step - 1, col // GROUP, :, col % GROUP : col % GROUP + 128] = qkv_unit_ref[
                0, parts[col // half], col % half : col % half + 128
            ].astype(F32)
        for k in range(3):
            qkv_copy(step - 1, k).start()

    grad_ref[0] = token_total(resid_ref, jlow_ref, qkv_bin_ref)

    @pl.when(step == last)
    def _():
        for c in range(up_sem.shape[0]):
            for p in range(2):
                up_copy(c, p).wait()
        for g in range(groups):
            for k in range(3):
                qkv_copy(g, k).wait()


def finish(core, resid, jlow, qkv_bin, units, sums):
    seqs, length, width = resid.shape
    count, rows, half = units.shape
    groups = rows // GROUP
    chunks = (count - 1 - groups) // 2
    assert chunks == seqs and groups == seqs - 1
    per_seq = lambda *shape: pl.BlockSpec((1,) + shape, lambda s, _: (s,) + (0,) * len(shape))
    late = lambda s: s - (s + 63) // 64
    like = lambda *shape: jax.ShapeDtypeStruct(shape, F32)
    anywhere = pl.BlockSpec(memory_space=pl.ANY)
    return pl.pallas_call(
        finish_kernel,
        grid_spec=pltpu.PrefetchScalarGridSpec(
            num_scalar_prefetch=1,
            grid=(chunks,),
            in_specs=[
                per_seq(length, width),
                per_seq(length, 3 * width),
                full(qkv_bin.shape),
                pl.BlockSpec((2, rows, half), lambda s, _: (s, 0, 0)),
                pl.BlockSpec((1, rows, half), lambda s, _: (2 * chunks, 0, 0)),
                pl.BlockSpec((1, rows, half), lambda s, _: (2 * chunks + 1 + late(s), 0, 0)),
                full(sums.shape),
            ],
            out_specs=[
                per_seq(length, width),
                anywhere,
                full((half, rows)),
                anywhere,
                pl.BlockSpec((half, rows), lambda s, _: (s, 0)),
                full((sums.shape[0], half)),
            ],
            scratch_shapes=[
                pltpu.VMEM((chunks, 2, half, half), F32),
                pltpu.VMEM((groups, 3, half, GROUP), F32),
                pltpu.SemaphoreType.DMA((chunks, 2)),
                pltpu.SemaphoreType.DMA((groups, 3)),
            ],
        ),
        out_shape=[
            like(seqs, length, width), like(half, 3 * rows), like(half, rows), like(half, 2 * chunks * half),
            like(chunks * half, rows), like(sums.shape[0], half),
        ],
        compiler_params=params(),
        cost_estimate=cost(6 * seqs * length * width * width, 16 * seqs * length * width),
        name="finish",
    )(core, resid, jlow, qkv_bin, units, units, units, sums)


def token_back(resid, jlow, qkv_bin):
    seqs, length, width = resid.shape
    per_seq = lambda *shape: pl.BlockSpec((1,) + shape, lambda s: (s,) + (0,) * len(shape))
    return pl.pallas_call(
        token_kernel,
        grid=(seqs,),
        in_specs=[per_seq(length, width), per_seq(length, 3 * width), full(qkv_bin.shape)],
        out_specs=per_seq(length, width),
        out_shape=jax.ShapeDtypeStruct((seqs, length, width), F32),
        compiler_params=params(),
        cost_estimate=cost(6 * seqs * length * width * width, 16 * seqs * length * width),
        name="token_back",
    )(resid, jlow, qkv_bin)


def swap(value):
    return lax.ppermute(value, "shard", [(0, 1), (1, 0)])


def small_rows(biases, gain, shift, hidden_bias):
    rows = biases.shape[0]
    return jnp.concatenate([biases.T, gain.T, shift.T, hidden_bias.reshape(-1, rows)], axis=0)


def reduce_plain(feed_grads, out_grads, qkv_grads, sums):
    def whole(mine, theirs):
        count, rows, half = mine.shape
        cut = lambda a: a.reshape(count, 2, half, half).transpose(0, 2, 1, 3).reshape(count, half, rows)
        return jnp.concatenate([cut(mine), cut(theirs)], axis=1)

    feed_all, out_all, qkv_all = whole(*feed_grads), whole(*out_grads), whole(*qkv_grads)
    chunks, groups, width = feed_all.shape[0] // 2, qkv_all.shape[0], feed_all.shape[2]
    half, units = width // 2, chunks * width
    grads = (
        qkv_all.reshape(groups, width, 3, GROUP).transpose(1, 2, 0, 3).reshape(width, 3 * width),
        out_all[0],
        feed_all[1::2].reshape(chunks, width, 2, half).transpose(1, 2, 0, 3).reshape(width, units),
        feed_all[0::2].reshape(chunks, 2, half, width).transpose(1, 0, 2, 3).reshape(units, width),
        sums[0:4].T.astype(BF),
        sums[8:].reshape(chunks, 2, half).transpose(1, 0, 2).reshape(-1).astype(BF),
        sums[4:6].T.astype(BF),
        sums[6:8].T.astype(BF),
    )
    owned = lax.psum_scatter(grads, "shard", scatter_dimension=0, tiled=True)
    return jax.tree.map(lambda part: part.astype(F32), lax.psum(owned, "rep"))


def body(tokens, teacher, block_ids, *weights):
    qkv, out, up, down, biases, hidden_bias, gain, shift = weights
    paired = lax.axis_size("shard") == 2 and lax.axis_size("rep") == 16
    if paired:
        core = lax.axis_index("shard").reshape(1)
        small = small_rows(biases, gain, shift, hidden_bias)
        small, qkv, out = ((a, swap(a)) for a in (small, qkv, out))
        up, down, _, _ = lax.optimization_barrier((up, down, qkv[1], small[1]))
        up, down = ((a, swap(a)) for a in (up, down))
    else:
        core = jnp.zeros((1,), jnp.int32)
        gathered = [lax.all_gather(w, "shard", axis=0, tiled=True) for w in weights]
        qkv, out, up, down, *rest = (jnp.split(w, 2, axis=0) for w in gathered)
        small = [small_rows(rest[0][i], rest[2][i], rest[3][i], rest[1][i]) for i in range(2)]
    joined, ctx, lse, norm, inv, small, qkv_bin, out_bin = attend(core, tokens, block_ids, qkv, out, small)
    final, first_low, hidden, slope, second, mixed, sums, up_bin, dn_bin = feed(core, norm, teacher, small, up, down)
    pre_low, *feed_grads, sums = feed_back(core, mixed, first_low, hidden, slope, dn_bin, sums)
    pre_low = pre_low.reshape(hidden.shape)
    operands = (second, pre_low, norm, inv, ctx, up_bin, out_bin, small, tokens, block_ids, joined, lse, sums)
    if not paired:
        resid, jlow, *grads, sums = late_back(*operands)
        token_grad = token_back(resid.reshape(tokens.shape), jlow, qkv_bin)
        out_grads, qkv_grads = ([a[cut] for a in grads] for cut in (slice(0, 1), slice(1, None)))
        return (final, token_grad) + tuple(reduce_plain(feed_grads, out_grads, qkv_grads, sums[:12]))
    resid, jlow, units, sums = late_back(*operands, feed_grads)
    resid = resid.reshape(tokens.shape)
    token_grad, qkv_grad, out_grad, up_grad, dn_grad, small = finish(core, resid, jlow, qkv_bin, units, sums)
    hidden_rows = hidden_bias.shape[0] // small.shape[1]
    return (
        final, token_grad, qkv_grad, out_grad, up_grad, dn_grad,
        small[0:4].T, small[8 : 8 + hidden_rows].reshape(-1), small[4:6].T, small[6:8].T,
    )


def solution(mesh):
    placed = (
        P(("shard", "rep"), None, None),
        P(("shard", "rep"), None, None),
        P(("shard", "rep"), None),
        P("shard", None),
        P("shard", None),
        P("shard", None),
        P("shard", None),
        P("shard", None),
        P("shard"),
        P("shard", None),
        P("shard", None),
    )
    return jax.shard_map(
        body,
        mesh=mesh,
        in_specs=placed,
        out_specs=placed[:2] + placed[3:],
        check_vma=False,
    )
```

```python
import functools

import jax
import jax.numpy as jnp
from jax import lax
from jax.experimental import pallas as pl
from jax.experimental.pallas import tpu as pltpu
from jax.sharding import PartitionSpec as P

HEAD_DIM = 64
GROUP = 256
EPS = 1e-05
NEG = -1e30
BF = jnp.bfloat16
F32 = jnp.float32
MB = 1 << 20


def params(mb=56, **kw):
    return pltpu.CompilerParams(vmem_limit_bytes=mb * MB, **kw)


def dot(a, b):
    return jnp.dot(a, b, preferred_element_type=F32)


def dot_nt(a, b):
    return lax.dot_general(a, b, (((1,), (1,)), ((), ())), preferred_element_type=F32)


def dot_tn(a, b):
    return lax.dot_general(a, b, (((0,), (0,)), ((), ())), preferred_element_type=F32)


def full(shape):
    return pl.BlockSpec(shape, lambda *_: (0,) * len(shape))


def cost(flops, nbytes, trans=0):
    return pl.CostEstimate(flops=int(flops), bytes_accessed=int(nbytes), transcendentals=int(trans))


def column(row):
    return jnp.broadcast_to(row.astype(F32), (8, row.shape[1])).T[:, 0:1]


def deal(core, acc, mine_ref, theirs_ref, at=0):
    half = acc.shape[0] // 2
    wide = acc.shape[1] // 2
    for ref, who in ((mine_ref, core), (theirs_ref, 1 - core)):
        rows = pl.ds(pl.multiple_of(who * half, half), half)
        ref[at, 0:half, :] = acc[rows, 0:wide].astype(BF)
        ref[at, half : 2 * half, :] = acc[rows, wide : 2 * wide].astype(BF)


def binary_halves(first, second):
    rows = 2 * first.shape[0]
    total = jnp.sum(jnp.abs(first.astype(F32)), axis=0, keepdims=True) + jnp.sum(
        jnp.abs(second.astype(F32)), axis=0, keepdims=True
    )
    scale = (total / rows).astype(BF)
    return (
        jnp.where(first >= 0, scale, -scale).astype(BF),
        jnp.where(second >= 0, scale, -scale).astype(BF),
    )


def binary_rows(core, own_ref, other_ref, out_ref):
    half, cols = own_ref.shape
    own_at = pl.ds(pl.multiple_of(core * half, half), half)
    other_at = pl.ds(pl.multiple_of((1 - core) * half, half), half)
    for j in range(0, cols, GROUP):
        at = slice(j, j + GROUP)
        out_ref[own_at, at], out_ref[other_at, at] = binary_halves(own_ref[:, at], other_ref[:, at])


def binary_up(core, own_ref, other_ref, out_ref):
    half, cols = own_ref.shape
    chunks = cols // (2 * half)
    own_at = pl.ds(pl.multiple_of(core * half, half), half)
    other_at = pl.ds(pl.multiple_of((1 - core) * half, half), half)

    def one(j, _):
        at = pl.ds(pl.multiple_of(j * half, half), half)
        to = pl.ds(pl.multiple_of((j % chunks) * 2 * half + (j // chunks) * half, half), half)
        out_ref[own_at, to], out_ref[other_at, to] = binary_halves(own_ref[:, at], other_ref[:, at])
        return 0

    lax.fori_loop(0, 2 * chunks, one, 0)


def binary_down(core, own_ref, other_ref, out_ref):
    rows, cols = own_ref.shape
    half = cols // 2

    def one(j, _):
        at = pl.ds(pl.multiple_of(j * GROUP, GROUP), GROUP)
        own, other = binary_halves(own_ref[:, at], other_ref[:, at])
        for c in range(rows // half):
            part = slice(c * half, (c + 1) * half)
            out_ref[pl.ds(pl.multiple_of((2 * c + core) * half, half), half), at] = own[part]
            out_ref[pl.ds(pl.multiple_of((2 * c + 1 - core) * half, half), half), at] = other[part]
        return 0

    lax.fori_loop(0, cols // GROUP, one, 0)


def attend_kernel(
    core_ref, tokens_ref, rows_ref, qkv_own, qkv_other, out_own, out_other, small_own, small_other,
    joined_ref, ctx_ref, lse_ref, norm_ref, inv_ref, small_ref, qkv_any, out_any,
    bias_ref, qkv_ref, out_ref, sems,
):
    length, width = tokens_ref.shape[1:]
    keep = (
        pltpu.make_async_copy(qkv_ref, qkv_any, sems.at[0]),
        pltpu.make_async_copy(out_ref, out_any, sems.at[1]),
    )

    @pl.when(pl.program_id(0) == 0)
    def _():
        core, half = core_ref[0], width // 2
        binary_rows(core, qkv_own, qkv_other, qkv_ref)
        binary_rows(core, out_own, out_other, out_ref)
        small_ref[:, pl.ds(pl.multiple_of(core * half, half), half)] = small_own[...].astype(F32)
        small_ref[:, pl.ds(pl.multiple_of((1 - core) * half, half), half)] = small_other[...].astype(F32)
        for copy in keep:
            copy.start()

    x = tokens_ref[0]
    for part, bias_row in ((0, 0), (1, None), (2, 1)):
        joined = dot(x, qkv_ref[:, part * width : (part + 1) * width])
        if bias_row is not None:
            joined = joined + small_ref[bias_row : bias_row + 1, :]
        joined_ref[0, :, part * width : (part + 1) * width] = joined.astype(BF)
    ids = rows_ref[pl.ds(pl.program_id(0), 1), :]
    bias_ref[...] = jnp.where(column(ids) >= ids.astype(F32), 0.0, NEG)
    lane = lax.broadcasted_iota(jnp.int32, (length, 128), 1)
    low = lane < HEAD_DIM
    lse_all = jnp.zeros((length, 128), F32)
    tile = min(TILE_F, length)
    for pair in range(width // 128):
        q2 = joined_ref[0, :, pair * 128 : pair * 128 + 128] * BF(0.125)
        k2 = joined_ref[0, :, width + pair * 128 : width + pair * 128 + 128]
        v2 = joined_ref[0, :, 2 * width + pair * 128 : 2 * width + pair * 128 + 128]
        for t in range(length // tile):
            rows = slice(t * tile, (t + 1) * tile)
            parts = []
            for h in range(2):
                mine = low[rows] if h == 0 else ~low[rows]
                qm = jnp.where(mine, q2[rows], BF(0))
                scores = dot_nt(qm, k2) + bias_ref[rows, :]
                peak = jnp.max(scores, axis=-1, keepdims=True)
                raised = jnp.exp(scores - peak)
                total = jnp.sum(raised, axis=-1, keepdims=True)
                parts.append(dot(raised.astype(BF), v2) / total)
                lse_ref_col = peak + jnp.log(total)
                bias_lane = lane[rows] == 2 * pair + h
                lse_cols = jnp.where(bias_lane, lse_ref_col, 0.0)
                if h == 0:
                    pair_lse = lse_cols
                else:
                    pair_lse = pair_lse + lse_cols
            ctx_ref[0, rows, pair * 128 : pair * 128 + 128] = jnp.where(low[rows], parts[0], parts[1]).astype(BF)
            if t == 0:
                tiles_lse = [pair_lse]
            else:
                tiles_lse.append(pair_lse)
        lse_all = lse_all + jnp.concatenate(tiles_lse, axis=0)
    lse_ref[0] = lse_all.T[0:16, :]
    resid = x.astype(F32) + dot(ctx_ref[0], out_ref[...]) + small_ref[2:3, :]
    center = resid - jnp.mean(resid, axis=-1, keepdims=True)
    inverse = lax.rsqrt(jnp.mean(center * center, axis=-1, keepdims=True) + EPS)
    norm_ref[0] = center * inverse
    inv_ref[0] = inverse

    @pl.when(pl.program_id(0) == pl.num_programs(0) - 1)
    def _():
        for copy in keep:
            copy.wait()


TILE_F = 512


def attend(core, tokens, block_ids, qkv, out, small):
    seqs, length, width = tokens.shape
    per_seq = lambda *shape: pl.BlockSpec((1,) + shape, lambda s, _: (s,) + (0,) * len(shape))
    once = lambda a: pl.BlockSpec(a.shape, lambda s, _: (0,) * a.ndim, pipeline_mode=pl.Buffered(1))
    anywhere = pl.BlockSpec(memory_space=pl.ANY)
    like = jax.ShapeDtypeStruct
    joined_width = qkv[0].shape[1]
    whole = (small[0].shape[0], width)
    return pl.pallas_call(
        attend_kernel,
        grid_spec=pltpu.PrefetchScalarGridSpec(
            num_scalar_prefetch=1,
            grid=(seqs,),
            in_specs=[per_seq(length, width)] + [once(a) for a in (block_ids, *qkv, *out, *small)],
            out_specs=[
                per_seq(length, joined_width),
                per_seq(length, width),
                per_seq(16, length),
                per_seq(length, width),
                per_seq(length, 1),
                full(whole),
                anywhere,
                anywhere,
            ],
            scratch_shapes=[
                pltpu.VMEM((length, length), F32),
                pltpu.VMEM((width, joined_width), BF),
                pltpu.VMEM((width, width), BF),
                pltpu.SemaphoreType.DMA((2,)),
            ],
        ),
        out_shape=[
            like((seqs, length, joined_width), BF),
            like((seqs, length, width), BF),
            like((seqs, 16, length), F32),
            like((seqs, length, width), F32),
            like((seqs, length, 1), F32),
            like(whole, F32),
            like((width, joined_width), BF),
            like((width, width), BF),
        ],
        compiler_params=params(),
        cost_estimate=cost(seqs * length * width * (8 * width + 16 * length), 30 * seqs * length * width),
        name="attend",
    )(core, tokens, block_ids, *qkv, *out, *small)


def gelu_pair(u):
    cdf = 0.5 + 0.5 * lax.erf(u * 0.7071067811865476)
    density = jnp.exp(-0.5 * u * u) * 0.3989422804014327
    return u * cdf, cdf + u * density


def norm_back(upstream, normed, inverse, gain):
    scaled = upstream * gain
    weighted = upstream * normed
    centered = (
        scaled
        - jnp.mean(scaled, axis=-1, keepdims=True)
        - normed * jnp.mean(weighted * gain, axis=-1, keepdims=True)
    )
    return centered * inverse, jnp.sum(weighted, axis=0, keepdims=True), jnp.sum(upstream, axis=0, keepdims=True)


def feed_kernel(
    core_ref, norm_ref, teacher_ref, small_ref, up_own, up_other, dn_own, dn_other,
    final_ref, first_low_ref, hidden_ref, slope_ref, second_ref, mixed_ref, sums_ref, up_any, dn_any,
    up_ref, dn_ref, sems,
):
    width = norm_ref.shape[2]
    keep = (
        pltpu.make_async_copy(up_ref, up_any, sems.at[0]),
        pltpu.make_async_copy(dn_ref, dn_any, sems.at[1]),
    )

    @pl.when(pl.program_id(0) == 0)
    def _():
        binary_up(core_ref[0], up_own, up_other, up_ref)
        binary_down(core_ref[0], dn_own, dn_other, dn_ref)
        for copy in keep:
            copy.start()

    first = norm_ref[0] * small_ref[4:5, :] + small_ref[6:7, :]
    first_low = first.astype(BF)
    first_low_ref[0] = first_low
    acc = first + small_ref[3:4, :]
    for c in range(up_ref.shape[1] // width):
        cols = slice(c * width, (c + 1) * width)
        pre = dot(first_low, up_ref[:, cols]) + small_ref[8 + c : 9 + c, :]
        value, slope = gelu_pair(pre)
        value = value.astype(BF)
        hidden_ref[0, :, cols] = value
        slope_ref[0, :, cols] = slope.astype(BF)
        acc = acc + dot(value, dn_ref[cols, :])
    center = acc - jnp.mean(acc, axis=-1, keepdims=True)
    inverse = lax.rsqrt(jnp.mean(center * center, axis=-1, keepdims=True) + EPS)
    normed = center * inverse
    gain = small_ref[5:6, :]
    final = normed * gain + small_ref[7:8, :]
    final_ref[0] = final.astype(BF)
    upstream = final - teacher_ref[0].astype(F32)
    second, gain_sum, shift_sum = norm_back(upstream, normed, inverse, gain)
    second_ref[0] = second
    mixed_ref[0] = second.astype(BF)

    @pl.when(pl.program_id(0) == 0)
    def _():
        sums_ref[...] = jnp.zeros_like(sums_ref)

    sums_ref[3:4, :] += jnp.sum(second, axis=0, keepdims=True)
    sums_ref[5:6, :] += gain_sum
    sums_ref[7:8, :] += shift_sum

    @pl.when(pl.program_id(0) == pl.num_programs(0) - 1)
    def _():
        for copy in keep:
            copy.wait()


def feed(core, norm, teacher, small, up, dn):
    seqs, length, width = norm.shape
    hidden = up[0].shape[1]
    per_seq = lambda *shape: pl.BlockSpec((1,) + shape, lambda s, _: (s,) + (0,) * len(shape))
    once = lambda a: pl.BlockSpec(a.shape, lambda s, _: (0,) * a.ndim, pipeline_mode=pl.Buffered(1))
    anywhere = pl.BlockSpec(memory_space=pl.ANY)
    like = jax.ShapeDtypeStruct
    row = lambda n, dt: like((seqs, length, n), dt)
    return pl.pallas_call(
        feed_kernel,
        grid_spec=pltpu.PrefetchScalarGridSpec(
            num_scalar_prefetch=1,
            grid=(seqs,),
            in_specs=[per_seq(length, width), per_seq(length, width)] + [once(a) for a in (small, *up, *dn)],
            out_specs=[
                per_seq(length, width),
                per_seq(length, width),
                per_seq(length, hidden),
                per_seq(length, hidden),
                per_seq(length, width),
                per_seq(length, width),
                full((16, width)),
                anywhere,
                anywhere,
            ],
            scratch_shapes=[
                pltpu.VMEM((width, hidden), BF),
                pltpu.VMEM((hidden, width), BF),
                pltpu.SemaphoreType.DMA((2,)),
            ],
        ),
        out_shape=[
            row(width, BF), row(width, BF), row(hidden, BF), row(hidden, BF), row(width, F32), row(width, BF),
            like((16, width), F32), like((width, hidden), BF), like((hidden, width), BF),
        ],
        compiler_params=params(60),
        cost_estimate=cost(4 * seqs * length * width * hidden, 36 * seqs * length * width),
        name="feed",
    )(core, norm, teacher, small, *up, *dn)


def feed_back_kernel(
    core_ref, mixed_ref, first_ref, hidden_ref, slope_ref, dn_ref, sums_in_ref,
    pre_ref, mine_ref, theirs_ref, sums_ref, acc,
):
    chunk = pl.program_id(0)

    @pl.when(chunk == 0)
    def _():
        sums_ref[...] = sums_in_ref[...]

    mixed = mixed_ref[0]
    pre_back = dot_nt(mixed, dn_ref[...]) * slope_ref[0].astype(F32)
    pre_low = pre_back.astype(BF)
    pre_ref[0] = pre_low
    acc[...] = dot_tn(hidden_ref[0], mixed)
    deal(core_ref[0], acc, mine_ref, theirs_ref, 0)
    acc[...] = dot_tn(first_ref[0], pre_low)
    deal(core_ref[0], acc, mine_ref, theirs_ref, 1)
    sums_ref[pl.ds(8 + chunk, 1), :] += jnp.sum(pre_back, axis=0, keepdims=True)


def feed_back(core, mixed, first_low, hidden, slope, dn_bin, sums):
    mixed, first_low, hidden, slope = (a.reshape(1, -1, a.shape[2]) for a in (mixed, first_low, hidden, slope))
    seqs, length, width = mixed.shape
    units = hidden.shape[2]
    chunks = units // width
    return pl.pallas_call(
        feed_back_kernel,
        grid_spec=pltpu.PrefetchScalarGridSpec(
            num_scalar_prefetch=1,
            grid=(chunks,),
            in_specs=[
                pl.BlockSpec((1, length, width), lambda c, _: (0, 0, 0)),
                pl.BlockSpec((1, length, width), lambda c, _: (0, 0, 0)),
                pl.BlockSpec((1, length, width), lambda c, _: (0, 0, c)),
                pl.BlockSpec((1, length, width), lambda c, _: (0, 0, c)),
                pl.BlockSpec((width, width), lambda c, _: (c, 0)),
                full(sums.shape),
            ],
            out_specs=[
                pl.BlockSpec((1, length, width), lambda c, _: (0, 0, c)),
                pl.BlockSpec((2, width, width // 2), lambda c, _: (c, 0, 0)),
                pl.BlockSpec((2, width, width // 2), lambda c, _: (c, 0, 0)),
                full(sums.shape),
            ],
            scratch_shapes=[pltpu.VMEM((width, width), F32)],
        ),
        out_shape=[
            jax.ShapeDtypeStruct((seqs, length, units), BF),
            jax.ShapeDtypeStruct((2 * chunks, width, width // 2), BF),
            jax.ShapeDtypeStruct((2 * chunks, width, width // 2), BF),
            jax.ShapeDtypeStruct(sums.shape, F32),
        ],
        compiler_params=params(),
        cost_estimate=cost(6 * seqs * length * width * units, 20 * seqs * length * units),
        name="feed_back",
    )(core, mixed, first_low, hidden, slope, dn_bin, sums)


def norm_step(second, pre_low, norm, inv, ctx, up_ref, out_ref, small_ref, sums_ref, pause):
    width = second.shape[1]
    back = second + dot_nt(pre_low, up_ref[...])
    pause(1)
    resid, gain_sum, shift_sum = norm_back(back, norm, inv, small_ref[4:5, :])
    sums_ref[2:3, :] += jnp.sum(resid, axis=0, keepdims=True)
    sums_ref[4:5, :] += gain_sum
    sums_ref[6:7, :] += shift_sum
    low = resid.astype(BF)
    cback = dot_nt(low, out_ref[...]).astype(BF)
    prod = cback.astype(F32) * ctx.astype(F32)
    high = prod.astype(BF)
    rest = (prod - high.astype(F32)).astype(BF)
    heads = lax.broadcasted_iota(jnp.int32, (16, width), 0)
    lanes = lax.broadcasted_iota(jnp.int32, (16, width), 1)
    pick = jnp.where((lanes >= heads * HEAD_DIM) & (lanes < heads * HEAD_DIM + HEAD_DIM), 1.0, 0.0).astype(BF)
    return low, cback, dot_nt(pick, high) + dot_nt(pick, rest), dot_tn(ctx, low)


MESH = pl.DeviceIdType.MESH

SMALL = 5

LOTS = (
    (0, 0, 384, "xyz"),
    (1, 0, 384, "yxz"),
    (2, 0, 384, "yxz"),
    (3, 0, 384, "yxz"),
    (4, 0, 384, "yxz"),
    (5, 0, 384, "xyz"),
    (6, 0, 384, "zxy"),
    (7, 0, 384, "yxz"),
    (8, 0, 384, "xyz"),
    (9, 0, 384, "xyz"),
    (10, 0, 384, "xyz"),
    (11, 0, 128, "zxy"),
    (11, 128, 128, "yxz"),
    (11, 256, 128, "yxz"),
)
EVENTS = (
    (),
    ((0, 0), (1, 0), (2, 0), (3, 0),),
    ((4, 0), (5, 0),),
    ((6, 0), (7, 0),),
    ((0, 1), (1, 1),),
    (),
    (),
    ((5, 1),),
    ((2, 1),),
    ((1, 2),),
    (),
    ((2, 2), (3, 1), (6, 1),),
    ((1, 3),),
    (),
    ((2, 3), (3, 2), (4, 1),),
    ((1, 4), (6, 2),),
    (),
    ((2, 4), (4, 2), (7, 1),),
    ((1, 5), (3, 3), (0, 2), (8, 0),),
    (),
    ((2, 5), (4, 3), (6, 3), (5, 2),),
    ((3, 4), (7, 2),),
    ((0, 3),),
    ((1, 6),),
    ((4, 4), (8, 1),),
    ((3, 5), (5, 3),),
    ((2, 6), (6, 4), (9, 0), (4, 5), (7, 3),),
    ((8, 2),),
    ((6, 5), (0, 4),),
    ((5, 4),),
    ((3, 6),),
    ((7, 4), (9, 1),),
    ((8, 3),),
    ((4, 6),),
    ((0, 5), (7, 5), (10, 0),),
    (),
    ((5, 5),),
    ((9, 2),),
    ((0, 6), (6, 6),),
    ((8, 4),),
    ((7, 6), (9, 3), (10, 1), (11, 0), (12, 0), (13, 0), (8, 5), (9, 4), (10, 2), (5, 6), (12, 1), (11, 1), (13, 1), (10, 3), (9, 5), (8, 6), (12, 2), (11, 2), (13, 2), (11, 3), (10, 4), (12, 3), (11, 4), (13, 3), (12, 4), (9, 6), (13, 4), (10, 5), (11, 5), (12, 5), (13, 5), (12, 6), (11, 6), (13, 6), (10, 6),),
)


class Exchange:
    def __init__(self, lots, copied, result_ref, held, from_core, inbox, kept, came, sems):
        (
            local_sem, core_send, core_recv, out_send, out_recv, back_send, back_recv, small_send, small_recv, done_sem
        ) = sems
        self.copied = copied
        core, rep = lax.axis_index("shard"), lax.axis_index("rep")
        place = {"x": rep % 2, "y": (rep // 2) % 2, "z": rep // 4, "p": rep % 4}
        ways = {"x": 2, "y": 2, "z": 4, "p": 4}
        sibling = {"shard": 1 - core}
        rows = held.shape[1]
        step_rows = rows // 16

        def peers(axis):
            if axis == "p":
                return [{"rep": rep - place["p"] + (place["p"] + d) % 4} for d in (1, 2, 3)]
            if axis == "z":
                return [{"rep": rep % 4 + 4 * ((place["z"] + d) % 4)} for d in (1, 2, 3)]
            stride = {"x": 1, "y": 2}[axis]
            return [{"rep": rep + stride - 2 * stride * place[axis]}]

        def meet():
            barrier = pltpu.get_barrier_semaphore()
            everyone = [sibling] + peers("p") + peers("z")
            for peer in everyone:
                pl.semaphore_signal(barrier, inc=1, device_id=peer, device_id_type=MESH)
            pl.semaphore_wait(barrier, len(everyone))

        def send(src, dst, send_sem, recv_sem, peer):
            return pltpu.make_async_remote_copy(
                src_ref=src, dst_ref=dst, send_sem=send_sem, recv_sem=recv_sem, device_id=peer, device_id_type=MESH
            )

        def block(at, size):
            return pl.ds(at if isinstance(at, int) else pl.multiple_of(at, step_rows), size)

        def columns(lot):
            return pl.ds(lots[lot][1], lots[lot][2])

        def chain(lot):
            base, size, inside, sem, out = 0, rows, 0, 0, []
            for axis in lots[lot][3]:
                part = size // ways[axis]
                mine = base + place[axis] * part
                out.append((axis, base, part, mine, inside, sem))
                base, size, inside, sem = mine, part, inside + size - part, sem + ways[axis] - 1
            return out

        def core_copy(lot, theirs=None):
            u, cols = lots[lot][0], columns(lot)
            here = from_core.at[u, :, cols]
            return send(here if theirs is None else theirs.at[:, cols], here, core_send.at[lot], core_recv.at[lot], sibling)

        def out_copies(lot, s):
            u, cols = lots[lot][0], columns(lot)
            axis, base, part, _, inside, sem = chain(lot)[s]
            copies = []
            for n, peer in enumerate(peers(axis)):
                away = base + ((place[axis] + n + 1) % ways[axis]) * part
                copy = send(
                    held.at[u, block(away, part), cols], inbox.at[u, block(inside + n * part, part), cols],
                    out_send.at[lot, sem + n], out_recv.at[lot, sem + n], peer,
                )
                copies.append((away, copy))
            return copies

        def back_copies(lot, s):
            u, cols = lots[lot][0], columns(lot)
            axis, _, part, mine, _, sem = chain(lot)[s]
            own = from_core.at[u, block(mine, part), cols]
            return [
                send(own, own, back_send.at[lot, sem + n], back_recv.at[lot, sem + n], peer)
                for n, peer in enumerate(peers(axis))
            ]

        def done_copy(lot):
            u, cols = lots[lot][0], columns(lot)
            return pltpu.make_async_copy(from_core.at[u, :, cols], result_ref.at[u, :, cols], done_sem.at[lot])

        def add(lot, at, size, terms, target):
            u, cols = lots[lot][0], columns(lot)
            some = min(size, rows // 4)

            def one(n, _):
                total = held[u, block(at + n * some, some), cols].astype(F32)
                for ref, shift in terms:
                    total = total + ref[u, block(at + shift + n * some, some), cols].astype(F32)
                target[u, block(at + n * some, some), cols] = total.astype(BF)
                return 0

            if size == some:
                one(0, 0)
            else:
                lax.fori_loop(0, size // some, one, 0)

        def fire(lot, k):
            links = chain(lot)
            last = len(links)
            if k == 0:
                core_copy(lot).wait_recv()
                if lot < self.copied:
                    pltpu.make_async_copy(from_core.at[lot], held.at[lot], local_sem.at[lot]).wait()
                terms = [(from_core, 0)]
            elif k <= last:
                for _, copy in out_copies(lot, k - 1):
                    copy.wait_recv()
                axis, _, part, mine, inside, _ = links[k - 1]
                terms = [(inbox, inside + n * part - mine) for n in range(ways[axis] - 1)]
            if k < last:
                _, _, part, mine, _, _ = links[k]
                for away, copy in out_copies(lot, k):
                    add(lot, away, part, terms, held)
                    copy.start()
                add(lot, mine, part, terms, held)
                return
            if k == last:
                _, _, part, mine, _, _ = links[k - 1]
                add(lot, mine, part, terms, from_core)
            else:
                for copy in back_copies(lot, 2 * last - k):
                    copy.wait_recv()
            if k < 2 * last:
                for copy in back_copies(lot, 2 * last - 1 - k):
                    copy.start()
            else:
                done_copy(lot).start()

        def begin(u, theirs, mine=None):
            for lot in range(len(lots)):
                if lots[lot][0] == u:
                    core_copy(lot, theirs).start()
            if mine is not None:
                pltpu.make_async_copy(mine, held.at[u], local_sem.at[u]).start()

        small_peers = [
            sibling, peers("x")[0], peers("y")[0],
            {"rep": rep + 4 - 8 * (place["z"] % 2)}, {"rep": rep + 8 - 16 * (place["z"] // 2)},
        ]

        def copy_small(k):
            return send(kept.at[k], came.at[k], small_send.at[k], small_recv.at[k], small_peers[k])

        def small_next(k):
            copy_small(k).wait_recv()
            kept[k + 1] = kept[k] + came[k]
            if k + 1 < SMALL:
                copy_small(k + 1).start()

        def settle():
            for k in range(SMALL):
                copy_small(k).wait_send()
            for lot in range(len(lots)):
                core_copy(lot).wait_send()
                for s in range(len(lots[lot][3])):
                    for _, copy in out_copies(lot, s):
                        copy.wait_send()
                    for copy in back_copies(lot, s):
                        copy.wait_send()
                done_copy(lot).wait()

        self.meet, self.begin, self.fire, self.settle = meet, begin, fire, settle
        self.small_start, self.small_next = (lambda: copy_small(0).start()), small_next

    @staticmethod
    def buffers(lots, units, rows, cols, small):
        dma = pltpu.SemaphoreType.DMA
        count = len(lots)
        return [
            pltpu.VMEM((units, rows, cols), BF),
            pltpu.VMEM((units, rows, cols), BF),
            pltpu.VMEM((units, rows - rows // 16, cols), BF),
            pltpu.VMEM((SMALL + 1,) + small, F32),
            pltpu.VMEM((SMALL,) + small, F32),
            dma((units,)), dma((count,)), dma((count,)),
        ] + [dma((count, 6))] * 4 + [dma((SMALL,))] * 2 + [dma((count,))]


HALVES = 2
TILE_B = 256


def late_back_kernel(linked, seqs, groups, *refs):
    (
        second_ref, pre_ref, norm_ref, inv_ref, ctx_ref, up_ref, out_ref, small_ref,
        tokens_ref, rows_ref, q_ref, k_ref, v_ref, lse_ref, sums_in_ref,
    ), refs = refs[:15], refs[15:]
    step = pl.program_id(0)
    last = pl.num_programs(0) - 1
    first = seqs * HALVES
    if linked:
        feed_mine, feed_theirs, resid_ref, jlow_ref, result_ref, total_ref = refs[:6]
        cback_ref, rowdot_ref, acc, bias_ref, theirs = refs[6:11]
        buffers, sems = refs[11:16], refs[16:]
        early = feed_mine.shape[0]
        exchange = Exchange(LOTS, early, result_ref, *buffers, sems)
        held, kept = buffers[0], buffers[3]
        core = lax.axis_index("shard")
        sums_ref = kept.at[0]
    else:
        resid_ref, jlow_ref, mine_ref, theirs_ref, sums_ref, cback_ref, rowdot_ref, acc, bias_ref = refs

    def pause(start, count, each, n):
        for i in range(count if linked else 0):
            events = EVENTS[start[1] + each * i + n]
            if events:

                @pl.when(step == start[0] + i)
                def _():
                    for lot, k in events:
                        exchange.fire(lot, k)

    pause_norm = functools.partial(pause, (0, 0), first, 2)
    pause_attend = functools.partial(pause, (first, 2 * first), seqs * groups, 2)

    def hand_over(n):
        if linked:
            deal(core, acc, held.at[pl.ds(early + n, 1)], theirs.at[pl.ds(n, 1)])
            for m in range(1 + groups):

                @pl.when(n == m)
                def _():
                    exchange.begin(early + m, theirs.at[m])

        else:
            deal(0, acc, mine_ref.at[pl.ds(n, 1)], theirs_ref.at[pl.ds(n, 1)])

    @pl.when(step == 0)
    def _():
        if linked:
            exchange.meet()
            for u in range(early):
                exchange.begin(u, feed_theirs.at[u], feed_mine.at[u])
        sums_ref[...] = sums_in_ref[...]

    @pl.when(step < first)
    def _():
        pause_norm(0)
        resid, cback, rowdot, part = norm_step(
            second_ref[0], pre_ref[0], norm_ref[0], inv_ref[0], ctx_ref[0], up_ref, out_ref, small_ref, sums_ref,
            pause_norm,
        )
        resid_ref[0] = resid
        size = resid.shape[0]
        s, some = step // HALVES, pl.ds(pl.multiple_of(step % HALVES * size, size), size)
        for n in range(groups):
            cback_ref[s, n, some, :] = cback[:, n * GROUP : (n + 1) * GROUP]
        rowdot_ref[s, :, some] = rowdot

        @pl.when(step == 0)
        def _():
            acc[...] = part

        @pl.when(step > 0)
        def _():
            acc[...] += part

        @pl.when(step == first - 1)
        def _():
            hand_over(step - (first - 1))

    @pl.when(step >= first)
    def _():
        g, s = (step - first) // seqs, (step - first) % seqs
        attend_step(
            g, s, tokens_ref, rows_ref, q_ref, k_ref, v_ref, cback_ref, lse_ref, rowdot_ref,
            jlow_ref, sums_ref, bias_ref, acc, pause_attend,
        )

        @pl.when(s == seqs - 1)
        def _():
            hand_over(1 + g)

    if linked:

        @pl.when(step == last)
        def _():
            exchange.small_start()
            rest = EVENTS[-1]
            share = -(-len(rest) // (SMALL + 1))
            for k in range(SMALL + 1):
                for lot, stage in rest[k * share : (k + 1) * share]:
                    exchange.fire(lot, stage)
                if k < SMALL:
                    exchange.small_next(k)
            total_ref[...] = kept[SMALL]
            exchange.settle()


def attend_step(
    g, s, tokens_ref, rows_ref, q_ref, k_ref, v_ref, cback_ref, lse_ref, rowdot_ref,
    jlow_ref, sums_ref, bias_ref, acc, pause,
):
    length = tokens_ref.shape[1]
    tile = min(TILE_B, length)
    ids = rows_ref[pl.ds(s, 1), :]
    bias_ref[...] = jnp.where(ids.astype(F32) >= column(ids), 0.0, NEG)
    lane = lax.broadcasted_iota(jnp.int32, (length, 128), 1)
    low = lane < HEAD_DIM

    for pair in range(GROUP // 128):
        pause(pair)
        at = slice(pair * 128, pair * 128 + 128)
        q2 = q_ref[0, :, at] * BF(0.125)
        k2 = k_ref[0, :, at]
        v2 = v_ref[0, :, at]
        do2 = cback_ref[s, g, :, at]
        dq = None
        for t in range(length // tile):
            rows = slice(t * tile, (t + 1) * tile)
            dks, dvs = [], []
            for h in range(2):
                mine = low[rows] if h == 0 else ~low[rows]
                km = jnp.where(mine, k2[rows], BF(0))
                vm = jnp.where(mine, v2[rows], BF(0))
                head = g * (GROUP // HEAD_DIM) + pair * 2 + h
                lse = lse_ref[0, pl.ds(head, 1), :]
                rowdot = rowdot_ref[s, pl.ds(head, 1), :]
                probs = jnp.exp(dot_nt(km, q2) + bias_ref[rows, :] - lse)
                dprobs = dot_nt(vm, do2)
                dscore = (probs * (dprobs - rowdot)).astype(BF)
                dvs.append(dot(probs.astype(BF), do2))
                dks.append(dot(dscore, q2))
                part = dot_tn(dscore, km * BF(0.125))
                dq = part if dq is None else dq + part
            dk = jnp.where(low[rows], dks[0], dks[1])
            dv = jnp.where(low[rows], dvs[0], dvs[1])
            jlow_ref[0, rows, GROUP + pair * 128 : GROUP + pair * 128 + 128] = dk.astype(BF)
            jlow_ref[0, rows, 2 * GROUP + pair * 128 : 2 * GROUP + pair * 128 + 128] = dv.astype(BF)
            vsum = jnp.sum(dv, axis=0, keepdims=True)
            vtotal = vsum if t == 0 else vtotal + vsum
        jlow_ref[0, :, at] = dq.astype(BF)
        lanes = pl.ds(pl.multiple_of(g * GROUP + pair * 128, 128), 128)
        sums_ref[0:1, lanes] += jnp.sum(dq, axis=0, keepdims=True)
        sums_ref[1:2, lanes] += vtotal

    part = dot_tn(tokens_ref[0], jlow_ref[0])

    @pl.when(s == 0)
    def _():
        acc[...] = part

    @pl.when(s > 0)
    def _():
        acc[...] += part


def late_back(second, pre_low, norm, inv, ctx, up_bin, out_bin, small, tokens, block_ids, joined, lse, sums, feed_grads=None):
    seqs, length, width = tokens.shape
    groups = width // GROUP
    linked = feed_grads is not None
    first = seqs * HALVES
    phase = lambda i: (i + 64 - first) // 64
    seq_one = lambda i: i + phase(i) * (first - 1 - i)
    seq_two = lambda i: phase(i) * ((i - first + seqs * first) % seqs)
    group_two = lambda i: phase(i) * ((i - first) // seqs)
    some = length // HALVES
    second, pre_low, norm, inv, ctx = (a.reshape(first, some, a.shape[2]) for a in (second, pre_low, norm, inv, ctx))
    one = lambda *shape: pl.BlockSpec((1,) + shape, lambda i: (seq_one(i),) + (0,) * len(shape))
    two = lambda *shape: pl.BlockSpec((1,) + shape, lambda i: (seq_two(i),) + (0,) * len(shape))
    part = lambda k: pl.BlockSpec((1, length, GROUP), lambda i: (seq_two(i), 0, k * groups + group_two(i)))
    held = lambda a: pl.BlockSpec(a.shape, lambda i: (0,) * a.ndim, pipeline_mode=pl.Buffered(1))
    anywhere = pl.BlockSpec(memory_space=pl.ANY)
    unit = (width, width // 2)
    like = jax.ShapeDtypeStruct
    in_specs = [
        one(some, width), one(some, pre_low.shape[2]), one(some, width), one(some, 1), one(some, width),
        held(up_bin), held(out_bin), held(small),
        two(length, width), held(block_ids), part(0), part(1), part(2), two(16, length), held(sums),
    ]
    operands = [
        second, pre_low, norm, inv, ctx, up_bin, out_bin, small,
        tokens, block_ids, joined, joined, joined, lse, sums,
    ]
    out_specs = [one(some, width), pl.BlockSpec((1, length, 3 * GROUP), lambda i: (seq_two(i), 0, group_two(i)))]
    out_shape = [like((first, some, width), BF), like((seqs, length, 3 * width), BF)]
    scratch = [
        pltpu.VMEM((seqs, groups, length, GROUP), BF), pltpu.VMEM((seqs, 16, length), F32),
        pltpu.VMEM((width, width), F32), pltpu.VMEM((length, length), F32),
    ]
    if linked:
        units = feed_grads[0].shape[0] + 1 + groups
        in_specs += [anywhere] * 2
        operands += feed_grads
        out_specs += [anywhere, full(sums.shape)]
        out_shape += [like((units,) + unit, BF), like(sums.shape, F32)]
        scratch += [pltpu.VMEM((1 + groups,) + unit, BF)] + Exchange.buffers(LOTS, units, *unit, sums.shape)
        extra = dict(collective_id=0, has_side_effects=True)
    else:
        out_specs += [full((1 + groups,) + unit)] * 2 + [full(sums.shape)]
        out_shape += [like((1 + groups,) + unit, BF)] * 2 + [like(sums.shape, F32)]
        extra = {}
    return pl.pallas_call(
        functools.partial(late_back_kernel, linked, seqs, groups),
        grid=(seqs * (HALVES + groups),),
        in_specs=in_specs,
        out_specs=out_specs,
        out_shape=out_shape,
        scratch_shapes=scratch,
        compiler_params=params(58, **extra),
        cost_estimate=cost(seqs * length * width * (20 * width + 40 * length), 70 * seqs * length * width),
        name="late_back",
    )(*operands)


def token_total(resid_ref, jlow_ref, qkv_ref):
    width = resid_ref.shape[2]
    groups = width // GROUP
    total = resid_ref[0].astype(F32)
    for g in range(groups):
        for k in range(3):
            at = (3 * g + k) * GROUP
            col = k * width + g * GROUP
            total = total + dot_nt(jlow_ref[0, :, at : at + GROUP], qkv_ref[:, col : col + GROUP])
    return total


def token_kernel(resid_ref, jlow_ref, qkv_ref, grad_ref):
    grad_ref[0] = token_total(resid_ref, jlow_ref, qkv_ref)


def finish_kernel(
    core_ref, resid_ref, jlow_ref, qkv_bin_ref, feed_ref, out_unit_ref, qkv_unit_ref, sums_ref,
    grad_ref, qkv_ref, out_ref, up_ref, dn_ref, small_ref, up_stage, qkv_stage, up_sem, qkv_sem,
):
    step, last = pl.program_id(0), pl.num_programs(0) - 1
    _, rows, half = feed_ref.shape
    groups = qkv_sem.shape[0]
    parts = (slice(0, half), slice(half, rows))

    def up_copy(c, p):
        at = pl.ds(pl.multiple_of((p * (last + 1) + c) * half, half), half)
        return pltpu.make_async_copy(up_stage.at[c, p], up_ref.at[:, at], up_sem.at[c, p])

    def qkv_copy(g, k):
        at = pl.ds(pl.multiple_of(k * rows + g * GROUP, GROUP), GROUP)
        return pltpu.make_async_copy(qkv_stage.at[g, k], qkv_ref.at[:, at], qkv_sem.at[g, k])

    for p in range(2):
        up_stage[step, p] = feed_ref[1, parts[p], :].astype(F32)
        up_copy(step, p).start()
        dn_ref[:, parts[p]] = feed_ref[0, parts[p], :].astype(F32)

    @pl.when(step == 0)
    def _():
        for p in range(2):
            out_ref[:, parts[p]] = out_unit_ref[0, parts[p], :].astype(F32)
        mine = pl.ds(pl.multiple_of(core_ref[0] * half, half), half)
        small_ref[...] = sums_ref[:, mine]

    @pl.when(step > 0)
    def _():
        for j in range(3 * GROUP // 128):
            col = j * 128
            qkv_stage[step - 1, col // GROUP, :, col % GROUP : col % GROUP + 128] = qkv_unit_ref[
                0, parts[col // half], col % half : col % half + 128
            ].astype(F32)
        for k in range(3):
            qkv_copy(step - 1, k).start()

    grad_ref[0] = token_total(resid_ref, jlow_ref, qkv_bin_ref)

    @pl.when(step == last)
    def _():
        for c in range(up_sem.shape[0]):
            for p in range(2):
                up_copy(c, p).wait()
        for g in range(groups):
            for k in range(3):
                qkv_copy(g, k).wait()


def finish(core, resid, jlow, qkv_bin, units, sums):
    seqs, length, width = resid.shape
    count, rows, half = units.shape
    groups = rows // GROUP
    chunks = (count - 1 - groups) // 2
    assert chunks == seqs and groups == seqs - 1
    per_seq = lambda *shape: pl.BlockSpec((1,) + shape, lambda s, _: (s,) + (0,) * len(shape))
    late = lambda s: s - (s + 63) // 64
    like = lambda *shape: jax.ShapeDtypeStruct(shape, F32)
    anywhere = pl.BlockSpec(memory_space=pl.ANY)
    return pl.pallas_call(
        finish_kernel,
        grid_spec=pltpu.PrefetchScalarGridSpec(
            num_scalar_prefetch=1,
            grid=(chunks,),
            in_specs=[
                per_seq(length, width),
                per_seq(length, 3 * width),
                full(qkv_bin.shape),
                pl.BlockSpec((2, rows, half), lambda s, _: (s, 0, 0)),
                pl.BlockSpec((1, rows, half), lambda s, _: (2 * chunks, 0, 0)),
                pl.BlockSpec((1, rows, half), lambda s, _: (2 * chunks + 1 + late(s), 0, 0)),
                full(sums.shape),
            ],
            out_specs=[
                per_seq(length, width),
                anywhere,
                full((half, rows)),
                anywhere,
                pl.BlockSpec((half, rows), lambda s, _: (s, 0)),
                full((sums.shape[0], half)),
            ],
            scratch_shapes=[
                pltpu.VMEM((chunks, 2, half, half), F32),
                pltpu.VMEM((groups, 3, half, GROUP), F32),
                pltpu.SemaphoreType.DMA((chunks, 2)),
                pltpu.SemaphoreType.DMA((groups, 3)),
            ],
        ),
        out_shape=[
            like(seqs, length, width), like(half, 3 * rows), like(half, rows), like(half, 2 * chunks * half),
            like(chunks * half, rows), like(sums.shape[0], half),
        ],
        compiler_params=params(),
        cost_estimate=cost(6 * seqs * length * width * width, 16 * seqs * length * width),
        name="finish",
    )(core, resid, jlow, qkv_bin, units, units, units, sums)


def token_back(resid, jlow, qkv_bin):
    seqs, length, width = resid.shape
    per_seq = lambda *shape: pl.BlockSpec((1,) + shape, lambda s: (s,) + (0,) * len(shape))
    return pl.pallas_call(
        token_kernel,
        grid=(seqs,),
        in_specs=[per_seq(length, width), per_seq(length, 3 * width), full(qkv_bin.shape)],
        out_specs=per_seq(length, width),
        out_shape=jax.ShapeDtypeStruct((seqs, length, width), F32),
        compiler_params=params(),
        cost_estimate=cost(6 * seqs * length * width * width, 16 * seqs * length * width),
        name="token_back",
    )(resid, jlow, qkv_bin)


def swap(value):
    return lax.ppermute(value, "shard", [(0, 1), (1, 0)])


def small_rows(biases, gain, shift, hidden_bias):
    rows = biases.shape[0]
    return jnp.concatenate([biases.T, gain.T, shift.T, hidden_bias.reshape(-1, rows)], axis=0)


def reduce_plain(feed_grads, out_grads, qkv_grads, sums):
    def whole(mine, theirs):
        count, rows, half = mine.shape
        cut = lambda a: a.reshape(count, 2, half, half).transpose(0, 2, 1, 3).reshape(count, half, rows)
        return jnp.concatenate([cut(mine), cut(theirs)], axis=1)

    feed_all, out_all, qkv_all = whole(*feed_grads), whole(*out_grads), whole(*qkv_grads)
    chunks, groups, width = feed_all.shape[0] // 2, qkv_all.shape[0], feed_all.shape[2]
    half, units = width // 2, chunks * width
    grads = (
        qkv_all.reshape(groups, width, 3, GROUP).transpose(1, 2, 0, 3).reshape(width, 3 * width),
        out_all[0],
        feed_all[1::2].reshape(chunks, width, 2, half).transpose(1, 2, 0, 3).reshape(width, units),
        feed_all[0::2].reshape(chunks, 2, half, width).transpose(1, 0, 2, 3).reshape(units, width),
        sums[0:4].T.astype(BF),
        sums[8:].reshape(chunks, 2, half).transpose(1, 0, 2).reshape(-1).astype(BF),
        sums[4:6].T.astype(BF),
        sums[6:8].T.astype(BF),
    )
    owned = lax.psum_scatter(grads, "shard", scatter_dimension=0, tiled=True)
    return jax.tree.map(lambda part: part.astype(F32), lax.psum(owned, "rep"))


def body(tokens, teacher, block_ids, *weights):
    qkv, out, up, down, biases, hidden_bias, gain, shift = weights
    paired = lax.axis_size("shard") == 2 and lax.axis_size("rep") == 16
    if paired:
        core = lax.axis_index("shard").reshape(1)
        small = small_rows(biases, gain, shift, hidden_bias)
        small, qkv, out = ((a, swap(a)) for a in (small, qkv, out))
        up, down, _, _ = lax.optimization_barrier((up, down, qkv[1], small[1]))
        up, down = ((a, swap(a)) for a in (up, down))
    else:
        core = jnp.zeros((1,), jnp.int32)
        gathered = [lax.all_gather(w, "shard", axis=0, tiled=True) for w in weights]
        qkv, out, up, down, *rest = (jnp.split(w, 2, axis=0) for w in gathered)
        small = [small_rows(rest[0][i], rest[2][i], rest[3][i], rest[1][i]) for i in range(2)]
    joined, ctx, lse, norm, inv, small, qkv_bin, out_bin = attend(core, tokens, block_ids, qkv, out, small)
    final, first_low, hidden, slope, second, mixed, sums, up_bin, dn_bin = feed(core, norm, teacher, small, up, down)
    pre_low, *feed_grads, sums = feed_back(core, mixed, first_low, hidden, slope, dn_bin, sums)
    pre_low = pre_low.reshape(hidden.shape)
    operands = (second, pre_low, norm, inv, ctx, up_bin, out_bin, small, tokens, block_ids, joined, lse, sums)
    if not paired:
        resid, jlow, *grads, sums = late_back(*operands)
        token_grad = token_back(resid.reshape(tokens.shape), jlow, qkv_bin)
        out_grads, qkv_grads = ([a[cut] for a in grads] for cut in (slice(0, 1), slice(1, None)))
        return (final, token_grad) + tuple(reduce_plain(feed_grads, out_grads, qkv_grads, sums[:12]))
    resid, jlow, units, sums = late_back(*operands, feed_grads)
    resid = resid.reshape(tokens.shape)
    token_grad, qkv_grad, out_grad, up_grad, dn_grad, small = finish(core, resid, jlow, qkv_bin, units, sums)
    hidden_rows = hidden_bias.shape[0] // small.shape[1]
    return (
        final, token_grad, qkv_grad, out_grad, up_grad, dn_grad,
        small[0:4].T, small[8 : 8 + hidden_rows].reshape(-1), small[4:6].T, small[6:8].T,
    )


def solution(mesh):
    placed = (
        P(("shard", "rep"), None, None),
        P(("shard", "rep"), None, None),
        P(("shard", "rep"), None),
        P("shard", None),
        P("shard", None),
        P("shard", None),
        P("shard", None),
        P("shard", None),
        P("shard"),
        P("shard", None),
        P("shard", None),
    )
    return jax.shard_map(
        body,
        mesh=mesh,
        in_specs=placed,
        out_specs=placed[:2] + placed[3:],
        check_vma=False,
    )
```

```python
import functools

import jax
import jax.numpy as jnp
from jax import lax
from jax.experimental import pallas as pl
from jax.experimental.pallas import tpu as pltpu
from jax.sharding import PartitionSpec as P

HEAD_DIM = 64
GROUP = 256
EPS = 1e-05
NEG = -1e30
BF = jnp.bfloat16
F32 = jnp.float32
MB = 1 << 20


def params(mb=56, **kw):
    return pltpu.CompilerParams(vmem_limit_bytes=mb * MB, **kw)


def dot(a, b):
    return jnp.dot(a, b, preferred_element_type=F32)


def dot_nt(a, b):
    return lax.dot_general(a, b, (((1,), (1,)), ((), ())), preferred_element_type=F32)


def dot_tn(a, b):
    return lax.dot_general(a, b, (((0,), (0,)), ((), ())), preferred_element_type=F32)


def full(shape):
    return pl.BlockSpec(shape, lambda *_: (0,) * len(shape))


def cost(flops, nbytes, trans=0):
    return pl.CostEstimate(flops=int(flops), bytes_accessed=int(nbytes), transcendentals=int(trans))


def column(row):
    return jnp.broadcast_to(row.astype(F32), (8, row.shape[1])).T[:, 0:1]


def deal(core, acc, mine_ref, theirs_ref, at=0):
    half = acc.shape[0] // 2
    wide = acc.shape[1] // 2
    for ref, who in ((mine_ref, core), (theirs_ref, 1 - core)):
        rows = pl.ds(pl.multiple_of(who * half, half), half)
        ref[at, 0:half, :] = acc[rows, 0:wide].astype(BF)
        ref[at, half : 2 * half, :] = acc[rows, wide : 2 * wide].astype(BF)


def binary_halves(first, second):
    rows = 2 * first.shape[0]
    total = jnp.sum(jnp.abs(first.astype(F32)), axis=0, keepdims=True) + jnp.sum(
        jnp.abs(second.astype(F32)), axis=0, keepdims=True
    )
    scale = (total / rows).astype(BF)
    return (
        jnp.where(first >= 0, scale, -scale).astype(BF),
        jnp.where(second >= 0, scale, -scale).astype(BF),
    )


def binary_rows(core, own_ref, other_ref, out_ref):
    half, cols = own_ref.shape
    own_at = pl.ds(pl.multiple_of(core * half, half), half)
    other_at = pl.ds(pl.multiple_of((1 - core) * half, half), half)
    for j in range(0, cols, GROUP):
        at = slice(j, j + GROUP)
        out_ref[own_at, at], out_ref[other_at, at] = binary_halves(own_ref[:, at], other_ref[:, at])


def binary_up(core, own_ref, other_ref, out_ref):
    half, cols = own_ref.shape
    chunks = cols // (2 * half)
    own_at = pl.ds(pl.multiple_of(core * half, half), half)
    other_at = pl.ds(pl.multiple_of((1 - core) * half, half), half)

    def one(j, _):
        at = pl.ds(pl.multiple_of(j * half, half), half)
        to = pl.ds(pl.multiple_of((j % chunks) * 2 * half + (j // chunks) * half, half), half)
        out_ref[own_at, to], out_ref[other_at, to] = binary_halves(own_ref[:, at], other_ref[:, at])
        return 0

    lax.fori_loop(0, 2 * chunks, one, 0)


def binary_down(core, own_ref, other_ref, out_ref):
    rows, cols = own_ref.shape
    half = cols // 2

    def one(j, _):
        at = pl.ds(pl.multiple_of(j * GROUP, GROUP), GROUP)
        own, other = binary_halves(own_ref[:, at], other_ref[:, at])
        for c in range(rows // half):
            part = slice(c * half, (c + 1) * half)
            out_ref[pl.ds(pl.multiple_of((2 * c + core) * half, half), half), at] = own[part]
            out_ref[pl.ds(pl.multiple_of((2 * c + 1 - core) * half, half), half), at] = other[part]
        return 0

    lax.fori_loop(0, cols // GROUP, one, 0)


def attend_kernel(
    core_ref, tokens_ref, rows_ref, qkv_own, qkv_other, out_own, out_other, small_own, small_other,
    joined_ref, ctx_ref, lse_ref, norm_ref, inv_ref, small_ref, qkv_any, out_any,
    bias_ref, qkv_ref, out_ref, sems,
):
    length, width = tokens_ref.shape[1:]
    keep = (
        pltpu.make_async_copy(qkv_ref, qkv_any, sems.at[0]),
        pltpu.make_async_copy(out_ref, out_any, sems.at[1]),
    )

    @pl.when(pl.program_id(0) == 0)
    def _():
        core, half = core_ref[0], width // 2
        binary_rows(core, qkv_own, qkv_other, qkv_ref)
        binary_rows(core, out_own, out_other, out_ref)
        small_ref[:, pl.ds(pl.multiple_of(core * half, half), half)] = small_own[...].astype(F32)
        small_ref[:, pl.ds(pl.multiple_of((1 - core) * half, half), half)] = small_other[...].astype(F32)
        for copy in keep:
            copy.start()

    x = tokens_ref[0]
    for part, bias_row in ((0, 0), (1, None), (2, 1)):
        joined = dot(x, qkv_ref[:, part * width : (part + 1) * width])
        if bias_row is not None:
            joined = joined + small_ref[bias_row : bias_row + 1, :]
        joined_ref[0, :, part * width : (part + 1) * width] = joined.astype(BF)
    ids = rows_ref[pl.ds(pl.program_id(0), 1), :]
    bias_ref[...] = jnp.where(column(ids) >= ids.astype(F32), 0.0, NEG)
    lane = lax.broadcasted_iota(jnp.int32, (length, 128), 1)
    low = lane < HEAD_DIM
    lse_all = jnp.zeros((length, 128), F32)
    tile = min(TILE_F, length)
    for pair in range(width // 128):
        q2 = joined_ref[0, :, pair * 128 : pair * 128 + 128] * BF(0.125)
        k2 = joined_ref[0, :, width + pair * 128 : width + pair * 128 + 128]
        v2 = joined_ref[0, :, 2 * width + pair * 128 : 2 * width + pair * 128 + 128]
        for t in range(length // tile):
            rows = slice(t * tile, (t + 1) * tile)
            parts = []
            for h in range(2):
                mine = low[rows] if h == 0 else ~low[rows]
                qm = jnp.where(mine, q2[rows], BF(0))
                scores = dot_nt(qm, k2) + bias_ref[rows, :]
                peak = jnp.max(scores, axis=-1, keepdims=True)
                raised = jnp.exp(scores - peak)
                total = jnp.sum(raised, axis=-1, keepdims=True)
                parts.append(dot(raised.astype(BF), v2) / total)
                lse_ref_col = peak + jnp.log(total)
                bias_lane = lane[rows] == 2 * pair + h
                lse_cols = jnp.where(bias_lane, lse_ref_col, 0.0)
                if h == 0:
                    pair_lse = lse_cols
                else:
                    pair_lse = pair_lse + lse_cols
            ctx_ref[0, rows, pair * 128 : pair * 128 + 128] = jnp.where(low[rows], parts[0], parts[1]).astype(BF)
            if t == 0:
                tiles_lse = [pair_lse]
            else:
                tiles_lse.append(pair_lse)
        lse_all = lse_all + jnp.concatenate(tiles_lse, axis=0)
    lse_ref[0] = lse_all.T[0:16, :]
    resid = x.astype(F32) + dot(ctx_ref[0], out_ref[...]) + small_ref[2:3, :]
    center = resid - jnp.mean(resid, axis=-1, keepdims=True)
    inverse = lax.rsqrt(jnp.mean(center * center, axis=-1, keepdims=True) + EPS)
    norm_ref[0] = center * inverse
    inv_ref[0] = inverse

    @pl.when(pl.program_id(0) == pl.num_programs(0) - 1)
    def _():
        for copy in keep:
            copy.wait()


TILE_F = 512


def attend(core, tokens, block_ids, qkv, out, small):
    seqs, length, width = tokens.shape
    per_seq = lambda *shape: pl.BlockSpec((1,) + shape, lambda s, _: (s,) + (0,) * len(shape))
    once = lambda a: pl.BlockSpec(a.shape, lambda s, _: (0,) * a.ndim, pipeline_mode=pl.Buffered(1))
    anywhere = pl.BlockSpec(memory_space=pl.ANY)
    like = jax.ShapeDtypeStruct
    joined_width = qkv[0].shape[1]
    whole = (small[0].shape[0], width)
    return pl.pallas_call(
        attend_kernel,
        grid_spec=pltpu.PrefetchScalarGridSpec(
            num_scalar_prefetch=1,
            grid=(seqs,),
            in_specs=[per_seq(length, width)] + [once(a) for a in (block_ids, *qkv, *out, *small)],
            out_specs=[
                per_seq(length, joined_width),
                per_seq(length, width),
                per_seq(16, length),
                per_seq(length, width),
                per_seq(length, 1),
                full(whole),
                anywhere,
                anywhere,
            ],
            scratch_shapes=[
                pltpu.VMEM((length, length), F32),
                pltpu.VMEM((width, joined_width), BF),
                pltpu.VMEM((width, width), BF),
                pltpu.SemaphoreType.DMA((2,)),
            ],
        ),
        out_shape=[
            like((seqs, length, joined_width), BF),
            like((seqs, length, width), BF),
            like((seqs, 16, length), F32),
            like((seqs, length, width), F32),
            like((seqs, length, 1), F32),
            like(whole, F32),
            like((width, joined_width), BF),
            like((width, width), BF),
        ],
        compiler_params=params(),
        cost_estimate=cost(seqs * length * width * (8 * width + 16 * length), 30 * seqs * length * width),
        name="attend",
    )(core, tokens, block_ids, *qkv, *out, *small)


def gelu_pair(u):
    cdf = 0.5 + 0.5 * lax.erf(u * 0.7071067811865476)
    density = jnp.exp(-0.5 * u * u) * 0.3989422804014327
    return u * cdf, cdf + u * density


def norm_back(upstream, normed, inverse, gain):
    scaled = upstream * gain
    weighted = upstream * normed
    centered = (
        scaled
        - jnp.mean(scaled, axis=-1, keepdims=True)
        - normed * jnp.mean(weighted * gain, axis=-1, keepdims=True)
    )
    return centered * inverse, jnp.sum(weighted, axis=0, keepdims=True), jnp.sum(upstream, axis=0, keepdims=True)


def feed_kernel(
    core_ref, norm_ref, teacher_ref, small_ref, up_own, up_other, dn_own, dn_other,
    final_ref, first_low_ref, hidden_ref, slope_ref, second_ref, mixed_ref, sums_ref, up_any, dn_any,
    up_ref, dn_ref, sems,
):
    width = norm_ref.shape[2]
    keep = (
        pltpu.make_async_copy(up_ref, up_any, sems.at[0]),
        pltpu.make_async_copy(dn_ref, dn_any, sems.at[1]),
    )

    @pl.when(pl.program_id(0) == 0)
    def _():
        binary_up(core_ref[0], up_own, up_other, up_ref)
        binary_down(core_ref[0], dn_own, dn_other, dn_ref)
        for copy in keep:
            copy.start()

    first = norm_ref[0] * small_ref[4:5, :] + small_ref[6:7, :]
    first_low = first.astype(BF)
    first_low_ref[0] = first_low
    acc = first + small_ref[3:4, :]
    for c in range(up_ref.shape[1] // width):
        cols = slice(c * width, (c + 1) * width)
        pre = dot(first_low, up_ref[:, cols]) + small_ref[8 + c : 9 + c, :]
        value, slope = gelu_pair(pre)
        value = value.astype(BF)
        hidden_ref[0, :, cols] = value
        slope_ref[0, :, cols] = slope.astype(BF)
        acc = acc + dot(value, dn_ref[cols, :])
    center = acc - jnp.mean(acc, axis=-1, keepdims=True)
    inverse = lax.rsqrt(jnp.mean(center * center, axis=-1, keepdims=True) + EPS)
    normed = center * inverse
    gain = small_ref[5:6, :]
    final = normed * gain + small_ref[7:8, :]
    final_ref[0] = final.astype(BF)
    upstream = final - teacher_ref[0].astype(F32)
    second, gain_sum, shift_sum = norm_back(upstream, normed, inverse, gain)
    second_ref[0] = second
    mixed_ref[0] = second.astype(BF)

    @pl.when(pl.program_id(0) == 0)
    def _():
        sums_ref[...] = jnp.zeros_like(sums_ref)

    sums_ref[3:4, :] += jnp.sum(second, axis=0, keepdims=True)
    sums_ref[5:6, :] += gain_sum
    sums_ref[7:8, :] += shift_sum

    @pl.when(pl.program_id(0) == pl.num_programs(0) - 1)
    def _():
        for copy in keep:
            copy.wait()


def feed(core, norm, teacher, small, up, dn):
    seqs, length, width = norm.shape
    hidden = up[0].shape[1]
    per_seq = lambda *shape: pl.BlockSpec((1,) + shape, lambda s, _: (s,) + (0,) * len(shape))
    once = lambda a: pl.BlockSpec(a.shape, lambda s, _: (0,) * a.ndim, pipeline_mode=pl.Buffered(1))
    anywhere = pl.BlockSpec(memory_space=pl.ANY)
    like = jax.ShapeDtypeStruct
    row = lambda n, dt: like((seqs, length, n), dt)
    return pl.pallas_call(
        feed_kernel,
        grid_spec=pltpu.PrefetchScalarGridSpec(
            num_scalar_prefetch=1,
            grid=(seqs,),
            in_specs=[per_seq(length, width), per_seq(length, width)] + [once(a) for a in (small, *up, *dn)],
            out_specs=[
                per_seq(length, width),
                per_seq(length, width),
                per_seq(length, hidden),
                per_seq(length, hidden),
                per_seq(length, width),
                per_seq(length, width),
                full((16, width)),
                anywhere,
                anywhere,
            ],
            scratch_shapes=[
                pltpu.VMEM((width, hidden), BF),
                pltpu.VMEM((hidden, width), BF),
                pltpu.SemaphoreType.DMA((2,)),
            ],
        ),
        out_shape=[
            row(width, BF), row(width, BF), row(hidden, BF), row(hidden, BF), row(width, F32), row(width, BF),
            like((16, width), F32), like((width, hidden), BF), like((hidden, width), BF),
        ],
        compiler_params=params(60),
        cost_estimate=cost(4 * seqs * length * width * hidden, 36 * seqs * length * width),
        name="feed",
    )(core, norm, teacher, small, *up, *dn)


def feed_back_kernel(
    core_ref, mixed_ref, first_ref, hidden_ref, slope_ref, dn_ref, sums_in_ref,
    pre_ref, mine_ref, theirs_ref, sums_ref, acc,
):
    chunk = pl.program_id(0)

    @pl.when(chunk == 0)
    def _():
        sums_ref[...] = sums_in_ref[...]

    mixed = mixed_ref[0]
    pre_back = dot_nt(mixed, dn_ref[...]) * slope_ref[0].astype(F32)
    pre_low = pre_back.astype(BF)
    pre_ref[0] = pre_low
    acc[...] = dot_tn(hidden_ref[0], mixed)
    deal(core_ref[0], acc, mine_ref, theirs_ref, 0)
    acc[...] = dot_tn(first_ref[0], pre_low)
    deal(core_ref[0], acc, mine_ref, theirs_ref, 1)
    sums_ref[pl.ds(8 + chunk, 1), :] += jnp.sum(pre_back, axis=0, keepdims=True)


def feed_back(core, mixed, first_low, hidden, slope, dn_bin, sums):
    mixed, first_low, hidden, slope = (a.reshape(1, -1, a.shape[2]) for a in (mixed, first_low, hidden, slope))
    seqs, length, width = mixed.shape
    units = hidden.shape[2]
    chunks = units // width
    return pl.pallas_call(
        feed_back_kernel,
        grid_spec=pltpu.PrefetchScalarGridSpec(
            num_scalar_prefetch=1,
            grid=(chunks,),
            in_specs=[
                pl.BlockSpec((1, length, width), lambda c, _: (0, 0, 0)),
                pl.BlockSpec((1, length, width), lambda c, _: (0, 0, 0)),
                pl.BlockSpec((1, length, width), lambda c, _: (0, 0, c)),
                pl.BlockSpec((1, length, width), lambda c, _: (0, 0, c)),
                pl.BlockSpec((width, width), lambda c, _: (c, 0)),
                full(sums.shape),
            ],
            out_specs=[
                pl.BlockSpec((1, length, width), lambda c, _: (0, 0, c)),
                pl.BlockSpec((2, width, width // 2), lambda c, _: (c, 0, 0)),
                pl.BlockSpec((2, width, width // 2), lambda c, _: (c, 0, 0)),
                full(sums.shape),
            ],
            scratch_shapes=[pltpu.VMEM((width, width), F32)],
        ),
        out_shape=[
            jax.ShapeDtypeStruct((seqs, length, units), BF),
            jax.ShapeDtypeStruct((2 * chunks, width, width // 2), BF),
            jax.ShapeDtypeStruct((2 * chunks, width, width // 2), BF),
            jax.ShapeDtypeStruct(sums.shape, F32),
        ],
        compiler_params=params(),
        cost_estimate=cost(6 * seqs * length * width * units, 20 * seqs * length * units),
        name="feed_back",
    )(core, mixed, first_low, hidden, slope, dn_bin, sums)


def norm_step(second, pre_low, norm, inv, ctx, up_ref, out_ref, small_ref, sums_ref, pause):
    width = second.shape[1]
    back = second + dot_nt(pre_low, up_ref[...])
    pause(1)
    resid, gain_sum, shift_sum = norm_back(back, norm, inv, small_ref[4:5, :])
    sums_ref[2:3, :] += jnp.sum(resid, axis=0, keepdims=True)
    sums_ref[4:5, :] += gain_sum
    sums_ref[6:7, :] += shift_sum
    low = resid.astype(BF)
    cback = dot_nt(low, out_ref[...]).astype(BF)
    prod = cback.astype(F32) * ctx.astype(F32)
    high = prod.astype(BF)
    rest = (prod - high.astype(F32)).astype(BF)
    heads = lax.broadcasted_iota(jnp.int32, (16, width), 0)
    lanes = lax.broadcasted_iota(jnp.int32, (16, width), 1)
    pick = jnp.where((lanes >= heads * HEAD_DIM) & (lanes < heads * HEAD_DIM + HEAD_DIM), 1.0, 0.0).astype(BF)
    return low, cback, dot_nt(pick, high) + dot_nt(pick, rest), dot_tn(ctx, low)


MESH = pl.DeviceIdType.MESH

SMALL = 5

LOTS = (
    (0, 0, 384, "xyz"),
    (1, 0, 384, "yxz"),
    (2, 0, 384, "yxz"),
    (3, 0, 384, "yxz"),
    (4, 0, 384, "yxz"),
    (5, 0, 384, "xyz"),
    (6, 0, 384, "zxy"),
    (7, 0, 384, "yxz"),
    (8, 0, 384, "xyz"),
    (9, 0, 384, "xyz"),
    (10, 0, 384, "xyz"),
    (11, 0, 128, "zxy"),
    (11, 128, 128, "yxz"),
    (11, 256, 128, "yxz"),
)
EVENTS = (
    (),
    ((0, 0), (1, 0), (2, 0), (3, 0),),
    ((4, 0), (5, 0),),
    ((6, 0), (7, 0),),
    ((0, 1), (1, 1),),
    (),
    (),
    ((5, 1),),
    ((2, 1),),
    ((1, 2),),
    (),
    ((2, 2), (3, 1), (6, 1),),
    ((1, 3),),
    (),
    ((2, 3), (3, 2), (4, 1),),
    ((1, 4), (6, 2),),
    (),
    ((2, 4), (4, 2), (7, 1),),
    ((1, 5), (3, 3), (0, 2), (8, 0),),
    (),
    ((2, 5), (4, 3), (6, 3), (5, 2),),
    ((3, 4), (7, 2),),
    ((0, 3),),
    ((1, 6),),
    ((4, 4), (8, 1),),
    ((3, 5), (5, 3),),
    ((2, 6), (6, 4), (9, 0), (4, 5), (7, 3),),
    ((8, 2),),
    ((6, 5), (0, 4),),
    ((5, 4),),
    ((3, 6),),
    ((7, 4), (9, 1),),
    ((8, 3),),
    ((4, 6),),
    ((0, 5), (7, 5), (10, 0),),
    (),
    ((5, 5),),
    ((9, 2),),
    ((0, 6), (6, 6),),
    ((8, 4),),
    ((7, 6), (9, 3), (10, 1), (11, 0), (12, 0), (13, 0), (8, 5), (9, 4), (10, 2), (5, 6), (12, 1), (11, 1), (13, 1), (10, 3), (9, 5), (8, 6), (12, 2), (11, 2), (13, 2), (11, 3), (10, 4), (12, 3), (11, 4), (13, 3), (12, 4), (9, 6), (13, 4), (10, 5), (11, 5), (12, 5), (13, 5), (12, 6), (11, 6), (13, 6), (10, 6),),
)


class Exchange:
    def __init__(self, lots, copied, result_ref, held, from_core, inbox, kept, came, sems):
        (
            local_sem, core_send, core_recv, out_send, out_recv, back_send, back_recv, small_send, small_recv, done_sem
        ) = sems
        self.copied = copied
        core, rep = lax.axis_index("shard"), lax.axis_index("rep")
        place = {"x": rep % 2, "y": (rep // 2) % 2, "z": rep // 4, "p": rep % 4}
        ways = {"x": 2, "y": 2, "z": 4, "p": 4}
        sibling = {"shard": 1 - core}
        rows = held.shape[1]
        step_rows = rows // 16

        def peers(axis):
            if axis == "p":
                return [{"rep": rep - place["p"] + (place["p"] + d) % 4} for d in (1, 2, 3)]
            if axis == "z":
                return [{"rep": rep % 4 + 4 * ((place["z"] + d) % 4)} for d in (1, 2, 3)]
            stride = {"x": 1, "y": 2}[axis]
            return [{"rep": rep + stride - 2 * stride * place[axis]}]

        def meet():
            barrier = pltpu.get_barrier_semaphore()
            everyone = [sibling] + peers("p") + peers("z")
            for peer in everyone:
                pl.semaphore_signal(barrier, inc=1, device_id=peer, device_id_type=MESH)
            pl.semaphore_wait(barrier, len(everyone))

        def send(src, dst, send_sem, recv_sem, peer):
            return pltpu.make_async_remote_copy(
                src_ref=src, dst_ref=dst, send_sem=send_sem, recv_sem=recv_sem, device_id=peer, device_id_type=MESH
            )

        def block(at, size):
            return pl.ds(at if isinstance(at, int) else pl.multiple_of(at, step_rows), size)

        def columns(lot):
            return pl.ds(lots[lot][1], lots[lot][2])

        def chain(lot):
            base, size, inside, sem, out = 0, rows, 0, 0, []
            for axis in lots[lot][3]:
                part = size // ways[axis]
                mine = base + place[axis] * part
                out.append((axis, base, part, mine, inside, sem))
                base, size, inside, sem = mine, part, inside + size - part, sem + ways[axis] - 1
            return out

        def core_copy(lot, theirs=None):
            u, cols = lots[lot][0], columns(lot)
            here = from_core.at[u, :, cols]
            return send(here if theirs is None else theirs.at[:, cols], here, core_send.at[lot], core_recv.at[lot], sibling)

        def out_copies(lot, s):
            u, cols = lots[lot][0], columns(lot)
            axis, base, part, _, inside, sem = chain(lot)[s]
            copies = []
            for n, peer in enumerate(peers(axis)):
                away = base + ((place[axis] + n + 1) % ways[axis]) * part
                copy = send(
                    held.at[u, block(away, part), cols], inbox.at[u, block(inside + n * part, part), cols],
                    out_send.at[lot, sem + n], out_recv.at[lot, sem + n], peer,
                )
                copies.append((away, copy))
            return copies

        def back_copies(lot, s):
            u, cols = lots[lot][0], columns(lot)
            axis, _, part, mine, _, sem = chain(lot)[s]
            own = from_core.at[u, block(mine, part), cols]
            return [
                send(own, own, back_send.at[lot, sem + n], back_recv.at[lot, sem + n], peer)
                for n, peer in enumerate(peers(axis))
            ]

        def done_copy(lot):
            u, cols = lots[lot][0], columns(lot)
            return pltpu.make_async_copy(from_core.at[u, :, cols], result_ref.at[u, :, cols], done_sem.at[lot])

        def add(lot, at, size, terms, target):
            u, cols = lots[lot][0], columns(lot)
            some = min(size, rows // 4)

            def one(n, _):
                total = held[u, block(at + n * some, some), cols].astype(F32)
                for ref, shift in terms:
                    total = total + ref[u, block(at + shift + n * some, some), cols].astype(F32)
                target[u, block(at + n * some, some), cols] = total.astype(BF)
                return 0

            if size == some:
                one(0, 0)
            else:
                lax.fori_loop(0, size // some, one, 0)

        def fire(lot, k):
            links = chain(lot)
            last = len(links)
            if k == 0:
                core_copy(lot).wait_recv()
                if lot < self.copied:
                    pltpu.make_async_copy(from_core.at[lot], held.at[lot], local_sem.at[lot]).wait()
                terms = [(from_core, 0)]
            elif k <= last:
                for _, copy in out_copies(lot, k - 1):
                    copy.wait_recv()
                axis, _, part, mine, inside, _ = links[k - 1]
                terms = [(inbox, inside + n * part - mine) for n in range(ways[axis] - 1)]
            if k < last:
                _, _, part, mine, _, _ = links[k]
                for away, copy in out_copies(lot, k):
                    add(lot, away, part, terms, held)
                    copy.start()
                add(lot, mine, part, terms, held)
                return
            if k == last:
                _, _, part, mine, _, _ = links[k - 1]
                add(lot, mine, part, terms, from_core)
            else:
                for copy in back_copies(lot, 2 * last - k):
                    copy.wait_recv()
            if k < 2 * last:
                for copy in back_copies(lot, 2 * last - 1 - k):
                    copy.start()
            else:
                done_copy(lot).start()

        def begin(u, theirs, mine=None):
            for lot in range(len(lots)):
                if lots[lot][0] == u:
                    core_copy(lot, theirs).start()
            if mine is not None:
                pltpu.make_async_copy(mine, held.at[u], local_sem.at[u]).start()

        small_peers = [
            sibling, peers("x")[0], peers("y")[0],
            {"rep": rep + 4 - 8 * (place["z"] % 2)}, {"rep": rep + 8 - 16 * (place["z"] // 2)},
        ]

        def copy_small(k):
            return send(kept.at[k], came.at[k], small_send.at[k], small_recv.at[k], small_peers[k])

        def small_next(k):
            copy_small(k).wait_recv()
            kept[k + 1] = kept[k] + came[k]
            if k + 1 < SMALL:
                copy_small(k + 1).start()

        def settle():
            for k in range(SMALL):
                copy_small(k).wait_send()
            for lot in range(len(lots)):
                core_copy(lot).wait_send()
                for s in range(len(lots[lot][3])):
                    for _, copy in out_copies(lot, s):
                        copy.wait_send()
                    for copy in back_copies(lot, s):
                        copy.wait_send()
                done_copy(lot).wait()

        self.meet, self.begin, self.fire, self.settle = meet, begin, fire, settle
        self.small_start, self.small_next = (lambda: copy_small(0).start()), small_next

    @staticmethod
    def buffers(lots, units, rows, cols, small):
        dma = pltpu.SemaphoreType.DMA
        count = len(lots)
        return [
            pltpu.VMEM((units, rows, cols), BF),
            pltpu.VMEM((units, rows, cols), BF),
            pltpu.VMEM((units, rows - rows // 16, cols), BF),
            pltpu.VMEM((SMALL + 1,) + small, F32),
            pltpu.VMEM((SMALL,) + small, F32),
            dma((units,)), dma((count,)), dma((count,)),
        ] + [dma((count, 6))] * 4 + [dma((SMALL,))] * 2 + [dma((count,))]


HALVES = 2
TILE_B = 256


def late_back_kernel(linked, seqs, groups, *refs):
    (
        second_ref, pre_ref, norm_ref, inv_ref, ctx_ref, up_ref, out_ref, small_ref,
        tokens_ref, rows_ref, q_ref, k_ref, v_ref, lse_ref, sums_in_ref,
    ), refs = refs[:15], refs[15:]
    step = pl.program_id(0)
    last = pl.num_programs(0) - 1
    first = seqs * HALVES
    if linked:
        feed_mine, feed_theirs, resid_ref, jlow_ref, result_ref, total_ref = refs[:6]
        cback_ref, rowdot_ref, acc, bias_ref, theirs = refs[6:11]
        buffers, sems = refs[11:16], refs[16:]
        early = feed_mine.shape[0]
        exchange = Exchange(LOTS, early, result_ref, *buffers, sems)
        held, kept = buffers[0], buffers[3]
        core = lax.axis_index("shard")
        sums_ref = kept.at[0]
    else:
        resid_ref, jlow_ref, mine_ref, theirs_ref, sums_ref, cback_ref, rowdot_ref, acc, bias_ref = refs

    def pause(start, count, each, n):
        for i in range(count if linked else 0):
            events = EVENTS[start[1] + each * i + n]
            if events:

                @pl.when(step == start[0] + i)
                def _():
                    for lot, k in events:
                        exchange.fire(lot, k)

    pause_norm = functools.partial(pause, (0, 0), first, 2)
    pause_attend = functools.partial(pause, (first, 2 * first), seqs * groups, 2)

    def hand_over(n):
        if linked:
            deal(core, acc, held.at[pl.ds(early + n, 1)], theirs.at[pl.ds(n, 1)])
            for m in range(1 + groups):

                @pl.when(n == m)
                def _():
                    exchange.begin(early + m, theirs.at[m])

        else:
            deal(0, acc, mine_ref.at[pl.ds(n, 1)], theirs_ref.at[pl.ds(n, 1)])

    @pl.when(step == 0)
    def _():
        if linked:
            exchange.meet()
            for u in range(early):
                exchange.begin(u, feed_theirs.at[u], feed_mine.at[u])
        sums_ref[...] = sums_in_ref[...]

    @pl.when(step < first)
    def _():
        pause_norm(0)
        resid, cback, rowdot, part = norm_step(
            second_ref[0], pre_ref[0], norm_ref[0], inv_ref[0], ctx_ref[0], up_ref, out_ref, small_ref, sums_ref,
            pause_norm,
        )
        resid_ref[0] = resid
        size = resid.shape[0]
        s, some = step // HALVES, pl.ds(pl.multiple_of(step % HALVES * size, size), size)
        for n in range(groups):
            cback_ref[s, n, some, :] = cback[:, n * GROUP : (n + 1) * GROUP]
        rowdot_ref[s, :, some] = rowdot

        @pl.when(step == 0)
        def _():
            acc[...] = part

        @pl.when(step > 0)
        def _():
            acc[...] += part

        @pl.when(step == first - 1)
        def _():
            hand_over(step - (first - 1))

    @pl.when(step >= first)
    def _():
        g, s = (step - first) // seqs, (step - first) % seqs
        attend_step(
            g, s, tokens_ref, rows_ref, q_ref, k_ref, v_ref, cback_ref, lse_ref, rowdot_ref,
            jlow_ref, sums_ref, bias_ref, acc, pause_attend,
        )

        @pl.when(s == seqs - 1)
        def _():
            hand_over(1 + g)

    if linked:

        @pl.when(step == last)
        def _():
            exchange.small_start()
            rest = EVENTS[-1]
            share = -(-len(rest) // (SMALL + 1))
            for k in range(SMALL + 1):
                for lot, stage in rest[k * share : (k + 1) * share]:
                    exchange.fire(lot, stage)
                if k < SMALL:
                    exchange.small_next(k)
            total_ref[...] = kept[SMALL]
            exchange.settle()


def attend_step(
    g, s, tokens_ref, rows_ref, q_ref, k_ref, v_ref, cback_ref, lse_ref, rowdot_ref,
    jlow_ref, sums_ref, bias_ref, acc, pause,
):
    length = tokens_ref.shape[1]
    tile = min(TILE_B, length)
    ids = rows_ref[pl.ds(s, 1), :]
    bias_ref[...] = jnp.where(ids.astype(F32) >= column(ids), 0.0, NEG)
    lane = lax.broadcasted_iota(jnp.int32, (length, 128), 1)
    low = lane < HEAD_DIM

    for pair in range(GROUP // 128):
        pause(pair)
        at = slice(pair * 128, pair * 128 + 128)
        q2 = q_ref[0, :, at] * BF(0.125)
        k2 = k_ref[0, :, at]
        v2 = v_ref[0, :, at]
        do2 = cback_ref[s, g, :, at]
        dq = None
        for t in range(length // tile):
            rows = slice(t * tile, (t + 1) * tile)
            dks, dvs = [], []
            for h in range(2):
                mine = low[rows] if h == 0 else ~low[rows]
                km = jnp.where(mine, k2[rows], BF(0))
                vm = jnp.where(mine, v2[rows], BF(0))
                head = g * (GROUP // HEAD_DIM) + pair * 2 + h
                lse = lse_ref[0, pl.ds(head, 1), :]
                rowdot = rowdot_ref[s, pl.ds(head, 1), :]
                probs = jnp.exp(dot_nt(km, q2) + bias_ref[rows, :] - lse)
                dprobs = dot_nt(vm, do2)
                dscore = (probs * (dprobs - rowdot)).astype(BF)
                dvs.append(dot(probs.astype(BF), do2))
                dks.append(dot(dscore, q2))
                part = dot_tn(dscore, km * BF(0.125))
                dq = part if dq is None else dq + part
            dk = jnp.where(low[rows], dks[0], dks[1])
            dv = jnp.where(low[rows], dvs[0], dvs[1])
            jlow_ref[0, rows, GROUP + pair * 128 : GROUP + pair * 128 + 128] = dk.astype(BF)
            jlow_ref[0, rows, 2 * GROUP + pair * 128 : 2 * GROUP + pair * 128 + 128] = dv.astype(BF)
            vsum = jnp.sum(dv, axis=0, keepdims=True)
            vtotal = vsum if t == 0 else vtotal + vsum
        jlow_ref[0, :, at] = dq.astype(BF)
        lanes = pl.ds(pl.multiple_of(g * GROUP + pair * 128, 128), 128)
        sums_ref[0:1, lanes] += jnp.sum(dq, axis=0, keepdims=True)
        sums_ref[1:2, lanes] += vtotal

    part = dot_tn(tokens_ref[0], jlow_ref[0])

    @pl.when(s == 0)
    def _():
        acc[...] = part

    @pl.when(s > 0)
    def _():
        acc[...] += part


def late_back(second, pre_low, norm, inv, ctx, up_bin, out_bin, small, tokens, block_ids, joined, lse, sums, feed_grads=None):
    seqs, length, width = tokens.shape
    groups = width // GROUP
    linked = feed_grads is not None
    first = seqs * HALVES
    phase = lambda i: (i + 64 - first) // 64
    seq_one = lambda i: i + phase(i) * (first - 1 - i)
    seq_two = lambda i: phase(i) * ((i - first + seqs * first) % seqs)
    group_two = lambda i: phase(i) * ((i - first) // seqs)
    some = length // HALVES
    second, pre_low, norm, inv, ctx = (a.reshape(first, some, a.shape[2]) for a in (second, pre_low, norm, inv, ctx))
    one = lambda *shape: pl.BlockSpec((1,) + shape, lambda i: (seq_one(i),) + (0,) * len(shape))
    two = lambda *shape: pl.BlockSpec((1,) + shape, lambda i: (seq_two(i),) + (0,) * len(shape))
    part = lambda k: pl.BlockSpec((1, length, GROUP), lambda i: (seq_two(i), 0, k * groups + group_two(i)))
    held = lambda a: pl.BlockSpec(a.shape, lambda i: (0,) * a.ndim, pipeline_mode=pl.Buffered(1))
    anywhere = pl.BlockSpec(memory_space=pl.ANY)
    unit = (width, width // 2)
    like = jax.ShapeDtypeStruct
    in_specs = [
        one(some, width), one(some, pre_low.shape[2]), one(some, width), one(some, 1), one(some, width),
        held(up_bin), held(out_bin), held(small),
        two(length, width), held(block_ids), part(0), part(1), part(2), two(16, length), held(sums),
    ]
    operands = [
        second, pre_low, norm, inv, ctx, up_bin, out_bin, small,
        tokens, block_ids, joined, joined, joined, lse, sums,
    ]
    out_specs = [one(some, width), pl.BlockSpec((1, length, 3 * GROUP), lambda i: (seq_two(i), 0, group_two(i)))]
    out_shape = [like((first, some, width), BF), like((seqs, length, 3 * width), BF)]
    scratch = [
        pltpu.VMEM((seqs, groups, length, GROUP), BF), pltpu.VMEM((seqs, 16, length), F32),
        pltpu.VMEM((width, width), F32), pltpu.VMEM((length, length), F32),
    ]
    if linked:
        units = feed_grads[0].shape[0] + 1 + groups
        in_specs += [anywhere] * 2
        operands += feed_grads
        out_specs += [anywhere, full(sums.shape)]
        out_shape += [like((units,) + unit, BF), like(sums.shape, F32)]
        scratch += [pltpu.VMEM((1 + groups,) + unit, BF)] + Exchange.buffers(LOTS, units, *unit, sums.shape)
        extra = dict(collective_id=0, has_side_effects=True)
    else:
        out_specs += [full((1 + groups,) + unit)] * 2 + [full(sums.shape)]
        out_shape += [like((1 + groups,) + unit, BF)] * 2 + [like(sums.shape, F32)]
        extra = {}
    return pl.pallas_call(
        functools.partial(late_back_kernel, linked, seqs, groups),
        grid=(seqs * (HALVES + groups),),
        in_specs=in_specs,
        out_specs=out_specs,
        out_shape=out_shape,
        scratch_shapes=scratch,
        compiler_params=params(58, **extra),
        cost_estimate=cost(seqs * length * width * (20 * width + 40 * length), 70 * seqs * length * width),
        name="late_back",
    )(*operands)


def token_total(resid_ref, jlow_ref, qkv_ref):
    width = resid_ref.shape[2]
    groups = width // GROUP
    total = resid_ref[0].astype(F32)
    for g in range(groups):
        for k in range(3):
            at = (3 * g + k) * GROUP
            col = k * width + g * GROUP
            total = total + dot_nt(jlow_ref[0, :, at : at + GROUP], qkv_ref[:, col : col + GROUP])
    return total


def token_kernel(resid_ref, jlow_ref, qkv_ref, grad_ref):
    grad_ref[0] = token_total(resid_ref, jlow_ref, qkv_ref)


def finish_kernel(
    core_ref, resid_ref, jlow_ref, qkv_bin_ref, feed_ref, out_unit_ref, qkv_unit_ref, sums_ref,
    grad_ref, qkv_ref, out_ref, up_ref, dn_ref, bias_ref, hidden_ref, gain_ref, shift_ref,
    up_stage, qkv_stage, up_sem, qkv_sem,
):
    step, last = pl.program_id(0), up_sem.shape[0] - 1
    _, rows, half = feed_ref.shape
    groups = qkv_sem.shape[0]
    parts = (slice(0, half), slice(half, rows))

    def up_copy(c, p):
        at = pl.ds(pl.multiple_of((p * (last + 1) + c) * half, half), half)
        return pltpu.make_async_copy(up_stage.at[c, p], up_ref.at[:, at], up_sem.at[c, p])

    def qkv_copy(g, k):
        at = pl.ds(pl.multiple_of(k * rows + g * GROUP, GROUP), GROUP)
        return pltpu.make_async_copy(qkv_stage.at[g, k], qkv_ref.at[:, at], qkv_sem.at[g, k])

    for p in range(2):
        up_stage[step, p] = feed_ref[1, parts[p], :].astype(F32)
        up_copy(step, p).start()
        dn_ref[:, parts[p]] = feed_ref[0, parts[p], :].astype(F32)

    @pl.when(step == 0)
    def _():
        for p in range(2):
            out_ref[:, parts[p]] = out_unit_ref[0, parts[p], :].astype(F32)
        mine = pl.ds(pl.multiple_of(core_ref[0] * half, half), half)
        total = sums_ref[:, mine]
        bias_ref[...] = total[0:4]
        gain_ref[...] = total[4:6]
        shift_ref[...] = total[6:8]
        for c in range(last + 1):
            for j in range(half // 128):
                at = c * (half // 128) + j
                hidden_ref[at : at + 1, :] = total[8 + c : 9 + c, j * 128 : (j + 1) * 128]

    @pl.when(step > 0)
    def _():
        for j in range(3 * GROUP // 128):
            col = j * 128
            qkv_stage[step - 1, col // GROUP, :, col % GROUP : col % GROUP + 128] = qkv_unit_ref[
                0, parts[col // half], col % half : col % half + 128
            ].astype(F32)
        for k in range(3):
            qkv_copy(step - 1, k).start()

    grad_ref[0] = token_total(resid_ref, jlow_ref, qkv_bin_ref)

    @pl.when(step == last)
    def _():
        for c in range(up_sem.shape[0]):
            for p in range(2):
                up_copy(c, p).wait()
        for g in range(groups):
            for k in range(3):
                qkv_copy(g, k).wait()


def finish(core, resid, jlow, qkv_bin, units, sums):
    seqs, length, width = resid.shape
    count, rows, half = units.shape
    groups = rows // GROUP
    chunks = (count - 1 - groups) // 2
    assert chunks == seqs and groups == seqs - 1
    per_seq = lambda *shape: pl.BlockSpec((1,) + shape, lambda s, _: (s,) + (0,) * len(shape))
    late = lambda s: s - (s + 63) // 64
    like = lambda *shape: jax.ShapeDtypeStruct(shape, F32)
    anywhere = pl.BlockSpec(memory_space=pl.ANY)
    return pl.pallas_call(
        finish_kernel,
        grid_spec=pltpu.PrefetchScalarGridSpec(
            num_scalar_prefetch=1,
            grid=(chunks,),
            in_specs=[
                per_seq(length, width),
                per_seq(length, 3 * width),
                full(qkv_bin.shape),
                pl.BlockSpec((2, rows, half), lambda s, _: (s, 0, 0)),
                pl.BlockSpec((1, rows, half), lambda s, _: (2 * chunks, 0, 0)),
                pl.BlockSpec((1, rows, half), lambda s, _: (2 * chunks + 1 + late(s), 0, 0)),
                full(sums.shape),
            ],
            out_specs=[
                per_seq(length, width),
                anywhere,
                full((half, rows)),
                anywhere,
                pl.BlockSpec((half, rows), lambda s, _: (s, 0)),
                full((4, half)),
                full((chunks * half // 128, 128)),
                full((2, half)),
                full((2, half)),
            ],
            scratch_shapes=[
                pltpu.VMEM((chunks, 2, half, half), F32),
                pltpu.VMEM((groups, 3, half, GROUP), F32),
                pltpu.SemaphoreType.DMA((chunks, 2)),
                pltpu.SemaphoreType.DMA((groups, 3)),
            ],
        ),
        out_shape=[
            like(seqs, length, width), like(half, 3 * rows), like(half, rows), like(half, 2 * chunks * half),
            like(chunks * half, rows), like(4, half), like(chunks * half // 128, 128), like(2, half), like(2, half),
        ],
        compiler_params=params(),
        cost_estimate=cost(6 * seqs * length * width * width, 16 * seqs * length * width),
        name="finish",
    )(core, resid, jlow, qkv_bin, units, units, units, sums)


def token_back(resid, jlow, qkv_bin):
    seqs, length, width = resid.shape
    per_seq = lambda *shape: pl.BlockSpec((1,) + shape, lambda s: (s,) + (0,) * len(shape))
    return pl.pallas_call(
        token_kernel,
        grid=(seqs,),
        in_specs=[per_seq(length, width), per_seq(length, 3 * width), full(qkv_bin.shape)],
        out_specs=per_seq(length, width),
        out_shape=jax.ShapeDtypeStruct((seqs, length, width), F32),
        compiler_params=params(),
        cost_estimate=cost(6 * seqs * length * width * width, 16 * seqs * length * width),
        name="token_back",
    )(resid, jlow, qkv_bin)


def swap(value):
    return lax.ppermute(value, "shard", [(0, 1), (1, 0)])


def small_rows(biases, gain, shift, hidden_bias):
    rows = biases.shape[0]
    return jnp.concatenate([biases.T, gain.T, shift.T, hidden_bias.reshape(-1, rows)], axis=0)


def reduce_plain(feed_grads, out_grads, qkv_grads, sums):
    def whole(mine, theirs):
        count, rows, half = mine.shape
        cut = lambda a: a.reshape(count, 2, half, half).transpose(0, 2, 1, 3).reshape(count, half, rows)
        return jnp.concatenate([cut(mine), cut(theirs)], axis=1)

    feed_all, out_all, qkv_all = whole(*feed_grads), whole(*out_grads), whole(*qkv_grads)
    chunks, groups, width = feed_all.shape[0] // 2, qkv_all.shape[0], feed_all.shape[2]
    half, units = width // 2, chunks * width
    grads = (
        qkv_all.reshape(groups, width, 3, GROUP).transpose(1, 2, 0, 3).reshape(width, 3 * width),
        out_all[0],
        feed_all[1::2].reshape(chunks, width, 2, half).transpose(1, 2, 0, 3).reshape(width, units),
        feed_all[0::2].reshape(chunks, 2, half, width).transpose(1, 0, 2, 3).reshape(units, width),
        sums[0:4].T.astype(BF),
        sums[8:].reshape(chunks, 2, half).transpose(1, 0, 2).reshape(-1).astype(BF),
        sums[4:6].T.astype(BF),
        sums[6:8].T.astype(BF),
    )
    owned = lax.psum_scatter(grads, "shard", scatter_dimension=0, tiled=True)
    return jax.tree.map(lambda part: part.astype(F32), lax.psum(owned, "rep"))


def body(tokens, teacher, block_ids, *weights):
    qkv, out, up, down, biases, hidden_bias, gain, shift = weights
    paired = lax.axis_size("shard") == 2 and lax.axis_size("rep") == 16
    if paired:
        core = lax.axis_index("shard").reshape(1)
        small = small_rows(biases, gain, shift, hidden_bias)
        small, qkv, out = ((a, swap(a)) for a in (small, qkv, out))
        up, down, _, _ = lax.optimization_barrier((up, down, qkv[1], small[1]))
        up, down = ((a, swap(a)) for a in (up, down))
    else:
        core = jnp.zeros((1,), jnp.int32)
        gathered = [lax.all_gather(w, "shard", axis=0, tiled=True) for w in weights]
        qkv, out, up, down, *rest = (jnp.split(w, 2, axis=0) for w in gathered)
        small = [small_rows(rest[0][i], rest[2][i], rest[3][i], rest[1][i]) for i in range(2)]
    joined, ctx, lse, norm, inv, small, qkv_bin, out_bin = attend(core, tokens, block_ids, qkv, out, small)
    final, first_low, hidden, slope, second, mixed, sums, up_bin, dn_bin = feed(core, norm, teacher, small, up, down)
    pre_low, *feed_grads, sums = feed_back(core, mixed, first_low, hidden, slope, dn_bin, sums)
    pre_low = pre_low.reshape(hidden.shape)
    operands = (second, pre_low, norm, inv, ctx, up_bin, out_bin, small, tokens, block_ids, joined, lse, sums)
    if not paired:
        resid, jlow, *grads, sums = late_back(*operands)
        token_grad = token_back(resid.reshape(tokens.shape), jlow, qkv_bin)
        out_grads, qkv_grads = ([a[cut] for a in grads] for cut in (slice(0, 1), slice(1, None)))
        return (final, token_grad) + tuple(reduce_plain(feed_grads, out_grads, qkv_grads, sums[:12]))
    resid, jlow, units, sums = late_back(*operands, feed_grads)
    resid = resid.reshape(tokens.shape)
    token_grad, *grads, bias, hidden, gains, shifts = finish(core, resid, jlow, qkv_bin, units, sums)
    return (final, token_grad, *grads, bias.T, hidden.reshape(-1), gains.T, shifts.T)


def solution(mesh):
    placed = (
        P(("shard", "rep"), None, None),
        P(("shard", "rep"), None, None),
        P(("shard", "rep"), None),
        P("shard", None),
        P("shard", None),
        P("shard", None),
        P("shard", None),
        P("shard", None),
        P("shard"),
        P("shard", None),
        P("shard", None),
    )
    return jax.shard_map(
        body,
        mesh=mesh,
        in_specs=placed,
        out_specs=placed[:2] + placed[3:],
        check_vma=False,
    )
```

```python
import functools

import jax
import jax.numpy as jnp
from jax import lax
from jax.experimental import pallas as pl
from jax.experimental.pallas import tpu as pltpu
from jax.sharding import PartitionSpec as P

HEAD_DIM = 64
GROUP = 256
EPS = 1e-05
NEG = -1e30
BF = jnp.bfloat16
F32 = jnp.float32
MB = 1 << 20


def params(mb=56, **kw):
    return pltpu.CompilerParams(vmem_limit_bytes=mb * MB, **kw)


def dot(a, b):
    return jnp.dot(a, b, preferred_element_type=F32)


def dot_nt(a, b):
    return lax.dot_general(a, b, (((1,), (1,)), ((), ())), preferred_element_type=F32)


def dot_tn(a, b):
    return lax.dot_general(a, b, (((0,), (0,)), ((), ())), preferred_element_type=F32)


def full(shape):
    return pl.BlockSpec(shape, lambda *_: (0,) * len(shape))


def cost(flops, nbytes, trans=0):
    return pl.CostEstimate(flops=int(flops), bytes_accessed=int(nbytes), transcendentals=int(trans))


def column(row):
    return jnp.broadcast_to(row.astype(F32), (8, row.shape[1])).T[:, 0:1]


def deal(core, acc, mine_ref, theirs_ref, at=0):
    half = acc.shape[0] // 2
    wide = acc.shape[1] // 2
    for ref, who in ((mine_ref, core), (theirs_ref, 1 - core)):
        rows = pl.ds(pl.multiple_of(who * half, half), half)
        ref[at, 0:half, :] = acc[rows, 0:wide].astype(BF)
        ref[at, half : 2 * half, :] = acc[rows, wide : 2 * wide].astype(BF)


def binary_halves(first, second):
    rows = 2 * first.shape[0]
    total = jnp.sum(jnp.abs(first.astype(F32)), axis=0, keepdims=True) + jnp.sum(
        jnp.abs(second.astype(F32)), axis=0, keepdims=True
    )
    scale = (total / rows).astype(BF)
    return (
        jnp.where(first >= 0, scale, -scale).astype(BF),
        jnp.where(second >= 0, scale, -scale).astype(BF),
    )


def binary_rows(core, own_ref, other_ref, out_ref):
    half, cols = own_ref.shape
    own_at = pl.ds(pl.multiple_of(core * half, half), half)
    other_at = pl.ds(pl.multiple_of((1 - core) * half, half), half)

    def one(j, _):
        at = pl.ds(pl.multiple_of(j * GROUP, GROUP), GROUP)
        out_ref[own_at, at], out_ref[other_at, at] = binary_halves(own_ref[:, at], other_ref[:, at])
        return 0

    lax.fori_loop(0, cols // GROUP, one, 0)


def binary_up(core, own_ref, other_ref, out_ref):
    half, cols = own_ref.shape
    chunks = cols // (2 * half)
    own_at = pl.ds(pl.multiple_of(core * half, half), half)
    other_at = pl.ds(pl.multiple_of((1 - core) * half, half), half)

    def one(j, _):
        at = pl.ds(pl.multiple_of(j * half, half), half)
        to = pl.ds(pl.multiple_of((j % chunks) * 2 * half + (j // chunks) * half, half), half)
        out_ref[own_at, to], out_ref[other_at, to] = binary_halves(own_ref[:, at], other_ref[:, at])
        return 0

    lax.fori_loop(0, 2 * chunks, one, 0)


def binary_down(core, own_ref, other_ref, out_ref):
    rows, cols = own_ref.shape
    half = cols // 2

    def one(j, _):
        at = pl.ds(pl.multiple_of(j * GROUP, GROUP), GROUP)
        own, other = binary_halves(own_ref[:, at], other_ref[:, at])
        for c in range(rows // half):
            part = slice(c * half, (c + 1) * half)
            out_ref[pl.ds(pl.multiple_of((2 * c + core) * half, half), half), at] = own[part]
            out_ref[pl.ds(pl.multiple_of((2 * c + 1 - core) * half, half), half), at] = other[part]
        return 0

    lax.fori_loop(0, cols // GROUP, one, 0)


def attend_kernel(
    core_ref, tokens_ref, rows_ref, qkv_own, qkv_other, out_own, out_other, small_own, small_other,
    joined_ref, ctx_ref, lse_ref, norm_ref, inv_ref, small_ref, qkv_any, out_any,
    bias_ref, qkv_ref, out_ref, sems,
):
    length, width = tokens_ref.shape[1:]
    keep = (
        pltpu.make_async_copy(qkv_ref, qkv_any, sems.at[0]),
        pltpu.make_async_copy(out_ref, out_any, sems.at[1]),
    )

    @pl.when(pl.program_id(0) == 0)
    def _():
        core, half = core_ref[0], width // 2
        binary_rows(core, qkv_own, qkv_other, qkv_ref)
        binary_rows(core, out_own, out_other, out_ref)
        small_ref[:, pl.ds(pl.multiple_of(core * half, half), half)] = small_own[...].astype(F32)
        small_ref[:, pl.ds(pl.multiple_of((1 - core) * half, half), half)] = small_other[...].astype(F32)
        for copy in keep:
            copy.start()

    x = tokens_ref[0]
    for part, bias_row in ((0, 0), (1, None), (2, 1)):
        joined = dot(x, qkv_ref[:, part * width : (part + 1) * width])
        if bias_row is not None:
            joined = joined + small_ref[bias_row : bias_row + 1, :]
        joined_ref[0, :, part * width : (part + 1) * width] = joined.astype(BF)
    ids = rows_ref[pl.ds(pl.program_id(0), 1), :]
    bias_ref[...] = jnp.where(column(ids) >= ids.astype(F32), 0.0, NEG)
    lane = lax.broadcasted_iota(jnp.int32, (length, 128), 1)
    low = lane < HEAD_DIM
    lse_all = jnp.zeros((length, 128), F32)
    tile = min(TILE_F, length)
    for pair in range(width // 128):
        q2 = joined_ref[0, :, pair * 128 : pair * 128 + 128] * BF(0.125)
        k2 = joined_ref[0, :, width + pair * 128 : width + pair * 128 + 128]
        v2 = joined_ref[0, :, 2 * width + pair * 128 : 2 * width + pair * 128 + 128]
        for t in range(length // tile):
            rows = slice(t * tile, (t + 1) * tile)
            parts = []
            for h in range(2):
                mine = low[rows] if h == 0 else ~low[rows]
                qm = jnp.where(mine, q2[rows], BF(0))
                scores = dot_nt(qm, k2) + bias_ref[rows, :]
                peak = jnp.max(scores, axis=-1, keepdims=True)
                raised = jnp.exp(scores - peak)
                total = jnp.sum(raised, axis=-1, keepdims=True)
                parts.append(dot(raised.astype(BF), v2) / total)
                lse_ref_col = peak + jnp.log(total)
                bias_lane = lane[rows] == 2 * pair + h
                lse_cols = jnp.where(bias_lane, lse_ref_col, 0.0)
                if h == 0:
                    pair_lse = lse_cols
                else:
                    pair_lse = pair_lse + lse_cols
            ctx_ref[0, rows, pair * 128 : pair * 128 + 128] = jnp.where(low[rows], parts[0], parts[1]).astype(BF)
            if t == 0:
                tiles_lse = [pair_lse]
            else:
                tiles_lse.append(pair_lse)
        lse_all = lse_all + jnp.concatenate(tiles_lse, axis=0)
    lse_ref[0] = lse_all.T[0:16, :]
    resid = x.astype(F32) + dot(ctx_ref[0], out_ref[...]) + small_ref[2:3, :]
    center = resid - jnp.mean(resid, axis=-1, keepdims=True)
    inverse = lax.rsqrt(jnp.mean(center * center, axis=-1, keepdims=True) + EPS)
    norm_ref[0] = center * inverse
    inv_ref[0] = inverse

    @pl.when(pl.program_id(0) == pl.num_programs(0) - 1)
    def _():
        for copy in keep:
            copy.wait()


TILE_F = 512


def attend(core, tokens, block_ids, qkv, out, small):
    seqs, length, width = tokens.shape
    per_seq = lambda *shape: pl.BlockSpec((1,) + shape, lambda s, _: (s,) + (0,) * len(shape))
    once = lambda a: pl.BlockSpec(a.shape, lambda s, _: (0,) * a.ndim, pipeline_mode=pl.Buffered(1))
    anywhere = pl.BlockSpec(memory_space=pl.ANY)
    like = jax.ShapeDtypeStruct
    joined_width = qkv[0].shape[1]
    whole = (small[0].shape[0], width)
    return pl.pallas_call(
        attend_kernel,
        grid_spec=pltpu.PrefetchScalarGridSpec(
            num_scalar_prefetch=1,
            grid=(seqs,),
            in_specs=[per_seq(length, width)] + [once(a) for a in (block_ids, *qkv, *out, *small)],
            out_specs=[
                per_seq(length, joined_width),
                per_seq(length, width),
                per_seq(16, length),
                per_seq(length, width),
                per_seq(length, 1),
                full(whole),
                anywhere,
                anywhere,
            ],
            scratch_shapes=[
                pltpu.VMEM((length, length), F32),
                pltpu.VMEM((width, joined_width), BF),
                pltpu.VMEM((width, width), BF),
                pltpu.SemaphoreType.DMA((2,)),
            ],
        ),
        out_shape=[
            like((seqs, length, joined_width), BF),
            like((seqs, length, width), BF),
            like((seqs, 16, length), F32),
            like((seqs, length, width), F32),
            like((seqs, length, 1), F32),
            like(whole, F32),
            like((width, joined_width), BF),
            like((width, width), BF),
        ],
        compiler_params=params(),
        cost_estimate=cost(seqs * length * width * (8 * width + 16 * length), 30 * seqs * length * width),
        name="attend",
    )(core, tokens, block_ids, *qkv, *out, *small)


def gelu_pair(u):
    cdf = 0.5 + 0.5 * lax.erf(u * 0.7071067811865476)
    density = jnp.exp(-0.5 * u * u) * 0.3989422804014327
    return u * cdf, cdf + u * density


def norm_back(upstream, normed, inverse, gain):
    scaled = upstream * gain
    weighted = upstream * normed
    centered = (
        scaled
        - jnp.mean(scaled, axis=-1, keepdims=True)
        - normed * jnp.mean(weighted * gain, axis=-1, keepdims=True)
    )
    return centered * inverse, jnp.sum(weighted, axis=0, keepdims=True), jnp.sum(upstream, axis=0, keepdims=True)


def feed_kernel(
    core_ref, norm_ref, teacher_ref, small_ref, up_own, up_other, dn_own, dn_other,
    final_ref, first_low_ref, hidden_ref, slope_ref, second_ref, mixed_ref, sums_ref, up_any, dn_any,
    up_ref, dn_ref, sems,
):
    width = norm_ref.shape[2]
    keep = (
        pltpu.make_async_copy(up_ref, up_any, sems.at[0]),
        pltpu.make_async_copy(dn_ref, dn_any, sems.at[1]),
    )

    @pl.when(pl.program_id(0) == 0)
    def _():
        binary_up(core_ref[0], up_own, up_other, up_ref)
        binary_down(core_ref[0], dn_own, dn_other, dn_ref)
        for copy in keep:
            copy.start()

    first = norm_ref[0] * small_ref[4:5, :] + small_ref[6:7, :]
    first_low = first.astype(BF)
    first_low_ref[0] = first_low
    acc = first + small_ref[3:4, :]
    for c in range(up_ref.shape[1] // width):
        cols = slice(c * width, (c + 1) * width)
        pre = dot(first_low, up_ref[:, cols]) + small_ref[8 + c : 9 + c, :]
        value, slope = gelu_pair(pre)
        value = value.astype(BF)
        hidden_ref[0, :, cols] = value
        slope_ref[0, :, cols] = slope.astype(BF)
        acc = acc + dot(value, dn_ref[cols, :])
    center = acc - jnp.mean(acc, axis=-1, keepdims=True)
    inverse = lax.rsqrt(jnp.mean(center * center, axis=-1, keepdims=True) + EPS)
    normed = center * inverse
    gain = small_ref[5:6, :]
    final = normed * gain + small_ref[7:8, :]
    final_ref[0] = final.astype(BF)
    upstream = final - teacher_ref[0].astype(F32)
    second, gain_sum, shift_sum = norm_back(upstream, normed, inverse, gain)
    second_ref[0] = second
    mixed_ref[0] = second.astype(BF)

    @pl.when(pl.program_id(0) == 0)
    def _():
        sums_ref[...] = jnp.zeros_like(sums_ref)

    sums_ref[3:4, :] += jnp.sum(second, axis=0, keepdims=True)
    sums_ref[5:6, :] += gain_sum
    sums_ref[7:8, :] += shift_sum

    @pl.when(pl.program_id(0) == pl.num_programs(0) - 1)
    def _():
        for copy in keep:
            copy.wait()


def feed(core, norm, teacher, small, up, dn):
    seqs, length, width = norm.shape
    hidden = up[0].shape[1]
    per_seq = lambda *shape: pl.BlockSpec((1,) + shape, lambda s, _: (s,) + (0,) * len(shape))
    once = lambda a: pl.BlockSpec(a.shape, lambda s, _: (0,) * a.ndim, pipeline_mode=pl.Buffered(1))
    anywhere = pl.BlockSpec(memory_space=pl.ANY)
    like = jax.ShapeDtypeStruct
    row = lambda n, dt: like((seqs, length, n), dt)
    return pl.pallas_call(
        feed_kernel,
        grid_spec=pltpu.PrefetchScalarGridSpec(
            num_scalar_prefetch=1,
            grid=(seqs,),
            in_specs=[per_seq(length, width), per_seq(length, width)] + [once(a) for a in (small, *up, *dn)],
            out_specs=[
                per_seq(length, width),
                per_seq(length, width),
                per_seq(length, hidden),
                per_seq(length, hidden),
                per_seq(length, width),
                per_seq(length, width),
                full((16, width)),
                anywhere,
                anywhere,
            ],
            scratch_shapes=[
                pltpu.VMEM((width, hidden), BF),
                pltpu.VMEM((hidden, width), BF),
                pltpu.SemaphoreType.DMA((2,)),
            ],
        ),
        out_shape=[
            row(width, BF), row(width, BF), row(hidden, BF), row(hidden, BF), row(width, F32), row(width, BF),
            like((16, width), F32), like((width, hidden), BF), like((hidden, width), BF),
        ],
        compiler_params=params(60),
        cost_estimate=cost(4 * seqs * length * width * hidden, 36 * seqs * length * width),
        name="feed",
    )(core, norm, teacher, small, *up, *dn)


def feed_back_kernel(
    core_ref, mixed_ref, first_ref, hidden_ref, slope_ref, dn_ref, sums_in_ref,
    pre_ref, mine_ref, theirs_ref, sums_ref, acc,
):
    chunk = pl.program_id(0)

    @pl.when(chunk == 0)
    def _():
        sums_ref[...] = sums_in_ref[...]

    mixed = mixed_ref[0]
    pre_back = dot_nt(mixed, dn_ref[...]) * slope_ref[0].astype(F32)
    pre_low = pre_back.astype(BF)
    pre_ref[0] = pre_low
    acc[...] = dot_tn(hidden_ref[0], mixed)
    deal(core_ref[0], acc, mine_ref, theirs_ref, 0)
    acc[...] = dot_tn(first_ref[0], pre_low)
    deal(core_ref[0], acc, mine_ref, theirs_ref, 1)
    sums_ref[pl.ds(8 + chunk, 1), :] += jnp.sum(pre_back, axis=0, keepdims=True)


def feed_back(core, mixed, first_low, hidden, slope, dn_bin, sums):
    mixed, first_low, hidden, slope = (a.reshape(1, -1, a.shape[2]) for a in (mixed, first_low, hidden, slope))
    seqs, length, width = mixed.shape
    units = hidden.shape[2]
    chunks = units // width
    return pl.pallas_call(
        feed_back_kernel,
        grid_spec=pltpu.PrefetchScalarGridSpec(
            num_scalar_prefetch=1,
            grid=(chunks,),
            in_specs=[
                pl.BlockSpec((1, length, width), lambda c, _: (0, 0, 0)),
                pl.BlockSpec((1, length, width), lambda c, _: (0, 0, 0)),
                pl.BlockSpec((1, length, width), lambda c, _: (0, 0, c)),
                pl.BlockSpec((1, length, width), lambda c, _: (0, 0, c)),
                pl.BlockSpec((width, width), lambda c, _: (c, 0)),
                full(sums.shape),
            ],
            out_specs=[
                pl.BlockSpec((1, length, width), lambda c, _: (0, 0, c)),
                pl.BlockSpec((2, width, width // 2), lambda c, _: (c, 0, 0)),
                pl.BlockSpec((2, width, width // 2), lambda c, _: (c, 0, 0)),
                full(sums.shape),
            ],
            scratch_shapes=[pltpu.VMEM((width, width), F32)],
        ),
        out_shape=[
            jax.ShapeDtypeStruct((seqs, length, units), BF),
            jax.ShapeDtypeStruct((2 * chunks, width, width // 2), BF),
            jax.ShapeDtypeStruct((2 * chunks, width, width // 2), BF),
            jax.ShapeDtypeStruct(sums.shape, F32),
        ],
        compiler_params=params(),
        cost_estimate=cost(6 * seqs * length * width * units, 20 * seqs * length * units),
        name="feed_back",
    )(core, mixed, first_low, hidden, slope, dn_bin, sums)


def norm_step(second, pre_low, norm, inv, ctx, up_ref, out_ref, small_ref, sums_ref, pause):
    width = second.shape[1]
    back = second + dot_nt(pre_low, up_ref[...])
    pause(1)
    resid, gain_sum, shift_sum = norm_back(back, norm, inv, small_ref[4:5, :])
    sums_ref[2:3, :] += jnp.sum(resid, axis=0, keepdims=True)
    sums_ref[4:5, :] += gain_sum
    sums_ref[6:7, :] += shift_sum
    low = resid.astype(BF)
    cback = dot_nt(low, out_ref[...]).astype(BF)
    prod = cback.astype(F32) * ctx.astype(F32)
    high = prod.astype(BF)
    rest = (prod - high.astype(F32)).astype(BF)
    heads = lax.broadcasted_iota(jnp.int32, (16, width), 0)
    lanes = lax.broadcasted_iota(jnp.int32, (16, width), 1)
    pick = jnp.where((lanes >= heads * HEAD_DIM) & (lanes < heads * HEAD_DIM + HEAD_DIM), 1.0, 0.0).astype(BF)
    return low, cback, dot_nt(pick, high) + dot_nt(pick, rest), dot_tn(ctx, low)


MESH = pl.DeviceIdType.MESH

SMALL = 5

LOTS = (
    (0, 0, 384, "xyz"),
    (1, 0, 384, "yxz"),
    (2, 0, 384, "yxz"),
    (3, 0, 384, "yxz"),
    (4, 0, 384, "yxz"),
    (5, 0, 384, "xyz"),
    (6, 0, 384, "zxy"),
    (7, 0, 384, "yxz"),
    (8, 0, 384, "xyz"),
    (9, 0, 384, "xyz"),
    (10, 0, 384, "xyz"),
    (11, 0, 128, "zxy"),
    (11, 128, 128, "yxz"),
    (11, 256, 128, "yxz"),
)
EVENTS = (
    (),
    ((0, 0), (1, 0), (2, 0), (3, 0),),
    ((4, 0), (5, 0),),
    ((6, 0), (7, 0),),
    ((0, 1), (1, 1),),
    (),
    (),
    ((5, 1),),
    ((2, 1),),
    ((1, 2),),
    (),
    ((2, 2), (3, 1), (6, 1),),
    ((1, 3),),
    (),
    ((2, 3), (3, 2), (4, 1),),
    ((1, 4), (6, 2),),
    (),
    ((2, 4), (4, 2), (7, 1),),
    ((1, 5), (3, 3), (0, 2), (8, 0),),
    (),
    ((2, 5), (4, 3), (6, 3), (5, 2),),
    ((3, 4), (7, 2),),
    ((0, 3),),
    ((1, 6),),
    ((4, 4), (8, 1),),
    ((3, 5), (5, 3),),
    ((2, 6), (6, 4), (9, 0), (4, 5), (7, 3),),
    ((8, 2),),
    ((6, 5), (0, 4),),
    ((5, 4),),
    ((3, 6),),
    ((7, 4), (9, 1),),
    ((8, 3),),
    ((4, 6),),
    ((0, 5), (7, 5), (10, 0),),
    (),
    ((5, 5),),
    ((9, 2),),
    ((0, 6), (6, 6),),
    ((8, 4),),
    ((7, 6), (9, 3), (10, 1), (11, 0), (12, 0), (13, 0), (8, 5), (9, 4), (10, 2), (5, 6), (12, 1), (11, 1), (13, 1), (10, 3), (9, 5), (8, 6), (12, 2), (11, 2), (13, 2), (11, 3), (10, 4), (12, 3), (11, 4), (13, 3), (12, 4), (9, 6), (13, 4), (10, 5), (11, 5), (12, 5), (13, 5), (12, 6), (11, 6), (13, 6), (10, 6),),
)


class Exchange:
    def __init__(self, lots, copied, result_ref, held, from_core, inbox, kept, came, sems):
        (
            local_sem, core_send, core_recv, out_send, out_recv, back_send, back_recv, small_send, small_recv, done_sem
        ) = sems
        self.copied = copied
        core, rep = lax.axis_index("shard"), lax.axis_index("rep")
        place = {"x": rep % 2, "y": (rep // 2) % 2, "z": rep // 4, "p": rep % 4}
        ways = {"x": 2, "y": 2, "z": 4, "p": 4}
        sibling = {"shard": 1 - core}
        rows = held.shape[1]
        step_rows = rows // 16

        def peers(axis):
            if axis == "p":
                return [{"rep": rep - place["p"] + (place["p"] + d) % 4} for d in (1, 2, 3)]
            if axis == "z":
                return [{"rep": rep % 4 + 4 * ((place["z"] + d) % 4)} for d in (1, 2, 3)]
            stride = {"x": 1, "y": 2}[axis]
            return [{"rep": rep + stride - 2 * stride * place[axis]}]

        def meet():
            barrier = pltpu.get_barrier_semaphore()
            everyone = [sibling] + peers("p") + peers("z")
            for peer in everyone:
                pl.semaphore_signal(barrier, inc=1, device_id=peer, device_id_type=MESH)
            pl.semaphore_wait(barrier, len(everyone))

        def send(src, dst, send_sem, recv_sem, peer):
            return pltpu.make_async_remote_copy(
                src_ref=src, dst_ref=dst, send_sem=send_sem, recv_sem=recv_sem, device_id=peer, device_id_type=MESH
            )

        def block(at, size):
            return pl.ds(at if isinstance(at, int) else pl.multiple_of(at, step_rows), size)

        def columns(lot):
            return pl.ds(lots[lot][1], lots[lot][2])

        def chain(lot):
            base, size, inside, sem, out = 0, rows, 0, 0, []
            for axis in lots[lot][3]:
                part = size // ways[axis]
                mine = base + place[axis] * part
                out.append((axis, base, part, mine, inside, sem))
                base, size, inside, sem = mine, part, inside + size - part, sem + ways[axis] - 1
            return out

        def core_copy(lot, theirs=None):
            u, cols = lots[lot][0], columns(lot)
            here = from_core.at[u, :, cols]
            return send(here if theirs is None else theirs.at[:, cols], here, core_send.at[lot], core_recv.at[lot], sibling)

        def out_copies(lot, s):
            u, cols = lots[lot][0], columns(lot)
            axis, base, part, _, inside, sem = chain(lot)[s]
            copies = []
            for n, peer in enumerate(peers(axis)):
                away = base + ((place[axis] + n + 1) % ways[axis]) * part
                copy = send(
                    held.at[u, block(away, part), cols], inbox.at[u, block(inside + n * part, part), cols],
                    out_send.at[lot, sem + n], out_recv.at[lot, sem + n], peer,
                )
                copies.append((away, copy))
            return copies

        def back_copies(lot, s):
            u, cols = lots[lot][0], columns(lot)
            axis, _, part, mine, _, sem = chain(lot)[s]
            own = from_core.at[u, block(mine, part), cols]
            return [
                send(own, own, back_send.at[lot, sem + n], back_recv.at[lot, sem + n], peer)
                for n, peer in enumerate(peers(axis))
            ]

        def done_copy(lot):
            u, cols = lots[lot][0], columns(lot)
            return pltpu.make_async_copy(from_core.at[u, :, cols], result_ref.at[u, :, cols], done_sem.at[lot])

        def add(lot, at, size, terms, target):
            u, cols = lots[lot][0], columns(lot)
            some = min(size, rows // 4)

            def one(n, _):
                total = held[u, block(at + n * some, some), cols].astype(F32)
                for ref, shift in terms:
                    total = total + ref[u, block(at + shift + n * some, some), cols].astype(F32)
                target[u, block(at + n * some, some), cols] = total.astype(BF)
                return 0

            if size == some:
                one(0, 0)
            else:
                lax.fori_loop(0, size // some, one, 0)

        def fire(lot, k):
            links = chain(lot)
            last = len(links)
            if k == 0:
                core_copy(lot).wait_recv()
                if lot < self.copied:
                    pltpu.make_async_copy(from_core.at[lot], held.at[lot], local_sem.at[lot]).wait()
                terms = [(from_core, 0)]
            elif k <= last:
                for _, copy in out_copies(lot, k - 1):
                    copy.wait_recv()
                axis, _, part, mine, inside, _ = links[k - 1]
                terms = [(inbox, inside + n * part - mine) for n in range(ways[axis] - 1)]
            if k < last:
                _, _, part, mine, _, _ = links[k]
                for away, copy in out_copies(lot, k):
                    add(lot, away, part, terms, held)
                    copy.start()
                add(lot, mine, part, terms, held)
                return
            if k == last:
                _, _, part, mine, _, _ = links[k - 1]
                add(lot, mine, part, terms, from_core)
            else:
                for copy in back_copies(lot, 2 * last - k):
                    copy.wait_recv()
            if k < 2 * last:
                for copy in back_copies(lot, 2 * last - 1 - k):
                    copy.start()
            else:
                done_copy(lot).start()

        def begin(u, theirs, mine=None):
            for lot in range(len(lots)):
                if lots[lot][0] == u:
                    core_copy(lot, theirs).start()
            if mine is not None:
                pltpu.make_async_copy(mine, held.at[u], local_sem.at[u]).start()

        small_peers = [
            sibling, peers("x")[0], peers("y")[0],
            {"rep": rep + 4 - 8 * (place["z"] % 2)}, {"rep": rep + 8 - 16 * (place["z"] // 2)},
        ]

        def copy_small(k):
            return send(kept.at[k], came.at[k], small_send.at[k], small_recv.at[k], small_peers[k])

        def small_next(k):
            copy_small(k).wait_recv()
            kept[k + 1] = kept[k] + came[k]
            if k + 1 < SMALL:
                copy_small(k + 1).start()

        def settle():
            for k in range(SMALL):
                copy_small(k).wait_send()
            for lot in range(len(lots)):
                core_copy(lot).wait_send()
                for s in range(len(lots[lot][3])):
                    for _, copy in out_copies(lot, s):
                        copy.wait_send()
                    for copy in back_copies(lot, s):
                        copy.wait_send()
                done_copy(lot).wait()

        self.meet, self.begin, self.fire, self.settle = meet, begin, fire, settle
        self.small_start, self.small_next = (lambda: copy_small(0).start()), small_next

    @staticmethod
    def buffers(lots, units, rows, cols, small):
        dma = pltpu.SemaphoreType.DMA
        count = len(lots)
        return [
            pltpu.VMEM((units, rows, cols), BF),
            pltpu.VMEM((units, rows, cols), BF),
            pltpu.VMEM((units, rows - rows // 16, cols), BF),
            pltpu.VMEM((SMALL + 1,) + small, F32),
            pltpu.VMEM((SMALL,) + small, F32),
            dma((units,)), dma((count,)), dma((count,)),
        ] + [dma((count, 6))] * 4 + [dma((SMALL,))] * 2 + [dma((count,))]


HALVES = 2
TILE_B = 256


def late_back_kernel(linked, seqs, groups, *refs):
    (
        second_ref, pre_ref, norm_ref, inv_ref, ctx_ref, up_ref, out_ref, small_ref,
        tokens_ref, rows_ref, q_ref, k_ref, v_ref, lse_ref, sums_in_ref,
    ), refs = refs[:15], refs[15:]
    step = pl.program_id(0)
    last = pl.num_programs(0) - 1
    first = seqs * HALVES
    if linked:
        feed_mine, feed_theirs, resid_ref, jlow_ref, result_ref, total_ref = refs[:6]
        cback_ref, rowdot_ref, acc, bias_ref, theirs = refs[6:11]
        buffers, sems = refs[11:16], refs[16:]
        early = feed_mine.shape[0]
        exchange = Exchange(LOTS, early, result_ref, *buffers, sems)
        held, kept = buffers[0], buffers[3]
        core = lax.axis_index("shard")
        sums_ref = kept.at[0]
    else:
        resid_ref, jlow_ref, mine_ref, theirs_ref, sums_ref, cback_ref, rowdot_ref, acc, bias_ref = refs

    def pause(start, count, each, n):
        for i in range(count if linked else 0):
            events = EVENTS[start[1] + each * i + n]
            if events:

                @pl.when(step == start[0] + i)
                def _():
                    for lot, k in events:
                        exchange.fire(lot, k)

    pause_norm = functools.partial(pause, (0, 0), first, 2)
    pause_attend = functools.partial(pause, (first, 2 * first), seqs * groups, 2)

    def hand_over(n):
        if linked:
            deal(core, acc, held.at[pl.ds(early + n, 1)], theirs.at[pl.ds(n, 1)])
            for m in range(1 + groups):

                @pl.when(n == m)
                def _():
                    exchange.begin(early + m, theirs.at[m])

        else:
            deal(0, acc, mine_ref.at[pl.ds(n, 1)], theirs_ref.at[pl.ds(n, 1)])

    @pl.when(step == 0)
    def _():
        if linked:
            exchange.meet()
            for u in range(early):
                exchange.begin(u, feed_theirs.at[u], feed_mine.at[u])
        sums_ref[...] = sums_in_ref[...]

    @pl.when(step < first)
    def _():
        pause_norm(0)
        resid, cback, rowdot, part = norm_step(
            second_ref[0], pre_ref[0], norm_ref[0], inv_ref[0], ctx_ref[0], up_ref, out_ref, small_ref, sums_ref,
            pause_norm,
        )
        resid_ref[0] = resid
        size = resid.shape[0]
        s, some = step // HALVES, pl.ds(pl.multiple_of(step % HALVES * size, size), size)
        for n in range(groups):
            cback_ref[s, n, some, :] = cback[:, n * GROUP : (n + 1) * GROUP]
        rowdot_ref[s, :, some] = rowdot

        @pl.when(step == 0)
        def _():
            acc[...] = part

        @pl.when(step > 0)
        def _():
            acc[...] += part

        @pl.when(step == first - 1)
        def _():
            hand_over(step - (first - 1))

    @pl.when(step >= first)
    def _():
        g, s = (step - first) // seqs, (step - first) % seqs
        attend_step(
            g, s, tokens_ref, rows_ref, q_ref, k_ref, v_ref, cback_ref, lse_ref, rowdot_ref,
            jlow_ref, sums_ref, bias_ref, acc, pause_attend,
        )

        @pl.when(s == seqs - 1)
        def _():
            hand_over(1 + g)

    if linked:

        @pl.when(step == last)
        def _():
            exchange.small_start()
            rest = EVENTS[-1]
            share = -(-len(rest) // (SMALL + 1))
            for k in range(SMALL + 1):
                for lot, stage in rest[k * share : (k + 1) * share]:
                    exchange.fire(lot, stage)
                if k < SMALL:
                    exchange.small_next(k)
            total_ref[...] = kept[SMALL]
            exchange.settle()


def attend_step(
    g, s, tokens_ref, rows_ref, q_ref, k_ref, v_ref, cback_ref, lse_ref, rowdot_ref,
    jlow_ref, sums_ref, bias_ref, acc, pause,
):
    length = tokens_ref.shape[1]
    tile = min(TILE_B, length)
    ids = rows_ref[pl.ds(s, 1), :]
    bias_ref[...] = jnp.where(ids.astype(F32) >= column(ids), 0.0, NEG)
    lane = lax.broadcasted_iota(jnp.int32, (length, 128), 1)
    low = lane < HEAD_DIM

    for pair in range(GROUP // 128):
        pause(pair)
        at = slice(pair * 128, pair * 128 + 128)
        q2 = q_ref[0, :, at] * BF(0.125)
        k2 = k_ref[0, :, at]
        v2 = v_ref[0, :, at]
        do2 = cback_ref[s, g, :, at]
        dq = None
        for t in range(length // tile):
            rows = slice(t * tile, (t + 1) * tile)
            dks, dvs = [], []
            for h in range(2):
                mine = low[rows] if h == 0 else ~low[rows]
                km = jnp.where(mine, k2[rows], BF(0))
                vm = jnp.where(mine, v2[rows], BF(0))
                head = g * (GROUP // HEAD_DIM) + pair * 2 + h
                lse = lse_ref[0, pl.ds(head, 1), :]
                rowdot = rowdot_ref[s, pl.ds(head, 1), :]
                probs = jnp.exp(dot_nt(km, q2) + bias_ref[rows, :] - lse)
                dprobs = dot_nt(vm, do2)
                dscore = (probs * (dprobs - rowdot)).astype(BF)
                dvs.append(dot(probs.astype(BF), do2))
                dks.append(dot(dscore, q2))
                part = dot_tn(dscore, km * BF(0.125))
                dq = part if dq is None else dq + part
            dk = jnp.where(low[rows], dks[0], dks[1])
            dv = jnp.where(low[rows], dvs[0], dvs[1])
            jlow_ref[0, rows, GROUP + pair * 128 : GROUP + pair * 128 + 128] = dk.astype(BF)
            jlow_ref[0, rows, 2 * GROUP + pair * 128 : 2 * GROUP + pair * 128 + 128] = dv.astype(BF)
            vsum = jnp.sum(dv, axis=0, keepdims=True)
            vtotal = vsum if t == 0 else vtotal + vsum
        jlow_ref[0, :, at] = dq.astype(BF)
        lanes = pl.ds(pl.multiple_of(g * GROUP + pair * 128, 128), 128)
        sums_ref[0:1, lanes] += jnp.sum(dq, axis=0, keepdims=True)
        sums_ref[1:2, lanes] += vtotal

    part = dot_tn(tokens_ref[0], jlow_ref[0])

    @pl.when(s == 0)
    def _():
        acc[...] = part

    @pl.when(s > 0)
    def _():
        acc[...] += part


def late_back(second, pre_low, norm, inv, ctx, up_bin, out_bin, small, tokens, block_ids, joined, lse, sums, feed_grads=None):
    seqs, length, width = tokens.shape
    groups = width // GROUP
    linked = feed_grads is not None
    first = seqs * HALVES
    phase = lambda i: (i + 64 - first) // 64
    seq_one = lambda i: i + phase(i) * (first - 1 - i)
    seq_two = lambda i: phase(i) * ((i - first + seqs * first) % seqs)
    group_two = lambda i: phase(i) * ((i - first) // seqs)
    some = length // HALVES
    second, pre_low, norm, inv, ctx = (a.reshape(first, some, a.shape[2]) for a in (second, pre_low, norm, inv, ctx))
    one = lambda *shape: pl.BlockSpec((1,) + shape, lambda i: (seq_one(i),) + (0,) * len(shape))
    two = lambda *shape: pl.BlockSpec((1,) + shape, lambda i: (seq_two(i),) + (0,) * len(shape))
    part = lambda k: pl.BlockSpec((1, length, GROUP), lambda i: (seq_two(i), 0, k * groups + group_two(i)))
    held = lambda a: pl.BlockSpec(a.shape, lambda i: (0,) * a.ndim, pipeline_mode=pl.Buffered(1))
    anywhere = pl.BlockSpec(memory_space=pl.ANY)
    unit = (width, width // 2)
    like = jax.ShapeDtypeStruct
    in_specs = [
        one(some, width), one(some, pre_low.shape[2]), one(some, width), one(some, 1), one(some, width),
        held(up_bin), held(out_bin), held(small),
        two(length, width), held(block_ids), part(0), part(1), part(2), two(16, length), held(sums),
    ]
    operands = [
        second, pre_low, norm, inv, ctx, up_bin, out_bin, small,
        tokens, block_ids, joined, joined, joined, lse, sums,
    ]
    out_specs = [one(some, width), pl.BlockSpec((1, length, 3 * GROUP), lambda i: (seq_two(i), 0, group_two(i)))]
    out_shape = [like((first, some, width), BF), like((seqs, length, 3 * width), BF)]
    scratch = [
        pltpu.VMEM((seqs, groups, length, GROUP), BF), pltpu.VMEM((seqs, 16, length), F32),
        pltpu.VMEM((width, width), F32), pltpu.VMEM((length, length), F32),
    ]
    if linked:
        units = feed_grads[0].shape[0] + 1 + groups
        in_specs += [anywhere] * 2
        operands += feed_grads
        out_specs += [anywhere, full(sums.shape)]
        out_shape += [like((units,) + unit, BF), like(sums.shape, F32)]
        scratch += [pltpu.VMEM((1 + groups,) + unit, BF)] + Exchange.buffers(LOTS, units, *unit, sums.shape)
        extra = dict(collective_id=0, has_side_effects=True)
    else:
        out_specs += [full((1 + groups,) + unit)] * 2 + [full(sums.shape)]
        out_shape += [like((1 + groups,) + unit, BF)] * 2 + [like(sums.shape, F32)]
        extra = {}
    return pl.pallas_call(
        functools.partial(late_back_kernel, linked, seqs, groups),
        grid=(seqs * (HALVES + groups),),
        in_specs=in_specs,
        out_specs=out_specs,
        out_shape=out_shape,
        scratch_shapes=scratch,
        compiler_params=params(58, **extra),
        cost_estimate=cost(seqs * length * width * (20 * width + 40 * length), 70 * seqs * length * width),
        name="late_back",
    )(*operands)


def token_total(resid_ref, jlow_ref, qkv_ref):
    width = resid_ref.shape[2]
    groups = width // GROUP
    total = resid_ref[0].astype(F32)
    for g in range(groups):
        for k in range(3):
            at = (3 * g + k) * GROUP
            col = k * width + g * GROUP
            total = total + dot_nt(jlow_ref[0, :, at : at + GROUP], qkv_ref[:, col : col + GROUP])
    return total


def token_kernel(resid_ref, jlow_ref, qkv_ref, grad_ref):
    grad_ref[0] = token_total(resid_ref, jlow_ref, qkv_ref)


def finish_kernel(
    core_ref, resid_ref, jlow_ref, qkv_bin_ref, feed_ref, out_unit_ref, qkv_unit_ref, sums_ref,
    grad_ref, qkv_ref, out_ref, up_ref, dn_ref, bias_ref, hidden_ref, gain_ref, shift_ref,
    up_stage, qkv_stage, up_sem, qkv_sem,
):
    step, last = pl.program_id(0), up_sem.shape[0] - 1
    _, rows, half = feed_ref.shape
    groups = qkv_sem.shape[0]
    parts = (slice(0, half), slice(half, rows))

    def up_copy(c, p):
        at = pl.ds(pl.multiple_of((p * (last + 1) + c) * half, half), half)
        return pltpu.make_async_copy(up_stage.at[c, p], up_ref.at[:, at], up_sem.at[c, p])

    def qkv_copy(g, k):
        at = pl.ds(pl.multiple_of(k * rows + g * GROUP, GROUP), GROUP)
        return pltpu.make_async_copy(qkv_stage.at[g, k], qkv_ref.at[:, at], qkv_sem.at[g, k])

    for p in range(2):
        up_stage[step, p] = feed_ref[1, parts[p], :].astype(F32)
        up_copy(step, p).start()
        dn_ref[:, parts[p]] = feed_ref[0, parts[p], :].astype(F32)

    @pl.when(step == 0)
    def _():
        for p in range(2):
            out_ref[:, parts[p]] = out_unit_ref[0, parts[p], :].astype(F32)
        mine = pl.ds(pl.multiple_of(core_ref[0] * half, half), half)
        total = sums_ref[:, mine]
        bias_ref[...] = total[0:4]
        gain_ref[...] = total[4:6]
        shift_ref[...] = total[6:8]
        for c in range(last + 1):
            for j in range(half // 128):
                at = c * (half // 128) + j
                hidden_ref[at : at + 1, :] = total[8 + c : 9 + c, j * 128 : (j + 1) * 128]

    @pl.when(step > 0)
    def _():
        for j in range(3 * GROUP // 128):
            col = j * 128
            qkv_stage[step - 1, col // GROUP, :, col % GROUP : col % GROUP + 128] = qkv_unit_ref[
                0, parts[col // half], col % half : col % half + 128
            ].astype(F32)
        for k in range(3):
            qkv_copy(step - 1, k).start()

    grad_ref[0] = token_total(resid_ref, jlow_ref, qkv_bin_ref)

    @pl.when(step == last)
    def _():
        for c in range(up_sem.shape[0]):
            for p in range(2):
                up_copy(c, p).wait()
        for g in range(groups):
            for k in range(3):
                qkv_copy(g, k).wait()


def finish(core, resid, jlow, qkv_bin, units, sums):
    seqs, length, width = resid.shape
    count, rows, half = units.shape
    groups = rows // GROUP
    chunks = (count - 1 - groups) // 2
    assert chunks == seqs and groups == seqs - 1
    per_seq = lambda *shape: pl.BlockSpec((1,) + shape, lambda s, _: (s,) + (0,) * len(shape))
    late = lambda s: s - (s + 63) // 64
    like = lambda *shape: jax.ShapeDtypeStruct(shape, F32)
    anywhere = pl.BlockSpec(memory_space=pl.ANY)
    return pl.pallas_call(
        finish_kernel,
        grid_spec=pltpu.PrefetchScalarGridSpec(
            num_scalar_prefetch=1,
            grid=(chunks,),
            in_specs=[
                per_seq(length, width),
                per_seq(length, 3 * width),
                full(qkv_bin.shape),
                pl.BlockSpec((2, rows, half), lambda s, _: (s, 0, 0)),
                pl.BlockSpec((1, rows, half), lambda s, _: (2 * chunks, 0, 0)),
                pl.BlockSpec((1, rows, half), lambda s, _: (2 * chunks + 1 + late(s), 0, 0)),
                full(sums.shape),
            ],
            out_specs=[
                per_seq(length, width),
                anywhere,
                full((half, rows)),
                anywhere,
                pl.BlockSpec((half, rows), lambda s, _: (s, 0)),
                full((4, half)),
                full((chunks * half // 128, 128)),
                full((2, half)),
                full((2, half)),
            ],
            scratch_shapes=[
                pltpu.VMEM((chunks, 2, half, half), F32),
                pltpu.VMEM((groups, 3, half, GROUP), F32),
                pltpu.SemaphoreType.DMA((chunks, 2)),
                pltpu.SemaphoreType.DMA((groups, 3)),
            ],
        ),
        out_shape=[
            like(seqs, length, width), like(half, 3 * rows), like(half, rows), like(half, 2 * chunks * half),
            like(chunks * half, rows), like(4, half), like(chunks * half // 128, 128), like(2, half), like(2, half),
        ],
        compiler_params=params(),
        cost_estimate=cost(6 * seqs * length * width * width, 16 * seqs * length * width),
        name="finish",
    )(core, resid, jlow, qkv_bin, units, units, units, sums)


def token_back(resid, jlow, qkv_bin):
    seqs, length, width = resid.shape
    per_seq = lambda *shape: pl.BlockSpec((1,) + shape, lambda s: (s,) + (0,) * len(shape))
    return pl.pallas_call(
        token_kernel,
        grid=(seqs,),
        in_specs=[per_seq(length, width), per_seq(length, 3 * width), full(qkv_bin.shape)],
        out_specs=per_seq(length, width),
        out_shape=jax.ShapeDtypeStruct((seqs, length, width), F32),
        compiler_params=params(),
        cost_estimate=cost(6 * seqs * length * width * width, 16 * seqs * length * width),
        name="token_back",
    )(resid, jlow, qkv_bin)


def swap(value):
    return lax.ppermute(value, "shard", [(0, 1), (1, 0)])


def small_rows(biases, gain, shift, hidden_bias):
    rows = biases.shape[0]
    return jnp.concatenate([biases.T, gain.T, shift.T, hidden_bias.reshape(-1, rows)], axis=0)


def reduce_plain(feed_grads, out_grads, qkv_grads, sums):
    def whole(mine, theirs):
        count, rows, half = mine.shape
        cut = lambda a: a.reshape(count, 2, half, half).transpose(0, 2, 1, 3).reshape(count, half, rows)
        return jnp.concatenate([cut(mine), cut(theirs)], axis=1)

    feed_all, out_all, qkv_all = whole(*feed_grads), whole(*out_grads), whole(*qkv_grads)
    chunks, groups, width = feed_all.shape[0] // 2, qkv_all.shape[0], feed_all.shape[2]
    half, units = width // 2, chunks * width
    grads = (
        qkv_all.reshape(groups, width, 3, GROUP).transpose(1, 2, 0, 3).reshape(width, 3 * width),
        out_all[0],
        feed_all[1::2].reshape(chunks, width, 2, half).transpose(1, 2, 0, 3).reshape(width, units),
        feed_all[0::2].reshape(chunks, 2, half, width).transpose(1, 0, 2, 3).reshape(units, width),
        sums[0:4].T.astype(BF),
        sums[8:].reshape(chunks, 2, half).transpose(1, 0, 2).reshape(-1).astype(BF),
        sums[4:6].T.astype(BF),
        sums[6:8].T.astype(BF),
    )
    owned = lax.psum_scatter(grads, "shard", scatter_dimension=0, tiled=True)
    return jax.tree.map(lambda part: part.astype(F32), lax.psum(owned, "rep"))


def body(tokens, teacher, block_ids, *weights):
    qkv, out, up, down, biases, hidden_bias, gain, shift = weights
    paired = lax.axis_size("shard") == 2 and lax.axis_size("rep") == 16
    if paired:
        core = lax.axis_index("shard").reshape(1)
        small = small_rows(biases, gain, shift, hidden_bias)
        small, qkv, out = ((a, swap(a)) for a in (small, qkv, out))
        up, down, _, _ = lax.optimization_barrier((up, down, qkv[1], small[1]))
        up, down = ((a, swap(a)) for a in (up, down))
    else:
        core = jnp.zeros((1,), jnp.int32)
        gathered = [lax.all_gather(w, "shard", axis=0, tiled=True) for w in weights]
        qkv, out, up, down, *rest = (jnp.split(w, 2, axis=0) for w in gathered)
        small = [small_rows(rest[0][i], rest[2][i], rest[3][i], rest[1][i]) for i in range(2)]
    joined, ctx, lse, norm, inv, small, qkv_bin, out_bin = attend(core, tokens, block_ids, qkv, out, small)
    final, first_low, hidden, slope, second, mixed, sums, up_bin, dn_bin = feed(core, norm, teacher, small, up, down)
    pre_low, *feed_grads, sums = feed_back(core, mixed, first_low, hidden, slope, dn_bin, sums)
    pre_low = pre_low.reshape(hidden.shape)
    operands = (second, pre_low, norm, inv, ctx, up_bin, out_bin, small, tokens, block_ids, joined, lse, sums)
    if not paired:
        resid, jlow, *grads, sums = late_back(*operands)
        token_grad = token_back(resid.reshape(tokens.shape), jlow, qkv_bin)
        out_grads, qkv_grads = ([a[cut] for a in grads] for cut in (slice(0, 1), slice(1, None)))
        return (final, token_grad) + tuple(reduce_plain(feed_grads, out_grads, qkv_grads, sums[:12]))
    resid, jlow, units, sums = late_back(*operands, feed_grads)
    resid = resid.reshape(tokens.shape)
    token_grad, *grads, bias, hidden, gains, shifts = finish(core, resid, jlow, qkv_bin, units, sums)
    return (final, token_grad, *grads, bias.T, hidden.reshape(-1), gains.T, shifts.T)


def solution(mesh):
    placed = (
        P(("shard", "rep"), None, None),
        P(("shard", "rep"), None, None),
        P(("shard", "rep"), None),
        P("shard", None),
        P("shard", None),
        P("shard", None),
        P("shard", None),
        P("shard", None),
        P("shard"),
        P("shard", None),
        P("shard", None),
    )
    return jax.shard_map(
        body,
        mesh=mesh,
        in_specs=placed,
        out_specs=placed[:2] + placed[3:],
        check_vma=False,
    )
```
